32 devices in a mesh: fsdp: 8 (over y, x, core), sp: 4 (over z).
Axes of the slice: x: 2, y: 2, z: 4, core: 2. Of those that a mesh axis runs over, the one named last changes fastest.
Arguments:
- hidden_in: bfloat16 [4096, 2048], P(('fsdp', 'sp')), may hold values from -6 to 6
- grad_out: bfloat16 [4096, 2048], P(('fsdp', 'sp')), may hold values from -6 to 6
- lengths: int32 [5], replicated, may hold values from 1 to 2048, 4096 in all
- attn_gain: bfloat16 [2048], P('fsdp'), may hold values from 0.25 to 1.75
- w_qkv: bfloat16 [4096, 2048], P('fsdp'), may hold values from -0.125 to 0.125
- w_head_gate: bfloat16 [16, 2048], P('fsdp'), may hold values from -0.125 to 0.125
- q_gain: bfloat16 [128], P('fsdp'), may hold values from 0.25 to 1.75
- k_gain: bfloat16 [128], P('fsdp'), may hold values from 0.25 to 1.75
- w_out: bfloat16 [2048, 2048], P('fsdp'), may hold values from -2.5 to 2.5
- ffn_gain: bfloat16 [2048], P('fsdp'), may hold values from 0.25 to 1.75
- w_gate: bfloat16 [6144, 2048], P('fsdp'), may hold values from -0.125 to 0.125
- w_up: bfloat16 [6144, 2048], P('fsdp'), may hold values from -0.125 to 0.125
- w_down: bfloat16 [6144, 2048], P('fsdp'), may hold values from -0.078125 to 0.078125
Outputs:
- hidden_out: bfloat16 [4096, 2048], P(('fsdp', 'sp'))
- grad_in: float32 [4096, 2048], P(('fsdp', 'sp'))
- grad_attn_gain: float32 [2048], P('fsdp')
- grad_w_qkv: float32 [4096, 2048], P('fsdp')
- grad_w_head_gate: float32 [16, 2048], P('fsdp')
- grad_q_gain: float32 [128], P('fsdp')
- grad_k_gain: float32 [128], P('fsdp')
- grad_w_out: float32 [2048, 2048], P('fsdp')
- grad_ffn_gain: float32 [2048], P('fsdp')
- grad_w_gate: float32 [6144, 2048], P('fsdp')
- grad_w_up: float32 [6144, 2048], P('fsdp')
- grad_w_down: float32 [6144, 2048], P('fsdp')
The draws below stay inside these ranges and needn't reach their ends.
Inputs may be any that keep to these rules, and one draw needn't show every extreme that they name: The 5 items are packed in token order; their lengths sum to 4096 and the longest is exactly 2048.
All inputs are finite; a program needn't handle non-finite values.
Results may differ from the reference program's by a relative error of at most 0.015.
Values may be sent and summed in bfloat16 or wider, within the bound.
A program may use at most 768 MiB of HBM per device.

```python
import math
import jax
import jax.numpy as jnp
import numpy as np
from jax import lax

D = 2048
HEADS = 16
KV_HEADS = 8
HEAD_DIM = 128
FF = 6144
ITEMS = 5
QKV_ROWS = 4096
TOKENS = 4096
LONGEST = 2048


def shard_levels(own_key, shape, shards, least, largest):
    gain = 1.0
    for dim, blocks in shards:
        draws = jax.random.uniform(jax.random.fold_in(jax.random.fold_in(own_key, 6), dim), (blocks,), jnp.float32, least / len(shards), largest / len(shards))
        gain = gain * jnp.repeat(jnp.exp(draws), shape[dim] // blocks).reshape((-1,) + (1,) * (len(shape) - 1 - dim))
    return gain


def length_profile(count, total, limit, lean):
    weights = [(1 << 20) // math.isqrt(rank ** lean) + 1 for rank in range(2, count + 1)]
    surplus, counts = total - limit - (count - 1), [1] * (count - 1)
    while surplus > 0:
        free = [i for i in range(count - 1) if counts[i] < limit]
        mass, budget = sum([weights[i] for i in free]), surplus
        for i in free:
            addition = min(limit - counts[i], max(1, budget * weights[i] // mass), surplus)
            counts[i] = counts[i] + addition
            surplus = surplus - addition
    return np.array([limit] + counts)


def ragged(rng, amount, total, reach, lean):
    if amount == 2:
        one = jax.random.randint(rng, (), max(1, total - reach), min(reach, total - 1) + 1)
        return jnp.stack([one, total - one])
    tallies = jnp.asarray(length_profile(amount, total, reach, lean), jnp.int32)
    twos = (amount - 1) // 2
    source_of, receiver = tallies[1:1 + 2 * twos:2], tallies[2:2 + 2 * twos:2]
    room = jnp.minimum(source_of - 1, reach - receiver)
    moved = jax.random.randint(jax.random.fold_in(rng, 1), (twos,), 0, 1 << 20) % (room + 1)
    tallies = tallies.at[1:1 + 2 * twos:2].set(source_of - moved).at[2:2 + 2 * twos:2].set(receiver + moved)
    return tallies[jax.random.permutation(jax.random.fold_in(rng, 2), amount)]


def bell_draw(stream_key, dims, scale, limit, split=(), kind=jnp.bfloat16):
    loudness = shard_levels(stream_key, dims, split, -0.22, 0.18) if split else 1.0
    values = jax.random.normal(stream_key, dims, jnp.float32) * scale * loudness
    return jnp.minimum(jnp.maximum(values, -limit), limit).astype(kind)


def setup_inputs(seed: int = 0) -> dict:
    key_of = jax.random.split(jax.random.key(seed), 14)
    return {
        "hidden_in": bell_draw(key_of[0], (TOKENS, D), 1.0, 6.0, ((0, 32),)),
        "grad_out": bell_draw(key_of[1], (TOKENS, D), 1.0, 6.0, ((0, 32),)),
        "lengths": ragged(key_of[2], ITEMS, TOKENS, LONGEST, 0).astype(jnp.int32),
        "attn_gain": jnp.clip(1.0 + 0.15 * jax.random.normal(key_of[3], (D,), jnp.float32), 0.25, 1.75).astype(jnp.bfloat16),
        "w_qkv": bell_draw(key_of[4], (QKV_ROWS, D), D ** -0.5, 0.125, ((0, 8),)),
        "w_head_gate": bell_draw(key_of[5], (HEADS, D), D ** -0.5, 0.125, ((0, 8),)),
        "q_gain": jnp.clip(1.0 + 0.15 * jax.random.normal(key_of[6], (HEAD_DIM,), jnp.float32), 0.25, 1.75).astype(jnp.bfloat16),
        "k_gain": jnp.clip(1.0 + 0.15 * jax.random.normal(key_of[7], (HEAD_DIM,), jnp.float32), 0.25, 1.75).astype(jnp.bfloat16),
        "w_out": bell_draw(key_of[8], (HEADS * HEAD_DIM, D), 6 ** -0.5, 2.5, ((0, 8),)),
        "ffn_gain": jnp.clip(1.0 + 0.15 * jax.random.normal(key_of[9], (D,), jnp.float32), 0.25, 1.75).astype(jnp.bfloat16),
        "w_gate": bell_draw(key_of[10], (FF, D), D ** -0.5, 0.125, ((0, 8),)),
        "w_up": bell_draw(key_of[11], (FF, D), D ** -0.5, 0.125, ((0, 8),)),
        "w_down": bell_draw(key_of[12], (FF, D), FF ** -0.5, 0.078125, ((0, 8),)),
    }


@jax.custom_vjp
def low(v):
    return lax.optimization_barrier(v.astype(jnp.bfloat16)).astype(jnp.float32)

@jax.custom_vjp
def low_back(v):
    return v

def low_keep(v):
    return (low(v), None)

def low_pass(kept, grad):
    return (grad,)

def back_keep(v):
    return (v, None)

def back_low(kept, grad):
    return (low(grad),)
low.defvjp(low_keep, low_pass)
low_back.defvjp(back_keep, back_low)
EPS = 1e-06
ROPE_BASE = 1000000.0

def dot_high(factor, others):
    return jnp.dot(factor, others, precision=lax.Precision.HIGHEST)

def rms_norm(values, scaling):
    return values * lax.rsqrt(lax.optimization_barrier(jnp.mean(values * values, axis=-1, keepdims=True)) + EPS) * scaling

def item_starts(token_index, lengths):
    ends = jnp.cumsum(lengths).astype(jnp.int32)
    starts = (ends - lengths).astype(jnp.int32)
    inside = (token_index[:, None] >= starts[None, :]) & (token_index[:, None] < ends[None, :])
    return lax.optimization_barrier(jnp.sum(jnp.where(inside, starts[None, :], 0), axis=1)).astype(jnp.int32)

def rope_tables(position):
    half_dim = HEAD_DIM // 2
    freq_steps = jnp.arange(half_dim, dtype=jnp.float32)
    frequency = jnp.exp(-math.log(ROPE_BASE) * 2.0 * freq_steps / HEAD_DIM)
    angles = position.astype(jnp.float32)[:, None] * frequency[None, :]
    return (jnp.cos(angles)[:, None, :], jnp.sin(angles)[:, None, :])

def rotate(values, cosine, sine):
    half_dim = values.shape[-1] // 2
    lower = values[..., :half_dim]
    upper = values[..., half_dim:]
    return jnp.concatenate([lower * cosine - upper * sine, upper * cosine + lower * sine], axis=-1)

def attention(query, key, value, item_start):
    query_block = min(512, TOKENS)
    window = min(TOKENS, LONGEST + query_block)
    head_group = HEADS // KV_HEADS
    score_scale = HEAD_DIM ** (-0.5)
    block_count = TOKENS // query_block

    def one_block(index):
        zero_index = jnp.zeros((), jnp.int32)
        block_index = (index // HEADS).astype(jnp.int32)
        head_index = (index % HEADS).astype(jnp.int32)
        row_first = (block_index * query_block).astype(jnp.int32)
        win_first = jnp.clip(row_first + query_block - window, 0, TOKENS - window).astype(jnp.int32)
        kv_index = (head_index // head_group).astype(jnp.int32)
        query_rows = lax.dynamic_slice(query, (row_first, head_index, zero_index), (query_block, 1, HEAD_DIM))[:, 0]
        key_rows = lax.dynamic_slice(key, (win_first, kv_index, zero_index), (window, 1, HEAD_DIM))[:, 0]
        value_rows = lax.dynamic_slice(value, (win_first, kv_index, zero_index), (window, 1, HEAD_DIM))[:, 0]
        scores = low_back(dot_high(query_rows, key_rows.T) * score_scale)
        row_index = row_first + jnp.arange(query_block, dtype=jnp.int32)
        col_index = win_first + jnp.arange(window, dtype=jnp.int32)
        row_starts = lax.dynamic_slice(item_start, (row_first,), (query_block,))
        allowed = (col_index[None, :] <= row_index[:, None]) & (col_index[None, :] >= row_starts[:, None])
        weights = jnp.where(allowed, jnp.exp(scores), 0.0)
        totals = lax.optimization_barrier(jnp.sum(weights, axis=1, keepdims=True))
        unnormed = low_back(dot_high(low(weights), value_rows))
        return unnormed / totals
    result = lax.map(jax.checkpoint(one_block), jnp.arange(block_count * HEADS, dtype=jnp.int32))
    result = result.reshape(block_count, HEADS, query_block, HEAD_DIM).transpose(0, 2, 1, 3)
    return result.reshape(TOKENS, HEADS, HEAD_DIM)

def layer(inputs, attn_scale, qkv_weight, head_gate_weight, query_scale, key_scale, out_weight, ffn_scale, gate_weight, up_weight, down_weight, item_start, cosine, sine):
    query_width = HEADS * HEAD_DIM
    kv_width = KV_HEADS * HEAD_DIM
    normed_a = low(rms_norm(inputs, attn_scale))
    projected = low_back(dot_high(normed_a, qkv_weight.T))
    gate_logit = low_back(dot_high(normed_a, head_gate_weight.T))
    q_raw = projected[:, :query_width].reshape(TOKENS, HEADS, HEAD_DIM)
    k_raw = projected[:, query_width:query_width + kv_width].reshape(TOKENS, KV_HEADS, HEAD_DIM)
    v_raw = projected[:, query_width + kv_width:].reshape(TOKENS, KV_HEADS, HEAD_DIM)
    query = low(low_back(rotate(rms_norm(q_raw, query_scale), cosine, sine)))
    key = low(low_back(rotate(rms_norm(k_raw, key_scale), cosine, sine)))
    value = low(low_back(v_raw))
    attended = attention(query, key, value, item_start)
    sent = low(low_back(attended))
    gated = low((sent * jax.nn.sigmoid(gate_logit)[:, :, None]).reshape(TOKENS, query_width))
    middle = inputs + low_back(dot_high(gated, out_weight))
    normed_b = low(rms_norm(middle, ffn_scale))
    gate_pre = low_back(dot_high(normed_b, gate_weight.T))
    up_pre = low_back(dot_high(normed_b, up_weight.T))
    hidden = low(jax.nn.silu(gate_pre) * up_pre)
    return middle + low_back(dot_high(hidden, down_weight))

def reference(hidden_in, grad_out, lengths, attn_gain, w_qkv, w_head_gate, q_gain, k_gain, w_out, ffn_gain, w_gate, w_up, w_down):
    token_index = jnp.arange(TOKENS, dtype=jnp.int32)
    item_start = item_starts(token_index, lengths.astype(jnp.int32))
    cosine, sine = rope_tables(token_index - item_start)
    floats = tuple((array.astype(jnp.float32) for array in (hidden_in, attn_gain, w_qkv, w_head_gate, q_gain, k_gain, w_out, ffn_gain, w_gate, w_up, w_down)))

    def forward(inputs, attn_scale, qkv_weight, head_gate_weight, query_scale, key_scale, out_weight, ffn_scale, gate_weight, up_weight, down_weight):
        return layer(inputs, attn_scale, qkv_weight, head_gate_weight, query_scale, key_scale, out_weight, ffn_scale, gate_weight, up_weight, down_weight, item_start, cosine, sine)
    output, pullback = jax.vjp(forward, *floats)
    grads = pullback(grad_out.astype(jnp.float32))
    return (output.astype(jnp.bfloat16), grads[0], grads[1], grads[2], grads[3], grads[4], grads[5], grads[6], grads[7], grads[8], grads[9], grads[10])
```

```python
import functools
import math

import jax
import jax.numpy as jnp
from jax import lax
from jax.experimental import pallas as pl
from jax.experimental.pallas import tpu as pltpu
from jax.sharding import PartitionSpec as P

HEADS = 16
KV_HEADS = 8
HEAD_DIM = 128


EPS = 1e-06
ROPE_BASE = 1000000.0


def mat_nt(factor, others):
    return lax.dot_general(
        factor, others, (((1,), (1,)), ((), ())), preferred_element_type=jnp.float32
    )


def mat_tn(factor, others):
    return lax.dot_general(
        factor, others, (((0,), (0,)), ((), ())), preferred_element_type=jnp.float32
    )


def inv_rms(values):
    return lax.rsqrt(jnp.mean(values * values, axis=-1, keepdims=True) + EPS)


def norm_back(grad_norm, values, inverse, scaling):
    scaled = grad_norm * scaling
    cubed = inverse * inverse * inverse
    return inverse * scaled - values * cubed * jnp.mean(scaled * values, axis=-1, keepdims=True)


def item_starts(token_index, lengths):
    ends = jnp.cumsum(lengths)
    starts = ends - lengths
    inside = (token_index[:, None] >= starts[None, :]) & (token_index[:, None] < ends[None, :])
    return jnp.sum(jnp.where(inside, starts[None, :], 0), axis=1)


def rope_tables(position):
    half_dim = HEAD_DIM // 2
    freq_steps = jnp.arange(half_dim, dtype=jnp.float32)
    frequency = jnp.exp(-math.log(ROPE_BASE) * 2.0 * freq_steps / HEAD_DIM)
    angles = position.astype(jnp.float32)[:, None] * frequency[None, :]
    return (jnp.cos(angles)[:, None, :], jnp.sin(angles)[:, None, :])


def rotate(values, cosine, sine):
    half_dim = values.shape[-1] // 2
    lower = values[..., :half_dim]
    upper = values[..., half_dim:]
    return jnp.concatenate([lower * cosine - upper * sine, upper * cosine + lower * sine], axis=-1)


def rotate_back(grad_rot, cosine, sine):
    half_dim = grad_rot.shape[-1] // 2
    lower = grad_rot[..., :half_dim]
    upper = grad_rot[..., half_dim:]
    return jnp.concatenate([lower * cosine + upper * sine, upper * cosine - lower * sine], axis=-1)


def local(
    hidden_in,
    grad_out,
    lengths,
    attn_gain,
    w_qkv,
    w_head_gate,
    q_gain,
    k_gain,
    w_out,
    ffn_gain,
    w_gate,
    w_up,
    w_down,
):
    fsdp_count = lax.axis_size("fsdp")
    sp_count = lax.axis_size("sp")
    fsdp_rank = lax.axis_index("fsdp")
    sp_rank = lax.axis_index("sp")
    tok_rows = hidden_in.shape[0]
    model_width = hidden_in.shape[1]
    query_width = HEADS * HEAD_DIM
    kv_width = KV_HEADS * HEAD_DIM
    local_kv = KV_HEADS // sp_count
    head_group = HEADS // KV_HEADS
    score_scale = HEAD_DIM ** (-0.5)
    qkv_full, out_full, gate_full, attn_gain_full, q_gain_full, k_gain_full, ffn_gain_full = (
        lax.all_gather(w_qkv, "fsdp", axis=0, tiled=True),
        lax.all_gather(w_out, "fsdp", axis=0, tiled=True),
        lax.all_gather(w_head_gate, "fsdp", axis=0, tiled=True),
        lax.all_gather(attn_gain, "fsdp", axis=0, tiled=True),
        lax.all_gather(q_gain, "fsdp", axis=0, tiled=True),
        lax.all_gather(k_gain, "fsdp", axis=0, tiled=True),
        lax.all_gather(ffn_gain, "fsdp", axis=0, tiled=True),
    )
    attn_scale = attn_gain_full.astype(jnp.float32)
    query_scale = q_gain_full.astype(jnp.float32)
    key_scale = k_gain_full.astype(jnp.float32)
    ffn_scale = ffn_gain_full.astype(jnp.float32)
    token_first = (fsdp_rank * sp_count + sp_rank) * tok_rows
    own_tokens = token_first + jnp.arange(tok_rows, dtype=jnp.int32)
    cosine, sine = rope_tables(own_tokens - item_starts(own_tokens, lengths))
    inputs = hidden_in.astype(jnp.float32)
    inv_first = inv_rms(inputs)
    normed_a = (inputs * inv_first * attn_scale).astype(jnp.bfloat16)
    projected = mat_nt(normed_a, qkv_full)
    gate_logit = mat_nt(normed_a, gate_full)
    q_raw = projected[:, :query_width].reshape(tok_rows, HEADS, HEAD_DIM)
    k_raw = projected[:, query_width : query_width + kv_width].reshape(tok_rows, KV_HEADS, HEAD_DIM)
    q_inv = inv_rms(q_raw)
    k_inv = inv_rms(k_raw)
    query = (
        rotate(q_raw * q_inv * query_scale, cosine, sine)
        .reshape(tok_rows, query_width)
        .astype(jnp.bfloat16)
    )
    keys = (
        rotate(k_raw * k_inv * key_scale, cosine, sine)
        .reshape(tok_rows, kv_width)
        .astype(jnp.bfloat16)
    )
    values = projected[:, query_width + kv_width :].astype(jnp.bfloat16)
    query_heads, key_heads, value_heads = (
        lax.all_to_all(query, "sp", split_axis=1, concat_axis=0, tiled=True),
        lax.all_to_all(keys, "sp", split_axis=1, concat_axis=0, tiled=True),
        lax.all_to_all(values, "sp", split_axis=1, concat_axis=0, tiled=True),
    )
    key_all, value_all = (
        lax.all_gather(key_heads, "fsdp", axis=0, tiled=True),
        lax.all_gather(value_heads, "fsdp", axis=0, tiled=True),
    )
    span_rows = query_heads.shape[0]
    span_first = fsdp_rank * span_rows
    span_tokens = span_first + jnp.arange(span_rows, dtype=jnp.int32)
    span_starts = item_starts(span_tokens, lengths)
    query_four = query_heads.reshape(span_rows, local_kv, head_group, HEAD_DIM)
    key_total = key_all.shape[0]
    key_block = min(1024, key_total)
    block_count = key_total // key_block
    key_blocks = key_all.reshape(block_count, key_block, local_kv, HEAD_DIM)
    value_blocks = value_all.reshape(block_count, key_block, local_kv, HEAD_DIM)
    block_firsts = jnp.arange(block_count, dtype=jnp.int32) * key_block
    lowest_key = span_starts[0]
    highest_key = span_first + span_rows - 1

    def needed(block_first):
        return (block_first <= highest_key) & (block_first + key_block - 1 >= lowest_key)

    def block_weights(key_piece, block_first):
        scores = (
            jnp.einsum("qkgd,jkd->kgqj", query_four, key_piece, preferred_element_type=jnp.float32)
            * score_scale
        )
        columns = block_first + jnp.arange(key_block, dtype=jnp.int32)
        allowed = (columns[None, :] <= span_tokens[:, None]) & (
            columns[None, :] >= span_starts[:, None]
        )
        return jnp.where(allowed[None, None], jnp.exp(scores), 0.0)

    def forward_step(running, pieces):
        key_piece, value_piece, block_first = pieces

        def forward_compute(current):
            totals, unnormed = current
            weights = block_weights(key_piece, block_first)
            totals = totals + jnp.sum(weights, axis=3)
            unnormed = unnormed + jnp.einsum(
                "kgqj,jkd->qkgd",
                weights.astype(jnp.bfloat16),
                value_piece,
                preferred_element_type=jnp.float32,
            )
            return (totals, unnormed)

        return (
            lax.cond(needed(block_first), forward_compute, lambda current: current, running),
            None,
        )

    start_state = (
        jnp.zeros((local_kv, head_group, span_rows), jnp.float32),
        jnp.zeros((span_rows, local_kv, head_group, HEAD_DIM), jnp.float32),
    )
    scanned = lax.scan(forward_step, start_state, (key_blocks, value_blocks, block_firsts))[0]
    totals, unnormed = scanned
    totals_rows = jnp.transpose(totals, (2, 0, 1))[..., None]
    attended_heads = unnormed / totals_rows
    attended_send = attended_heads.reshape(span_rows, local_kv * head_group * HEAD_DIM).astype(
        jnp.bfloat16
    )
    returned = lax.all_to_all(attended_send, "sp", split_axis=0, concat_axis=1, tiled=True)
    gate_prob = jax.nn.sigmoid(gate_logit)
    attended_tok = returned.astype(jnp.float32).reshape(tok_rows, HEADS, HEAD_DIM)
    gated = (
        (attended_tok * gate_prob[:, :, None]).reshape(tok_rows, query_width).astype(jnp.bfloat16)
    )
    middle = inputs + jnp.dot(gated, out_full, preferred_element_type=jnp.float32)
    inv_second = inv_rms(middle)
    normed_b = (middle * inv_second * ffn_scale).astype(jnp.bfloat16)
    gate_piece = lax.all_gather(w_gate, "fsdp", axis=0, tiled=True)
    up_piece = lax.all_gather(w_up, "fsdp", axis=0, tiled=True)
    down_piece = lax.all_gather(w_down, "fsdp", axis=0, tiled=True)
    gate_pre = mat_nt(normed_b, gate_piece)
    up_pre = mat_nt(normed_b, up_piece)
    hidden = (jax.nn.silu(gate_pre) * up_pre).astype(jnp.bfloat16)
    ffn_part = jnp.dot(hidden, down_piece, preferred_element_type=jnp.float32)
    hidden_out = (middle + ffn_part).astype(jnp.bfloat16)
    gate_piece = lax.all_gather(w_gate, "fsdp", axis=0, tiled=True)
    up_piece = lax.all_gather(w_up, "fsdp", axis=0, tiled=True)
    down_piece = lax.all_gather(w_down, "fsdp", axis=0, tiled=True)
    gate_pre = mat_nt(normed_b, gate_piece)
    up_pre = mat_nt(normed_b, up_piece)
    sigma = jax.nn.sigmoid(gate_pre)
    swish = gate_pre * sigma
    hidden = (swish * up_pre).astype(jnp.bfloat16)
    grad_hidden = mat_nt(grad_out, down_piece)
    grad_gate = (grad_hidden * up_pre * sigma * (1.0 + gate_pre * (1.0 - sigma))).astype(
        jnp.bfloat16
    )
    grad_up = (grad_hidden * swish).astype(jnp.bfloat16)
    grad_acc = jnp.dot(grad_gate, gate_piece, preferred_element_type=jnp.float32) + jnp.dot(
        grad_up, up_piece, preferred_element_type=jnp.float32
    )
    grad_ffn_gain_local = jnp.sum(grad_acc * middle * inv_second, axis=0)
    grad_middle = grad_out.astype(jnp.float32) + norm_back(grad_acc, middle, inv_second, ffn_scale)
    grad_mid_b = grad_middle.astype(jnp.bfloat16)
    grad_gated = mat_nt(grad_mid_b, out_full).reshape(tok_rows, HEADS, HEAD_DIM)
    grad_attended = (
        (grad_gated * gate_prob[:, :, None]).reshape(tok_rows, query_width).astype(jnp.bfloat16)
    )
    gate_grad = (jnp.sum(grad_gated * attended_tok, axis=2) * gate_prob * (1.0 - gate_prob)).astype(
        jnp.bfloat16
    )
    grad_heads = lax.all_to_all(grad_attended, "sp", split_axis=1, concat_axis=0, tiled=True)
    grad_four = grad_heads.astype(jnp.float32).reshape(span_rows, local_kv, head_group, HEAD_DIM)
    grad_scaled = (grad_four / totals_rows).astype(jnp.bfloat16)
    delta_rows = jnp.sum(grad_four * attended_heads, axis=3) / totals_rows[..., 0]
    delta_heads = jnp.transpose(delta_rows, (1, 2, 0))

    def backward_step(grad_query, pieces):
        key_piece, value_piece, block_first = pieces

        def backward_compute(current):
            weights = block_weights(key_piece, block_first)
            grad_prob = jnp.einsum(
                "qkgd,jkd->kgqj", grad_scaled, value_piece, preferred_element_type=jnp.float32
            )
            grad_score = (weights * (grad_prob - delta_heads[..., None])).astype(jnp.bfloat16)
            current = (
                current
                + jnp.einsum(
                    "kgqj,jkd->qkgd", grad_score, key_piece, preferred_element_type=jnp.float32
                )
                * score_scale
            )
            grad_key = (
                jnp.einsum(
                    "kgqj,qkgd->jkd", grad_score, query_four, preferred_element_type=jnp.float32
                )
                * score_scale
            )
            grad_value = jnp.einsum(
                "kgqj,qkgd->jkd",
                weights.astype(jnp.bfloat16),
                grad_scaled,
                preferred_element_type=jnp.float32,
            )
            return (current, (grad_key, grad_value))

        def skip(current):
            nothing = jnp.zeros((key_block, local_kv, HEAD_DIM), jnp.float32)
            return (current, (nothing, nothing))

        return lax.cond(needed(block_first), backward_compute, skip, grad_query)

    grad_query, key_value_grads = lax.scan(
        backward_step,
        jnp.zeros((span_rows, local_kv, head_group, HEAD_DIM), jnp.float32),
        (key_blocks, value_blocks, block_firsts),
    )
    key_grads, value_grads = key_value_grads
    key_sum, value_sum = (
        lax.psum_scatter(
            key_grads.reshape(key_total, local_kv * HEAD_DIM),
            "fsdp",
            scatter_dimension=0,
            tiled=True,
        ),
        lax.psum_scatter(
            value_grads.reshape(key_total, local_kv * HEAD_DIM),
            "fsdp",
            scatter_dimension=0,
            tiled=True,
        ),
    )
    query_send = grad_query.reshape(span_rows, local_kv * head_group * HEAD_DIM).astype(
        jnp.bfloat16
    )
    back_query, back_key, back_value = (
        lax.all_to_all(query_send, "sp", split_axis=0, concat_axis=1, tiled=True),
        lax.all_to_all(key_sum.astype(jnp.bfloat16), "sp", split_axis=0, concat_axis=1, tiled=True),
        lax.all_to_all(
            value_sum.astype(jnp.bfloat16), "sp", split_axis=0, concat_axis=1, tiled=True
        ),
    )
    grad_qn = rotate_back(
        back_query.astype(jnp.float32).reshape(tok_rows, HEADS, HEAD_DIM), cosine, sine
    )
    grad_kn = rotate_back(
        back_key.astype(jnp.float32).reshape(tok_rows, KV_HEADS, HEAD_DIM), cosine, sine
    )
    grad_q_gain_local = jnp.sum(grad_qn * q_raw * q_inv, axis=(0, 1))
    grad_k_gain_local = jnp.sum(grad_kn * k_raw * k_inv, axis=(0, 1))
    grad_q_raw = norm_back(grad_qn, q_raw, q_inv, query_scale).reshape(tok_rows, query_width)
    grad_k_raw = norm_back(grad_kn, k_raw, k_inv, key_scale).reshape(tok_rows, kv_width)
    grad_proj = jnp.concatenate(
        [grad_q_raw.astype(jnp.bfloat16), grad_k_raw.astype(jnp.bfloat16), back_value], axis=1
    )
    grad_normed_a = jnp.dot(grad_proj, qkv_full, preferred_element_type=jnp.float32) + jnp.dot(
        gate_grad, gate_full, preferred_element_type=jnp.float32
    )
    grad_attn_gain_local = jnp.sum(grad_normed_a * inputs * inv_first, axis=0)
    grad_in = grad_middle + norm_back(grad_normed_a, inputs, inv_first, attn_scale)
    qkv_rows = w_qkv.shape[0]
    out_rows = w_out.shape[0]
    gate_rows = w_head_gate.shape[0]
    block_rows = qkv_rows + out_rows + gate_rows + 3
    small_rows = jnp.stack(
        [
            grad_attn_gain_local,
            grad_ffn_gain_local,
            jnp.concatenate(
                [
                    grad_q_gain_local,
                    grad_k_gain_local,
                    jnp.zeros((model_width - 2 * HEAD_DIM,), jnp.float32),
                ]
            ),
        ],
        axis=0,
    )
    ffn_partial = lax.psum_scatter(
        jnp.concatenate(
            [mat_tn(grad_gate, normed_b), mat_tn(grad_up, normed_b), mat_tn(hidden, grad_out)],
            axis=1,
        ).astype(jnp.bfloat16),
        "fsdp",
        scatter_dimension=0,
        tiled=True,
    ).astype(jnp.float32)
    proj_split = grad_proj.reshape(tok_rows, fsdp_count, qkv_rows)
    gated_split = gated.reshape(tok_rows, fsdp_count, out_rows)
    gate_split = gate_grad.reshape(tok_rows, fsdp_count, gate_rows)
    owners = block_rows * lax.axis_size("fsdp") // block_rows
    qkv_term = jnp.einsum("tor,td->ord", proj_split, normed_a, preferred_element_type=jnp.float32)
    out_term = jnp.einsum(
        "tor,td->ord", gated_split, grad_mid_b, preferred_element_type=jnp.float32
    )
    gate_term = jnp.einsum("tor,td->ord", gate_split, normed_a, preferred_element_type=jnp.float32)
    small_term = jnp.broadcast_to(small_rows[None], (owners, 3, model_width))
    joined = jnp.concatenate([qkv_term, out_term, gate_term, small_term], axis=1)
    attn_partial = lax.psum_scatter(
        joined.reshape(owners * block_rows, model_width), "fsdp", scatter_dimension=0, tiled=True
    )
    ffn_total, attn_total = lax.psum((ffn_partial, attn_partial), "sp")
    grad_w_gate = ffn_total[:, :model_width]
    grad_w_up = ffn_total[:, model_width : 2 * model_width]
    grad_w_down = ffn_total[:, 2 * model_width :]
    grad_w_qkv = attn_total[:qkv_rows]
    grad_w_out = attn_total[qkv_rows : qkv_rows + out_rows]
    grad_w_head_gate = attn_total[qkv_rows + out_rows : qkv_rows + out_rows + gate_rows]
    gain_sums = attn_total[qkv_rows + out_rows + gate_rows :]
    gain_part = model_width // fsdp_count
    head_part = HEAD_DIM // fsdp_count
    grad_attn_gain = lax.dynamic_slice_in_dim(gain_sums[0], fsdp_rank * gain_part, gain_part)
    grad_ffn_gain = lax.dynamic_slice_in_dim(gain_sums[1], fsdp_rank * gain_part, gain_part)
    grad_q_gain = lax.dynamic_slice_in_dim(gain_sums[2], fsdp_rank * head_part, head_part)
    grad_k_gain = lax.dynamic_slice_in_dim(
        gain_sums[2], HEAD_DIM + fsdp_rank * head_part, head_part
    )
    return (
        hidden_out,
        grad_in,
        grad_attn_gain,
        grad_w_qkv,
        grad_w_head_gate,
        grad_q_gain,
        grad_k_gain,
        grad_w_out,
        grad_ffn_gain,
        grad_w_gate,
        grad_w_up,
        grad_w_down,
    )


MESH = pl.DeviceIdType.MESH
VMEM_LIMIT = 60 * 1024 * 1024


def peer_copy(src, dst, send_sem, recv_sem, rank, plane):
    return pltpu.make_async_remote_copy(
        src_ref=src,
        dst_ref=dst,
        send_sem=send_sem,
        recv_sem=recv_sem,
        device_id=(rank, plane),
        device_id_type=MESH,
    )


def greet(peers):
    barrier = pltpu.get_barrier_semaphore()
    for peer in peers:
        pl.semaphore_signal(barrier, inc=1, device_id=peer, device_id_type=MESH)
    pl.semaphore_wait(barrier, len(peers))


def gather_gains_kernel(x_ref, s_ref, o_ref, so_ref, send_sem, recv_sem, sib_send, sib_recv, own_sem, small_send, small_recv):
    rank, plane = lax.axis_index("fsdp"), lax.axis_index("sp")
    greet([(rank ^ k, plane) for k in range(1, 8)])
    small = []
    for k in range(1, 8):
        copy = peer_copy(
            s_ref, so_ref.at[rank], small_send.at[k - 1], small_recv.at[k - 1], rank ^ k, plane
        )
        copy.start()
        small.append(copy)
    so_ref[rank] = s_ref[...]
    gather_blocks(x_ref, o_ref, send_sem, recv_sem, sib_send, sib_recv, own_sem)
    for copy in small:
        copy.wait()


def gather_kernel(x_ref, o_ref, *sems):
    rank, plane = lax.axis_index("fsdp"), lax.axis_index("sp")
    greet([(rank ^ k, plane) for k in (1, 2, 4, 6)])
    gather_blocks(x_ref, o_ref, *sems)


def gather_blocks(x_ref, o_ref, send_sem, recv_sem, sib_send, sib_recv, own_sem):
    rank, plane = lax.axis_index("fsdp"), lax.axis_index("sp")
    half = x_ref.shape[0] // 2
    own = pltpu.make_async_copy(x_ref, o_ref.at[rank], own_sem)
    own.start()
    far = {}
    for h in range(2):
        rows = pl.ds(h * half, half)
        for i, k in enumerate((6, 2, 4)):
            far[h, i] = peer_copy(
                x_ref.at[rows],
                o_ref.at[rank, rows],
                send_sem.at[h, i],
                recv_sem.at[h, i],
                rank ^ k,
                plane,
            )
            far[h, i].start()
    near = []
    first = peer_copy(
        x_ref, o_ref.at[rank], sib_send.at[0, 3], sib_recv.at[0, 3], rank ^ 1, plane
    )
    first.start()
    near.append(first)
    for h in range(2):
        rows = pl.ds(h * half, half)
        for i, k in enumerate((6, 2, 4)):
            far[h, i].wait_recv()
            block = o_ref.at[rank ^ k, rows]
            forward = peer_copy(
                block, block, sib_send.at[h, i], sib_recv.at[h, i], rank ^ 1, plane
            )
            forward.start()
            near.append(forward)
    for copy in near:
        copy.wait()
    for copy in far.values():
        copy.wait_send()
    own.wait()


def gather_plane(x, collective_id, small=None):
    rows, width = x.shape
    ranks = lax.axis_size("fsdp")
    big = pl.BlockSpec(memory_space=pl.ANY)
    sems = [
        pltpu.SemaphoreType.DMA((2, 3)),
        pltpu.SemaphoreType.DMA((2, 3)),
        pltpu.SemaphoreType.DMA((2, 4)),
        pltpu.SemaphoreType.DMA((2, 4)),
        pltpu.SemaphoreType.DMA,
    ]
    out = jax.ShapeDtypeStruct((ranks, rows, width), x.dtype)
    if small is not None:
        vmem = pl.BlockSpec(memory_space=pltpu.VMEM)
        return pl.pallas_call(
            gather_gains_kernel,
            out_shape=(out, jax.ShapeDtypeStruct((ranks,) + small.shape, small.dtype)),
            in_specs=[big, vmem],
            out_specs=(big, vmem),
            scratch_shapes=sems + [pltpu.SemaphoreType.DMA((7,)), pltpu.SemaphoreType.DMA((7,))],
            compiler_params=pltpu.CompilerParams(
                collective_id=collective_id, has_side_effects=True, vmem_limit_bytes=VMEM_LIMIT
            ),
            name="gather_gains",
        )(x, small)
    return pl.pallas_call(
        gather_kernel,
        out_shape=out,
        in_specs=[big],
        out_specs=big,
        scratch_shapes=sems,
        compiler_params=pltpu.CompilerParams(
            collective_id=collective_id, has_side_effects=True, vmem_limit_bytes=VMEM_LIMIT
        ),
        name="gather_plane",
    )(x)


def scatter_gains_kernel(planes, p_ref, s_ref, g_ref, o_ref, so_ref, go_ref, small_buf, line_out, line_buf, small_send, small_recv, line_send, line_recv, *rest):
    rank, plane = lax.axis_index("fsdp"), lax.axis_index("sp")
    others = [lax.rem(plane + k, planes) for k in range(1, planes)]
    greet([(rank ^ k, plane) for k in range(1, 8)] + [(rank, other) for other in others])
    small = []
    for k in range(1, 8):
        copy = peer_copy(
            s_ref.at[rank ^ k],
            small_buf.at[k - 1],
            small_send.at[k - 1],
            small_recv.at[k - 1],
            rank ^ k,
            plane,
        )
        copy.start()
        small.append(copy)
    scatter_blocks(p_ref, o_ref, *rest)
    total = s_ref[rank]
    for k in range(1, 8):
        small[k - 1].wait()
        total = total + small_buf[k - 1]
    tail = total.shape[0]
    line_out[:tail] = total
    line_out[tail:] = g_ref[...]
    line = []
    for k in range(1, planes):
        copy = peer_copy(
            line_out,
            line_buf.at[k - 1],
            line_send.at[k - 1],
            line_recv.at[k - 1],
            rank,
            others[k - 1],
        )
        copy.start()
        line.append(copy)
    final = line_out[...]
    for k in range(1, planes):
        line[k - 1].wait()
        final = final + line_buf[k - 1]
    so_ref[...] = final[:tail]
    go_ref[...] = final[tail:]


def scatter_kernel(*refs):
    rank, plane = lax.axis_index("fsdp"), lax.axis_index("sp")
    greet([(rank ^ k, plane) for k in (1, 2, 4, 6)])
    scatter_blocks(*refs)


def scatter_blocks(p_ref, o_ref, near_buf, out_buf, far_buf, sib_send, sib_recv, send_sem, recv_sem):
    rank, plane = lax.axis_index("fsdp"), lax.axis_index("sp")
    order = (6, 2, 4, 0)
    near = []
    for i, k in enumerate(order):
        copy = peer_copy(
            p_ref.at[rank ^ 1 ^ k], near_buf.at[i], sib_send.at[i], sib_recv.at[i], rank ^ 1, plane
        )
        copy.start()
        near.append(copy)
    far = []
    for i, k in enumerate(order):
        near[i].wait_recv()
        joined = p_ref[rank ^ k].astype(jnp.float32) + near_buf[i].astype(jnp.float32)
        if k:
            out_buf[i] = joined.astype(out_buf.dtype)
            copy = peer_copy(
                out_buf.at[i], far_buf.at[i], send_sem.at[i], recv_sem.at[i], rank ^ k, plane
            )
            copy.start()
            far.append(copy)
        else:
            o_ref[...] = joined
    for i in (1, 2, 0):
        far[i].wait_recv()
        o_ref[...] += far_buf[i].astype(jnp.float32)
    for copy in near + far:
        copy.wait_send()


def scatter_plane(p, collective_id, small=None, gate=None):
    ranks, rows, width = p.shape
    vmem = pl.BlockSpec(memory_space=pltpu.VMEM)
    scratch = [
        pltpu.VMEM((4, rows, width), p.dtype),
        pltpu.VMEM((3, rows, width), p.dtype),
        pltpu.VMEM((3, rows, width), p.dtype),
        pltpu.SemaphoreType.DMA((4,)),
        pltpu.SemaphoreType.DMA((4,)),
        pltpu.SemaphoreType.DMA((3,)),
        pltpu.SemaphoreType.DMA((3,)),
    ]
    out = jax.ShapeDtypeStruct((rows, width), jnp.float32)
    params = pltpu.CompilerParams(
        collective_id=collective_id, has_side_effects=True, vmem_limit_bytes=VMEM_LIMIT
    )
    if small is not None:
        planes = lax.axis_size("sp")
        joint = (small.shape[1] + gate.shape[0], small.shape[2])
        return pl.pallas_call(
            functools.partial(scatter_gains_kernel, planes),
            out_shape=(
                out,
                jax.ShapeDtypeStruct(small.shape[1:], small.dtype),
                jax.ShapeDtypeStruct(gate.shape, gate.dtype),
            ),
            in_specs=[vmem, vmem, vmem],
            out_specs=(vmem, vmem, vmem),
            scratch_shapes=[
                pltpu.VMEM((7,) + small.shape[1:], small.dtype),
                pltpu.VMEM(joint, small.dtype),
                pltpu.VMEM((planes - 1,) + joint, small.dtype),
                pltpu.SemaphoreType.DMA((7,)),
                pltpu.SemaphoreType.DMA((7,)),
                pltpu.SemaphoreType.DMA((planes - 1,)),
                pltpu.SemaphoreType.DMA((planes - 1,)),
            ]
            + scratch,
            compiler_params=params,
            name="scatter_gains",
        )(p, small, gate)
    return pl.pallas_call(
        scatter_kernel,
        out_shape=out,
        in_specs=[vmem],
        out_specs=vmem,
        scratch_shapes=scratch,
        compiler_params=params,
        name="scatter_plane",
    )(p)


def greet_line(ranks, planes):
    rank, plane = lax.axis_index("fsdp"), lax.axis_index("sp")
    barrier = pltpu.get_barrier_semaphore()
    for k in range(1, ranks):
        pl.semaphore_signal(
            barrier, inc=1, device_id=(rank ^ k, plane), device_id_type=MESH
        )

    @pl.when(plane > 0)
    def _():
        pl.semaphore_signal(barrier, inc=1, device_id=(rank, plane - 1), device_id_type=MESH)

    @pl.when(plane < planes - 1)
    def _():
        pl.semaphore_signal(barrier, inc=1, device_id=(rank, plane + 1), device_id_type=MESH)

    lower = (plane > 0).astype(jnp.int32)
    upper = (plane < planes - 1).astype(jnp.int32)
    pl.semaphore_wait(barrier, ranks - 1 + lower + upper)


def heads_kernel(planes, n_ref, q_ref, kv_ref, own_sem, q_send, q_recv, kv_send, kv_recv, line_send, line_recv):
    rank, plane = lax.axis_index("fsdp"), lax.axis_index("sp")
    greet_line(8, planes)

    def q_copy(m, to):
        return peer_copy(n_ref.at[pl.ds(2 * m, 2)], q_ref, q_send.at[m], q_recv, to, plane)

    def kv_copy(m, which, to):
        return peer_copy(
            n_ref.at[m], kv_ref.at[plane, which], kv_send.at[m], kv_recv.at[which], to, plane
        )

    def q_local():
        return pltpu.make_async_copy(n_ref.at[pl.ds(0, 2)], q_ref, own_sem)

    def kv_local(m, which):
        return pltpu.make_async_copy(n_ref.at[m], kv_ref.at[plane, which], own_sem)

    @pl.when(rank < 4)
    def _():
        for m in range(2):
            @pl.when(2 * rank + m != rank)
            def _():
                q_copy(m, 2 * rank + m).start()

    @pl.when(rank == 0)
    def _():
        q_local().start()

    for which in range(2):
        first = 4 + 2 * which
        own_m = (first + 1) % 4

        @pl.when((rank == first) | (rank == first + 1))
        def _():
            for m in range(4):
                to = 4 * (rank - first) + m

                @pl.when(to != rank)
                def _():
                    kv_copy(m, which, to).start()

        @pl.when(rank == first + 1)
        def _():
            kv_local(own_m, which).start()

    for which in range(2):
        first = 4 + 2 * which
        own_m = (first + 1) % 4

        @pl.when(rank == first + 1)
        def _():
            kv_local(own_m, which).wait()

        @pl.when(rank != first + 1)
        def _():
            kv_copy(0, which, 0).wait_recv()

        line_step(planes, kv_ref, which, 0, line_send, line_recv)
    for j in range(1, planes):
        for which in range(2):
            line_step(planes, kv_ref, which, j, line_send, line_recv)

    @pl.when(rank == 0)
    def _():
        q_local().wait()

    @pl.when(rank != 0)
    def _():
        q_copy(0, 0).wait_recv()

    @pl.when(rank < 4)
    def _():
        for m in range(2):
            @pl.when(2 * rank + m != rank)
            def _():
                q_copy(m, 0).wait_send()

    for which in range(2):
        first = 4 + 2 * which

        @pl.when((rank == first) | (rank == first + 1))
        def _():
            for m in range(4):
                @pl.when(4 * (rank - first) + m != rank)
                def _():
                    kv_copy(m, which, 0).wait_send()

    for j in range(planes - 1):
        for which in range(2):
            for side in range(2):
                @pl.when(line_sends(planes, plane, j, side))
                def _():
                    line_copy(kv_ref, which, j, side, line_send, line_recv).wait_send()


def line_sends(planes, plane, j, side):
    if side == 0:
        return (plane >= j) & (plane < planes - 1)
    return (plane + j <= planes - 1) & (plane > 0)


def line_copy(kv_ref, which, j, side, line_send, line_recv):
    rank, plane = lax.axis_index("fsdp"), lax.axis_index("sp")
    origin = plane - j if side == 0 else plane + j
    block = kv_ref.at[origin, which]
    to = plane + 1 if side == 0 else plane - 1
    return peer_copy(
        block, block, line_send.at[side, j, which], line_recv.at[side, j, which], rank, to
    )


def line_step(planes, kv_ref, which, j, line_send, line_recv):
    rank, plane = lax.axis_index("fsdp"), lax.axis_index("sp")
    for side in range(2):
        if j:
            arrives = (plane >= j) if side == 0 else (plane + j <= planes - 1)

            @pl.when(arrives)
            def _():
                origin = plane - j if side == 0 else plane + j
                block = kv_ref.at[origin, which]
                peer_copy(
                    block,
                    block,
                    line_send.at[side, j - 1, which],
                    line_recv.at[side, j - 1, which],
                    rank,
                    plane,
                ).wait_recv()

        if j < planes - 1:
            @pl.when(line_sends(planes, plane, j, side))
            def _():
                line_copy(kv_ref, which, j, side, line_send, line_recv).start()


def exchange_heads(natural, collective_id):
    _, tokens, width = natural.shape
    planes = lax.axis_size("sp")
    return pl.pallas_call(
        functools.partial(heads_kernel, planes),
        out_shape=(
            jax.ShapeDtypeStruct((2, tokens, width), natural.dtype),
            jax.ShapeDtypeStruct((planes, 2, tokens, width), natural.dtype),
        ),
        in_specs=[pl.BlockSpec(memory_space=pl.ANY)],
        out_specs=(pl.BlockSpec(memory_space=pl.ANY), pl.BlockSpec(memory_space=pl.ANY)),
        scratch_shapes=[
            pltpu.SemaphoreType.DMA,
            pltpu.SemaphoreType.DMA((2,)),
            pltpu.SemaphoreType.DMA,
            pltpu.SemaphoreType.DMA((4,)),
            pltpu.SemaphoreType.DMA((2,)),
            pltpu.SemaphoreType.DMA((2, planes - 1, 2)),
            pltpu.SemaphoreType.DMA((2, planes - 1, 2)),
        ],
        compiler_params=pltpu.CompilerParams(
            collective_id=collective_id, has_side_effects=True, vmem_limit_bytes=VMEM_LIMIT
        ),
        name="exchange_heads",
    )(natural)


def unheads_kernel(planes, dq_ref, dkv_ref, n_ref, line_out, line_in, done, own_sem, q_send, q_recv, kv_send, kv_recv, line_send, line_recv):
    rank, plane = lax.axis_index("fsdp"), lax.axis_index("sp")
    greet_line(8, planes)

    def q_copy(m, to):
        return peer_copy(dq_ref, n_ref.at[pl.ds(2 * m, 2)], q_send, q_recv.at[m], to, plane)

    def kv_copy(m, which, to):
        return peer_copy(done.at[which], n_ref.at[m], kv_send.at[which], kv_recv.at[m], to, plane)

    def q_local():
        return pltpu.make_async_copy(dq_ref, n_ref.at[pl.ds(0, 2)], own_sem)

    def kv_local(m, which):
        return pltpu.make_async_copy(done.at[which], n_ref.at[m], own_sem)

    @pl.when(rank == 0)
    def _():
        q_local().start()

    for m in range(2):
        @pl.when((rank % 2 == m) & (rank != 0))
        def _():
            q_copy(m, rank // 2).start()

    def step_copy(j, which, side):
        to = plane + 1 if side == 0 else plane - 1
        return peer_copy(
            line_out.at[side, j, which],
            line_in.at[side, j, which],
            line_send.at[side, j, which],
            line_recv.at[side, j, which],
            rank,
            to,
        )

    def sends(j, side):
        return plane < planes - 1 - j if side == 0 else plane > j

    def target(j, side):
        return planes - 1 - j if side == 0 else j

    for j in range(planes - 1):
        for which in range(2):
            for side in range(2):
                inner = plane > 0 if side == 0 else plane < planes - 1

                @pl.when(sends(j, side) & inner)
                def _():
                    step_copy(j, which, side).wait_recv()
                    total = dkv_ref[target(j, side), which].astype(jnp.float32) + line_in[
                        side, j, which
                    ].astype(jnp.float32)
                    line_out[side, j, which] = total.astype(line_out.dtype)

                @pl.when(sends(j, side) & jnp.logical_not(inner))
                def _():
                    line_out[side, j, which] = dkv_ref[target(j, side), which]

                @pl.when(sends(j, side))
                def _():
                    step_copy(j, which, side).start()

    for which in range(2):
        total = dkv_ref[plane, which].astype(jnp.float32)
        done32 = total
        for j in range(planes - 1):
            for side in range(2):
                @pl.when(plane == target(j, side))
                def _():
                    step_copy(j, which, side).wait_recv()
        low = jnp.minimum(planes - 1 - plane, planes - 2)
        high = jnp.minimum(plane, planes - 2)
        below = line_in[0, low, which].astype(jnp.float32)
        above = line_in[1, high, which].astype(jnp.float32)
        done32 = done32 + jnp.where(plane > 0, below, 0.0) + jnp.where(plane < planes - 1, above, 0.0)
        done[which] = done32.astype(done.dtype)
        first = 4 + 2 * which
        to = first + rank // 4
        for m in range(4):
            @pl.when((rank % 4 == m) & (to != rank))
            def _():
                kv_copy(m, which, to).start()

            @pl.when((rank % 4 == m) & (to == rank))
            def _():
                kv_local(m, which).start()

    @pl.when(rank < 4)
    def _():
        for m in range(2):
            @pl.when(2 * rank + m != rank)
            def _():
                q_copy(m, 0).wait_recv()

            @pl.when(2 * rank + m == rank)
            def _():
                q_local().wait()

    for which in range(2):
        first = 4 + 2 * which

        @pl.when((rank == first) | (rank == first + 1))
        def _():
            for m in range(4):
                @pl.when(4 * (rank - first) + m != rank)
                def _():
                    kv_copy(m, which, 0).wait_recv()

                @pl.when(4 * (rank - first) + m == rank)
                def _():
                    kv_local(m, which).wait()

    @pl.when(rank != 0)
    def _():
        q_copy(0, 0).wait_send()

    for which in range(2):
        @pl.when(4 + 2 * which + rank // 4 != rank)
        def _():
            kv_copy(0, which, 0).wait_send()

    for j in range(planes - 1):
        for which in range(2):
            for side in range(2):
                @pl.when(sends(j, side))
                def _():
                    step_copy(j, which, side).wait_send()


def return_heads(grad_query, grad_kv, collective_id):
    _, tokens, width = grad_query.shape
    planes = lax.axis_size("sp")
    vmem = pl.BlockSpec(memory_space=pltpu.VMEM)
    return pl.pallas_call(
        functools.partial(unheads_kernel, planes),
        out_shape=jax.ShapeDtypeStruct((4, tokens, width), grad_query.dtype),
        in_specs=[vmem, vmem],
        out_specs=vmem,
        scratch_shapes=[
            pltpu.VMEM((2, planes - 1, 2, tokens, width), grad_query.dtype),
            pltpu.VMEM((2, planes - 1, 2, tokens, width), grad_query.dtype),
            pltpu.VMEM((2, tokens, width), grad_query.dtype),
            pltpu.SemaphoreType.DMA,
            pltpu.SemaphoreType.DMA,
            pltpu.SemaphoreType.DMA((2,)),
            pltpu.SemaphoreType.DMA((2,)),
            pltpu.SemaphoreType.DMA((4,)),
            pltpu.SemaphoreType.DMA((2, planes - 1, 2)),
            pltpu.SemaphoreType.DMA((2, planes - 1, 2)),
        ],
        compiler_params=pltpu.CompilerParams(
            collective_id=collective_id, has_side_effects=True, vmem_limit_bytes=VMEM_LIMIT
        ),
        name="return_heads",
    )(grad_query, grad_kv)


def stack_heads(ref):
    return ref[...].reshape(ref.shape[0] * ref.shape[1], ref.shape[2])


def block_bounds(lengths_ref, ranks, planes, rows):
    block = pl.program_id(0)
    span = planes * rows
    first = block * span + lax.axis_index("sp") * rows
    start, end = jnp.int32(0), jnp.int32(0)
    for item in range(lengths_ref.shape[0]):
        end = end + lengths_ref[item]
        start = jnp.where(first >= end, end, start)
    return start // span, block, first


def row_starts(lengths_ref, tokens):
    start, end = jnp.zeros_like(tokens), jnp.int32(0)
    for item in range(lengths_ref.shape[0]):
        end = end + lengths_ref[item]
        start = jnp.where(tokens >= end, end, start)
    return start


def chunk_weights(query, key, scale, tokens, starts, first_key):
    scores = mat_nt(query, key) * scale
    columns = first_key + lax.broadcasted_iota(jnp.int32, scores.shape, 1)
    allowed = (columns <= tokens) & (columns >= starts)
    return jnp.where(allowed, jnp.exp(scores), 0.0)


def query_tokens(first, rows, group):
    row = lax.broadcasted_iota(jnp.int32, (group * rows, 1), 0)
    return first + lax.rem(row, rows)


def attend_kernel(ranks, planes, lengths_ref, q_ref, kv_ref, gate_ref, att_ref, total_ref, gated_ref):
    group, rows, width = q_ref.shape
    scale = HEAD_DIM ** (-0.5)
    low, high, first = block_bounds(lengths_ref, ranks, planes, rows)
    tokens = query_tokens(first, rows, group)
    starts = row_starts(lengths_ref, tokens)
    query = stack_heads(q_ref)
    span = planes * rows

    def step(chunk, running):
        total, unnorm = running
        key = kv_ref[:, 0, chunk].reshape(span, width)
        value = kv_ref[:, 1, chunk].reshape(span, width)
        weights = chunk_weights(query, key, scale, tokens, starts, chunk * span)
        total = total + jnp.sum(weights, axis=1, keepdims=True)
        unnorm = unnorm + jnp.dot(
            weights.astype(jnp.bfloat16), value, preferred_element_type=jnp.float32
        )
        return total, unnorm

    total, unnorm = lax.fori_loop(
        low,
        high + 1,
        step,
        (
            jnp.zeros((group * rows, 1), jnp.float32),
            jnp.zeros((group * rows, width), jnp.float32),
        ),
    )
    attended = unnorm / total
    att_ref[...] = attended.reshape(group, rows, width)
    total_ref[...] = total.reshape(group, rows, 1)
    sent = attended.astype(jnp.bfloat16).astype(jnp.float32)
    for head in range(group):
        gated = sent[head * rows : (head + 1) * rows] * jax.nn.sigmoid(gate_ref[head])
        gated_ref[:, head * width : (head + 1) * width] = gated.astype(jnp.bfloat16)


def attend(lengths, query, kv, gate_logit, rows):
    group, tokens, width = query.shape
    planes = kv.shape[0]
    ranks = tokens // rows
    kv_blocks = kv.reshape(planes, 2, ranks, rows, width)
    block = pl.BlockSpec((group, rows, width), lambda i, *_: (0, i, 0))
    thin = pl.BlockSpec((group, rows, 1), lambda i, *_: (0, i, 0))
    return pl.pallas_call(
        functools.partial(attend_kernel, ranks, planes),
        grid_spec=pltpu.PrefetchScalarGridSpec(
            num_scalar_prefetch=1,
            grid=(ranks,),
            in_specs=[
                block,
                pl.BlockSpec((planes, 2, ranks, rows, width), lambda i, *_: (0, 0, 0, 0, 0)),
                thin,
            ],
            out_specs=(
                block,
                thin,
                pl.BlockSpec((rows, group * width), lambda i, *_: (i, 0)),
            ),
        ),
        out_shape=(
            jax.ShapeDtypeStruct((group, tokens, width), jnp.float32),
            jax.ShapeDtypeStruct((group, tokens, 1), jnp.float32),
            jax.ShapeDtypeStruct((tokens, group * width), jnp.bfloat16),
        ),
        compiler_params=pltpu.CompilerParams(vmem_limit_bytes=VMEM_LIMIT),
        name="attend",
    )(lengths, query, kv_blocks, gate_logit)


def attend_back_kernel(
    ranks, planes, lengths_ref, q_ref, kv_ref, gate_ref, att_ref, total_ref, dgated_ref, dq_ref, dkv_ref, dgate_ref, sums
):
    group, rows, width = q_ref.shape
    scale = HEAD_DIM ** (-0.5)
    low, high, first = block_bounds(lengths_ref, ranks, planes, rows)
    tokens = query_tokens(first, rows, group)
    starts = row_starts(lengths_ref, tokens)
    query = stack_heads(q_ref)
    span = planes * rows

    @pl.when(pl.program_id(0) == 0)
    def _():
        sums[...] = jnp.zeros_like(sums)

    attended = stack_heads(att_ref)
    sent = attended.astype(jnp.bfloat16).astype(jnp.float32)
    total = stack_heads(total_ref)
    logit = stack_heads(gate_ref)
    prob = jax.nn.sigmoid(logit)
    dgated = jnp.concatenate(
        [dgated_ref[:, head * width : (head + 1) * width] for head in range(group)], axis=0
    )
    dattended = (dgated * prob).astype(jnp.bfloat16)
    dlogit = jnp.sum(dgated * sent, axis=1, keepdims=True) * prob * (1.0 - prob)
    dgate_ref[...] = dlogit.astype(jnp.bfloat16).reshape(group, rows, 1)
    dattended = dattended.astype(jnp.float32)
    scaled = (dattended / total).astype(jnp.bfloat16)
    delta = jnp.sum(dattended * attended, axis=1, keepdims=True) / total

    def step(chunk, dquery):
        key = kv_ref[:, 0, chunk].reshape(span, width)
        value = kv_ref[:, 1, chunk].reshape(span, width)
        weights = chunk_weights(query, key, scale, tokens, starts, chunk * span)
        dprob = mat_nt(scaled, value)
        dscore = (weights * (dprob - delta)).astype(jnp.bfloat16)
        dquery = dquery + jnp.dot(dscore, key, preferred_element_type=jnp.float32)
        dkey = mat_tn(dscore, query)
        dvalue = mat_tn(weights.astype(jnp.bfloat16), scaled)
        sums[:, 0, chunk] += dkey.reshape(planes, rows, width)
        sums[:, 1, chunk] += dvalue.reshape(planes, rows, width)
        return dquery

    dquery = lax.fori_loop(
        low, high + 1, step, jnp.zeros((group * rows, width), jnp.float32)
    )
    dq_ref[...] = (dquery * scale).astype(jnp.bfloat16).reshape(group, rows, width)

    @pl.when(pl.program_id(0) == ranks - 1)
    def _():
        for chunk in range(ranks):
            dkv_ref[:, 0, chunk] = (sums[:, 0, chunk] * scale).astype(jnp.bfloat16)
            dkv_ref[:, 1, chunk] = sums[:, 1, chunk].astype(jnp.bfloat16)


def attend_back(lengths, query, kv, gate_logit, attended, total, dgated, rows):
    group, tokens, width = query.shape
    planes = kv.shape[0]
    ranks = tokens // rows
    kv_blocks = kv.reshape(planes, 2, ranks, rows, width)
    block = pl.BlockSpec((group, rows, width), lambda i, *_: (0, i, 0))
    thin = pl.BlockSpec((group, rows, 1), lambda i, *_: (0, i, 0))
    whole = pl.BlockSpec((planes, 2, ranks, rows, width), lambda i, *_: (0, 0, 0, 0, 0))
    dquery, dkv, dgate = pl.pallas_call(
        functools.partial(attend_back_kernel, ranks, planes),
        grid_spec=pltpu.PrefetchScalarGridSpec(
            num_scalar_prefetch=1,
            grid=(ranks,),
            in_specs=[
                block,
                whole,
                thin,
                block,
                thin,
                pl.BlockSpec((rows, group * width), lambda i, *_: (i, 0)),
            ],
            out_specs=(block, whole, thin),
            scratch_shapes=[pltpu.VMEM((planes, 2, ranks, rows, width), jnp.float32)],
        ),
        out_shape=(
            jax.ShapeDtypeStruct((group, tokens, width), jnp.bfloat16),
            jax.ShapeDtypeStruct((planes, 2, ranks, rows, width), jnp.bfloat16),
            jax.ShapeDtypeStruct((group, tokens, 1), jnp.bfloat16),
        ),
        compiler_params=pltpu.CompilerParams(vmem_limit_bytes=VMEM_LIMIT),
        name="attend_back",
    )(lengths, query, kv_blocks, gate_logit, attended, total, dgated)
    return dquery, dkv.reshape(planes, 2, tokens, width), dgate


GATHER_COPIES = 13


def gather_copy(buf, i, send_sem, recv_sem):
    rank, plane = lax.axis_index("fsdp"), lax.axis_index("sp")
    rows = buf.shape[1]
    top, low = pl.ds(0, rows // 2), pl.ds(rows // 2, rows // 2)
    block, part, to = (
        (0, top, 2),
        (0, low, 2),
        (0, low, 4),
        (0, top, 4),
        (2, top, 4),
        (4, low, 2),
        (0, pl.ds(0, rows), 1),
        (2, top, 1),
        (2, low, 1),
        (4, low, 1),
        (4, top, 1),
        (6, top, 1),
        (6, low, 1),
    )[i]
    piece = buf.at[rank ^ block, part]
    return peer_copy(piece, piece, send_sem.at[i], recv_sem.at[i], rank ^ to, plane)


def gather_start(buf, send_sem, recv_sem):
    for i in (6, 0, 2, 1, 3):
        gather_copy(buf, i, send_sem, recv_sem).start()


def gather_pass(buf, send_sem, recv_sem, pairs):
    for arrived, onward in pairs:
        gather_copy(buf, arrived, send_sem, recv_sem).wait_recv()
        for i in onward:
            gather_copy(buf, i, send_sem, recv_sem).start()


def gather_wait(buf, send_sem, recv_sem, copies):
    for i in copies:
        gather_copy(buf, i, send_sem, recv_sem).wait_recv()


NEIGHBOURS_FIRST = ((0, (4, 7)), (2, (5, 9)), (1, (8,)), (3, (10,)))
DIAGONAL = ((4, (11,)), (5, (12,)))


def middle_kernel(
    gated_ref,
    wout_ref,
    x_ref,
    scale_ref,
    dy_hbm,
    wg_hbm,
    wu_hbm,
    wd_hbm,
    xb_ref,
    down_hbm,
    mid_ref,
    dmid_ref,
    gain_ref,
    pm_ref,
    dgated_ref,
    wg,
    wu,
    wd,
    dy,
    dhid,
    xg,
    near_out,
    near_in,
    far_out,
    far_in,
    keep,
    down_buf,
    load_sem,
    dy_sem,
    down_sem,
    near_send,
    near_recv,
    far_send,
    far_recv,
    ag_send,
    ag_recv,
):
    rank, plane = lax.axis_index("fsdp"), lax.axis_index("sp")
    ranks, rows, width = xg.shape
    loads = [
        pltpu.make_async_copy(wd_hbm, wd, load_sem.at[0]),
        pltpu.make_async_copy(wg_hbm, wg, load_sem.at[1]),
        pltpu.make_async_copy(wu_hbm, wu, load_sem.at[2]),
    ]
    dy_loads = [
        pltpu.make_async_copy(dy_hbm.at[r, plane], dy.at[r], dy_sem.at[r]) for r in range(ranks)
    ]
    greet([(rank ^ k, plane) for k in (1, 2, 4, 6)])

    def near(phase, i):
        return peer_copy(
            near_out.at[phase, i],
            near_in.at[phase, i],
            near_send.at[phase, i],
            near_recv.at[phase, i],
            rank ^ 1,
            plane,
        )

    def far(phase, i, k):
        return peer_copy(
            far_out.at[phase, i],
            far_in.at[phase, i],
            far_send.at[phase, i],
            far_recv.at[phase, i],
            rank ^ k,
            plane,
        )

    order = (6, 2, 4, 0)
    for i, k in enumerate(order):
        part = jnp.dot(
            gated_ref[rank ^ 1 ^ k], wout_ref[...], preferred_element_type=jnp.float32
        )
        near_out[0, i] = part.astype(jnp.bfloat16)
        near(0, i).start()
    for copy in dy_loads + loads:
        copy.start()
    for i, k in enumerate(order):
        part = jnp.dot(gated_ref[rank ^ k], wout_ref[...], preferred_element_type=jnp.float32)
        near(0, i).wait_recv()
        part = part + near_in[0, i].astype(jnp.float32)
        if k:
            far_out[0, i] = part.astype(jnp.bfloat16)
            far(0, i, k).start()
        else:
            keep[...] = part

    for copy in dy_loads:
        copy.wait()
    loads[0].wait()

    @pl.loop(0, ranks // 2)
    def _(p):
        pair = dy[pl.ds(2 * p, 2)].reshape(2 * rows, width)
        dhid[p] = mat_nt(pair, wd[...])

    loads[1].wait()
    loads[2].wait()
    middle = x_ref[...].astype(jnp.float32) + keep[...]
    for i in (1, 2, 0):
        far(0, i, order[i]).wait_recv()
        middle = middle + far_in[0, i].astype(jnp.float32)
    inverse = inv_rms(middle)
    mid_ref[...] = middle
    normed = (middle * inverse * scale_ref[...]).astype(jnp.bfloat16)
    xb_ref[...] = normed
    xg[rank] = normed
    sems = (ag_send.at[0], ag_recv.at[0])
    gather_start(xg, *sems)

    slots = {2: 0, 4: 1, 6: 2, 0: 3}

    def down_copy(p, slot):
        return pltpu.make_async_copy(
            down_buf.at[slot], down_hbm.at[pl.ds(2 * p, 2)], down_sem.at[slot]
        )

    def feed(k):
        p = (rank ^ k) // 2
        slot = (0, 2, 4, 6).index(k) % 2
        pair = xg[pl.ds(2 * p, 2)].reshape(2 * rows, width)
        gate_pre = mat_nt(pair, wg[...])
        up_pre = mat_nt(pair, wu[...])
        grad_hidden = dhid[p]
        sigma = jax.nn.sigmoid(gate_pre)
        swish = gate_pre * sigma
        grad_gate = (grad_hidden * up_pre * sigma * (1.0 + gate_pre * (1.0 - sigma))).astype(
            jnp.bfloat16
        )
        grad_up = (grad_hidden * swish).astype(jnp.bfloat16)
        part = jnp.dot(grad_gate, wg[...], preferred_element_type=jnp.float32) + jnp.dot(
            grad_up, wu[...], preferred_element_type=jnp.float32
        )
        i = slots[k]
        halves = part.reshape(2, rows, width)
        mine_first = lax.rem(rank, 2) == 0
        mine = jnp.where(mine_first, halves[0], halves[1])
        theirs = jnp.where(mine_first, halves[1], halves[0])
        near_out[1, i] = theirs.astype(jnp.bfloat16)
        near(1, i).start()
        hidden = (swish * up_pre).astype(jnp.bfloat16)
        down = jnp.dot(hidden, wd[...], preferred_element_type=jnp.float32)
        if k in (4, 6):
            down_copy(p, slot).wait()
        down_buf[slot] = down.astype(jnp.bfloat16).reshape(2, rows, width)
        down_copy(p, slot).start()
        near(1, i).wait_recv()
        mine = mine + near_in[1, i].astype(jnp.float32)
        if k:
            far_out[1, i] = mine.astype(jnp.bfloat16)
            far(1, i, k).start()
        else:
            keep[...] = mine

    gather_wait(xg, *sems, (6,))
    feed(0)
    gather_pass(xg, *sems, NEIGHBOURS_FIRST)
    gather_wait(xg, *sems, (7, 8))
    feed(2)
    gather_pass(xg, *sems, DIAGONAL)
    gather_wait(xg, *sems, (9, 10))
    feed(4)
    gather_wait(xg, *sems, (11, 12))
    feed(6)

    grad = keep[...]
    for i, k in enumerate((2, 4, 6)):
        far(1, i, k).wait_recv()
        grad = grad + far_in[1, i].astype(jnp.float32)
    middle = mid_ref[...]
    inverse = inv_rms(middle)
    gain_ref[...] = jnp.sum(grad * middle * inverse, axis=0, keepdims=True)
    grad_middle = dy[rank].astype(jnp.float32) + norm_back(
        grad, middle, inverse, scale_ref[...]
    )
    dmid_ref[...] = grad_middle
    pm_ref[rank] = grad_middle.astype(jnp.bfloat16)
    sems2 = (ag_send.at[1], ag_recv.at[1])
    gather_start(pm_ref, *sems2)

    def gated_grad(k):
        p = (rank ^ k) // 2
        pair = pm_ref[pl.ds(2 * p, 2)].reshape(2 * rows, width)
        dgated_ref[pl.ds(2 * p, 2)] = mat_nt(pair, wout_ref[...]).reshape(
            2, rows, wout_ref.shape[0]
        )

    gather_wait(pm_ref, *sems2, (6,))
    gated_grad(0)
    gather_pass(pm_ref, *sems2, NEIGHBOURS_FIRST)
    gather_wait(pm_ref, *sems2, (7, 8))
    gated_grad(2)
    gather_wait(pm_ref, *sems2, (9, 10))
    gated_grad(4)
    gather_pass(pm_ref, *sems2, DIAGONAL)
    gather_wait(pm_ref, *sems2, (11, 12))
    gated_grad(6)

    for i in range(GATHER_COPIES):
        gather_copy(xg, i, *sems).wait_send()
        gather_copy(pm_ref, i, *sems2).wait_send()
    for phase in range(2):
        for i in range(4):
            near(phase, i).wait_send()
        for i in range(3):
            far(phase, i, 2).wait_send()
    down_copy(0, 0).wait()
    down_copy(0, 1).wait()


def middle_layer(gated, w_out, x, scale, grad_all, w_gate, w_up, w_down, collective_id):
    ranks, rows, _ = gated.shape
    width = x.shape[1]
    hidden = w_gate.shape[0]
    features = w_out.shape[0]
    vmem = pl.BlockSpec(memory_space=pltpu.VMEM)
    hbm = pl.BlockSpec(memory_space=pl.ANY)
    half, full = jnp.bfloat16, jnp.float32
    return pl.pallas_call(
        middle_kernel,
        out_shape=(
            jax.ShapeDtypeStruct((rows, width), half),
            jax.ShapeDtypeStruct((ranks, rows, width), half),
            jax.ShapeDtypeStruct((rows, width), full),
            jax.ShapeDtypeStruct((rows, width), full),
            jax.ShapeDtypeStruct((1, width), full),
            jax.ShapeDtypeStruct((ranks, rows, width), half),
            jax.ShapeDtypeStruct((ranks, rows, features), full),
        ),
        in_specs=[vmem, vmem, vmem, vmem, hbm, hbm, hbm, hbm],
        out_specs=(vmem, hbm, vmem, vmem, vmem, vmem, vmem),
        scratch_shapes=[
            pltpu.VMEM((hidden, width), half),
            pltpu.VMEM((hidden, width), half),
            pltpu.VMEM((hidden, width), half),
            pltpu.VMEM((ranks, rows, width), half),
            pltpu.VMEM((ranks // 2, 2 * rows, hidden), full),
            pltpu.VMEM((ranks, rows, width), half),
            pltpu.VMEM((2, 4, rows, width), half),
            pltpu.VMEM((2, 4, rows, width), half),
            pltpu.VMEM((2, 3, rows, width), half),
            pltpu.VMEM((2, 3, rows, width), half),
            pltpu.VMEM((rows, width), full),
            pltpu.VMEM((2, 2, rows, width), half),
            pltpu.SemaphoreType.DMA((3,)),
            pltpu.SemaphoreType.DMA((ranks,)),
            pltpu.SemaphoreType.DMA((2,)),
            pltpu.SemaphoreType.DMA((2, 4)),
            pltpu.SemaphoreType.DMA((2, 4)),
            pltpu.SemaphoreType.DMA((2, 3)),
            pltpu.SemaphoreType.DMA((2, 3)),
            pltpu.SemaphoreType.DMA((2, GATHER_COPIES)),
            pltpu.SemaphoreType.DMA((2, GATHER_COPIES)),
        ],
        compiler_params=pltpu.CompilerParams(
            collective_id=collective_id, has_side_effects=True, vmem_limit_bytes=VMEM_LIMIT
        ),
        name="middle_layer",
    )(gated, w_out, x, scale, grad_all, w_gate, w_up, w_down)


def feed_weights_kernel(x_ref, g_ref, wg_ref, wu_ref, wd_ref, og_ref, ou_ref, od_ref):
    normed, grad = x_ref[...], g_ref[...]
    gate_pre = mat_nt(normed, wg_ref[...])
    up_pre = mat_nt(normed, wu_ref[...])
    grad_hidden = mat_nt(grad, wd_ref[...])
    sigma = jax.nn.sigmoid(gate_pre)
    swish = gate_pre * sigma
    hidden = (swish * up_pre).astype(jnp.bfloat16)
    grad_gate = (grad_hidden * up_pre * sigma * (1.0 + gate_pre * (1.0 - sigma))).astype(
        jnp.bfloat16
    )
    grad_up = (grad_hidden * swish).astype(jnp.bfloat16)

    @pl.when(pl.program_id(0) == 0)
    def _():
        for ref in (og_ref, ou_ref, od_ref):
            ref[...] = jnp.zeros_like(ref)

    og_ref[...] += mat_tn(grad_gate, normed)
    ou_ref[...] += mat_tn(grad_up, normed)
    od_ref[...] += mat_tn(hidden, grad)


def feed_weights(normed, grad, w_gate, w_up, w_down):
    tokens, width = normed.shape
    chunk = 512
    moving = pl.BlockSpec((chunk, width), lambda i: (i, 0))
    still = pl.BlockSpec(w_gate.shape, lambda i: (0, 0), pipeline_mode=pl.Buffered(1))
    flops = 12 * tokens * w_gate.size
    return pl.pallas_call(
        feed_weights_kernel,
        grid=(tokens // chunk,),
        in_specs=[moving, moving, still, still, still],
        out_specs=(still, still, still),
        out_shape=[jax.ShapeDtypeStruct(w_gate.shape, jnp.float32)] * 3,
        cost_estimate=pl.CostEstimate(
            flops=flops,
            bytes_accessed=4 * normed.size + 18 * w_gate.size,
            transcendentals=tokens * w_gate.shape[0],
        ),
        compiler_params=pltpu.CompilerParams(vmem_limit_bytes=VMEM_LIMIT),
        name="feed_weights",
    )(normed, grad, w_gate, w_up, w_down)


def local_planes(
    hidden_in,
    grad_out,
    lengths,
    attn_gain,
    w_qkv,
    w_head_gate,
    q_gain,
    k_gain,
    w_out,
    ffn_gain,
    w_gate,
    w_up,
    w_down,
):
    ranks, planes = lax.axis_size("fsdp"), lax.axis_size("sp")
    rank, plane = lax.axis_index("fsdp"), lax.axis_index("sp")
    rows, model_width = hidden_in.shape
    tokens = ranks * rows
    both = ("fsdp", "sp")
    own_heads = w_qkv.shape[0] // HEAD_DIM
    local_heads = HEADS // ranks

    wide, thin = attn_gain.shape[0], q_gain.shape[0]
    used = 2 * wide + 2 * thin
    own_gains = jnp.concatenate(
        [attn_gain, ffn_gain, q_gain, k_gain, jnp.zeros((8 * HEAD_DIM - used,), attn_gain.dtype)]
    ).astype(jnp.float32)
    gathered, gains = gather_plane(hidden_in, 0, own_gains.reshape(8, HEAD_DIM))
    gains = gains.reshape(ranks, 8 * HEAD_DIM)
    attn_scale = gains[:, :wide].reshape(-1)
    ffn_scale = gains[:, wide : 2 * wide].reshape(-1)
    query_scale = gains[:, 2 * wide : 2 * wide + thin].reshape(-1)
    key_scale = gains[:, 2 * wide + thin : used].reshape(-1)

    grad_later, gathered = lax.optimization_barrier((grad_out, gathered))
    grad_all = lax.all_gather(grad_later, both, axis=0, tiled=True)

    token_block = jnp.arange(ranks, dtype=jnp.int32) * (planes * rows) + plane * rows
    plane_tokens = (token_block[:, None] + jnp.arange(rows, dtype=jnp.int32)[None]).reshape(-1)
    cosine, sine = rope_tables(plane_tokens - item_starts(plane_tokens, lengths))

    inputs = gathered.reshape(tokens, model_width).astype(jnp.float32)
    inv_first = inv_rms(inputs)
    normed_a = (inputs * inv_first * attn_scale).astype(jnp.bfloat16)
    projected = mat_nt(normed_a, w_qkv)
    gate_logit = mat_nt(w_head_gate, normed_a)[:, :, None]
    raw = projected.reshape(tokens, own_heads, HEAD_DIM)
    raw_inv = inv_rms(raw)
    is_query, is_value = rank < ranks // 2, rank >= 3 * ranks // 4
    head_scale = jnp.where(is_query, query_scale, key_scale)
    turned = rotate(raw * raw_inv * head_scale, cosine, sine)
    natural = jnp.where(is_value, raw, turned).astype(jnp.bfloat16)
    query, kv = exchange_heads(jnp.transpose(natural, (1, 0, 2)), 1)

    attended, total, gated = attend(lengths, query, kv, gate_logit, rows)
    own_inputs = hidden_in.astype(jnp.float32)
    normed_b, down_part, middle, grad_middle, grad_ffn_gain_local, plane_mid, grad_gated = middle_layer(
        gated.reshape(ranks, rows, -1),
        w_out,
        hidden_in,
        ffn_scale.reshape(1, -1),
        grad_all.reshape(ranks, planes, rows, model_width),
        w_gate,
        w_up,
        w_down,
        2,
    )
    plane_mid = plane_mid.reshape(tokens, model_width)
    grad_gated = grad_gated.reshape(tokens, -1)
    all_b = lax.all_gather(normed_b, both, axis=0, tiled=True)
    grad_query, grad_kv, gate_grad = attend_back(
        lengths, query, kv, gate_logit, attended, total, grad_gated, rows
    )
    back = return_heads(grad_query, grad_kv, 6)
    back = jnp.transpose(back, (1, 0, 2))
    turned_back = rotate_back(back.astype(jnp.float32), cosine, sine)
    gain_terms = jnp.sum(turned_back * raw * raw_inv, axis=(0, 1))
    raw_back = norm_back(turned_back, raw, raw_inv, head_scale).astype(jnp.bfloat16)
    grad_proj = jnp.where(is_value, back, raw_back).reshape(tokens, own_heads * HEAD_DIM)
    gate_grad = gate_grad.reshape(local_heads, tokens)
    grad_a_part = jnp.dot(grad_proj, w_qkv, preferred_element_type=jnp.float32) + mat_tn(
        gate_grad, w_head_gate
    )
    nothing = jnp.zeros((HEAD_DIM,), jnp.float32)
    gain_parts = jnp.concatenate(
        [
            jnp.sum(grad_a_part * inputs * inv_first, axis=0).reshape(ranks, wide),
            grad_ffn_gain_local.reshape(ranks, wide),
            jnp.where(is_query, gain_terms, nothing).reshape(ranks, thin),
            jnp.where(is_query | is_value, nothing, gain_terms).reshape(ranks, thin),
            jnp.zeros((ranks, 8 * HEAD_DIM - used), jnp.float32),
        ],
        axis=1,
    )
    grad_a_part, grad_proj, down_part, plane_mid, all_b = lax.optimization_barrier(
        (grad_a_part, grad_proj, down_part, plane_mid, all_b)
    )
    ffn_out = lax.psum_scatter(
        down_part.reshape(tokens, model_width), "fsdp", scatter_dimension=0, tiled=True
    )
    hidden_out = (middle + ffn_out.astype(jnp.float32)).astype(jnp.bfloat16)
    gate_rows_part = jnp.dot(gate_grad, normed_a, preferred_element_type=jnp.float32)
    grad_a, gain_total, gate_total = scatter_plane(
        grad_a_part.astype(jnp.bfloat16).reshape(ranks, rows, model_width),
        7,
        gain_parts.reshape(ranks, 8, HEAD_DIM),
        gate_rows_part.reshape(-1, HEAD_DIM),
    )
    own_inv = inv_rms(own_inputs)
    grad_in = grad_middle + norm_back(grad_a, own_inputs, own_inv, attn_scale)

    def over_planes(part):
        reduced = lax.psum_scatter(
            part.astype(jnp.bfloat16), "sp", scatter_dimension=0, tiled=True
        )
        return lax.all_gather(reduced, "sp", axis=0, tiled=True).astype(jnp.float32)

    grad_w_out = over_planes(mat_tn(gated, plane_mid))
    grad_w_qkv = over_planes(mat_tn(grad_proj, normed_a))
    grad_w_head_gate = gate_total.reshape(w_head_gate.shape)

    all_b, grad_a = lax.optimization_barrier((all_b, grad_a))
    grad_w_gate, grad_w_up, grad_w_down = feed_weights(all_b, grad_all, w_gate, w_up, w_down)

    gain_total = gain_total.reshape(-1)
    grad_attn_gain = gain_total[:wide]
    grad_ffn_gain = gain_total[wide : 2 * wide]
    grad_q_gain = gain_total[2 * wide : 2 * wide + thin]
    grad_k_gain = gain_total[2 * wide + thin : used]
    return (
        hidden_out,
        grad_in,
        grad_attn_gain,
        grad_w_qkv,
        grad_w_head_gate,
        grad_q_gain,
        grad_k_gain,
        grad_w_out,
        grad_ffn_gain,
        grad_w_gate,
        grad_w_up,
        grad_w_down,
    )


def solution(mesh):
    planar = mesh.shape["fsdp"] == 8 and mesh.shape["sp"] == 4
    return jax.shard_map(
        local_planes if planar else local,
        mesh=mesh,
        in_specs=(
            P(("fsdp", "sp"), None),
            P(("fsdp", "sp"), None),
            P(),
            P("fsdp"),
            P("fsdp", None),
            P("fsdp", None),
            P("fsdp"),
            P("fsdp"),
            P("fsdp", None),
            P("fsdp"),
            P("fsdp", None),
            P("fsdp", None),
            P("fsdp", None),
        ),
        out_specs=(
            P(("fsdp", "sp"), None),
            P(("fsdp", "sp"), None),
            P("fsdp"),
            P("fsdp", None),
            P("fsdp", None),
            P("fsdp"),
            P("fsdp"),
            P("fsdp", None),
            P("fsdp"),
            P("fsdp", None),
            P("fsdp", None),
            P("fsdp", None),
        ),
        check_vma=False,
    )
```

```python
import functools
import math

import jax
import jax.numpy as jnp
from jax import lax
from jax.experimental import pallas as pl
from jax.experimental.pallas import tpu as pltpu
from jax.sharding import PartitionSpec as P

HEADS = 16
KV_HEADS = 8
HEAD_DIM = 128


EPS = 1e-06
ROPE_BASE = 1000000.0


def mat_nt(factor, others):
    return lax.dot_general(
        factor, others, (((1,), (1,)), ((), ())), preferred_element_type=jnp.float32
    )


def mat_tn(factor, others):
    return lax.dot_general(
        factor, others, (((0,), (0,)), ((), ())), preferred_element_type=jnp.float32
    )


def inv_rms(values):
    return lax.rsqrt(jnp.mean(values * values, axis=-1, keepdims=True) + EPS)


def norm_back(grad_norm, values, inverse, scaling):
    scaled = grad_norm * scaling
    cubed = inverse * inverse * inverse
    return inverse * scaled - values * cubed * jnp.mean(scaled * values, axis=-1, keepdims=True)


def item_starts(token_index, lengths):
    ends = jnp.cumsum(lengths)
    starts = ends - lengths
    inside = (token_index[:, None] >= starts[None, :]) & (token_index[:, None] < ends[None, :])
    return jnp.sum(jnp.where(inside, starts[None, :], 0), axis=1)


def rope_tables(position):
    half_dim = HEAD_DIM // 2
    freq_steps = jnp.arange(half_dim, dtype=jnp.float32)
    frequency = jnp.exp(-math.log(ROPE_BASE) * 2.0 * freq_steps / HEAD_DIM)
    angles = position.astype(jnp.float32)[:, None] * frequency[None, :]
    return (jnp.cos(angles)[:, None, :], jnp.sin(angles)[:, None, :])


def rotate(values, cosine, sine):
    half_dim = values.shape[-1] // 2
    lower = values[..., :half_dim]
    upper = values[..., half_dim:]
    return jnp.concatenate([lower * cosine - upper * sine, upper * cosine + lower * sine], axis=-1)


def rotate_back(grad_rot, cosine, sine):
    half_dim = grad_rot.shape[-1] // 2
    lower = grad_rot[..., :half_dim]
    upper = grad_rot[..., half_dim:]
    return jnp.concatenate([lower * cosine + upper * sine, upper * cosine - lower * sine], axis=-1)


def local(
    hidden_in,
    grad_out,
    lengths,
    attn_gain,
    w_qkv,
    w_head_gate,
    q_gain,
    k_gain,
    w_out,
    ffn_gain,
    w_gate,
    w_up,
    w_down,
):
    fsdp_count = lax.axis_size("fsdp")
    sp_count = lax.axis_size("sp")
    fsdp_rank = lax.axis_index("fsdp")
    sp_rank = lax.axis_index("sp")
    tok_rows = hidden_in.shape[0]
    model_width = hidden_in.shape[1]
    query_width = HEADS * HEAD_DIM
    kv_width = KV_HEADS * HEAD_DIM
    local_kv = KV_HEADS // sp_count
    head_group = HEADS // KV_HEADS
    score_scale = HEAD_DIM ** (-0.5)
    qkv_full, out_full, gate_full, attn_gain_full, q_gain_full, k_gain_full, ffn_gain_full = (
        lax.all_gather(w_qkv, "fsdp", axis=0, tiled=True),
        lax.all_gather(w_out, "fsdp", axis=0, tiled=True),
        lax.all_gather(w_head_gate, "fsdp", axis=0, tiled=True),
        lax.all_gather(attn_gain, "fsdp", axis=0, tiled=True),
        lax.all_gather(q_gain, "fsdp", axis=0, tiled=True),
        lax.all_gather(k_gain, "fsdp", axis=0, tiled=True),
        lax.all_gather(ffn_gain, "fsdp", axis=0, tiled=True),
    )
    attn_scale = attn_gain_full.astype(jnp.float32)
    query_scale = q_gain_full.astype(jnp.float32)
    key_scale = k_gain_full.astype(jnp.float32)
    ffn_scale = ffn_gain_full.astype(jnp.float32)
    token_first = (fsdp_rank * sp_count + sp_rank) * tok_rows
    own_tokens = token_first + jnp.arange(tok_rows, dtype=jnp.int32)
    cosine, sine = rope_tables(own_tokens - item_starts(own_tokens, lengths))
    inputs = hidden_in.astype(jnp.float32)
    inv_first = inv_rms(inputs)
    normed_a = (inputs * inv_first * attn_scale).astype(jnp.bfloat16)
    projected = mat_nt(normed_a, qkv_full)
    gate_logit = mat_nt(normed_a, gate_full)
    q_raw = projected[:, :query_width].reshape(tok_rows, HEADS, HEAD_DIM)
    k_raw = projected[:, query_width : query_width + kv_width].reshape(tok_rows, KV_HEADS, HEAD_DIM)
    q_inv = inv_rms(q_raw)
    k_inv = inv_rms(k_raw)
    query = (
        rotate(q_raw * q_inv * query_scale, cosine, sine)
        .reshape(tok_rows, query_width)
        .astype(jnp.bfloat16)
    )
    keys = (
        rotate(k_raw * k_inv * key_scale, cosine, sine)
        .reshape(tok_rows, kv_width)
        .astype(jnp.bfloat16)
    )
    values = projected[:, query_width + kv_width :].astype(jnp.bfloat16)
    query_heads, key_heads, value_heads = (
        lax.all_to_all(query, "sp", split_axis=1, concat_axis=0, tiled=True),
        lax.all_to_all(keys, "sp", split_axis=1, concat_axis=0, tiled=True),
        lax.all_to_all(values, "sp", split_axis=1, concat_axis=0, tiled=True),
    )
    key_all, value_all = (
        lax.all_gather(key_heads, "fsdp", axis=0, tiled=True),
        lax.all_gather(value_heads, "fsdp", axis=0, tiled=True),
    )
    span_rows = query_heads.shape[0]
    span_first = fsdp_rank * span_rows
    span_tokens = span_first + jnp.arange(span_rows, dtype=jnp.int32)
    span_starts = item_starts(span_tokens, lengths)
    query_four = query_heads.reshape(span_rows, local_kv, head_group, HEAD_DIM)
    key_total = key_all.shape[0]
    key_block = min(1024, key_total)
    block_count = key_total // key_block
    key_blocks = key_all.reshape(block_count, key_block, local_kv, HEAD_DIM)
    value_blocks = value_all.reshape(block_count, key_block, local_kv, HEAD_DIM)
    block_firsts = jnp.arange(block_count, dtype=jnp.int32) * key_block
    lowest_key = span_starts[0]
    highest_key = span_first + span_rows - 1

    def needed(block_first):
        return (block_first <= highest_key) & (block_first + key_block - 1 >= lowest_key)

    def block_weights(key_piece, block_first):
        scores = (
            jnp.einsum("qkgd,jkd->kgqj", query_four, key_piece, preferred_element_type=jnp.float32)
            * score_scale
        )
        columns = block_first + jnp.arange(key_block, dtype=jnp.int32)
        allowed = (columns[None, :] <= span_tokens[:, None]) & (
            columns[None, :] >= span_starts[:, None]
        )
        return jnp.where(allowed[None, None], jnp.exp(scores), 0.0)

    def forward_step(running, pieces):
        key_piece, value_piece, block_first = pieces

        def forward_compute(current):
            totals, unnormed = current
            weights = block_weights(key_piece, block_first)
            totals = totals + jnp.sum(weights, axis=3)
            unnormed = unnormed + jnp.einsum(
                "kgqj,jkd->qkgd",
                weights.astype(jnp.bfloat16),
                value_piece,
                preferred_element_type=jnp.float32,
            )
            return (totals, unnormed)

        return (
            lax.cond(needed(block_first), forward_compute, lambda current: current, running),
            None,
        )

    start_state = (
        jnp.zeros((local_kv, head_group, span_rows), jnp.float32),
        jnp.zeros((span_rows, local_kv, head_group, HEAD_DIM), jnp.float32),
    )
    scanned = lax.scan(forward_step, start_state, (key_blocks, value_blocks, block_firsts))[0]
    totals, unnormed = scanned
    totals_rows = jnp.transpose(totals, (2, 0, 1))[..., None]
    attended_heads = unnormed / totals_rows
    attended_send = attended_heads.reshape(span_rows, local_kv * head_group * HEAD_DIM).astype(
        jnp.bfloat16
    )
    returned = lax.all_to_all(attended_send, "sp", split_axis=0, concat_axis=1, tiled=True)
    gate_prob = jax.nn.sigmoid(gate_logit)
    attended_tok = returned.astype(jnp.float32).reshape(tok_rows, HEADS, HEAD_DIM)
    gated = (
        (attended_tok * gate_prob[:, :, None]).reshape(tok_rows, query_width).astype(jnp.bfloat16)
    )
    middle = inputs + jnp.dot(gated, out_full, preferred_element_type=jnp.float32)
    inv_second = inv_rms(middle)
    normed_b = (middle * inv_second * ffn_scale).astype(jnp.bfloat16)
    gate_piece = lax.all_gather(w_gate, "fsdp", axis=0, tiled=True)
    up_piece = lax.all_gather(w_up, "fsdp", axis=0, tiled=True)
    down_piece = lax.all_gather(w_down, "fsdp", axis=0, tiled=True)
    gate_pre = mat_nt(normed_b, gate_piece)
    up_pre = mat_nt(normed_b, up_piece)
    hidden = (jax.nn.silu(gate_pre) * up_pre).astype(jnp.bfloat16)
    ffn_part = jnp.dot(hidden, down_piece, preferred_element_type=jnp.float32)
    hidden_out = (middle + ffn_part).astype(jnp.bfloat16)
    gate_piece = lax.all_gather(w_gate, "fsdp", axis=0, tiled=True)
    up_piece = lax.all_gather(w_up, "fsdp", axis=0, tiled=True)
    down_piece = lax.all_gather(w_down, "fsdp", axis=0, tiled=True)
    gate_pre = mat_nt(normed_b, gate_piece)
    up_pre = mat_nt(normed_b, up_piece)
    sigma = jax.nn.sigmoid(gate_pre)
    swish = gate_pre * sigma
    hidden = (swish * up_pre).astype(jnp.bfloat16)
    grad_hidden = mat_nt(grad_out, down_piece)
    grad_gate = (grad_hidden * up_pre * sigma * (1.0 + gate_pre * (1.0 - sigma))).astype(
        jnp.bfloat16
    )
    grad_up = (grad_hidden * swish).astype(jnp.bfloat16)
    grad_acc = jnp.dot(grad_gate, gate_piece, preferred_element_type=jnp.float32) + jnp.dot(
        grad_up, up_piece, preferred_element_type=jnp.float32
    )
    grad_ffn_gain_local = jnp.sum(grad_acc * middle * inv_second, axis=0)
    grad_middle = grad_out.astype(jnp.float32) + norm_back(grad_acc, middle, inv_second, ffn_scale)
    grad_mid_b = grad_middle.astype(jnp.bfloat16)
    grad_gated = mat_nt(grad_mid_b, out_full).reshape(tok_rows, HEADS, HEAD_DIM)
    grad_attended = (
        (grad_gated * gate_prob[:, :, None]).reshape(tok_rows, query_width).astype(jnp.bfloat16)
    )
    gate_grad = (jnp.sum(grad_gated * attended_tok, axis=2) * gate_prob * (1.0 - gate_prob)).astype(
        jnp.bfloat16
    )
    grad_heads = lax.all_to_all(grad_attended, "sp", split_axis=1, concat_axis=0, tiled=True)
    grad_four = grad_heads.astype(jnp.float32).reshape(span_rows, local_kv, head_group, HEAD_DIM)
    grad_scaled = (grad_four / totals_rows).astype(jnp.bfloat16)
    delta_rows = jnp.sum(grad_four * attended_heads, axis=3) / totals_rows[..., 0]
    delta_heads = jnp.transpose(delta_rows, (1, 2, 0))

    def backward_step(grad_query, pieces):
        key_piece, value_piece, block_first = pieces

        def backward_compute(current):
            weights = block_weights(key_piece, block_first)
            grad_prob = jnp.einsum(
                "qkgd,jkd->kgqj", grad_scaled, value_piece, preferred_element_type=jnp.float32
            )
            grad_score = (weights * (grad_prob - delta_heads[..., None])).astype(jnp.bfloat16)
            current = (
                current
                + jnp.einsum(
                    "kgqj,jkd->qkgd", grad_score, key_piece, preferred_element_type=jnp.float32
                )
                * score_scale
            )
            grad_key = (
                jnp.einsum(
                    "kgqj,qkgd->jkd", grad_score, query_four, preferred_element_type=jnp.float32
                )
                * score_scale
            )
            grad_value = jnp.einsum(
                "kgqj,qkgd->jkd",
                weights.astype(jnp.bfloat16),
                grad_scaled,
                preferred_element_type=jnp.float32,
            )
            return (current, (grad_key, grad_value))

        def skip(current):
            nothing = jnp.zeros((key_block, local_kv, HEAD_DIM), jnp.float32)
            return (current, (nothing, nothing))

        return lax.cond(needed(block_first), backward_compute, skip, grad_query)

    grad_query, key_value_grads = lax.scan(
        backward_step,
        jnp.zeros((span_rows, local_kv, head_group, HEAD_DIM), jnp.float32),
        (key_blocks, value_blocks, block_firsts),
    )
    key_grads, value_grads = key_value_grads
    key_sum, value_sum = (
        lax.psum_scatter(
            key_grads.reshape(key_total, local_kv * HEAD_DIM),
            "fsdp",
            scatter_dimension=0,
            tiled=True,
        ),
        lax.psum_scatter(
            value_grads.reshape(key_total, local_kv * HEAD_DIM),
            "fsdp",
            scatter_dimension=0,
            tiled=True,
        ),
    )
    query_send = grad_query.reshape(span_rows, local_kv * head_group * HEAD_DIM).astype(
        jnp.bfloat16
    )
    back_query, back_key, back_value = (
        lax.all_to_all(query_send, "sp", split_axis=0, concat_axis=1, tiled=True),
        lax.all_to_all(key_sum.astype(jnp.bfloat16), "sp", split_axis=0, concat_axis=1, tiled=True),
        lax.all_to_all(
            value_sum.astype(jnp.bfloat16), "sp", split_axis=0, concat_axis=1, tiled=True
        ),
    )
    grad_qn = rotate_back(
        back_query.astype(jnp.float32).reshape(tok_rows, HEADS, HEAD_DIM), cosine, sine
    )
    grad_kn = rotate_back(
        back_key.astype(jnp.float32).reshape(tok_rows, KV_HEADS, HEAD_DIM), cosine, sine
    )
    grad_q_gain_local = jnp.sum(grad_qn * q_raw * q_inv, axis=(0, 1))
    grad_k_gain_local = jnp.sum(grad_kn * k_raw * k_inv, axis=(0, 1))
    grad_q_raw = norm_back(grad_qn, q_raw, q_inv, query_scale).reshape(tok_rows, query_width)
    grad_k_raw = norm_back(grad_kn, k_raw, k_inv, key_scale).reshape(tok_rows, kv_width)
    grad_proj = jnp.concatenate(
        [grad_q_raw.astype(jnp.bfloat16), grad_k_raw.astype(jnp.bfloat16), back_value], axis=1
    )
    grad_normed_a = jnp.dot(grad_proj, qkv_full, preferred_element_type=jnp.float32) + jnp.dot(
        gate_grad, gate_full, preferred_element_type=jnp.float32
    )
    grad_attn_gain_local = jnp.sum(grad_normed_a * inputs * inv_first, axis=0)
    grad_in = grad_middle + norm_back(grad_normed_a, inputs, inv_first, attn_scale)
    qkv_rows = w_qkv.shape[0]
    out_rows = w_out.shape[0]
    gate_rows = w_head_gate.shape[0]
    block_rows = qkv_rows + out_rows + gate_rows + 3
    small_rows = jnp.stack(
        [
            grad_attn_gain_local,
            grad_ffn_gain_local,
            jnp.concatenate(
                [
                    grad_q_gain_local,
                    grad_k_gain_local,
                    jnp.zeros((model_width - 2 * HEAD_DIM,), jnp.float32),
                ]
            ),
        ],
        axis=0,
    )
    ffn_partial = lax.psum_scatter(
        jnp.concatenate(
            [mat_tn(grad_gate, normed_b), mat_tn(grad_up, normed_b), mat_tn(hidden, grad_out)],
            axis=1,
        ).astype(jnp.bfloat16),
        "fsdp",
        scatter_dimension=0,
        tiled=True,
    ).astype(jnp.float32)
    proj_split = grad_proj.reshape(tok_rows, fsdp_count, qkv_rows)
    gated_split = gated.reshape(tok_rows, fsdp_count, out_rows)
    gate_split = gate_grad.reshape(tok_rows, fsdp_count, gate_rows)
    owners = block_rows * lax.axis_size("fsdp") // block_rows
    qkv_term = jnp.einsum("tor,td->ord", proj_split, normed_a, preferred_element_type=jnp.float32)
    out_term = jnp.einsum(
        "tor,td->ord", gated_split, grad_mid_b, preferred_element_type=jnp.float32
    )
    gate_term = jnp.einsum("tor,td->ord", gate_split, normed_a, preferred_element_type=jnp.float32)
    small_term = jnp.broadcast_to(small_rows[None], (owners, 3, model_width))
    joined = jnp.concatenate([qkv_term, out_term, gate_term, small_term], axis=1)
    attn_partial = lax.psum_scatter(
        joined.reshape(owners * block_rows, model_width), "fsdp", scatter_dimension=0, tiled=True
    )
    ffn_total, attn_total = lax.psum((ffn_partial, attn_partial), "sp")
    grad_w_gate = ffn_total[:, :model_width]
    grad_w_up = ffn_total[:, model_width : 2 * model_width]
    grad_w_down = ffn_total[:, 2 * model_width :]
    grad_w_qkv = attn_total[:qkv_rows]
    grad_w_out = attn_total[qkv_rows : qkv_rows + out_rows]
    grad_w_head_gate = attn_total[qkv_rows + out_rows : qkv_rows + out_rows + gate_rows]
    gain_sums = attn_total[qkv_rows + out_rows + gate_rows :]
    gain_part = model_width // fsdp_count
    head_part = HEAD_DIM // fsdp_count
    grad_attn_gain = lax.dynamic_slice_in_dim(gain_sums[0], fsdp_rank * gain_part, gain_part)
    grad_ffn_gain = lax.dynamic_slice_in_dim(gain_sums[1], fsdp_rank * gain_part, gain_part)
    grad_q_gain = lax.dynamic_slice_in_dim(gain_sums[2], fsdp_rank * head_part, head_part)
    grad_k_gain = lax.dynamic_slice_in_dim(
        gain_sums[2], HEAD_DIM + fsdp_rank * head_part, head_part
    )
    return (
        hidden_out,
        grad_in,
        grad_attn_gain,
        grad_w_qkv,
        grad_w_head_gate,
        grad_q_gain,
        grad_k_gain,
        grad_w_out,
        grad_ffn_gain,
        grad_w_gate,
        grad_w_up,
        grad_w_down,
    )


MESH = pl.DeviceIdType.MESH
VMEM_LIMIT = 60 * 1024 * 1024


def peer_copy(src, dst, send_sem, recv_sem, rank, plane):
    return pltpu.make_async_remote_copy(
        src_ref=src,
        dst_ref=dst,
        send_sem=send_sem,
        recv_sem=recv_sem,
        device_id=(rank, plane),
        device_id_type=MESH,
    )


def greet(peers):
    barrier = pltpu.get_barrier_semaphore()
    for peer in peers:
        pl.semaphore_signal(barrier, inc=1, device_id=peer, device_id_type=MESH)
    pl.semaphore_wait(barrier, len(peers))


def gather_gains_kernel(x_ref, s_ref, o_ref, so_ref, send_sem, recv_sem, sib_send, sib_recv, own_sem, small_send, small_recv):
    rank, plane = lax.axis_index("fsdp"), lax.axis_index("sp")
    greet([(rank ^ k, plane) for k in range(1, 8)])
    small = []
    for k in range(1, 8):
        copy = peer_copy(
            s_ref, so_ref.at[rank], small_send.at[k - 1], small_recv.at[k - 1], rank ^ k, plane
        )
        copy.start()
        small.append(copy)
    so_ref[rank] = s_ref[...]
    gather_blocks(x_ref, o_ref, send_sem, recv_sem, sib_send, sib_recv, own_sem)
    for copy in small:
        copy.wait()


def gather_kernel(x_ref, o_ref, *sems):
    rank, plane = lax.axis_index("fsdp"), lax.axis_index("sp")
    greet([(rank ^ k, plane) for k in (1, 2, 4, 6)])
    gather_blocks(x_ref, o_ref, *sems)


def gather_blocks(x_ref, o_ref, send_sem, recv_sem, sib_send, sib_recv, own_sem):
    rank, plane = lax.axis_index("fsdp"), lax.axis_index("sp")
    half = x_ref.shape[0] // 2
    own = pltpu.make_async_copy(x_ref, o_ref.at[rank], own_sem)
    own.start()
    far = {}
    for h in range(2):
        rows = pl.ds(h * half, half)
        for i, k in enumerate((6, 2, 4)):
            far[h, i] = peer_copy(
                x_ref.at[rows],
                o_ref.at[rank, rows],
                send_sem.at[h, i],
                recv_sem.at[h, i],
                rank ^ k,
                plane,
            )
            far[h, i].start()
    near = []
    first = peer_copy(
        x_ref, o_ref.at[rank], sib_send.at[0, 3], sib_recv.at[0, 3], rank ^ 1, plane
    )
    first.start()
    near.append(first)
    for h in range(2):
        rows = pl.ds(h * half, half)
        for i, k in enumerate((6, 2, 4)):
            far[h, i].wait_recv()
            block = o_ref.at[rank ^ k, rows]
            forward = peer_copy(
                block, block, sib_send.at[h, i], sib_recv.at[h, i], rank ^ 1, plane
            )
            forward.start()
            near.append(forward)
    for copy in near:
        copy.wait()
    for copy in far.values():
        copy.wait_send()
    own.wait()


def gather_plane(x, collective_id, small=None):
    rows, width = x.shape
    ranks = lax.axis_size("fsdp")
    big = pl.BlockSpec(memory_space=pl.ANY)
    sems = [
        pltpu.SemaphoreType.DMA((2, 3)),
        pltpu.SemaphoreType.DMA((2, 3)),
        pltpu.SemaphoreType.DMA((2, 4)),
        pltpu.SemaphoreType.DMA((2, 4)),
        pltpu.SemaphoreType.DMA,
    ]
    out = jax.ShapeDtypeStruct((ranks, rows, width), x.dtype)
    if small is not None:
        vmem = pl.BlockSpec(memory_space=pltpu.VMEM)
        return pl.pallas_call(
            gather_gains_kernel,
            out_shape=(out, jax.ShapeDtypeStruct((ranks,) + small.shape, small.dtype)),
            in_specs=[big, vmem],
            out_specs=(big, vmem),
            scratch_shapes=sems + [pltpu.SemaphoreType.DMA((7,)), pltpu.SemaphoreType.DMA((7,))],
            compiler_params=pltpu.CompilerParams(
                collective_id=collective_id, has_side_effects=True, vmem_limit_bytes=VMEM_LIMIT
            ),
            name="gather_gains",
        )(x, small)
    return pl.pallas_call(
        gather_kernel,
        out_shape=out,
        in_specs=[big],
        out_specs=big,
        scratch_shapes=sems,
        compiler_params=pltpu.CompilerParams(
            collective_id=collective_id, has_side_effects=True, vmem_limit_bytes=VMEM_LIMIT
        ),
        name="gather_plane",
    )(x)


def scatter_gains_kernel(planes, p_ref, s_ref, g_ref, o_ref, so_ref, go_ref, small_buf, line_out, line_buf, small_send, small_recv, line_send, line_recv, *rest):
    rank, plane = lax.axis_index("fsdp"), lax.axis_index("sp")
    others = [lax.rem(plane + k, planes) for k in range(1, planes)]
    greet([(rank ^ k, plane) for k in range(1, 8)] + [(rank, other) for other in others])
    small = []
    for k in range(1, 8):
        copy = peer_copy(
            s_ref.at[rank ^ k],
            small_buf.at[k - 1],
            small_send.at[k - 1],
            small_recv.at[k - 1],
            rank ^ k,
            plane,
        )
        copy.start()
        small.append(copy)
    scatter_blocks(p_ref, o_ref, *rest)
    total = s_ref[rank]
    for k in range(1, 8):
        small[k - 1].wait()
        total = total + small_buf[k - 1]
    tail = total.shape[0]
    line_out[:tail] = total
    line_out[tail:] = g_ref[...]
    line = []
    for k in range(1, planes):
        copy = peer_copy(
            line_out,
            line_buf.at[k - 1],
            line_send.at[k - 1],
            line_recv.at[k - 1],
            rank,
            others[k - 1],
        )
        copy.start()
        line.append(copy)
    final = line_out[...]
    for k in range(1, planes):
        line[k - 1].wait()
        final = final + line_buf[k - 1]
    so_ref[...] = final[:tail]
    go_ref[...] = final[tail:]


def scatter_kernel(*refs):
    rank, plane = lax.axis_index("fsdp"), lax.axis_index("sp")
    greet([(rank ^ k, plane) for k in (1, 2, 4, 6)])
    scatter_blocks(*refs)


def scatter_blocks(p_ref, o_ref, near_buf, out_buf, far_buf, sib_send, sib_recv, send_sem, recv_sem):
    rank, plane = lax.axis_index("fsdp"), lax.axis_index("sp")
    order = (6, 2, 4, 0)
    near = []
    for i, k in enumerate(order):
        copy = peer_copy(
            p_ref.at[rank ^ 1 ^ k], near_buf.at[i], sib_send.at[i], sib_recv.at[i], rank ^ 1, plane
        )
        copy.start()
        near.append(copy)
    far = []
    for i, k in enumerate(order):
        near[i].wait_recv()
        joined = p_ref[rank ^ k].astype(jnp.float32) + near_buf[i].astype(jnp.float32)
        if k:
            out_buf[i] = joined.astype(out_buf.dtype)
            copy = peer_copy(
                out_buf.at[i], far_buf.at[i], send_sem.at[i], recv_sem.at[i], rank ^ k, plane
            )
            copy.start()
            far.append(copy)
        else:
            o_ref[...] = joined
    for i in (1, 2, 0):
        far[i].wait_recv()
        o_ref[...] += far_buf[i].astype(jnp.float32)
    for copy in near + far:
        copy.wait_send()


def scatter_plane(p, collective_id, small=None, gate=None):
    ranks, rows, width = p.shape
    vmem = pl.BlockSpec(memory_space=pltpu.VMEM)
    scratch = [
        pltpu.VMEM((4, rows, width), p.dtype),
        pltpu.VMEM((3, rows, width), p.dtype),
        pltpu.VMEM((3, rows, width), p.dtype),
        pltpu.SemaphoreType.DMA((4,)),
        pltpu.SemaphoreType.DMA((4,)),
        pltpu.SemaphoreType.DMA((3,)),
        pltpu.SemaphoreType.DMA((3,)),
    ]
    out = jax.ShapeDtypeStruct((rows, width), jnp.float32)
    params = pltpu.CompilerParams(
        collective_id=collective_id, has_side_effects=True, vmem_limit_bytes=VMEM_LIMIT
    )
    if small is not None:
        planes = lax.axis_size("sp")
        joint = (small.shape[1] + gate.shape[0], small.shape[2])
        return pl.pallas_call(
            functools.partial(scatter_gains_kernel, planes),
            out_shape=(
                out,
                jax.ShapeDtypeStruct(small.shape[1:], small.dtype),
                jax.ShapeDtypeStruct(gate.shape, gate.dtype),
            ),
            in_specs=[vmem, vmem, vmem],
            out_specs=(vmem, vmem, vmem),
            scratch_shapes=[
                pltpu.VMEM((7,) + small.shape[1:], small.dtype),
                pltpu.VMEM(joint, small.dtype),
                pltpu.VMEM((planes - 1,) + joint, small.dtype),
                pltpu.SemaphoreType.DMA((7,)),
                pltpu.SemaphoreType.DMA((7,)),
                pltpu.SemaphoreType.DMA((planes - 1,)),
                pltpu.SemaphoreType.DMA((planes - 1,)),
            ]
            + scratch,
            compiler_params=params,
            name="scatter_gains",
        )(p, small, gate)
    return pl.pallas_call(
        scatter_kernel,
        out_shape=out,
        in_specs=[vmem],
        out_specs=vmem,
        scratch_shapes=scratch,
        compiler_params=params,
        name="scatter_plane",
    )(p)


GATHER_COPIES = 13


def gather_copy(buf, i, send_sem, recv_sem, own=None):
    rank, plane = lax.axis_index("fsdp"), lax.axis_index("sp")
    rows = buf.shape[1]
    top, low = pl.ds(0, rows // 2), pl.ds(rows // 2, rows // 2)
    block, part, to = (
        (0, top, 2),
        (0, low, 2),
        (0, low, 4),
        (0, top, 4),
        (2, top, 4),
        (4, low, 2),
        (0, pl.ds(0, rows), 1),
        (2, top, 1),
        (2, low, 1),
        (4, low, 1),
        (4, top, 1),
        (6, top, 1),
        (6, low, 1),
    )[i]
    piece = buf.at[rank ^ block, part]
    source = piece if own is None or block else own.at[part]
    return peer_copy(source, piece, send_sem.at[i], recv_sem.at[i], rank ^ to, plane)


def gather_start(buf, send_sem, recv_sem, own=None):
    for i in (6, 0, 2, 1, 3):
        gather_copy(buf, i, send_sem, recv_sem, own).start()


def gather_pass(buf, send_sem, recv_sem, pairs):
    for arrived, onward in pairs:
        gather_copy(buf, arrived, send_sem, recv_sem).wait_recv()
        for i in onward:
            gather_copy(buf, i, send_sem, recv_sem).start()


def gather_wait(buf, send_sem, recv_sem, copies):
    for i in copies:
        gather_copy(buf, i, send_sem, recv_sem).wait_recv()


def gather_sent(buf, send_sem, recv_sem):
    for i in range(GATHER_COPIES):
        gather_copy(buf, i, send_sem, recv_sem).wait_send()


NEIGHBOURS_FIRST = ((0, (4, 7)), (2, (5, 9)), (1, (8,)), (3, (10,)))
DIAGONAL = ((4, (11,)), (5, (12,)))
FROM_SIBLING = (6, 7, 8, 9, 10, 11, 12)


def greet_line(ranks, planes):
    rank, plane = lax.axis_index("fsdp"), lax.axis_index("sp")
    barrier = pltpu.get_barrier_semaphore()
    for k in range(1, ranks):
        pl.semaphore_signal(
            barrier, inc=1, device_id=(rank ^ k, plane), device_id_type=MESH
        )

    @pl.when(plane > 0)
    def _():
        pl.semaphore_signal(barrier, inc=1, device_id=(rank, plane - 1), device_id_type=MESH)

    @pl.when(plane < planes - 1)
    def _():
        pl.semaphore_signal(barrier, inc=1, device_id=(rank, plane + 1), device_id_type=MESH)

    lower = (plane > 0).astype(jnp.int32)
    upper = (plane < planes - 1).astype(jnp.int32)
    pl.semaphore_wait(barrier, ranks - 1 + lower + upper)


def heads_kernel(planes, n_ref, g_ref, q_ref, kv_ref, dy_ref, g_sem, ag_send, ag_recv, own_sem, q_send, q_recv, kv_send, kv_recv, line_send, line_recv):
    rank, plane = lax.axis_index("fsdp"), lax.axis_index("sp")
    greet_line(8, planes)
    own_block = pltpu.make_async_copy(g_ref, dy_ref.at[rank], g_sem)
    own_block.start()

    def q_copy(m, to):
        return peer_copy(n_ref.at[pl.ds(2 * m, 2)], q_ref, q_send.at[m], q_recv, to, plane)

    def kv_copy(m, which, to):
        return peer_copy(
            n_ref.at[m], kv_ref.at[plane, which], kv_send.at[m], kv_recv.at[which], to, plane
        )

    def q_local():
        return pltpu.make_async_copy(n_ref.at[pl.ds(0, 2)], q_ref, own_sem)

    def kv_local(m, which):
        return pltpu.make_async_copy(n_ref.at[m], kv_ref.at[plane, which], own_sem)

    @pl.when(rank < 4)
    def _():
        for m in range(2):
            @pl.when(2 * rank + m != rank)
            def _():
                q_copy(m, 2 * rank + m).start()

    @pl.when(rank == 0)
    def _():
        q_local().start()

    for which in range(2):
        first = 4 + 2 * which
        own_m = (first + 1) % 4

        @pl.when((rank == first) | (rank == first + 1))
        def _():
            for m in range(4):
                to = 4 * (rank - first) + m

                @pl.when(to != rank)
                def _():
                    kv_copy(m, which, to).start()

        @pl.when(rank == first + 1)
        def _():
            kv_local(own_m, which).start()

    for which in range(2):
        first = 4 + 2 * which
        own_m = (first + 1) % 4

        @pl.when(rank == first + 1)
        def _():
            kv_local(own_m, which).wait()

        @pl.when(rank != first + 1)
        def _():
            kv_copy(0, which, 0).wait_recv()

        line_step(planes, kv_ref, which, 0, line_send, line_recv)
    gather_start(dy_ref, ag_send, ag_recv, g_ref)
    for j in range(1, planes):
        for which in range(2):
            line_step(planes, kv_ref, which, j, line_send, line_recv)
        if j == 1:
            gather_pass(dy_ref, ag_send, ag_recv, NEIGHBOURS_FIRST)
        if j == 2:
            gather_pass(dy_ref, ag_send, ag_recv, DIAGONAL)
    gather_wait(dy_ref, ag_send, ag_recv, FROM_SIBLING)
    gather_sent(dy_ref, ag_send, ag_recv)
    own_block.wait()

    @pl.when(rank == 0)
    def _():
        q_local().wait()

    @pl.when(rank != 0)
    def _():
        q_copy(0, 0).wait_recv()

    @pl.when(rank < 4)
    def _():
        for m in range(2):
            @pl.when(2 * rank + m != rank)
            def _():
                q_copy(m, 0).wait_send()

    for which in range(2):
        first = 4 + 2 * which

        @pl.when((rank == first) | (rank == first + 1))
        def _():
            for m in range(4):
                @pl.when(4 * (rank - first) + m != rank)
                def _():
                    kv_copy(m, which, 0).wait_send()

    for j in range(planes - 1):
        for which in range(2):
            for side in range(2):
                @pl.when(line_sends(planes, plane, j, side))
                def _():
                    line_copy(kv_ref, which, j, side, line_send, line_recv).wait_send()


def line_sends(planes, plane, j, side):
    if side == 0:
        return (plane >= j) & (plane < planes - 1)
    return (plane + j <= planes - 1) & (plane > 0)


def line_copy(kv_ref, which, j, side, line_send, line_recv):
    rank, plane = lax.axis_index("fsdp"), lax.axis_index("sp")
    origin = plane - j if side == 0 else plane + j
    block = kv_ref.at[origin, which]
    to = plane + 1 if side == 0 else plane - 1
    return peer_copy(
        block, block, line_send.at[side, j, which], line_recv.at[side, j, which], rank, to
    )


def line_step(planes, kv_ref, which, j, line_send, line_recv):
    rank, plane = lax.axis_index("fsdp"), lax.axis_index("sp")
    for side in range(2):
        if j:
            arrives = (plane >= j) if side == 0 else (plane + j <= planes - 1)

            @pl.when(arrives)
            def _():
                origin = plane - j if side == 0 else plane + j
                block = kv_ref.at[origin, which]
                peer_copy(
                    block,
                    block,
                    line_send.at[side, j - 1, which],
                    line_recv.at[side, j - 1, which],
                    rank,
                    plane,
                ).wait_recv()

        if j < planes - 1:
            @pl.when(line_sends(planes, plane, j, side))
            def _():
                line_copy(kv_ref, which, j, side, line_send, line_recv).start()


def exchange_heads(natural, grad, collective_id):
    _, tokens, width = natural.shape
    planes = lax.axis_size("sp")
    ranks = lax.axis_size("fsdp")
    hbm = pl.BlockSpec(memory_space=pl.ANY)
    return pl.pallas_call(
        functools.partial(heads_kernel, planes),
        out_shape=(
            jax.ShapeDtypeStruct((2, tokens, width), natural.dtype),
            jax.ShapeDtypeStruct((planes, 2, tokens, width), natural.dtype),
            jax.ShapeDtypeStruct((ranks,) + grad.shape, grad.dtype),
        ),
        in_specs=[hbm, hbm],
        out_specs=(hbm, hbm, hbm),
        scratch_shapes=[
            pltpu.SemaphoreType.DMA,
            pltpu.SemaphoreType.DMA((GATHER_COPIES,)),
            pltpu.SemaphoreType.DMA((GATHER_COPIES,)),
            pltpu.SemaphoreType.DMA,
            pltpu.SemaphoreType.DMA((2,)),
            pltpu.SemaphoreType.DMA,
            pltpu.SemaphoreType.DMA((4,)),
            pltpu.SemaphoreType.DMA((2,)),
            pltpu.SemaphoreType.DMA((2, planes - 1, 2)),
            pltpu.SemaphoreType.DMA((2, planes - 1, 2)),
        ],
        compiler_params=pltpu.CompilerParams(
            collective_id=collective_id, has_side_effects=True, vmem_limit_bytes=VMEM_LIMIT
        ),
        name="exchange_heads",
    )(natural, grad)


def unheads_kernel(planes, dq_ref, dkv_ref, dz_ref, n_ref, dy_ref, g_sem, ag_send, ag_recv, line_out, line_in, done, own_sem, q_send, q_recv, kv_send, kv_recv, line_send, line_recv):
    rank, plane = lax.axis_index("fsdp"), lax.axis_index("sp")
    greet_line(8, planes)
    own_blocks = [
        pltpu.make_async_copy(dz_ref.at[j], dy_ref.at[j, rank], g_sem.at[j])
        for j in range(planes - 1)
    ]
    for copy in own_blocks:
        copy.start()
    gathers = [
        (dy_ref.at[j], ag_send.at[j], ag_recv.at[j]) for j in range(planes - 1)
    ]

    def q_copy(m, to):
        return peer_copy(dq_ref, n_ref.at[pl.ds(2 * m, 2)], q_send, q_recv.at[m], to, plane)

    def kv_copy(m, which, to):
        return peer_copy(done.at[which], n_ref.at[m], kv_send.at[which], kv_recv.at[m], to, plane)

    def q_local():
        return pltpu.make_async_copy(dq_ref, n_ref.at[pl.ds(0, 2)], own_sem)

    def kv_local(m, which):
        return pltpu.make_async_copy(done.at[which], n_ref.at[m], own_sem)

    @pl.when(rank == 0)
    def _():
        q_local().start()

    for m in range(2):
        @pl.when((rank % 2 == m) & (rank != 0))
        def _():
            q_copy(m, rank // 2).start()

    def step_copy(j, which, side):
        to = plane + 1 if side == 0 else plane - 1
        return peer_copy(
            line_out.at[side, j, which],
            line_in.at[side, j, which],
            line_send.at[side, j, which],
            line_recv.at[side, j, which],
            rank,
            to,
        )

    def sends(j, side):
        return plane < planes - 1 - j if side == 0 else plane > j

    def target(j, side):
        return planes - 1 - j if side == 0 else j

    for j in range(planes - 1):
        for which in range(2):
            for side in range(2):
                inner = plane > 0 if side == 0 else plane < planes - 1

                @pl.when(sends(j, side) & inner)
                def _():
                    step_copy(j, which, side).wait_recv()
                    total = dkv_ref[target(j, side), which].astype(jnp.float32) + line_in[
                        side, j, which
                    ].astype(jnp.float32)
                    line_out[side, j, which] = total.astype(line_out.dtype)

                @pl.when(sends(j, side) & jnp.logical_not(inner))
                def _():
                    line_out[side, j, which] = dkv_ref[target(j, side), which]

                @pl.when(sends(j, side))
                def _():
                    step_copy(j, which, side).start()

        gather_start(*gathers[j], own=dz_ref.at[j])
        if j:
            gather_pass(*gathers[j - 1], NEIGHBOURS_FIRST)
        if j > 1:
            gather_pass(*gathers[j - 2], DIAGONAL)

    for which in range(2):
        total = dkv_ref[plane, which].astype(jnp.float32)
        done32 = total
        for j in range(planes - 1):
            for side in range(2):
                @pl.when(plane == target(j, side))
                def _():
                    step_copy(j, which, side).wait_recv()
        low = jnp.minimum(planes - 1 - plane, planes - 2)
        high = jnp.minimum(plane, planes - 2)
        below = line_in[0, low, which].astype(jnp.float32)
        above = line_in[1, high, which].astype(jnp.float32)
        done32 = done32 + jnp.where(plane > 0, below, 0.0) + jnp.where(plane < planes - 1, above, 0.0)
        done[which] = done32.astype(done.dtype)
        first = 4 + 2 * which
        to = first + rank // 4
        for m in range(4):
            @pl.when((rank % 4 == m) & (to != rank))
            def _():
                kv_copy(m, which, to).start()

            @pl.when((rank % 4 == m) & (to == rank))
            def _():
                kv_local(m, which).start()

    gather_pass(*gathers[planes - 2], NEIGHBOURS_FIRST)
    for j in range(max(planes - 3, 0), planes - 1):
        gather_pass(*gathers[j], DIAGONAL)
    for gather in gathers:
        gather_wait(*gather, FROM_SIBLING)
        gather_sent(*gather)
    for copy in own_blocks:
        copy.wait()

    @pl.when(rank < 4)
    def _():
        for m in range(2):
            @pl.when(2 * rank + m != rank)
            def _():
                q_copy(m, 0).wait_recv()

            @pl.when(2 * rank + m == rank)
            def _():
                q_local().wait()

    for which in range(2):
        first = 4 + 2 * which

        @pl.when((rank == first) | (rank == first + 1))
        def _():
            for m in range(4):
                @pl.when(4 * (rank - first) + m != rank)
                def _():
                    kv_copy(m, which, 0).wait_recv()

                @pl.when(4 * (rank - first) + m == rank)
                def _():
                    kv_local(m, which).wait()

    @pl.when(rank != 0)
    def _():
        q_copy(0, 0).wait_send()

    for which in range(2):
        @pl.when(4 + 2 * which + rank // 4 != rank)
        def _():
            kv_copy(0, which, 0).wait_send()

    for j in range(planes - 1):
        for which in range(2):
            for side in range(2):
                @pl.when(sends(j, side))
                def _():
                    step_copy(j, which, side).wait_send()


def return_heads(grad_query, grad_kv, grad_line, collective_id):
    _, tokens, width = grad_query.shape
    planes = lax.axis_size("sp")
    ranks = lax.axis_size("fsdp")
    vmem = pl.BlockSpec(memory_space=pltpu.VMEM)
    hbm = pl.BlockSpec(memory_space=pl.ANY)
    return pl.pallas_call(
        functools.partial(unheads_kernel, planes),
        out_shape=(
            jax.ShapeDtypeStruct((4, tokens, width), grad_query.dtype),
            jax.ShapeDtypeStruct((planes - 1, ranks) + grad_line.shape[1:], grad_line.dtype),
        ),
        in_specs=[vmem, vmem, hbm],
        out_specs=(vmem, hbm),
        scratch_shapes=[
            pltpu.SemaphoreType.DMA((planes - 1,)),
            pltpu.SemaphoreType.DMA((planes - 1, GATHER_COPIES)),
            pltpu.SemaphoreType.DMA((planes - 1, GATHER_COPIES)),
            pltpu.VMEM((2, planes - 1, 2, tokens, width), grad_query.dtype),
            pltpu.VMEM((2, planes - 1, 2, tokens, width), grad_query.dtype),
            pltpu.VMEM((2, tokens, width), grad_query.dtype),
            pltpu.SemaphoreType.DMA,
            pltpu.SemaphoreType.DMA,
            pltpu.SemaphoreType.DMA((2,)),
            pltpu.SemaphoreType.DMA((2,)),
            pltpu.SemaphoreType.DMA((4,)),
            pltpu.SemaphoreType.DMA((2, planes - 1, 2)),
            pltpu.SemaphoreType.DMA((2, planes - 1, 2)),
        ],
        compiler_params=pltpu.CompilerParams(
            collective_id=collective_id, has_side_effects=True, vmem_limit_bytes=VMEM_LIMIT
        ),
        name="return_heads",
    )(grad_query, grad_kv, grad_line)


def stack_heads(ref):
    return ref[...].reshape(ref.shape[0] * ref.shape[1], ref.shape[2])


def block_bounds(lengths_ref, ranks, planes, rows):
    block = pl.program_id(0)
    span = planes * rows
    first = block * span + lax.axis_index("sp") * rows
    start, end = jnp.int32(0), jnp.int32(0)
    for item in range(lengths_ref.shape[0]):
        end = end + lengths_ref[item]
        start = jnp.where(first >= end, end, start)
    return start // span, block, first


def row_starts(lengths_ref, tokens):
    start, end = jnp.zeros_like(tokens), jnp.int32(0)
    for item in range(lengths_ref.shape[0]):
        end = end + lengths_ref[item]
        start = jnp.where(tokens >= end, end, start)
    return start


def chunk_weights(query, key, scale, tokens, starts, first_key):
    scores = mat_nt(query, key) * scale
    columns = first_key + lax.broadcasted_iota(jnp.int32, scores.shape, 1)
    allowed = (columns <= tokens) & (columns >= starts)
    return jnp.where(allowed, jnp.exp(scores), 0.0)


def query_tokens(first, rows, group):
    row = lax.broadcasted_iota(jnp.int32, (group * rows, 1), 0)
    return first + lax.rem(row, rows)


def attend_kernel(ranks, planes, lengths_ref, q_ref, kv_ref, gate_ref, att_ref, total_ref, gated_ref):
    group, rows, width = q_ref.shape
    scale = HEAD_DIM ** (-0.5)
    low, high, first = block_bounds(lengths_ref, ranks, planes, rows)
    tokens = query_tokens(first, rows, group)
    starts = row_starts(lengths_ref, tokens)
    query = stack_heads(q_ref)
    span = planes * rows

    def step(chunk, running):
        total, unnorm = running
        key = kv_ref[:, 0, chunk].reshape(span, width)
        value = kv_ref[:, 1, chunk].reshape(span, width)
        weights = chunk_weights(query, key, scale, tokens, starts, chunk * span)
        total = total + jnp.sum(weights, axis=1, keepdims=True)
        unnorm = unnorm + jnp.dot(
            weights.astype(jnp.bfloat16), value, preferred_element_type=jnp.float32
        )
        return total, unnorm

    total, unnorm = lax.fori_loop(
        low,
        high + 1,
        step,
        (
            jnp.zeros((group * rows, 1), jnp.float32),
            jnp.zeros((group * rows, width), jnp.float32),
        ),
    )
    attended = unnorm / total
    att_ref[...] = attended.reshape(group, rows, width)
    total_ref[...] = total.reshape(group, rows, 1)
    sent = attended.astype(jnp.bfloat16).astype(jnp.float32)
    for head in range(group):
        gated = sent[head * rows : (head + 1) * rows] * jax.nn.sigmoid(gate_ref[head])
        gated_ref[:, head * width : (head + 1) * width] = gated.astype(jnp.bfloat16)


def attend(lengths, query, kv, gate_logit, rows):
    group, tokens, width = query.shape
    planes = kv.shape[0]
    ranks = tokens // rows
    kv_blocks = kv.reshape(planes, 2, ranks, rows, width)
    block = pl.BlockSpec((group, rows, width), lambda i, *_: (0, i, 0))
    thin = pl.BlockSpec((group, rows, 1), lambda i, *_: (0, i, 0))
    return pl.pallas_call(
        functools.partial(attend_kernel, ranks, planes),
        grid_spec=pltpu.PrefetchScalarGridSpec(
            num_scalar_prefetch=1,
            grid=(ranks,),
            in_specs=[
                block,
                pl.BlockSpec((planes, 2, ranks, rows, width), lambda i, *_: (0, 0, 0, 0, 0)),
                thin,
            ],
            out_specs=(
                block,
                thin,
                pl.BlockSpec((rows, group * width), lambda i, *_: (i, 0)),
            ),
        ),
        out_shape=(
            jax.ShapeDtypeStruct((group, tokens, width), jnp.float32),
            jax.ShapeDtypeStruct((group, tokens, 1), jnp.float32),
            jax.ShapeDtypeStruct((tokens, group * width), jnp.bfloat16),
        ),
        compiler_params=pltpu.CompilerParams(vmem_limit_bytes=VMEM_LIMIT),
        name="attend",
    )(lengths, query, kv_blocks, gate_logit)


def attend_back_kernel(
    ranks, planes, lengths_ref, q_ref, kv_ref, gate_ref, att_ref, total_ref, dgated_ref, dq_ref, dkv_ref, dgate_ref, sums
):
    group, rows, width = q_ref.shape
    scale = HEAD_DIM ** (-0.5)
    low, high, first = block_bounds(lengths_ref, ranks, planes, rows)
    tokens = query_tokens(first, rows, group)
    starts = row_starts(lengths_ref, tokens)
    query = stack_heads(q_ref)
    span = planes * rows

    @pl.when(pl.program_id(0) == 0)
    def _():
        sums[...] = jnp.zeros_like(sums)

    attended = stack_heads(att_ref)
    sent = attended.astype(jnp.bfloat16).astype(jnp.float32)
    total = stack_heads(total_ref)
    logit = stack_heads(gate_ref)
    prob = jax.nn.sigmoid(logit)
    dgated = jnp.concatenate(
        [dgated_ref[:, head * width : (head + 1) * width] for head in range(group)], axis=0
    )
    dattended = (dgated * prob).astype(jnp.bfloat16)
    dlogit = jnp.sum(dgated * sent, axis=1, keepdims=True) * prob * (1.0 - prob)
    dgate_ref[...] = dlogit.astype(jnp.bfloat16).reshape(group, rows, 1)
    dattended = dattended.astype(jnp.float32)
    scaled = (dattended / total).astype(jnp.bfloat16)
    delta = jnp.sum(dattended * attended, axis=1, keepdims=True) / total

    def step(chunk, dquery):
        key = kv_ref[:, 0, chunk].reshape(span, width)
        value = kv_ref[:, 1, chunk].reshape(span, width)
        weights = chunk_weights(query, key, scale, tokens, starts, chunk * span)
        dprob = mat_nt(scaled, value)
        dscore = (weights * (dprob - delta)).astype(jnp.bfloat16)
        dquery = dquery + jnp.dot(dscore, key, preferred_element_type=jnp.float32)
        dkey = mat_tn(dscore, query)
        dvalue = mat_tn(weights.astype(jnp.bfloat16), scaled)
        sums[:, 0, chunk] += dkey.reshape(planes, rows, width)
        sums[:, 1, chunk] += dvalue.reshape(planes, rows, width)
        return dquery

    dquery = lax.fori_loop(
        low, high + 1, step, jnp.zeros((group * rows, width), jnp.float32)
    )
    dq_ref[...] = (dquery * scale).astype(jnp.bfloat16).reshape(group, rows, width)

    @pl.when(pl.program_id(0) == ranks - 1)
    def _():
        for chunk in range(ranks):
            dkv_ref[:, 0, chunk] = (sums[:, 0, chunk] * scale).astype(jnp.bfloat16)
            dkv_ref[:, 1, chunk] = sums[:, 1, chunk].astype(jnp.bfloat16)


def attend_back(lengths, query, kv, gate_logit, attended, total, dgated, rows):
    group, tokens, width = query.shape
    planes = kv.shape[0]
    ranks = tokens // rows
    kv_blocks = kv.reshape(planes, 2, ranks, rows, width)
    block = pl.BlockSpec((group, rows, width), lambda i, *_: (0, i, 0))
    thin = pl.BlockSpec((group, rows, 1), lambda i, *_: (0, i, 0))
    whole = pl.BlockSpec((planes, 2, ranks, rows, width), lambda i, *_: (0, 0, 0, 0, 0))
    dquery, dkv, dgate = pl.pallas_call(
        functools.partial(attend_back_kernel, ranks, planes),
        grid_spec=pltpu.PrefetchScalarGridSpec(
            num_scalar_prefetch=1,
            grid=(ranks,),
            in_specs=[
                block,
                whole,
                thin,
                block,
                thin,
                pl.BlockSpec((rows, group * width), lambda i, *_: (i, 0)),
            ],
            out_specs=(block, whole, thin),
            scratch_shapes=[pltpu.VMEM((planes, 2, ranks, rows, width), jnp.float32)],
        ),
        out_shape=(
            jax.ShapeDtypeStruct((group, tokens, width), jnp.bfloat16),
            jax.ShapeDtypeStruct((planes, 2, ranks, rows, width), jnp.bfloat16),
            jax.ShapeDtypeStruct((group, tokens, 1), jnp.bfloat16),
        ),
        compiler_params=pltpu.CompilerParams(vmem_limit_bytes=VMEM_LIMIT),
        name="attend_back",
    )(lengths, query, kv_blocks, gate_logit, attended, total, dgated)
    return dquery, dkv.reshape(planes, 2, tokens, width), dgate


def middle_kernel(
    planes,
    gated_ref,
    wout_ref,
    x_ref,
    scale_ref,
    dy_hbm,
    wg_hbm,
    wu_hbm,
    wd_hbm,
    xg,
    xz_hbm,
    dz_hbm,
    down_hbm,
    mid_ref,
    dmid_ref,
    gain_ref,
    pm_ref,
    dgated_ref,
    wg,
    wu,
    wd,
    dy,
    dhid,
    near_out,
    near_in,
    far_out,
    far_in,
    keep,
    down_buf,
    load_sem,
    dy_sem,
    down_sem,
    near_send,
    near_recv,
    far_send,
    far_recv,
    ag_send,
    ag_recv,
    line_send,
    line_recv,
):
    rank, plane = lax.axis_index("fsdp"), lax.axis_index("sp")
    ranks, rows, width = xg.shape
    loads = [
        pltpu.make_async_copy(wd_hbm, wd, load_sem.at[0]),
        pltpu.make_async_copy(wg_hbm, wg, load_sem.at[1]),
        pltpu.make_async_copy(wu_hbm, wu, load_sem.at[2]),
    ]
    dy_load = pltpu.make_async_copy(dy_hbm, dy, dy_sem)
    others = [lax.rem(plane + k, planes) for k in range(1, planes)]
    greet([(rank ^ k, plane) for k in (1, 2, 4, 6)] + [(rank, other) for other in others])

    def along(source, target, which):
        return [
            peer_copy(
                source,
                target.at[j - 1],
                line_send.at[which, j - 1],
                line_recv.at[which, j - 1],
                rank,
                lax.rem(plane + planes - j, planes),
            )
            for j in range(1, planes)
        ]

    def near(phase, i):
        return peer_copy(
            near_out.at[phase, i],
            near_in.at[phase, i],
            near_send.at[phase, i],
            near_recv.at[phase, i],
            rank ^ 1,
            plane,
        )

    def far(phase, i, k):
        return peer_copy(
            far_out.at[phase, i],
            far_in.at[phase, i],
            far_send.at[phase, i],
            far_recv.at[phase, i],
            rank ^ k,
            plane,
        )

    order = (6, 2, 4, 0)
    for i, k in enumerate(order):
        part = jnp.dot(
            gated_ref[rank ^ 1 ^ k], wout_ref[...], preferred_element_type=jnp.float32
        )
        near_out[0, i] = part.astype(jnp.bfloat16)
        near(0, i).start()
    dy_load.start()
    for copy in loads:
        copy.start()
    dy_line = along(dy_hbm.at[rank], dz_hbm, 0)
    for copy in dy_line:
        copy.start()
    for i, k in enumerate(order):
        part = jnp.dot(gated_ref[rank ^ k], wout_ref[...], preferred_element_type=jnp.float32)
        near(0, i).wait_recv()
        part = part + near_in[0, i].astype(jnp.float32)
        if k:
            far_out[0, i] = part.astype(jnp.bfloat16)
            far(0, i, k).start()
        else:
            keep[...] = part

    dy_load.wait()
    loads[0].wait()

    @pl.loop(0, ranks // 2)
    def _(p):
        pair = dy[pl.ds(2 * p, 2)].reshape(2 * rows, width)
        dhid[p] = mat_nt(pair, wd[...])

    loads[1].wait()
    loads[2].wait()
    middle = x_ref[...].astype(jnp.float32) + keep[...]
    for i in (1, 2, 0):
        far(0, i, order[i]).wait_recv()
        middle = middle + far_in[0, i].astype(jnp.float32)
    inverse = inv_rms(middle)
    mid_ref[...] = middle
    normed = (middle * inverse * scale_ref[...]).astype(jnp.bfloat16)
    xg[rank] = normed
    sems = (ag_send.at[0], ag_recv.at[0])
    gather_start(xg, *sems)
    xb_line = along(xg.at[rank], xz_hbm, 1)
    for copy in xb_line:
        copy.start()

    slots = {2: 0, 4: 1, 6: 2, 0: 3}

    def down_copy(p, slot):
        return pltpu.make_async_copy(
            down_buf.at[slot], down_hbm.at[pl.ds(2 * p, 2)], down_sem.at[slot]
        )

    def feed(k):
        p = (rank ^ k) // 2
        slot = (0, 2, 4, 6).index(k) % 2
        pair = xg[pl.ds(2 * p, 2)].reshape(2 * rows, width)
        gate_pre = mat_nt(pair, wg[...])
        up_pre = mat_nt(pair, wu[...])
        grad_hidden = dhid[p]
        sigma = jax.nn.sigmoid(gate_pre)
        swish = gate_pre * sigma
        grad_gate = (grad_hidden * up_pre * sigma * (1.0 + gate_pre * (1.0 - sigma))).astype(
            jnp.bfloat16
        )
        grad_up = (grad_hidden * swish).astype(jnp.bfloat16)
        part = jnp.dot(grad_gate, wg[...], preferred_element_type=jnp.float32) + jnp.dot(
            grad_up, wu[...], preferred_element_type=jnp.float32
        )
        i = slots[k]
        halves = part.reshape(2, rows, width)
        mine_first = lax.rem(rank, 2) == 0
        mine = jnp.where(mine_first, halves[0], halves[1])
        theirs = jnp.where(mine_first, halves[1], halves[0])
        near_out[1, i] = theirs.astype(jnp.bfloat16)
        near(1, i).start()
        hidden = (swish * up_pre).astype(jnp.bfloat16)
        down = jnp.dot(hidden, wd[...], preferred_element_type=jnp.float32)
        if k in (4, 6):
            down_copy(p, slot).wait()
        down_buf[slot] = down.astype(jnp.bfloat16).reshape(2, rows, width)
        down_copy(p, slot).start()
        near(1, i).wait_recv()
        mine = mine + near_in[1, i].astype(jnp.float32)
        if k:
            far_out[1, i] = mine.astype(jnp.bfloat16)
            far(1, i, k).start()
        else:
            keep[...] = mine

    gather_wait(xg, *sems, (6,))
    feed(0)
    gather_pass(xg, *sems, NEIGHBOURS_FIRST)
    gather_wait(xg, *sems, (7, 8))
    feed(2)
    gather_pass(xg, *sems, DIAGONAL)
    gather_wait(xg, *sems, (9, 10))
    feed(4)
    gather_wait(xg, *sems, (11, 12))
    feed(6)

    grad = keep[...]
    for i, k in enumerate((2, 4, 6)):
        far(1, i, k).wait_recv()
        grad = grad + far_in[1, i].astype(jnp.float32)
    middle = mid_ref[...]
    inverse = inv_rms(middle)
    gain_ref[...] = jnp.sum(grad * middle * inverse, axis=0, keepdims=True)
    grad_middle = dy[rank].astype(jnp.float32) + norm_back(
        grad, middle, inverse, scale_ref[...]
    )
    dmid_ref[...] = grad_middle
    pm_ref[rank] = grad_middle.astype(jnp.bfloat16)
    sems2 = (ag_send.at[1], ag_recv.at[1])
    gather_start(pm_ref, *sems2)

    def gated_grad(k):
        p = (rank ^ k) // 2
        pair = pm_ref[pl.ds(2 * p, 2)].reshape(2 * rows, width)
        dgated_ref[pl.ds(2 * p, 2)] = mat_nt(pair, wout_ref[...]).reshape(
            2, rows, wout_ref.shape[0]
        )

    gather_wait(pm_ref, *sems2, (6,))
    gated_grad(0)
    gather_pass(pm_ref, *sems2, NEIGHBOURS_FIRST)
    gather_wait(pm_ref, *sems2, (7, 8))
    gated_grad(2)
    gather_wait(pm_ref, *sems2, (9, 10))
    gated_grad(4)
    gather_pass(pm_ref, *sems2, DIAGONAL)
    gather_wait(pm_ref, *sems2, (11, 12))
    gated_grad(6)

    gather_sent(xg, *sems)
    gather_sent(pm_ref, *sems2)
    for copy in dy_line + xb_line:
        copy.wait()
    for phase in range(2):
        for i in range(4):
            near(phase, i).wait_send()
        for i in range(3):
            far(phase, i, 2).wait_send()
    down_copy(0, 0).wait()
    down_copy(0, 1).wait()


def middle_layer(gated, w_out, x, scale, grad_plane, w_gate, w_up, w_down, collective_id):
    ranks, rows, _ = gated.shape
    planes = lax.axis_size("sp")
    width = x.shape[1]
    hidden = w_gate.shape[0]
    features = w_out.shape[0]
    vmem = pl.BlockSpec(memory_space=pltpu.VMEM)
    hbm = pl.BlockSpec(memory_space=pl.ANY)
    half, full = jnp.bfloat16, jnp.float32
    return pl.pallas_call(
        functools.partial(middle_kernel, planes),
        out_shape=(
            jax.ShapeDtypeStruct((ranks, rows, width), half),
            jax.ShapeDtypeStruct((planes - 1, rows, width), half),
            jax.ShapeDtypeStruct((planes - 1, rows, width), half),
            jax.ShapeDtypeStruct((ranks, rows, width), half),
            jax.ShapeDtypeStruct((rows, width), full),
            jax.ShapeDtypeStruct((rows, width), full),
            jax.ShapeDtypeStruct((1, width), full),
            jax.ShapeDtypeStruct((ranks, rows, width), half),
            jax.ShapeDtypeStruct((ranks, rows, features), full),
        ),
        in_specs=[vmem, vmem, vmem, vmem, hbm, hbm, hbm, hbm],
        out_specs=(vmem, hbm, hbm, hbm, vmem, vmem, vmem, vmem, vmem),
        scratch_shapes=[
            pltpu.VMEM((hidden, width), half),
            pltpu.VMEM((hidden, width), half),
            pltpu.VMEM((hidden, width), half),
            pltpu.VMEM((ranks, rows, width), half),
            pltpu.VMEM((ranks // 2, 2 * rows, hidden), full),
            pltpu.VMEM((2, 4, rows, width), half),
            pltpu.VMEM((2, 4, rows, width), half),
            pltpu.VMEM((2, 3, rows, width), half),
            pltpu.VMEM((2, 3, rows, width), half),
            pltpu.VMEM((rows, width), full),
            pltpu.VMEM((2, 2, rows, width), half),
            pltpu.SemaphoreType.DMA((3,)),
            pltpu.SemaphoreType.DMA,
            pltpu.SemaphoreType.DMA((2,)),
            pltpu.SemaphoreType.DMA((2, 4)),
            pltpu.SemaphoreType.DMA((2, 4)),
            pltpu.SemaphoreType.DMA((2, 3)),
            pltpu.SemaphoreType.DMA((2, 3)),
            pltpu.SemaphoreType.DMA((2, GATHER_COPIES)),
            pltpu.SemaphoreType.DMA((2, GATHER_COPIES)),
            pltpu.SemaphoreType.DMA((2, planes - 1)),
            pltpu.SemaphoreType.DMA((2, planes - 1)),
        ],
        compiler_params=pltpu.CompilerParams(
            collective_id=collective_id, has_side_effects=True, vmem_limit_bytes=VMEM_LIMIT
        ),
        name="middle_layer",
    )(gated, w_out, x, scale, grad_plane, w_gate, w_up, w_down)


def feed_weights_kernel(
    planes, xp_hbm, dp_hbm, xz_hbm, dy_hbm, wg_ref, wu_ref, wd_ref, og_ref, ou_ref, od_ref, xo_hbm, xbuf, dbuf, x_sem, d_sem, own_sem, ag_send, ag_recv
):
    rank, plane = lax.axis_index("fsdp"), lax.axis_index("sp")
    ranks, rows, width = xp_hbm.shape
    part = ranks // 2
    greet([(rank ^ k, plane) for k in (1, 2, 4)])
    own_blocks = [
        pltpu.make_async_copy(xz_hbm.at[j], xo_hbm.at[j, rank], own_sem.at[j])
        for j in range(planes - 1)
    ]
    gathers = [(xo_hbm.at[j], ag_send.at[j], ag_recv.at[j]) for j in range(planes - 1)]

    def load(step, start):
        slot = lax.rem(step, 2)
        block = pl.ds(part * lax.rem(step, 2), part)
        group = step // 2

        def go(x_from, d_from):
            for copy in (
                pltpu.make_async_copy(x_from, xbuf.at[slot], x_sem.at[slot]),
                pltpu.make_async_copy(d_from, dbuf.at[slot], d_sem.at[slot]),
            ):
                if start:
                    copy.start()
                else:
                    copy.wait()

        @pl.when(group == 0)
        def _():
            go(xp_hbm.at[block], dp_hbm.at[block])

        @pl.when(group > 0)
        def _():
            go(xo_hbm.at[group - 1, block], dy_hbm.at[group - 1, block])

    load(0, True)
    for copy in own_blocks:
        copy.start()
    gather_start(*gathers[0], own=xz_hbm.at[0])

    @pl.loop(0, 2 * planes)
    def _(step):
        for j in range(planes - 1):
            @pl.when(step == 2 * j + 1)
            def _():
                gather_pass(*gathers[j], NEIGHBOURS_FIRST)
                if j < planes - 2:
                    gather_start(*gathers[j + 1], own=xz_hbm.at[j + 1])

            @pl.when(step == 2 * j + 2)
            def _():
                gather_pass(*gathers[j], DIAGONAL)
                gather_wait(*gathers[j], FROM_SIBLING)
                own_blocks[j].wait()
                load(step, True)

        load(step, False)

        @pl.when(lax.rem(step, 2) == 0)
        def _():
            load(step + 1, True)

        slot = lax.rem(step, 2)
        normed = xbuf[slot].reshape(part * rows, width)
        grad = dbuf[slot].reshape(part * rows, width)
        gate_pre = mat_nt(normed, wg_ref[...])
        up_pre = mat_nt(normed, wu_ref[...])
        grad_hidden = mat_nt(grad, wd_ref[...])
        sigma = jax.nn.sigmoid(gate_pre)
        swish = gate_pre * sigma
        hidden = (swish * up_pre).astype(jnp.bfloat16)
        grad_gate = (grad_hidden * up_pre * sigma * (1.0 + gate_pre * (1.0 - sigma))).astype(
            jnp.bfloat16
        )
        grad_up = (grad_hidden * swish).astype(jnp.bfloat16)

        @pl.when(step == 0)
        def _():
            for ref in (og_ref, ou_ref, od_ref):
                ref[...] = jnp.zeros_like(ref)

        og_ref[...] += mat_tn(grad_gate, normed)
        ou_ref[...] += mat_tn(grad_up, normed)
        od_ref[...] += mat_tn(hidden, grad)

    for gather in gathers:
        gather_sent(*gather)


def feed_weights(plane_x, plane_grad, line_x, other_grad, w_gate, w_up, w_down, collective_id):
    ranks, rows, width = plane_x.shape
    planes = lax.axis_size("sp")
    vmem = pl.BlockSpec(memory_space=pltpu.VMEM)
    hbm = pl.BlockSpec(memory_space=pl.ANY)
    tokens = planes * ranks * rows
    return pl.pallas_call(
        functools.partial(feed_weights_kernel, planes),
        in_specs=[hbm, hbm, hbm, hbm, vmem, vmem, vmem],
        out_specs=(vmem, vmem, vmem, hbm),
        out_shape=[jax.ShapeDtypeStruct(w_gate.shape, jnp.float32)] * 3
        + [jax.ShapeDtypeStruct((planes - 1, ranks, rows, width), plane_x.dtype)],
        scratch_shapes=[
            pltpu.VMEM((2, ranks // 2, rows, width), plane_x.dtype),
            pltpu.VMEM((2, ranks // 2, rows, width), plane_x.dtype),
            pltpu.SemaphoreType.DMA((2,)),
            pltpu.SemaphoreType.DMA((2,)),
            pltpu.SemaphoreType.DMA((planes - 1,)),
            pltpu.SemaphoreType.DMA((planes - 1, GATHER_COPIES)),
            pltpu.SemaphoreType.DMA((planes - 1, GATHER_COPIES)),
        ],
        cost_estimate=pl.CostEstimate(
            flops=12 * tokens * w_gate.size,
            bytes_accessed=4 * tokens * width + 18 * w_gate.size,
            transcendentals=tokens * w_gate.shape[0],
        ),
        compiler_params=pltpu.CompilerParams(
            collective_id=collective_id, has_side_effects=True, vmem_limit_bytes=VMEM_LIMIT
        ),
        name="feed_weights",
    )(plane_x, plane_grad, line_x, other_grad, w_gate, w_up, w_down)[:3]


def local_planes(
    hidden_in,
    grad_out,
    lengths,
    attn_gain,
    w_qkv,
    w_head_gate,
    q_gain,
    k_gain,
    w_out,
    ffn_gain,
    w_gate,
    w_up,
    w_down,
):
    ranks, planes = lax.axis_size("fsdp"), lax.axis_size("sp")
    rank, plane = lax.axis_index("fsdp"), lax.axis_index("sp")
    rows, model_width = hidden_in.shape
    tokens = ranks * rows
    own_heads = w_qkv.shape[0] // HEAD_DIM
    local_heads = HEADS // ranks

    wide, thin = attn_gain.shape[0], q_gain.shape[0]
    used = 2 * wide + 2 * thin
    own_gains = jnp.concatenate(
        [attn_gain, ffn_gain, q_gain, k_gain, jnp.zeros((8 * HEAD_DIM - used,), attn_gain.dtype)]
    ).astype(jnp.float32)
    gathered, gains = gather_plane(hidden_in, 0, own_gains.reshape(8, HEAD_DIM))
    gains = gains.reshape(ranks, 8 * HEAD_DIM)
    attn_scale = gains[:, :wide].reshape(-1)
    ffn_scale = gains[:, wide : 2 * wide].reshape(-1)
    query_scale = gains[:, 2 * wide : 2 * wide + thin].reshape(-1)
    key_scale = gains[:, 2 * wide + thin : used].reshape(-1)

    token_block = jnp.arange(ranks, dtype=jnp.int32) * (planes * rows) + plane * rows
    plane_tokens = (token_block[:, None] + jnp.arange(rows, dtype=jnp.int32)[None]).reshape(-1)
    cosine, sine = rope_tables(plane_tokens - item_starts(plane_tokens, lengths))

    inputs = gathered.reshape(tokens, model_width).astype(jnp.float32)
    inv_first = inv_rms(inputs)
    normed_a = (inputs * inv_first * attn_scale).astype(jnp.bfloat16)
    projected = mat_nt(normed_a, w_qkv)
    gate_logit = mat_nt(w_head_gate, normed_a)[:, :, None]
    raw = projected.reshape(tokens, own_heads, HEAD_DIM)
    raw_inv = inv_rms(raw)
    is_query, is_value = rank < ranks // 2, rank >= 3 * ranks // 4
    head_scale = jnp.where(is_query, query_scale, key_scale)
    turned = rotate(raw * raw_inv * head_scale, cosine, sine)
    natural = jnp.where(is_value, raw, turned).astype(jnp.bfloat16)
    query, kv, plane_grad = exchange_heads(jnp.transpose(natural, (1, 0, 2)), grad_out, 1)

    attended, total, gated = attend(lengths, query, kv, gate_logit, rows)
    own_inputs = hidden_in.astype(jnp.float32)
    plane_b, line_b, line_grad, down_part, middle, grad_middle, grad_ffn_gain_local, plane_mid, grad_gated = middle_layer(
        gated.reshape(ranks, rows, -1),
        w_out,
        hidden_in,
        ffn_scale.reshape(1, -1),
        plane_grad,
        w_gate,
        w_up,
        w_down,
        2,
    )
    plane_mid = plane_mid.reshape(tokens, model_width)
    grad_gated = grad_gated.reshape(tokens, -1)
    grad_query, grad_kv, gate_grad = attend_back(
        lengths, query, kv, gate_logit, attended, total, grad_gated, rows
    )
    back, other_grad = return_heads(grad_query, grad_kv, line_grad, 6)
    back = jnp.transpose(back, (1, 0, 2))
    turned_back = rotate_back(back.astype(jnp.float32), cosine, sine)
    gain_terms = jnp.sum(turned_back * raw * raw_inv, axis=(0, 1))
    raw_back = norm_back(turned_back, raw, raw_inv, head_scale).astype(jnp.bfloat16)
    grad_proj = jnp.where(is_value, back, raw_back).reshape(tokens, own_heads * HEAD_DIM)
    gate_grad = gate_grad.reshape(local_heads, tokens)
    grad_a_part = jnp.dot(grad_proj, w_qkv, preferred_element_type=jnp.float32) + mat_tn(
        gate_grad, w_head_gate
    )
    nothing = jnp.zeros((HEAD_DIM,), jnp.float32)
    gain_parts = jnp.concatenate(
        [
            jnp.sum(grad_a_part * inputs * inv_first, axis=0).reshape(ranks, wide),
            grad_ffn_gain_local.reshape(ranks, wide),
            jnp.where(is_query, gain_terms, nothing).reshape(ranks, thin),
            jnp.where(is_query | is_value, nothing, gain_terms).reshape(ranks, thin),
            jnp.zeros((ranks, 8 * HEAD_DIM - used), jnp.float32),
        ],
        axis=1,
    )
    ffn_out = lax.psum_scatter(
        down_part.reshape(tokens, model_width), "fsdp", scatter_dimension=0, tiled=True
    )
    hidden_out = (middle + ffn_out.astype(jnp.float32)).astype(jnp.bfloat16)
    gate_rows_part = jnp.dot(gate_grad, normed_a, preferred_element_type=jnp.float32)
    grad_a, gain_total, gate_total = scatter_plane(
        grad_a_part.astype(jnp.bfloat16).reshape(ranks, rows, model_width),
        7,
        gain_parts.reshape(ranks, 8, HEAD_DIM),
        gate_rows_part.reshape(-1, HEAD_DIM),
    )
    own_inv = inv_rms(own_inputs)
    grad_in = grad_middle + norm_back(grad_a, own_inputs, own_inv, attn_scale)

    def over_planes(part):
        reduced = lax.psum_scatter(
            part.astype(jnp.bfloat16), "sp", scatter_dimension=0, tiled=True
        )
        return lax.all_gather(reduced, "sp", axis=0, tiled=True).astype(jnp.float32)

    grad_w_out = over_planes(mat_tn(gated, plane_mid))
    grad_w_qkv = over_planes(mat_tn(grad_proj, normed_a))
    grad_w_head_gate = gate_total.reshape(w_head_gate.shape)

    line_b, grad_a = lax.optimization_barrier((line_b, grad_a))
    grad_w_gate, grad_w_up, grad_w_down = feed_weights(
        plane_b, plane_grad, line_b, other_grad, w_gate, w_up, w_down, 4
    )

    gain_total = gain_total.reshape(-1)
    grad_attn_gain = gain_total[:wide]
    grad_ffn_gain = gain_total[wide : 2 * wide]
    grad_q_gain = gain_total[2 * wide : 2 * wide + thin]
    grad_k_gain = gain_total[2 * wide + thin : used]
    return (
        hidden_out,
        grad_in,
        grad_attn_gain,
        grad_w_qkv,
        grad_w_head_gate,
        grad_q_gain,
        grad_k_gain,
        grad_w_out,
        grad_ffn_gain,
        grad_w_gate,
        grad_w_up,
        grad_w_down,
    )


def solution(mesh):
    planar = mesh.shape["fsdp"] == 8 and mesh.shape["sp"] == 4
    return jax.shard_map(
        local_planes if planar else local,
        mesh=mesh,
        in_specs=(
            P(("fsdp", "sp"), None),
            P(("fsdp", "sp"), None),
            P(),
            P("fsdp"),
            P("fsdp", None),
            P("fsdp", None),
            P("fsdp"),
            P("fsdp"),
            P("fsdp", None),
            P("fsdp"),
            P("fsdp", None),
            P("fsdp", None),
            P("fsdp", None),
        ),
        out_specs=(
            P(("fsdp", "sp"), None),
            P(("fsdp", "sp"), None),
            P("fsdp"),
            P("fsdp", None),
            P("fsdp", None),
            P("fsdp"),
            P("fsdp"),
            P("fsdp", None),
            P("fsdp"),
            P("fsdp", None),
            P("fsdp", None),
            P("fsdp", None),
        ),
        check_vma=False,
    )
```

```python
import functools
import math

import jax
import jax.numpy as jnp
from jax import lax
from jax.experimental import pallas as pl
from jax.experimental.pallas import tpu as pltpu
from jax.sharding import PartitionSpec as P

HEADS = 16
KV_HEADS = 8
HEAD_DIM = 128


EPS = 1e-06
ROPE_BASE = 1000000.0


def mat_nt(factor, others):
    return lax.dot_general(
        factor, others, (((1,), (1,)), ((), ())), preferred_element_type=jnp.float32
    )


def mat_tn(factor, others):
    return lax.dot_general(
        factor, others, (((0,), (0,)), ((), ())), preferred_element_type=jnp.float32
    )


def inv_rms(values):
    return lax.rsqrt(jnp.mean(values * values, axis=-1, keepdims=True) + EPS)


def norm_back(grad_norm, values, inverse, scaling):
    scaled = grad_norm * scaling
    cubed = inverse * inverse * inverse
    return inverse * scaled - values * cubed * jnp.mean(scaled * values, axis=-1, keepdims=True)


def item_starts(token_index, lengths):
    ends = jnp.cumsum(lengths)
    starts = ends - lengths
    inside = (token_index[:, None] >= starts[None, :]) & (token_index[:, None] < ends[None, :])
    return jnp.sum(jnp.where(inside, starts[None, :], 0), axis=1)


def rope_tables(position):
    half_dim = HEAD_DIM // 2
    freq_steps = jnp.arange(half_dim, dtype=jnp.float32)
    frequency = jnp.exp(-math.log(ROPE_BASE) * 2.0 * freq_steps / HEAD_DIM)
    angles = position.astype(jnp.float32)[:, None] * frequency[None, :]
    return (jnp.cos(angles)[:, None, :], jnp.sin(angles)[:, None, :])


def rotate(values, cosine, sine):
    half_dim = values.shape[-1] // 2
    lower = values[..., :half_dim]
    upper = values[..., half_dim:]
    return jnp.concatenate([lower * cosine - upper * sine, upper * cosine + lower * sine], axis=-1)


def rotate_back(grad_rot, cosine, sine):
    half_dim = grad_rot.shape[-1] // 2
    lower = grad_rot[..., :half_dim]
    upper = grad_rot[..., half_dim:]
    return jnp.concatenate([lower * cosine + upper * sine, upper * cosine - lower * sine], axis=-1)


def local(
    hidden_in,
    grad_out,
    lengths,
    attn_gain,
    w_qkv,
    w_head_gate,
    q_gain,
    k_gain,
    w_out,
    ffn_gain,
    w_gate,
    w_up,
    w_down,
):
    fsdp_count = lax.axis_size("fsdp")
    sp_count = lax.axis_size("sp")
    fsdp_rank = lax.axis_index("fsdp")
    sp_rank = lax.axis_index("sp")
    tok_rows = hidden_in.shape[0]
    model_width = hidden_in.shape[1]
    query_width = HEADS * HEAD_DIM
    kv_width = KV_HEADS * HEAD_DIM
    local_kv = KV_HEADS // sp_count
    head_group = HEADS // KV_HEADS
    score_scale = HEAD_DIM ** (-0.5)
    qkv_full, out_full, gate_full, attn_gain_full, q_gain_full, k_gain_full, ffn_gain_full = (
        lax.all_gather(w_qkv, "fsdp", axis=0, tiled=True),
        lax.all_gather(w_out, "fsdp", axis=0, tiled=True),
        lax.all_gather(w_head_gate, "fsdp", axis=0, tiled=True),
        lax.all_gather(attn_gain, "fsdp", axis=0, tiled=True),
        lax.all_gather(q_gain, "fsdp", axis=0, tiled=True),
        lax.all_gather(k_gain, "fsdp", axis=0, tiled=True),
        lax.all_gather(ffn_gain, "fsdp", axis=0, tiled=True),
    )
    attn_scale = attn_gain_full.astype(jnp.float32)
    query_scale = q_gain_full.astype(jnp.float32)
    key_scale = k_gain_full.astype(jnp.float32)
    ffn_scale = ffn_gain_full.astype(jnp.float32)
    token_first = (fsdp_rank * sp_count + sp_rank) * tok_rows
    own_tokens = token_first + jnp.arange(tok_rows, dtype=jnp.int32)
    cosine, sine = rope_tables(own_tokens - item_starts(own_tokens, lengths))
    inputs = hidden_in.astype(jnp.float32)
    inv_first = inv_rms(inputs)
    normed_a = (inputs * inv_first * attn_scale).astype(jnp.bfloat16)
    projected = mat_nt(normed_a, qkv_full)
    gate_logit = mat_nt(normed_a, gate_full)
    q_raw = projected[:, :query_width].reshape(tok_rows, HEADS, HEAD_DIM)
    k_raw = projected[:, query_width : query_width + kv_width].reshape(tok_rows, KV_HEADS, HEAD_DIM)
    q_inv = inv_rms(q_raw)
    k_inv = inv_rms(k_raw)
    query = (
        rotate(q_raw * q_inv * query_scale, cosine, sine)
        .reshape(tok_rows, query_width)
        .astype(jnp.bfloat16)
    )
    keys = (
        rotate(k_raw * k_inv * key_scale, cosine, sine)
        .reshape(tok_rows, kv_width)
        .astype(jnp.bfloat16)
    )
    values = projected[:, query_width + kv_width :].astype(jnp.bfloat16)
    query_heads, key_heads, value_heads = (
        lax.all_to_all(query, "sp", split_axis=1, concat_axis=0, tiled=True),
        lax.all_to_all(keys, "sp", split_axis=1, concat_axis=0, tiled=True),
        lax.all_to_all(values, "sp", split_axis=1, concat_axis=0, tiled=True),
    )
    key_all, value_all = (
        lax.all_gather(key_heads, "fsdp", axis=0, tiled=True),
        lax.all_gather(value_heads, "fsdp", axis=0, tiled=True),
    )
    span_rows = query_heads.shape[0]
    span_first = fsdp_rank * span_rows
    span_tokens = span_first + jnp.arange(span_rows, dtype=jnp.int32)
    span_starts = item_starts(span_tokens, lengths)
    query_four = query_heads.reshape(span_rows, local_kv, head_group, HEAD_DIM)
    key_total = key_all.shape[0]
    key_block = min(1024, key_total)
    block_count = key_total // key_block
    key_blocks = key_all.reshape(block_count, key_block, local_kv, HEAD_DIM)
    value_blocks = value_all.reshape(block_count, key_block, local_kv, HEAD_DIM)
    block_firsts = jnp.arange(block_count, dtype=jnp.int32) * key_block
    lowest_key = span_starts[0]
    highest_key = span_first + span_rows - 1

    def needed(block_first):
        return (block_first <= highest_key) & (block_first + key_block - 1 >= lowest_key)

    def block_weights(key_piece, block_first):
        scores = (
            jnp.einsum("qkgd,jkd->kgqj", query_four, key_piece, preferred_element_type=jnp.float32)
            * score_scale
        )
        columns = block_first + jnp.arange(key_block, dtype=jnp.int32)
        allowed = (columns[None, :] <= span_tokens[:, None]) & (
            columns[None, :] >= span_starts[:, None]
        )
        return jnp.where(allowed[None, None], jnp.exp(scores), 0.0)

    def forward_step(running, pieces):
        key_piece, value_piece, block_first = pieces

        def forward_compute(current):
            totals, unnormed = current
            weights = block_weights(key_piece, block_first)
            totals = totals + jnp.sum(weights, axis=3)
            unnormed = unnormed + jnp.einsum(
                "kgqj,jkd->qkgd",
                weights.astype(jnp.bfloat16),
                value_piece,
                preferred_element_type=jnp.float32,
            )
            return (totals, unnormed)

        return (
            lax.cond(needed(block_first), forward_compute, lambda current: current, running),
            None,
        )

    start_state = (
        jnp.zeros((local_kv, head_group, span_rows), jnp.float32),
        jnp.zeros((span_rows, local_kv, head_group, HEAD_DIM), jnp.float32),
    )
    scanned = lax.scan(forward_step, start_state, (key_blocks, value_blocks, block_firsts))[0]
    totals, unnormed = scanned
    totals_rows = jnp.transpose(totals, (2, 0, 1))[..., None]
    attended_heads = unnormed / totals_rows
    attended_send = attended_heads.reshape(span_rows, local_kv * head_group * HEAD_DIM).astype(
        jnp.bfloat16
    )
    returned = lax.all_to_all(attended_send, "sp", split_axis=0, concat_axis=1, tiled=True)
    gate_prob = jax.nn.sigmoid(gate_logit)
    attended_tok = returned.astype(jnp.float32).reshape(tok_rows, HEADS, HEAD_DIM)
    gated = (
        (attended_tok * gate_prob[:, :, None]).reshape(tok_rows, query_width).astype(jnp.bfloat16)
    )
    middle = inputs + jnp.dot(gated, out_full, preferred_element_type=jnp.float32)
    inv_second = inv_rms(middle)
    normed_b = (middle * inv_second * ffn_scale).astype(jnp.bfloat16)
    gate_piece = lax.all_gather(w_gate, "fsdp", axis=0, tiled=True)
    up_piece = lax.all_gather(w_up, "fsdp", axis=0, tiled=True)
    down_piece = lax.all_gather(w_down, "fsdp", axis=0, tiled=True)
    gate_pre = mat_nt(normed_b, gate_piece)
    up_pre = mat_nt(normed_b, up_piece)
    hidden = (jax.nn.silu(gate_pre) * up_pre).astype(jnp.bfloat16)
    ffn_part = jnp.dot(hidden, down_piece, preferred_element_type=jnp.float32)
    hidden_out = (middle + ffn_part).astype(jnp.bfloat16)
    gate_piece = lax.all_gather(w_gate, "fsdp", axis=0, tiled=True)
    up_piece = lax.all_gather(w_up, "fsdp", axis=0, tiled=True)
    down_piece = lax.all_gather(w_down, "fsdp", axis=0, tiled=True)
    gate_pre = mat_nt(normed_b, gate_piece)
    up_pre = mat_nt(normed_b, up_piece)
    sigma = jax.nn.sigmoid(gate_pre)
    swish = gate_pre * sigma
    hidden = (swish * up_pre).astype(jnp.bfloat16)
    grad_hidden = mat_nt(grad_out, down_piece)
    grad_gate = (grad_hidden * up_pre * sigma * (1.0 + gate_pre * (1.0 - sigma))).astype(
        jnp.bfloat16
    )
    grad_up = (grad_hidden * swish).astype(jnp.bfloat16)
    grad_acc = jnp.dot(grad_gate, gate_piece, preferred_element_type=jnp.float32) + jnp.dot(
        grad_up, up_piece, preferred_element_type=jnp.float32
    )
    grad_ffn_gain_local = jnp.sum(grad_acc * middle * inv_second, axis=0)
    grad_middle = grad_out.astype(jnp.float32) + norm_back(grad_acc, middle, inv_second, ffn_scale)
    grad_mid_b = grad_middle.astype(jnp.bfloat16)
    grad_gated = mat_nt(grad_mid_b, out_full).reshape(tok_rows, HEADS, HEAD_DIM)
    grad_attended = (
        (grad_gated * gate_prob[:, :, None]).reshape(tok_rows, query_width).astype(jnp.bfloat16)
    )
    gate_grad = (jnp.sum(grad_gated * attended_tok, axis=2) * gate_prob * (1.0 - gate_prob)).astype(
        jnp.bfloat16
    )
    grad_heads = lax.all_to_all(grad_attended, "sp", split_axis=1, concat_axis=0, tiled=True)
    grad_four = grad_heads.astype(jnp.float32).reshape(span_rows, local_kv, head_group, HEAD_DIM)
    grad_scaled = (grad_four / totals_rows).astype(jnp.bfloat16)
    delta_rows = jnp.sum(grad_four * attended_heads, axis=3) / totals_rows[..., 0]
    delta_heads = jnp.transpose(delta_rows, (1, 2, 0))

    def backward_step(grad_query, pieces):
        key_piece, value_piece, block_first = pieces

        def backward_compute(current):
            weights = block_weights(key_piece, block_first)
            grad_prob = jnp.einsum(
                "qkgd,jkd->kgqj", grad_scaled, value_piece, preferred_element_type=jnp.float32
            )
            grad_score = (weights * (grad_prob - delta_heads[..., None])).astype(jnp.bfloat16)
            current = (
                current
                + jnp.einsum(
                    "kgqj,jkd->qkgd", grad_score, key_piece, preferred_element_type=jnp.float32
                )
                * score_scale
            )
            grad_key = (
                jnp.einsum(
                    "kgqj,qkgd->jkd", grad_score, query_four, preferred_element_type=jnp.float32
                )
                * score_scale
            )
            grad_value = jnp.einsum(
                "kgqj,qkgd->jkd",
                weights.astype(jnp.bfloat16),
                grad_scaled,
                preferred_element_type=jnp.float32,
            )
            return (current, (grad_key, grad_value))

        def skip(current):
            nothing = jnp.zeros((key_block, local_kv, HEAD_DIM), jnp.float32)
            return (current, (nothing, nothing))

        return lax.cond(needed(block_first), backward_compute, skip, grad_query)

    grad_query, key_value_grads = lax.scan(
        backward_step,
        jnp.zeros((span_rows, local_kv, head_group, HEAD_DIM), jnp.float32),
        (key_blocks, value_blocks, block_firsts),
    )
    key_grads, value_grads = key_value_grads
    key_sum, value_sum = (
        lax.psum_scatter(
            key_grads.reshape(key_total, local_kv * HEAD_DIM),
            "fsdp",
            scatter_dimension=0,
            tiled=True,
        ),
        lax.psum_scatter(
            value_grads.reshape(key_total, local_kv * HEAD_DIM),
            "fsdp",
            scatter_dimension=0,
            tiled=True,
        ),
    )
    query_send = grad_query.reshape(span_rows, local_kv * head_group * HEAD_DIM).astype(
        jnp.bfloat16
    )
    back_query, back_key, back_value = (
        lax.all_to_all(query_send, "sp", split_axis=0, concat_axis=1, tiled=True),
        lax.all_to_all(key_sum.astype(jnp.bfloat16), "sp", split_axis=0, concat_axis=1, tiled=True),
        lax.all_to_all(
            value_sum.astype(jnp.bfloat16), "sp", split_axis=0, concat_axis=1, tiled=True
        ),
    )
    grad_qn = rotate_back(
        back_query.astype(jnp.float32).reshape(tok_rows, HEADS, HEAD_DIM), cosine, sine
    )
    grad_kn = rotate_back(
        back_key.astype(jnp.float32).reshape(tok_rows, KV_HEADS, HEAD_DIM), cosine, sine
    )
    grad_q_gain_local = jnp.sum(grad_qn * q_raw * q_inv, axis=(0, 1))
    grad_k_gain_local = jnp.sum(grad_kn * k_raw * k_inv, axis=(0, 1))
    grad_q_raw = norm_back(grad_qn, q_raw, q_inv, query_scale).reshape(tok_rows, query_width)
    grad_k_raw = norm_back(grad_kn, k_raw, k_inv, key_scale).reshape(tok_rows, kv_width)
    grad_proj = jnp.concatenate(
        [grad_q_raw.astype(jnp.bfloat16), grad_k_raw.astype(jnp.bfloat16), back_value], axis=1
    )
    grad_normed_a = jnp.dot(grad_proj, qkv_full, preferred_element_type=jnp.float32) + jnp.dot(
        gate_grad, gate_full, preferred_element_type=jnp.float32
    )
    grad_attn_gain_local = jnp.sum(grad_normed_a * inputs * inv_first, axis=0)
    grad_in = grad_middle + norm_back(grad_normed_a, inputs, inv_first, attn_scale)
    qkv_rows = w_qkv.shape[0]
    out_rows = w_out.shape[0]
    gate_rows = w_head_gate.shape[0]
    block_rows = qkv_rows + out_rows + gate_rows + 3
    small_rows = jnp.stack(
        [
            grad_attn_gain_local,
            grad_ffn_gain_local,
            jnp.concatenate(
                [
                    grad_q_gain_local,
                    grad_k_gain_local,
                    jnp.zeros((model_width - 2 * HEAD_DIM,), jnp.float32),
                ]
            ),
        ],
        axis=0,
    )
    ffn_partial = lax.psum_scatter(
        jnp.concatenate(
            [mat_tn(grad_gate, normed_b), mat_tn(grad_up, normed_b), mat_tn(hidden, grad_out)],
            axis=1,
        ).astype(jnp.bfloat16),
        "fsdp",
        scatter_dimension=0,
        tiled=True,
    ).astype(jnp.float32)
    proj_split = grad_proj.reshape(tok_rows, fsdp_count, qkv_rows)
    gated_split = gated.reshape(tok_rows, fsdp_count, out_rows)
    gate_split = gate_grad.reshape(tok_rows, fsdp_count, gate_rows)
    owners = block_rows * lax.axis_size("fsdp") // block_rows
    qkv_term = jnp.einsum("tor,td->ord", proj_split, normed_a, preferred_element_type=jnp.float32)
    out_term = jnp.einsum(
        "tor,td->ord", gated_split, grad_mid_b, preferred_element_type=jnp.float32
    )
    gate_term = jnp.einsum("tor,td->ord", gate_split, normed_a, preferred_element_type=jnp.float32)
    small_term = jnp.broadcast_to(small_rows[None], (owners, 3, model_width))
    joined = jnp.concatenate([qkv_term, out_term, gate_term, small_term], axis=1)
    attn_partial = lax.psum_scatter(
        joined.reshape(owners * block_rows, model_width), "fsdp", scatter_dimension=0, tiled=True
    )
    ffn_total, attn_total = lax.psum((ffn_partial, attn_partial), "sp")
    grad_w_gate = ffn_total[:, :model_width]
    grad_w_up = ffn_total[:, model_width : 2 * model_width]
    grad_w_down = ffn_total[:, 2 * model_width :]
    grad_w_qkv = attn_total[:qkv_rows]
    grad_w_out = attn_total[qkv_rows : qkv_rows + out_rows]
    grad_w_head_gate = attn_total[qkv_rows + out_rows : qkv_rows + out_rows + gate_rows]
    gain_sums = attn_total[qkv_rows + out_rows + gate_rows :]
    gain_part = model_width // fsdp_count
    head_part = HEAD_DIM // fsdp_count
    grad_attn_gain = lax.dynamic_slice_in_dim(gain_sums[0], fsdp_rank * gain_part, gain_part)
    grad_ffn_gain = lax.dynamic_slice_in_dim(gain_sums[1], fsdp_rank * gain_part, gain_part)
    grad_q_gain = lax.dynamic_slice_in_dim(gain_sums[2], fsdp_rank * head_part, head_part)
    grad_k_gain = lax.dynamic_slice_in_dim(
        gain_sums[2], HEAD_DIM + fsdp_rank * head_part, head_part
    )
    return (
        hidden_out,
        grad_in,
        grad_attn_gain,
        grad_w_qkv,
        grad_w_head_gate,
        grad_q_gain,
        grad_k_gain,
        grad_w_out,
        grad_ffn_gain,
        grad_w_gate,
        grad_w_up,
        grad_w_down,
    )


MESH = pl.DeviceIdType.MESH
VMEM_LIMIT = 62 * 1024 * 1024


def peer_copy(src, dst, send_sem, recv_sem, rank, plane):
    return pltpu.make_async_remote_copy(
        src_ref=src,
        dst_ref=dst,
        send_sem=send_sem,
        recv_sem=recv_sem,
        device_id=(rank, plane),
        device_id_type=MESH,
    )


def greet(peers):
    barrier = pltpu.get_barrier_semaphore()
    for peer in peers:
        pl.semaphore_signal(barrier, inc=1, device_id=peer, device_id_type=MESH)
    pl.semaphore_wait(barrier, len(peers))


def scatter_gains_kernel(
    p_ref, attn_ref, ffn_ref, head_ref, x_ref, scale_ref, dmid_ref, blocks_ref, o_ref, so_ref, next_ref, parts, small_buf, grad, small_send, small_recv, ag_send, ag_recv, own_sem, *rest
):
    rank, plane = lax.axis_index("fsdp"), lax.axis_index("sp")
    ranks = p_ref.shape[0]
    greet([(rank ^ k, plane) for k in range(1, 8)])
    block = blocks_ref.at[1, 1]
    own = pltpu.make_async_copy(block, next_ref.at[rank], own_sem)
    own.start()
    for i in range(4):
        scatter_near(p_ref, i, rest[0], rest[3], rest[4]).start()
    for r in range(ranks):
        for i in range(2):
            columns = slice((2 * r + i) * HEAD_DIM, (2 * r + i + 1) * HEAD_DIM)
            parts[r, i : i + 1] = attn_ref[:, columns]
            parts[r, 2 + i : 3 + i] = ffn_ref[:, columns]
        parts[r, 4:5] = jnp.where(rank < ranks // 2, head_ref[...], 0.0)
        parts[r, 5:6] = jnp.where(
            (rank >= ranks // 2) & (rank < 3 * ranks // 4), head_ref[...], 0.0
        )
        parts[r, 6:8] = jnp.zeros((2, HEAD_DIM), jnp.float32)
    small = []
    for k in range(1, 8):
        copy = peer_copy(
            parts.at[rank ^ k],
            small_buf.at[k - 1],
            small_send.at[k - 1],
            small_recv.at[k - 1],
            rank ^ k,
            plane,
        )
        copy.start()
        small.append(copy)
    scatter_begin(p_ref, grad, *rest, started=True)
    gather_start(next_ref, ag_send, ag_recv, own=block)
    total = parts[rank]
    for k in range(1, 8):
        small[k - 1].wait()
        total = total + small_buf[k - 1]
    so_ref[...] = total
    gather_pass(next_ref, ag_send, ag_recv, NEIGHBOURS_FIRST)
    scatter_end(p_ref, grad, *rest)
    gather_pass(next_ref, ag_send, ag_recv, DIAGONAL)
    inputs = x_ref[...].astype(jnp.float32)
    o_ref[...] = dmid_ref[...] + norm_back(grad[...], inputs, inv_rms(inputs), scale_ref[...])
    gather_wait(next_ref, ag_send, ag_recv, FROM_SIBLING)
    gather_sent(next_ref, ag_send, ag_recv)
    own.wait()


SCATTER_ORDER = (6, 2, 4, 0)


def scatter_far(i, out_buf, far_buf, send_sem, recv_sem):
    rank, plane = lax.axis_index("fsdp"), lax.axis_index("sp")
    return peer_copy(
        out_buf.at[i],
        far_buf.at[i],
        send_sem.at[i],
        recv_sem.at[i],
        rank ^ SCATTER_ORDER[i],
        plane,
    )


def scatter_near(p_ref, i, near_buf, sib_send, sib_recv):
    rank, plane = lax.axis_index("fsdp"), lax.axis_index("sp")
    return peer_copy(
        p_ref.at[rank ^ 1 ^ SCATTER_ORDER[i]],
        near_buf.at[i],
        sib_send.at[i],
        sib_recv.at[i],
        rank ^ 1,
        plane,
    )


def scatter_begin(p_ref, o_ref, near_buf, out_buf, far_buf, sib_send, sib_recv, send_sem, recv_sem, started=False):
    rank = lax.axis_index("fsdp")
    for i in range(0 if started else 4):
        scatter_near(p_ref, i, near_buf, sib_send, sib_recv).start()
    for i, k in enumerate(SCATTER_ORDER):
        scatter_near(p_ref, i, near_buf, sib_send, sib_recv).wait_recv()
        joined = p_ref[rank ^ k].astype(jnp.float32) + near_buf[i].astype(jnp.float32)
        if k:
            out_buf[i] = joined.astype(out_buf.dtype)
            scatter_far(i, out_buf, far_buf, send_sem, recv_sem).start()
        else:
            o_ref[...] = joined


def scatter_end(p_ref, o_ref, near_buf, out_buf, far_buf, sib_send, sib_recv, send_sem, recv_sem):
    for i in (1, 2, 0):
        scatter_far(i, out_buf, far_buf, send_sem, recv_sem).wait_recv()
        o_ref[...] += far_buf[i].astype(jnp.float32)
    for i in range(4):
        scatter_near(p_ref, i, near_buf, sib_send, sib_recv).wait_send()
    for i in range(3):
        scatter_far(i, out_buf, far_buf, send_sem, recv_sem).wait_send()


def scatter_scratch(rows, width, dtype):
    return [
        pltpu.VMEM((4, rows, width), dtype),
        pltpu.VMEM((3, rows, width), dtype),
        pltpu.VMEM((3, rows, width), dtype),
        pltpu.SemaphoreType.DMA((4,)),
        pltpu.SemaphoreType.DMA((4,)),
        pltpu.SemaphoreType.DMA((3,)),
        pltpu.SemaphoreType.DMA((3,)),
    ]


def scatter_gains(p, attn, ffn, head, x, scale, grad_middle, blocks, collective_id):
    ranks, rows, width = p.shape
    vmem = pl.BlockSpec(memory_space=pltpu.VMEM)
    hbm = pl.BlockSpec(memory_space=pl.ANY)
    small = (8, HEAD_DIM)
    return pl.pallas_call(
        scatter_gains_kernel,
        out_shape=(
            jax.ShapeDtypeStruct((rows, width), jnp.float32),
            jax.ShapeDtypeStruct(small, jnp.float32),
            jax.ShapeDtypeStruct(p.shape, blocks.dtype),
        ),
        in_specs=[vmem] * 7 + [hbm],
        out_specs=(vmem, vmem, hbm),
        scratch_shapes=[
            pltpu.VMEM((ranks,) + small, jnp.float32),
            pltpu.VMEM((7,) + small, jnp.float32),
            pltpu.VMEM((rows, width), jnp.float32),
            pltpu.SemaphoreType.DMA((7,)),
            pltpu.SemaphoreType.DMA((7,)),
            pltpu.SemaphoreType.DMA((GATHER_COPIES,)),
            pltpu.SemaphoreType.DMA((GATHER_COPIES,)),
            pltpu.SemaphoreType.DMA,
        ]
        + scatter_scratch(rows, width, p.dtype),
        compiler_params=pltpu.CompilerParams(
            collective_id=collective_id, has_side_effects=True, vmem_limit_bytes=VMEM_LIMIT
        ),
        name="scatter_gains",
    )(p, attn, ffn, head, x, scale, grad_middle, blocks)


def projection_back_kernel(
    back_ref, raw_ref, cos_ref, sin_ref, xa_ref, x_ref, dgate_ref, gated_ref, pm_ref, w_ref, wg_ref, head_ref, dxa_ref, pieces_ref, gate_ref, attn_ref, terms_ref, sums
):
    rank = lax.axis_index("fsdp")
    group, rows, width = back_ref.shape
    out_rows = gated_ref.shape[1]

    @pl.when(pl.program_id(0) == 0)
    def _():
        for ref in (sums, gate_ref, attn_ref, terms_ref):
            ref[...] = jnp.zeros_like(ref)

    cosine, sine = cos_ref[...], sin_ref[...]
    columns = []
    for m in range(group):
        back = back_ref[m]
        grad = back.astype(jnp.float32)
        turned = grad * cosine - pltpu.roll(grad, width // 2, 1) * sine
        raw = raw_ref[:, m * width : (m + 1) * width]
        inverse = inv_rms(raw)
        terms_ref[...] += jnp.sum(turned * raw * inverse, axis=0, keepdims=True)
        grad_raw = norm_back(turned, raw, inverse, head_ref[...])
        columns.append(jnp.where(rank >= 6, grad, grad_raw).astype(jnp.bfloat16))
    grad_proj = jnp.concatenate(columns, axis=1)
    grad_a = jnp.dot(grad_proj, w_ref[...], preferred_element_type=jnp.float32)
    normed = xa_ref[...].reshape(rows, -1)
    normed32 = normed.astype(jnp.float32)
    for head in range(dgate_ref.shape[0]):
        gate = dgate_ref[head].astype(jnp.float32)
        grad_a = grad_a + gate * wg_ref[head : head + 1].astype(jnp.float32)
        gate_ref[head : head + 1] += jnp.sum(gate * normed32, axis=0, keepdims=True)
    inputs = x_ref[...].reshape(rows, -1).astype(jnp.float32)
    attn_ref[...] += jnp.sum(grad_a * inputs * inv_rms(inputs), axis=0, keepdims=True)
    dxa_ref[...] = grad_a.astype(jnp.bfloat16).reshape(dxa_ref.shape)
    sums[:out_rows] += mat_tn(gated_ref[...], pm_ref[...].reshape(rows, -1))
    sums[out_rows:] += mat_tn(grad_proj, normed)

    @pl.when(pl.program_id(0) == pl.num_programs(0) - 1)
    def _():
        pieces_ref[...] = sums[...].astype(jnp.bfloat16)


def projection_back(back, raw, cosine, sine, normed, inputs, gate_grad, gated, plane_mid, w_qkv, w_head_gate, head_scale):
    ranks, rows, model_width = normed.shape
    group, tokens, width = back.shape
    pair = 2 * rows
    blocks = pl.BlockSpec((2, rows, model_width), lambda i: (i, 0, 0))
    thin = pl.BlockSpec((pair, width), lambda i: (i, 0))
    heads, out_rows = gate_grad.shape[0], gated.shape[1]

    def still(shape):
        return pl.BlockSpec(shape, lambda i: (0, 0))

    total = (out_rows + w_qkv.shape[0], model_width)
    return pl.pallas_call(
        projection_back_kernel,
        grid=(tokens // pair,),
        in_specs=[
            pl.BlockSpec((group, pair, width), lambda i: (0, i, 0)),
            pl.BlockSpec((pair, group * width), lambda i: (i, 0)),
            thin,
            thin,
            blocks,
            blocks,
            pl.BlockSpec((heads, pair, 1), lambda i: (0, i, 0)),
            pl.BlockSpec((pair, out_rows), lambda i: (i, 0)),
            blocks,
            still(w_qkv.shape),
            still(w_head_gate.shape),
            still(head_scale.shape),
        ],
        out_specs=(
            blocks,
            still(total),
            still(w_head_gate.shape),
            still((1, model_width)),
            still((1, width)),
        ),
        out_shape=(
            jax.ShapeDtypeStruct(normed.shape, jnp.bfloat16),
            jax.ShapeDtypeStruct(total, jnp.bfloat16),
            jax.ShapeDtypeStruct(w_head_gate.shape, jnp.float32),
            jax.ShapeDtypeStruct((1, model_width), jnp.float32),
            jax.ShapeDtypeStruct((1, width), jnp.float32),
        ),
        scratch_shapes=[pltpu.VMEM(total, jnp.float32)],
        compiler_params=pltpu.CompilerParams(vmem_limit_bytes=VMEM_LIMIT),
        name="projection_back",
    )(back, raw, cosine, sine, normed, inputs, gate_grad, gated, plane_mid, w_qkv, w_head_gate, head_scale)


GATHER_COPIES = 13


def gather_copy(buf, i, send_sem, recv_sem, own=None):
    rank, plane = lax.axis_index("fsdp"), lax.axis_index("sp")
    rows = buf.shape[1]
    top, low = pl.ds(0, rows // 2), pl.ds(rows // 2, rows // 2)
    block, part, to = (
        (0, top, 2),
        (0, low, 2),
        (0, low, 4),
        (0, top, 4),
        (2, top, 4),
        (4, low, 2),
        (0, pl.ds(0, rows), 1),
        (2, top, 1),
        (2, low, 1),
        (4, low, 1),
        (4, top, 1),
        (6, top, 1),
        (6, low, 1),
    )[i]
    piece = buf.at[rank ^ block, part]
    source = piece if own is None or block else own.at[part]
    return peer_copy(source, piece, send_sem.at[i], recv_sem.at[i], rank ^ to, plane)


def gather_start(buf, send_sem, recv_sem, own=None):
    for i in (6, 0, 2, 1, 3):
        gather_copy(buf, i, send_sem, recv_sem, own).start()


def gather_pass(buf, send_sem, recv_sem, pairs):
    for arrived, onward in pairs:
        gather_copy(buf, arrived, send_sem, recv_sem).wait_recv()
        for i in onward:
            gather_copy(buf, i, send_sem, recv_sem).start()


def gather_wait(buf, send_sem, recv_sem, copies):
    for i in copies:
        gather_copy(buf, i, send_sem, recv_sem).wait_recv()


def gather_sent(buf, send_sem, recv_sem):
    for i in range(GATHER_COPIES):
        gather_copy(buf, i, send_sem, recv_sem).wait_send()


NEIGHBOURS_FIRST = ((0, (4, 7)), (2, (5, 9)), (1, (8,)), (3, (10,)))
DIAGONAL = ((4, (11,)), (5, (12,)))
FROM_SIBLING = (6, 7, 8, 9, 10, 11, 12)


def greet_line(ranks, planes):
    rank, plane = lax.axis_index("fsdp"), lax.axis_index("sp")
    barrier = pltpu.get_barrier_semaphore()
    for k in range(1, ranks):
        pl.semaphore_signal(
            barrier, inc=1, device_id=(rank ^ k, plane), device_id_type=MESH
        )

    @pl.when(plane > 0)
    def _():
        pl.semaphore_signal(barrier, inc=1, device_id=(rank, plane - 1), device_id_type=MESH)

    @pl.when(plane < planes - 1)
    def _():
        pl.semaphore_signal(barrier, inc=1, device_id=(rank, plane + 1), device_id_type=MESH)

    lower = (plane > 0).astype(jnp.int32)
    upper = (plane < planes - 1).astype(jnp.int32)
    pl.semaphore_wait(barrier, ranks - 1 + lower + upper)


def line_sends(planes, plane, j, side):
    if side == 0:
        return (plane >= j) & (plane < planes - 1)
    return (plane + j <= planes - 1) & (plane > 0)


def unheads_kernel(planes, dq_ref, dkv_ref, blocks_ref, n_ref, next_ref, ag_send, ag_recv, own_sem2, line_out, line_in, done, own_sem, q_send, q_recv, kv_send, kv_recv, line_send, line_recv):
    rank, plane = lax.axis_index("fsdp"), lax.axis_index("sp")
    greet_line(8, planes)
    gathers = [(next_ref.at[which], ag_send.at[which], ag_recv.at[which]) for which in range(2)]
    own_blocks = [
        pltpu.make_async_copy(blocks_ref.at[which, 0], next_ref.at[which, rank], own_sem2.at[which])
        for which in range(2)
    ]
    for copy in own_blocks:
        copy.start()

    def q_copy(m, to):
        return peer_copy(dq_ref, n_ref.at[pl.ds(2 * m, 2)], q_send, q_recv.at[m], to, plane)

    def kv_copy(m, which, to):
        return peer_copy(done.at[which], n_ref.at[m], kv_send.at[which], kv_recv.at[m], to, plane)

    def q_local():
        return pltpu.make_async_copy(dq_ref, n_ref.at[pl.ds(0, 2)], own_sem)

    def kv_local(m, which):
        return pltpu.make_async_copy(done.at[which], n_ref.at[m], own_sem)

    @pl.when(rank == 0)
    def _():
        q_local().start()

    for m in range(2):
        @pl.when((rank % 2 == m) & (rank != 0))
        def _():
            q_copy(m, rank // 2).start()

    def step_copy(j, which, side):
        to = plane + 1 if side == 0 else plane - 1
        return peer_copy(
            line_out.at[side, j, which],
            line_in.at[side, j, which],
            line_send.at[side, j, which],
            line_recv.at[side, j, which],
            rank,
            to,
        )

    def sends(j, side):
        return plane < planes - 1 - j if side == 0 else plane > j

    def target(j, side):
        return planes - 1 - j if side == 0 else j

    for j in range(planes - 1):
        for which in range(2):
            for side in range(2):
                inner = plane > 0 if side == 0 else plane < planes - 1

                @pl.when(sends(j, side) & inner)
                def _():
                    step_copy(j, which, side).wait_recv()
                    total = dkv_ref[target(j, side), which].astype(jnp.float32) + line_in[
                        side, j, which
                    ].astype(jnp.float32)
                    line_out[side, j, which] = total.astype(line_out.dtype)

                @pl.when(sends(j, side) & jnp.logical_not(inner))
                def _():
                    line_out[side, j, which] = dkv_ref[target(j, side), which]

                @pl.when(sends(j, side))
                def _():
                    step_copy(j, which, side).start()

        if j == 0:
            gather_start(*gathers[0], own=blocks_ref.at[0, 0])
            gather_start(*gathers[1], own=blocks_ref.at[1, 0])
        if j == 2:
            gather_pass(*gathers[0], NEIGHBOURS_FIRST)
            gather_pass(*gathers[1], NEIGHBOURS_FIRST)

    for which in range(2):
        total = dkv_ref[plane, which].astype(jnp.float32)
        done32 = total
        for j in range(planes - 1):
            for side in range(2):
                @pl.when(plane == target(j, side))
                def _():
                    step_copy(j, which, side).wait_recv()
        low = jnp.minimum(planes - 1 - plane, planes - 2)
        high = jnp.minimum(plane, planes - 2)
        below = line_in[0, low, which].astype(jnp.float32)
        above = line_in[1, high, which].astype(jnp.float32)
        done32 = done32 + jnp.where(plane > 0, below, 0.0) + jnp.where(plane < planes - 1, above, 0.0)
        done[which] = done32.astype(done.dtype)
        first = 4 + 2 * which
        to = first + rank // 4
        for m in range(4):
            @pl.when((rank % 4 == m) & (to != rank))
            def _():
                kv_copy(m, which, to).start()

            @pl.when((rank % 4 == m) & (to == rank))
            def _():
                kv_local(m, which).start()

    for gather in gathers:
        gather_pass(*gather, DIAGONAL)
    for gather in gathers:
        gather_wait(*gather, FROM_SIBLING)
        gather_sent(*gather)
    for copy in own_blocks:
        copy.wait()

    @pl.when(rank < 4)
    def _():
        for m in range(2):
            @pl.when(2 * rank + m != rank)
            def _():
                q_copy(m, 0).wait_recv()

            @pl.when(2 * rank + m == rank)
            def _():
                q_local().wait()

    for which in range(2):
        first = 4 + 2 * which

        @pl.when((rank == first) | (rank == first + 1))
        def _():
            for m in range(4):
                @pl.when(4 * (rank - first) + m != rank)
                def _():
                    kv_copy(m, which, 0).wait_recv()

                @pl.when(4 * (rank - first) + m == rank)
                def _():
                    kv_local(m, which).wait()

    @pl.when(rank != 0)
    def _():
        q_copy(0, 0).wait_send()

    for which in range(2):
        @pl.when(4 + 2 * which + rank // 4 != rank)
        def _():
            kv_copy(0, which, 0).wait_send()

    for j in range(planes - 1):
        for which in range(2):
            for side in range(2):
                @pl.when(sends(j, side))
                def _():
                    step_copy(j, which, side).wait_send()


def return_heads(grad_query, grad_kv, line_blocks, collective_id):
    _, tokens, width = grad_query.shape
    planes = lax.axis_size("sp")
    ranks = lax.axis_size("fsdp")
    vmem = pl.BlockSpec(memory_space=pltpu.VMEM)
    hbm = pl.BlockSpec(memory_space=pl.ANY)
    return pl.pallas_call(
        functools.partial(unheads_kernel, planes),
        out_shape=(
            jax.ShapeDtypeStruct((4, tokens, width), grad_query.dtype),
            jax.ShapeDtypeStruct((2, ranks) + line_blocks.shape[2:], line_blocks.dtype),
        ),
        in_specs=[vmem, vmem, hbm],
        out_specs=(vmem, hbm),
        scratch_shapes=[
            pltpu.SemaphoreType.DMA((2, GATHER_COPIES)),
            pltpu.SemaphoreType.DMA((2, GATHER_COPIES)),
            pltpu.SemaphoreType.DMA((2,)),
            pltpu.VMEM((2, planes - 1, 2, tokens, width), grad_query.dtype),
            pltpu.VMEM((2, planes - 1, 2, tokens, width), grad_query.dtype),
            pltpu.VMEM((2, tokens, width), grad_query.dtype),
            pltpu.SemaphoreType.DMA,
            pltpu.SemaphoreType.DMA,
            pltpu.SemaphoreType.DMA((2,)),
            pltpu.SemaphoreType.DMA((2,)),
            pltpu.SemaphoreType.DMA((4,)),
            pltpu.SemaphoreType.DMA((2, planes - 1, 2)),
            pltpu.SemaphoreType.DMA((2, planes - 1, 2)),
        ],
        compiler_params=pltpu.CompilerParams(
            collective_id=collective_id, has_side_effects=True, vmem_limit_bytes=VMEM_LIMIT
        ),
        name="return_heads",
    )(grad_query, grad_kv, line_blocks)


def stack_heads(ref):
    return ref[...].reshape(ref.shape[0] * ref.shape[1], ref.shape[2])


def block_bounds(lengths_ref, ranks, planes, rows):
    block = pl.program_id(0)
    span = planes * rows
    first = block * span + lax.axis_index("sp") * rows
    start, end = jnp.int32(0), jnp.int32(0)
    for item in range(lengths_ref.shape[0]):
        end = end + lengths_ref[item]
        start = jnp.where(first >= end, end, start)
    return start // span, block, first


def row_starts(lengths_ref, tokens):
    start, end = jnp.zeros_like(tokens), jnp.int32(0)
    for item in range(lengths_ref.shape[0]):
        end = end + lengths_ref[item]
        start = jnp.where(tokens >= end, end, start)
    return start


def chunk_weights(query, key, scale, tokens, starts, first_key):
    scores = mat_nt(query, key) * scale
    columns = first_key + lax.broadcasted_iota(jnp.int32, scores.shape, 1)
    allowed = (columns <= tokens) & (columns >= starts)
    return jnp.where(allowed, jnp.exp(scores), 0.0)


def query_tokens(first, rows, group):
    row = lax.broadcasted_iota(jnp.int32, (group * rows, 1), 0)
    return first + lax.rem(row, rows)


def attend_kernel(ranks, planes, lengths_ref, q_ref, kv_ref, gate_ref, att_ref, total_ref, gated_ref):
    group, rows, width = q_ref.shape
    scale = HEAD_DIM ** (-0.5)
    low, high, first = block_bounds(lengths_ref, ranks, planes, rows)
    tokens = query_tokens(first, rows, group)
    starts = row_starts(lengths_ref, tokens)
    query = stack_heads(q_ref)
    span = planes * rows

    def step(chunk, running):
        total, unnorm = running
        key = kv_ref[:, 0, chunk].reshape(span, width)
        value = kv_ref[:, 1, chunk].reshape(span, width)
        weights = chunk_weights(query, key, scale, tokens, starts, chunk * span)
        total = total + jnp.sum(weights, axis=1, keepdims=True)
        unnorm = unnorm + jnp.dot(
            weights.astype(jnp.bfloat16), value, preferred_element_type=jnp.float32
        )
        return total, unnorm

    total, unnorm = lax.fori_loop(
        low,
        high + 1,
        step,
        (
            jnp.zeros((group * rows, 1), jnp.float32),
            jnp.zeros((group * rows, width), jnp.float32),
        ),
    )
    attended = unnorm / total
    att_ref[...] = attended.reshape(group, rows, width)
    total_ref[...] = total.reshape(group, rows, 1)
    sent = attended.astype(jnp.bfloat16).astype(jnp.float32)
    for head in range(group):
        gated = sent[head * rows : (head + 1) * rows] * jax.nn.sigmoid(gate_ref[head])
        gated_ref[:, head * width : (head + 1) * width] = gated.astype(jnp.bfloat16)


def attend(lengths, query, kv, gate_logit, rows):
    group, tokens, width = query.shape
    planes = kv.shape[0]
    ranks = tokens // rows
    kv_blocks = kv.reshape(planes, 2, ranks, rows, width)
    block = pl.BlockSpec((group, rows, width), lambda i, *_: (0, i, 0))
    thin = pl.BlockSpec((group, rows, 1), lambda i, *_: (0, i, 0))
    return pl.pallas_call(
        functools.partial(attend_kernel, ranks, planes),
        grid_spec=pltpu.PrefetchScalarGridSpec(
            num_scalar_prefetch=1,
            grid=(ranks,),
            in_specs=[
                block,
                pl.BlockSpec((planes, 2, ranks, rows, width), lambda i, *_: (0, 0, 0, 0, 0)),
                thin,
            ],
            out_specs=(
                block,
                thin,
                pl.BlockSpec((rows, group * width), lambda i, *_: (i, 0)),
            ),
        ),
        out_shape=(
            jax.ShapeDtypeStruct((group, tokens, width), jnp.float32),
            jax.ShapeDtypeStruct((group, tokens, 1), jnp.float32),
            jax.ShapeDtypeStruct((tokens, group * width), jnp.bfloat16),
        ),
        compiler_params=pltpu.CompilerParams(vmem_limit_bytes=VMEM_LIMIT),
        name="attend",
    )(lengths, query, kv_blocks, gate_logit)


def attend_back_kernel(
    ranks, planes, lengths_ref, q_ref, kv_ref, gate_ref, att_ref, total_ref, dgated_ref, dq_ref, dkv_ref, dgate_ref, sums
):
    group, rows, width = q_ref.shape
    scale = HEAD_DIM ** (-0.5)
    low, high, first = block_bounds(lengths_ref, ranks, planes, rows)
    tokens = query_tokens(first, rows, group)
    starts = row_starts(lengths_ref, tokens)
    query = stack_heads(q_ref)
    span = planes * rows

    @pl.when(pl.program_id(0) == 0)
    def _():
        sums[...] = jnp.zeros_like(sums)

    attended = stack_heads(att_ref)
    sent = attended.astype(jnp.bfloat16).astype(jnp.float32)
    total = stack_heads(total_ref)
    logit = stack_heads(gate_ref)
    prob = jax.nn.sigmoid(logit)
    dgated = jnp.concatenate(
        [dgated_ref[:, head * width : (head + 1) * width] for head in range(group)], axis=0
    )
    dattended = (dgated * prob).astype(jnp.bfloat16)
    dlogit = jnp.sum(dgated * sent, axis=1, keepdims=True) * prob * (1.0 - prob)
    dgate_ref[...] = dlogit.astype(jnp.bfloat16).reshape(group, rows, 1)
    dattended = dattended.astype(jnp.float32)
    scaled = (dattended / total).astype(jnp.bfloat16)
    delta = jnp.sum(dattended * attended, axis=1, keepdims=True) / total

    def step(chunk, dquery):
        key = kv_ref[:, 0, chunk].reshape(span, width)
        value = kv_ref[:, 1, chunk].reshape(span, width)
        weights = chunk_weights(query, key, scale, tokens, starts, chunk * span)
        dprob = mat_nt(scaled, value)
        dscore = (weights * (dprob - delta)).astype(jnp.bfloat16)
        dquery = dquery + jnp.dot(dscore, key, preferred_element_type=jnp.float32)
        dkey = mat_tn(dscore, query)
        dvalue = mat_tn(weights.astype(jnp.bfloat16), scaled)
        sums[:, 0, chunk] += dkey.reshape(planes, rows, width)
        sums[:, 1, chunk] += dvalue.reshape(planes, rows, width)
        return dquery

    dquery = lax.fori_loop(
        low, high + 1, step, jnp.zeros((group * rows, width), jnp.float32)
    )
    dq_ref[...] = (dquery * scale).astype(jnp.bfloat16).reshape(group, rows, width)

    @pl.when(pl.program_id(0) == ranks - 1)
    def _():
        for chunk in range(ranks):
            dkv_ref[:, 0, chunk] = (sums[:, 0, chunk] * scale).astype(jnp.bfloat16)
            dkv_ref[:, 1, chunk] = sums[:, 1, chunk].astype(jnp.bfloat16)


def attend_back(lengths, query, kv, gate_logit, attended, total, dgated, rows):
    group, tokens, width = query.shape
    planes = kv.shape[0]
    ranks = tokens // rows
    kv_blocks = kv.reshape(planes, 2, ranks, rows, width)
    block = pl.BlockSpec((group, rows, width), lambda i, *_: (0, i, 0))
    thin = pl.BlockSpec((group, rows, 1), lambda i, *_: (0, i, 0))
    whole = pl.BlockSpec((planes, 2, ranks, rows, width), lambda i, *_: (0, 0, 0, 0, 0))
    dquery, dkv, dgate = pl.pallas_call(
        functools.partial(attend_back_kernel, ranks, planes),
        grid_spec=pltpu.PrefetchScalarGridSpec(
            num_scalar_prefetch=1,
            grid=(ranks,),
            in_specs=[
                block,
                whole,
                thin,
                block,
                thin,
                pl.BlockSpec((rows, group * width), lambda i, *_: (i, 0)),
            ],
            out_specs=(block, whole, thin),
            scratch_shapes=[pltpu.VMEM((planes, 2, ranks, rows, width), jnp.float32)],
        ),
        out_shape=(
            jax.ShapeDtypeStruct((group, tokens, width), jnp.bfloat16),
            jax.ShapeDtypeStruct((planes, 2, ranks, rows, width), jnp.bfloat16),
            jax.ShapeDtypeStruct((group, tokens, 1), jnp.bfloat16),
        ),
        compiler_params=pltpu.CompilerParams(vmem_limit_bytes=VMEM_LIMIT),
        name="attend_back",
    )(lengths, query, kv_blocks, gate_logit, attended, total, dgated)
    return dquery, dkv.reshape(planes, 2, tokens, width), dgate


def middle_kernel(
    planes,
    gated_ref,
    wout_ref,
    x_ref,
    scale_ref,
    dy_hbm,
    wg_hbm,
    wu_hbm,
    wd_hbm,
    xg,
    line_hbm,
    down_hbm,
    mid_ref,
    dmid_ref,
    gain_ref,
    pm_ref,
    dgated_ref,
    act_ref,
    wg,
    wu,
    wd,
    dy,
    dhid,
    near_out,
    near_in,
    far_out,
    far_in,
    keep,
    down_buf,
    load_sem,
    dy_sem,
    down_sem,
    near_send,
    near_recv,
    far_send,
    far_recv,
    ag_send,
    ag_recv,
    line_send,
    line_recv,
):
    rank, plane = lax.axis_index("fsdp"), lax.axis_index("sp")
    ranks, rows, width = xg.shape
    loads = [
        pltpu.make_async_copy(wd_hbm, wd, load_sem.at[0]),
        pltpu.make_async_copy(wg_hbm, wg, load_sem.at[1]),
        pltpu.make_async_copy(wu_hbm, wu, load_sem.at[2]),
    ]
    dy_load = pltpu.make_async_copy(dy_hbm, dy, dy_sem)
    others = [lax.rem(plane + k, planes) for k in range(1, planes)]
    greet([(rank ^ k, plane) for k in (1, 2, 4, 6)] + [(rank, other) for other in others])

    def along(source, which):
        return [
            peer_copy(
                source,
                line_hbm.at[which, j - 1],
                line_send.at[which, j - 1],
                line_recv.at[which, j - 1],
                rank,
                lax.rem(plane + planes - j, planes),
            )
            for j in range(1, planes)
        ]

    def near(phase, i):
        return peer_copy(
            near_out.at[phase, i],
            near_in.at[phase, i],
            near_send.at[phase, i],
            near_recv.at[phase, i],
            rank ^ 1,
            plane,
        )

    def far(phase, i, k):
        return peer_copy(
            far_out.at[phase, i],
            far_in.at[phase, i],
            far_send.at[phase, i],
            far_recv.at[phase, i],
            rank ^ k,
            plane,
        )

    order = (6, 2, 4, 0)
    for i, k in enumerate(order):
        part = jnp.dot(
            gated_ref[rank ^ 1 ^ k], wout_ref[...], preferred_element_type=jnp.float32
        )
        near_out[0, i] = part.astype(jnp.bfloat16)
        near(0, i).start()
    dy_load.start()
    for copy in loads:
        copy.start()
    dy_line = along(dy_hbm.at[rank], 1)
    for copy in dy_line:
        copy.start()
    for i, k in enumerate(order):
        part = jnp.dot(gated_ref[rank ^ k], wout_ref[...], preferred_element_type=jnp.float32)
        near(0, i).wait_recv()
        part = part + near_in[0, i].astype(jnp.float32)
        if k:
            far_out[0, i] = part.astype(jnp.bfloat16)
            far(0, i, k).start()
        else:
            keep[...] = part

    dy_load.wait()
    loads[0].wait()

    @pl.loop(0, ranks // 2)
    def _(p):
        pair = dy[pl.ds(2 * p, 2)].reshape(2 * rows, width)
        dhid[p] = mat_nt(pair, wd[...])

    loads[1].wait()
    loads[2].wait()
    middle = x_ref[...].astype(jnp.float32) + keep[...]
    for i in (1, 2, 0):
        far(0, i, order[i]).wait_recv()
        middle = middle + far_in[0, i].astype(jnp.float32)
    inverse = inv_rms(middle)
    mid_ref[...] = middle
    normed = (middle * inverse * scale_ref[...]).astype(jnp.bfloat16)
    xg[rank] = normed
    sems = (ag_send.at[0], ag_recv.at[0])
    gather_start(xg, *sems)
    xb_line = along(xg.at[rank], 0)
    for copy in xb_line:
        copy.start()

    slots = {2: 0, 4: 1, 6: 2, 0: 3}

    def down_copy(p, slot):
        return pltpu.make_async_copy(
            down_buf.at[slot], down_hbm.at[pl.ds(2 * p, 2)], down_sem.at[slot]
        )

    def feed(k):
        p = (rank ^ k) // 2
        slot = (0, 2, 4, 6).index(k) % 2
        pair = xg[pl.ds(2 * p, 2)].reshape(2 * rows, width)
        gate_pre = mat_nt(pair, wg[...])
        up_pre = mat_nt(pair, wu[...])
        grad_hidden = dhid[p]
        sigma = jax.nn.sigmoid(gate_pre)
        swish = gate_pre * sigma
        grad_gate = (grad_hidden * up_pre * sigma * (1.0 + gate_pre * (1.0 - sigma))).astype(
            jnp.bfloat16
        )
        grad_up = (grad_hidden * swish).astype(jnp.bfloat16)
        part = jnp.dot(grad_gate, wg[...], preferred_element_type=jnp.float32) + jnp.dot(
            grad_up, wu[...], preferred_element_type=jnp.float32
        )
        i = slots[k]
        halves = part.reshape(2, rows, width)
        mine_first = lax.rem(rank, 2) == 0
        mine = jnp.where(mine_first, halves[0], halves[1])
        theirs = jnp.where(mine_first, halves[1], halves[0])
        near_out[1, i] = theirs.astype(jnp.bfloat16)
        near(1, i).start()
        hidden = (swish * up_pre).astype(jnp.bfloat16)
        for kept, value in enumerate((grad_gate, grad_up, hidden)):
            act_ref[kept, pl.ds(pl.multiple_of(2 * rows * p, 2 * rows), 2 * rows)] = value
        down = jnp.dot(hidden, wd[...], preferred_element_type=jnp.float32)
        if k in (4, 6):
            down_copy(p, slot).wait()
        down_buf[slot] = down.astype(jnp.bfloat16).reshape(2, rows, width)
        down_copy(p, slot).start()
        near(1, i).wait_recv()
        mine = mine + near_in[1, i].astype(jnp.float32)
        if k:
            far_out[1, i] = mine.astype(jnp.bfloat16)
            far(1, i, k).start()
        else:
            keep[...] = mine

    gather_wait(xg, *sems, (6,))
    feed(0)
    gather_pass(xg, *sems, NEIGHBOURS_FIRST)
    gather_wait(xg, *sems, (7, 8))
    feed(2)
    gather_pass(xg, *sems, DIAGONAL)
    gather_wait(xg, *sems, (9, 10))
    feed(4)
    gather_wait(xg, *sems, (11, 12))
    feed(6)

    grad = keep[...]
    for i, k in enumerate((2, 4, 6)):
        far(1, i, k).wait_recv()
        grad = grad + far_in[1, i].astype(jnp.float32)
    middle = mid_ref[...]
    inverse = inv_rms(middle)
    gain_ref[...] = jnp.sum(grad * middle * inverse, axis=0, keepdims=True)
    grad_middle = dy[rank].astype(jnp.float32) + norm_back(
        grad, middle, inverse, scale_ref[...]
    )
    dmid_ref[...] = grad_middle
    pm_ref[rank] = grad_middle.astype(jnp.bfloat16)
    sems2 = (ag_send.at[1], ag_recv.at[1])
    gather_start(pm_ref, *sems2)

    def gated_grad(k):
        p = (rank ^ k) // 2
        pair = pm_ref[pl.ds(2 * p, 2)].reshape(2 * rows, width)
        dgated_ref[pl.ds(2 * p, 2)] = mat_nt(pair, wout_ref[...]).reshape(
            2, rows, wout_ref.shape[0]
        )

    gather_wait(pm_ref, *sems2, (6,))
    gated_grad(0)
    gather_pass(pm_ref, *sems2, NEIGHBOURS_FIRST)
    gather_wait(pm_ref, *sems2, (7, 8))
    gated_grad(2)
    gather_wait(pm_ref, *sems2, (9, 10))
    gated_grad(4)
    gather_pass(pm_ref, *sems2, DIAGONAL)
    gather_wait(pm_ref, *sems2, (11, 12))
    gated_grad(6)

    gather_sent(xg, *sems)
    gather_sent(pm_ref, *sems2)
    for copy in dy_line + xb_line:
        copy.wait()
    for phase in range(2):
        for i in range(4):
            near(phase, i).wait_send()
        for i in range(3):
            far(phase, i, 2).wait_send()
    down_copy(0, 0).wait()
    down_copy(0, 1).wait()


def middle_layer(gated, w_out, x, scale, grad_plane, w_gate, w_up, w_down, collective_id):
    ranks, rows, _ = gated.shape
    planes = lax.axis_size("sp")
    width = x.shape[1]
    hidden = w_gate.shape[0]
    features = w_out.shape[0]
    vmem = pl.BlockSpec(memory_space=pltpu.VMEM)
    hbm = pl.BlockSpec(memory_space=pl.ANY)
    half, full = jnp.bfloat16, jnp.float32
    return pl.pallas_call(
        functools.partial(middle_kernel, planes),
        out_shape=(
            jax.ShapeDtypeStruct((ranks, rows, width), half),
            jax.ShapeDtypeStruct((2, planes - 1, rows, width), half),
            jax.ShapeDtypeStruct((ranks, rows, width), half),
            jax.ShapeDtypeStruct((rows, width), full),
            jax.ShapeDtypeStruct((rows, width), full),
            jax.ShapeDtypeStruct((1, width), full),
            jax.ShapeDtypeStruct((ranks, rows, width), half),
            jax.ShapeDtypeStruct((ranks, rows, features), full),
            jax.ShapeDtypeStruct((3, ranks * rows, hidden), half),
        ),
        in_specs=[vmem, vmem, vmem, vmem, hbm, hbm, hbm, hbm],
        out_specs=(vmem, hbm, hbm, vmem, vmem, vmem, vmem, vmem, vmem),
        scratch_shapes=[
            pltpu.VMEM((hidden, width), half),
            pltpu.VMEM((hidden, width), half),
            pltpu.VMEM((hidden, width), half),
            pltpu.VMEM((ranks, rows, width), half),
            pltpu.VMEM((ranks // 2, 2 * rows, hidden), full),
            pltpu.VMEM((2, 4, rows, width), half),
            pltpu.VMEM((2, 4, rows, width), half),
            pltpu.VMEM((2, 3, rows, width), half),
            pltpu.VMEM((2, 3, rows, width), half),
            pltpu.VMEM((rows, width), full),
            pltpu.VMEM((2, 2, rows, width), half),
            pltpu.SemaphoreType.DMA((3,)),
            pltpu.SemaphoreType.DMA,
            pltpu.SemaphoreType.DMA((2,)),
            pltpu.SemaphoreType.DMA((2, 4)),
            pltpu.SemaphoreType.DMA((2, 4)),
            pltpu.SemaphoreType.DMA((2, 3)),
            pltpu.SemaphoreType.DMA((2, 3)),
            pltpu.SemaphoreType.DMA((2, GATHER_COPIES)),
            pltpu.SemaphoreType.DMA((2, GATHER_COPIES)),
            pltpu.SemaphoreType.DMA((2, planes - 1)),
            pltpu.SemaphoreType.DMA((2, planes - 1)),
        ],
        compiler_params=pltpu.CompilerParams(
            collective_id=collective_id, has_side_effects=True, vmem_limit_bytes=VMEM_LIMIT
        ),
        name="middle_layer",
    )(gated, w_out, x, scale, grad_plane, w_gate, w_up, w_down)


def feed_weights_kernel(
    planes,
    xp_hbm,
    dp_hbm,
    act_hbm,
    blocks_hbm,
    first_hbm,
    second_hbm,
    down_hbm,
    mid_ref,
    small_ref,
    rows_ref,
    wg_ref,
    wu_ref,
    wd_ref,
    og_ref,
    ou_ref,
    od_ref,
    h_ref,
    so_ref,
    go_ref,
    more_hbm,
    xbuf,
    dbuf,
    act,
    parts,
    small_buf,
    rows_buf,
    x_sem,
    d_sem,
    act_sem,
    part_sem,
    own_sem,
    ag_send,
    ag_recv,
    line_send,
    line_recv,
    near_buf,
    out_buf,
    far_buf,
    sib_send,
    sib_recv,
    send_sem,
    recv_sem,
):
    rank, plane = lax.axis_index("fsdp"), lax.axis_index("sp")
    ranks, rows, width = xp_hbm.shape
    part = ranks // 2
    chunk = part * rows
    others = [lax.rem(plane + k, planes) for k in range(1, planes)]
    greet([(rank ^ k, plane) for k in (1, 2, 4, 6)] + [(rank, other) for other in others])

    picks = ((0, 1), (1, 2), (0, 2))
    gathers = [(more_hbm.at[g], ag_send.at[g], ag_recv.at[g]) for g in range(3)]
    own_blocks = [
        pltpu.make_async_copy(blocks_hbm.at[pick], more_hbm.at[g, rank], own_sem.at[g])
        for g, pick in enumerate(picks)
    ]

    def begin(g):
        gather_start(*gathers[g], own=blocks_hbm.at[picks[g]])

    def load(step, start):
        slot = lax.rem(step, 2)
        block = pl.ds(part * lax.rem(step, 2), part)
        group = step // 2
        sources = (
            (first_hbm.at[0, block], first_hbm.at[1, block]),
            (xp_hbm.at[block], dp_hbm.at[block]),
            (more_hbm.at[0, block], second_hbm.at[block]),
            (more_hbm.at[2, block], more_hbm.at[1, block]),
        )
        for index, (x_from, d_from) in enumerate(sources):
            @pl.when(group == index)
            def _():
                for copy in (
                    pltpu.make_async_copy(x_from, xbuf.at[slot], x_sem.at[slot]),
                    pltpu.make_async_copy(d_from, dbuf.at[slot], d_sem.at[slot]),
                ):
                    if start:
                        copy.start()
                    else:
                        copy.wait()

    def kept(step):
        where = pl.ds(pl.multiple_of(step * chunk, chunk), chunk)
        return pltpu.make_async_copy(act_hbm.at[:, where], act, act_sem)

    scatter = (near_buf, sib_send, sib_recv)
    own_parts = [
        pltpu.make_async_copy(down_hbm.at[rank ^ k], parts.at[i], part_sem.at[i])
        for i, k in enumerate(SCATTER_ORDER)
    ]
    small = [
        peer_copy(
            source,
            buffer.at[k],
            line_send.at[which, k],
            line_recv.at[which, k],
            rank,
            others[k],
        )
        for which, (source, buffer) in enumerate(((small_ref, small_buf), (rows_ref, rows_buf)))
        for k in range(planes - 1)
    ]

    load(0, True)
    for copy in own_blocks + small + own_parts:
        copy.start()
    begin(0)
    for i in range(4):
        scatter_near(down_hbm, i, *scatter).start()

    @pl.loop(0, 2 * planes)
    def _(step):
        @pl.when(step == 1)
        def _():
            gather_pass(*gathers[0], NEIGHBOURS_FIRST)
            begin(1)

        @pl.when(step == 2)
        def _():
            kept(0).start()
            gather_pass(*gathers[0], DIAGONAL)
            gather_pass(*gathers[1], NEIGHBOURS_FIRST)
            begin(2)

        @pl.when(step == 3)
        def _():
            kept(1).start()
            for i, k in enumerate(SCATTER_ORDER):
                own_parts[i].wait()
                scatter_near(down_hbm, i, *scatter).wait_recv()
                joined = parts[i].astype(jnp.float32) + near_buf[i].astype(jnp.float32)
                if k:
                    out_buf[i] = joined.astype(out_buf.dtype)
                else:
                    parts[i] = joined.astype(parts.dtype)

        @pl.when(step == 4)
        def _():
            gather_wait(*gathers[0], FROM_SIBLING)
            own_blocks[0].wait()
            load(step, True)
            gather_pass(*gathers[1], DIAGONAL)

        @pl.when(step == 5)
        def _():
            gather_pass(*gathers[2], NEIGHBOURS_FIRST)
            for i in range(3):
                scatter_far(i, out_buf, far_buf, send_sem, recv_sem).start()

        @pl.when(step == 6)
        def _():
            gather_pass(*gathers[2], DIAGONAL)
            for g in (1, 2):
                gather_wait(*gathers[g], FROM_SIBLING)
                own_blocks[g].wait()
            load(step, True)

        load(step, False)

        @pl.when((lax.rem(step, 2) == 0) | (step == 1))
        def _():
            load(step + 1, True)

        slot = lax.rem(step, 2)
        normed = xbuf[slot].reshape(chunk, width)
        grad = dbuf[slot].reshape(chunk, width)

        own = step // 2 == 1

        @pl.when(own)
        def _():
            kept(0).wait()

        @pl.when(jnp.logical_not(own))
        def _():
            gate_pre = mat_nt(normed, wg_ref[...])
            up_pre = mat_nt(normed, wu_ref[...])
            grad_hidden = mat_nt(grad, wd_ref[...])
            sigma = jax.nn.sigmoid(gate_pre)
            swish = gate_pre * sigma
            act[0] = (grad_hidden * up_pre * sigma * (1.0 + gate_pre * (1.0 - sigma))).astype(
                jnp.bfloat16
            )
            act[1] = (grad_hidden * swish).astype(jnp.bfloat16)
            act[2] = (swish * up_pre).astype(jnp.bfloat16)

        @pl.when(step == 0)
        def _():
            for ref in (og_ref, ou_ref, od_ref):
                ref[...] = jnp.zeros_like(ref)

        og_ref[...] += mat_tn(act[0], normed)
        ou_ref[...] += mat_tn(act[1], normed)
        od_ref[...] += mat_tn(act[2], grad)

    output = mid_ref[...] + parts[3].astype(jnp.float32)
    for i in range(3):
        scatter_far(i, out_buf, far_buf, send_sem, recv_sem).wait()
        output = output + far_buf[i].astype(jnp.float32)
    h_ref[...] = output.astype(h_ref.dtype)
    for copy in small:
        copy.wait()
    total, gate_rows = small_ref[...], rows_ref[...]
    for k in range(planes - 1):
        total = total + small_buf[k]
        gate_rows = gate_rows + rows_buf[k]
    so_ref[...] = total
    go_ref[...] = gate_rows
    for i in range(4):
        scatter_near(down_hbm, i, *scatter).wait_send()
    for gather in gathers:
        gather_sent(*gather)


def feed_weights(plane_x, plane_grad, acts, blocks, first, second, down, middle, small, gate_rows, w_gate, w_up, w_down, collective_id):
    ranks, rows, width = plane_x.shape
    planes = lax.axis_size("sp")
    hidden = w_gate.shape[0]
    vmem = pl.BlockSpec(memory_space=pltpu.VMEM)
    hbm = pl.BlockSpec(memory_space=pl.ANY)
    tokens = planes * ranks * rows
    half, full = plane_x.dtype, jnp.float32
    return pl.pallas_call(
        functools.partial(feed_weights_kernel, planes),
        in_specs=[hbm] * 7 + [vmem] * 6,
        out_specs=(vmem,) * 6 + (hbm,),
        out_shape=[jax.ShapeDtypeStruct(w_gate.shape, full)] * 3
        + [
            jax.ShapeDtypeStruct((rows, width), half),
            jax.ShapeDtypeStruct(small.shape, full),
            jax.ShapeDtypeStruct(gate_rows.shape, full),
            jax.ShapeDtypeStruct((3, ranks, rows, width), half),
        ],
        scratch_shapes=[
            pltpu.VMEM((2, ranks // 2, rows, width), half),
            pltpu.VMEM((2, ranks // 2, rows, width), half),
            pltpu.VMEM((3, ranks // 2 * rows, hidden), half),
            pltpu.VMEM((4, rows, width), half),
            pltpu.VMEM((planes - 1,) + small.shape, full),
            pltpu.VMEM((planes - 1,) + gate_rows.shape, full),
            pltpu.SemaphoreType.DMA((2,)),
            pltpu.SemaphoreType.DMA((2,)),
            pltpu.SemaphoreType.DMA,
            pltpu.SemaphoreType.DMA((4,)),
            pltpu.SemaphoreType.DMA((3,)),
            pltpu.SemaphoreType.DMA((3, GATHER_COPIES)),
            pltpu.SemaphoreType.DMA((3, GATHER_COPIES)),
            pltpu.SemaphoreType.DMA((2, planes - 1)),
            pltpu.SemaphoreType.DMA((2, planes - 1)),
        ]
        + scatter_scratch(rows, width, half),
        cost_estimate=pl.CostEstimate(
            flops=12 * tokens * w_gate.size,
            bytes_accessed=4 * tokens * width + 18 * w_gate.size,
            transcendentals=tokens * w_gate.shape[0],
        ),
        compiler_params=pltpu.CompilerParams(
            collective_id=collective_id, has_side_effects=True, vmem_limit_bytes=VMEM_LIMIT
        ),
        name="feed_weights",
    )(plane_x, plane_grad, acts, blocks, first, second, down, middle, small, gate_rows, w_gate, w_up, w_down)[:6]


def front_kernel(
    planes,
    lengths_ref,
    x_ref,
    small_ref,
    w_ref,
    wg_ref,
    dyo_ref,
    q_ref,
    kv_ref,
    dy_ref,
    xg,
    xa_ref,
    raw_ref,
    gate_ref,
    attn_ref,
    ffn_ref,
    head_ref,
    cos_ref,
    sin_ref,
    nat,
    gains,
    small_send,
    small_recv,
    ag_send,
    ag_recv,
    own_sem,
    local_sem,
    q_send,
    q_recv,
    kv_send,
    kv_recv,
    line_send,
    line_recv,
):
    rank, plane = lax.axis_index("fsdp"), lax.axis_index("sp")
    ranks, rows, width = xg.shape
    pair_rows = 2 * rows
    chip = rank // 2
    greet_line(ranks, planes)
    own_block = pltpu.make_async_copy(dyo_ref, dy_ref.at[rank], own_sem)
    own_block.start()
    small = []
    for k in range(1, ranks):
        copy = peer_copy(
            small_ref, gains.at[rank], small_send.at[k - 1], small_recv.at[k - 1], rank ^ k, plane
        )
        copy.start()
        small.append(copy)
    sems = (ag_send.at[0], ag_recv.at[0])
    gather_start(xg, *sems, own=x_ref)
    xg[rank] = x_ref[...]
    gains[rank] = small_ref[...]

    half = HEAD_DIM // 2
    lane = lax.broadcasted_iota(jnp.int32, (1, HEAD_DIM), 1)
    step = lax.rem(lane, half).astype(jnp.float32)
    frequency = jnp.exp(-math.log(ROPE_BASE) * 2.0 * step / HEAD_DIM)
    sign = jnp.where(lane < half, -1.0, 1.0)

    @pl.loop(0, ranks)
    def _(block):
        tokens = (block * planes + plane) * rows + lax.broadcasted_iota(jnp.int32, (rows, 1), 0)
        position = tokens - row_starts(lengths_ref, tokens)
        angles = position.astype(jnp.float32) * frequency
        where = pl.ds(pl.multiple_of(block * rows, rows), rows)
        cos_ref[where] = jnp.cos(angles)
        sin_ref[where] = jnp.sin(angles) * sign

    for copy in small:
        copy.wait_recv()
    head_q, head_k = gains[0, 4:5], gains[0, 5:6]
    for r in range(1, ranks):
        head_q = head_q + gains[r, 4:5]
        head_k = head_k + gains[r, 5:6]
    head_ref[...] = jnp.where(rank < ranks // 2, head_q, head_k)
    for r in range(ranks):
        for i in range(2):
            columns = slice((2 * r + i) * HEAD_DIM, (2 * r + i + 1) * HEAD_DIM)
            attn_ref[:, columns] = gains[r, i : i + 1]
            ffn_ref[:, columns] = gains[r, 2 + i : 3 + i]

    def token_rows(p):
        return pl.ds(pl.multiple_of(p * pair_rows, pair_rows), pair_rows)

    def q_copy(m, p, to):
        return peer_copy(
            nat.at[pl.ds(2 * m, 2), token_rows(p)],
            q_ref.at[:, token_rows(p)],
            q_send.at[m, p],
            q_recv.at[p],
            to,
            plane,
        )

    def kv_copy(m, which, p, to):
        return peer_copy(
            nat.at[m, token_rows(p)],
            kv_ref.at[plane, which, token_rows(p)],
            kv_send.at[m, p],
            kv_recv.at[which, p],
            to,
            plane,
        )

    def q_local(p):
        return pltpu.make_async_copy(
            nat.at[pl.ds(0, 2), token_rows(p)], q_ref.at[:, token_rows(p)], local_sem.at[p]
        )

    def kv_local(m, which, p):
        return pltpu.make_async_copy(
            nat.at[m, token_rows(p)], kv_ref.at[plane, which, token_rows(p)], local_sem.at[p]
        )

    def process(k):
        p = chip ^ (k // 2)
        inputs = xg[pl.ds(2 * p, 2)].reshape(pair_rows, width).astype(jnp.float32)
        normed = (inputs * inv_rms(inputs) * attn_ref[...]).astype(jnp.bfloat16)
        xa_ref[pl.ds(2 * p, 2)] = normed.reshape(2, rows, width)
        projected = mat_nt(normed, w_ref[...])
        raw_ref[token_rows(p)] = projected
        logits = mat_nt(normed, wg_ref[...])
        for head in range(gate_ref.shape[0]):
            gate_ref[head, token_rows(p)] = logits[:, head : head + 1]
        cosine, sine = cos_ref[token_rows(p)], sin_ref[token_rows(p)]
        for m in range(4):
            head = projected[:, m * HEAD_DIM : (m + 1) * HEAD_DIM]
            scaled = head * inv_rms(head) * head_ref[...]
            turned = scaled * cosine + pltpu.roll(scaled, half, 1) * sine
            nat[m, token_rows(p)] = jnp.where(rank >= 6, head, turned).astype(jnp.bfloat16)

        @pl.when(rank < 4)
        def _():
            for m in range(2):
                @pl.when(2 * rank + m != rank)
                def _():
                    q_copy(m, p, 2 * rank + m).start()

        @pl.when(rank == 0)
        def _():
            q_local(p).start()

        for which in range(2):
            first = 4 + 2 * which

            @pl.when((rank == first) | (rank == first + 1))
            def _():
                for m in range(4):
                    to = 4 * (rank - first) + m

                    @pl.when(to != rank)
                    def _():
                        kv_copy(m, which, p, to).start()

            @pl.when(rank == first + 1)
            def _():
                kv_local((first + 1) % 4, which, p).start()

    def line_piece(origin, which, p, side, j, to):
        piece = kv_ref.at[origin, which, token_rows(p)]
        return peer_copy(
            piece,
            piece,
            line_send.at[side, j, which, p],
            line_recv.at[side, j, which, p],
            rank,
            to,
        )

    def origin_of(side, j):
        return plane - j if side == 0 else plane + j

    def next_of(side):
        return plane + 1 if side == 0 else plane - 1

    def line_go(which, p, j):
        if j == 0:
            @pl.when(rank == 5 + 2 * which)
            def _():
                kv_local((5 + 2 * which) % 4, which, p).wait()

            @pl.when(rank != 5 + 2 * which)
            def _():
                kv_copy(0, which, p, 0).wait_recv()

        for side in range(2):
            if j:
                arrives = (plane >= j) if side == 0 else (plane + j <= planes - 1)

                @pl.when(arrives)
                def _():
                    line_piece(origin_of(side, j), which, p, side, j - 1, plane).wait_recv()

            if j < planes - 1:
                @pl.when(line_sends(planes, plane, j, side))
                def _():
                    line_piece(origin_of(side, j), which, p, side, j, next_of(side)).start()

    slots = (((0, 2), (1, 3)), ((0, 3), (1, 2)), ((0, 0), (1, 1)), ((0, 1), (1, 0)))

    def slot_go(slot, j):
        for which, p in slots[slot]:
            line_go(which, p, j)

    gather_wait(xg, *sems, (6,))
    process(0)
    slot_go(0, 0)
    gather_pass(xg, *sems, NEIGHBOURS_FIRST)
    gather_wait(xg, *sems, (7, 8))
    process(2)
    slot_go(0, 1)
    gather_wait(xg, *sems, (9, 10))
    process(4)
    gather_pass(xg, *sems, DIAGONAL)
    slot_go(1, 0)
    slot_go(0, 2)
    gather_wait(xg, *sems, (11, 12))
    process(6)
    sems2 = (ag_send.at[1], ag_recv.at[1])
    slot_go(2, 0)
    slot_go(1, 1)
    slot_go(3, 0)
    gather_start(dy_ref, *sems2, own=dyo_ref)
    slot_go(0, 3)
    slot_go(1, 2)
    slot_go(2, 1)
    slot_go(3, 1)
    slot_go(1, 3)
    slot_go(2, 2)
    gather_pass(dy_ref, *sems2, NEIGHBOURS_FIRST)
    slot_go(3, 2)
    slot_go(2, 3)
    gather_pass(dy_ref, *sems2, DIAGONAL)
    slot_go(3, 3)
    gather_wait(dy_ref, *sems2, FROM_SIBLING)

    for p in range(ranks // 2):
        @pl.when(rank == 0)
        def _():
            q_local(p).wait()

        @pl.when(rank != 0)
        def _():
            q_copy(0, p, 0).wait_recv()

    for copy in small:
        copy.wait_send()
    gather_sent(xg, *sems)
    gather_sent(dy_ref, *sems2)
    own_block.wait()
    for p in range(ranks // 2):
        @pl.when(rank < 4)
        def _():
            for m in range(2):
                @pl.when(2 * rank + m != rank)
                def _():
                    q_copy(m, p, 0).wait_send()

        for which in range(2):
            first = 4 + 2 * which

            @pl.when((rank == first) | (rank == first + 1))
            def _():
                for m in range(4):
                    @pl.when(4 * (rank - first) + m != rank)
                    def _():
                        kv_copy(m, which, p, 0).wait_send()

            for j in range(planes - 1):
                for side in range(2):
                    @pl.when(line_sends(planes, plane, j, side))
                    def _():
                        line_piece(0, which, p, side, j, next_of(side)).wait_send()


def front(lengths, x, small, w_qkv, w_head_gate, grad, collective_id):
    rows, width = x.shape
    ranks, planes = lax.axis_size("fsdp"), lax.axis_size("sp")
    tokens = ranks * rows
    heads = w_head_gate.shape[0]
    vmem = pl.BlockSpec(memory_space=pltpu.VMEM)
    hbm = pl.BlockSpec(memory_space=pl.ANY)
    half, full = jnp.bfloat16, jnp.float32
    pairs = ranks // 2
    return pl.pallas_call(
        functools.partial(front_kernel, planes),
        out_shape=(
            jax.ShapeDtypeStruct((2, tokens, HEAD_DIM), half),
            jax.ShapeDtypeStruct((planes, 2, tokens, HEAD_DIM), half),
            jax.ShapeDtypeStruct((ranks, rows, width), half),
            jax.ShapeDtypeStruct((ranks, rows, width), half),
            jax.ShapeDtypeStruct((ranks, rows, width), half),
            jax.ShapeDtypeStruct((tokens, w_qkv.shape[0]), full),
            jax.ShapeDtypeStruct((heads, tokens, 1), full),
            jax.ShapeDtypeStruct((1, width), full),
            jax.ShapeDtypeStruct((1, width), full),
            jax.ShapeDtypeStruct((1, HEAD_DIM), full),
            jax.ShapeDtypeStruct((tokens, HEAD_DIM), full),
            jax.ShapeDtypeStruct((tokens, HEAD_DIM), full),
        ),
        in_specs=[pl.BlockSpec(memory_space=pltpu.SMEM), vmem, vmem, vmem, vmem, hbm],
        out_specs=(hbm, hbm, hbm) + (vmem,) * 9,
        scratch_shapes=[
            pltpu.VMEM((4, tokens, HEAD_DIM), half),
            pltpu.VMEM((ranks,) + small.shape, small.dtype),
            pltpu.SemaphoreType.DMA((ranks - 1,)),
            pltpu.SemaphoreType.DMA((ranks - 1,)),
            pltpu.SemaphoreType.DMA((2, GATHER_COPIES)),
            pltpu.SemaphoreType.DMA((2, GATHER_COPIES)),
            pltpu.SemaphoreType.DMA,
            pltpu.SemaphoreType.DMA((pairs,)),
            pltpu.SemaphoreType.DMA((2, pairs)),
            pltpu.SemaphoreType.DMA((pairs,)),
            pltpu.SemaphoreType.DMA((4, pairs)),
            pltpu.SemaphoreType.DMA((2, pairs)),
            pltpu.SemaphoreType.DMA((2, planes - 1, 2, pairs)),
            pltpu.SemaphoreType.DMA((2, planes - 1, 2, pairs)),
        ],
        compiler_params=pltpu.CompilerParams(
            collective_id=collective_id, has_side_effects=True, vmem_limit_bytes=VMEM_LIMIT
        ),
        name="front",
    )(lengths, x, small, w_qkv, w_head_gate, grad)


def local_planes(
    hidden_in,
    grad_out,
    lengths,
    attn_gain,
    w_qkv,
    w_head_gate,
    q_gain,
    k_gain,
    w_out,
    ffn_gain,
    w_gate,
    w_up,
    w_down,
):
    ranks, planes = lax.axis_size("fsdp"), lax.axis_size("sp")
    rank, plane = lax.axis_index("fsdp"), lax.axis_index("sp")
    rows, model_width = hidden_in.shape
    tokens = ranks * rows
    own_heads = w_qkv.shape[0] // HEAD_DIM
    local_heads = HEADS // ranks

    thin = q_gain.shape[0]
    spread = jnp.zeros((2, HEAD_DIM), attn_gain.dtype)
    spread = lax.dynamic_update_slice(
        spread, jnp.stack([q_gain, k_gain]), (jnp.int32(0), rank * thin)
    )
    own_gains = jnp.concatenate(
        [
            attn_gain.reshape(-1, HEAD_DIM),
            ffn_gain.reshape(-1, HEAD_DIM),
            spread,
            jnp.zeros((2, HEAD_DIM), attn_gain.dtype),
        ],
        axis=0,
    ).astype(jnp.float32)
    (
        query,
        kv,
        plane_grad,
        gathered,
        normed_a,
        projected,
        gate_logit,
        attn_scale,
        ffn_scale,
        head_scale,
        cosine,
        sine,
    ) = front(lengths, hidden_in, own_gains, w_qkv, w_head_gate, grad_out, 0)
    attended, total, gated = attend(lengths, query, kv, gate_logit, rows)
    plane_b, line_blocks, down_part, middle, grad_middle, grad_ffn_gain_local, plane_mid, grad_gated, acts = middle_layer(
        gated.reshape(ranks, rows, -1),
        w_out,
        hidden_in,
        ffn_scale,
        plane_grad,
        w_gate,
        w_up,
        w_down,
        2,
    )
    grad_gated = grad_gated.reshape(tokens, -1)
    grad_query, grad_kv, gate_grad = attend_back(
        lengths, query, kv, gate_logit, attended, total, grad_gated, rows
    )
    back, first_plane = return_heads(grad_query, grad_kv, line_blocks, 6)
    grad_a_part, pieces, gate_rows, attn_terms, head_terms = projection_back(
        back,
        projected,
        cosine,
        sine,
        normed_a,
        gathered,
        gate_grad,
        gated,
        plane_mid,
        w_qkv,
        w_head_gate,
        head_scale,
    )
    reduced = lax.psum_scatter(pieces, "sp", scatter_dimension=0, tiled=True)
    complete = lax.all_gather(reduced, "sp", axis=0, tiled=True).astype(jnp.float32)
    grad_w_out, grad_w_qkv = complete[: w_out.shape[0]], complete[w_out.shape[0] :]
    grad_in, gain_sums, second_grad = scatter_gains(
        grad_a_part,
        attn_terms,
        grad_ffn_gain_local,
        head_terms,
        hidden_in,
        attn_scale,
        grad_middle,
        line_blocks,
        7,
    )
    grad_w_gate, grad_w_up, grad_w_down, hidden_out, gain_total, grad_w_head_gate = feed_weights(
        plane_b,
        plane_grad,
        acts,
        line_blocks,
        first_plane,
        second_grad,
        down_part,
        middle,
        gain_sums,
        gate_rows,
        w_gate,
        w_up,
        w_down,
        4,
    )
    grad_attn_gain = gain_total[:2].reshape(-1)
    grad_ffn_gain = gain_total[2:4].reshape(-1)
    grad_q_gain = lax.dynamic_slice_in_dim(gain_total[4], rank * thin, thin)
    grad_k_gain = lax.dynamic_slice_in_dim(gain_total[5], rank * thin, thin)
    return (
        hidden_out,
        grad_in,
        grad_attn_gain,
        grad_w_qkv,
        grad_w_head_gate,
        grad_q_gain,
        grad_k_gain,
        grad_w_out,
        grad_ffn_gain,
        grad_w_gate,
        grad_w_up,
        grad_w_down,
    )


def solution(mesh):
    planar = mesh.shape["fsdp"] == 8 and mesh.shape["sp"] == 4
    return jax.shard_map(
        local_planes if planar else local,
        mesh=mesh,
        in_specs=(
            P(("fsdp", "sp"), None),
            P(("fsdp", "sp"), None),
            P(),
            P("fsdp"),
            P("fsdp", None),
            P("fsdp", None),
            P("fsdp"),
            P("fsdp"),
            P("fsdp", None),
            P("fsdp"),
            P("fsdp", None),
            P("fsdp", None),
            P("fsdp", None),
        ),
        out_specs=(
            P(("fsdp", "sp"), None),
            P(("fsdp", "sp"), None),
            P("fsdp"),
            P("fsdp", None),
            P("fsdp", None),
            P("fsdp"),
            P("fsdp"),
            P("fsdp", None),
            P("fsdp"),
            P("fsdp", None),
            P("fsdp", None),
            P("fsdp", None),
        ),
        check_vma=False,
    )
```

```python
import functools
import math

import jax
import jax.numpy as jnp
from jax import lax
from jax.experimental import pallas as pl
from jax.experimental.pallas import tpu as pltpu
from jax.sharding import PartitionSpec as P

HEADS = 16
KV_HEADS = 8
HEAD_DIM = 128


EPS = 1e-06
ROPE_BASE = 1000000.0


def mat_nt(factor, others):
    return lax.dot_general(
        factor, others, (((1,), (1,)), ((), ())), preferred_element_type=jnp.float32
    )


def mat_tn(factor, others):
    return lax.dot_general(
        factor, others, (((0,), (0,)), ((), ())), preferred_element_type=jnp.float32
    )


def inv_rms(values):
    return lax.rsqrt(jnp.mean(values * values, axis=-1, keepdims=True) + EPS)


def norm_back(grad_norm, values, inverse, scaling):
    scaled = grad_norm * scaling
    cubed = inverse * inverse * inverse
    return inverse * scaled - values * cubed * jnp.mean(scaled * values, axis=-1, keepdims=True)


def item_starts(token_index, lengths):
    ends = jnp.cumsum(lengths)
    starts = ends - lengths
    inside = (token_index[:, None] >= starts[None, :]) & (token_index[:, None] < ends[None, :])
    return jnp.sum(jnp.where(inside, starts[None, :], 0), axis=1)


def rope_tables(position):
    half_dim = HEAD_DIM // 2
    freq_steps = jnp.arange(half_dim, dtype=jnp.float32)
    frequency = jnp.exp(-math.log(ROPE_BASE) * 2.0 * freq_steps / HEAD_DIM)
    angles = position.astype(jnp.float32)[:, None] * frequency[None, :]
    return (jnp.cos(angles)[:, None, :], jnp.sin(angles)[:, None, :])


def rotate(values, cosine, sine):
    half_dim = values.shape[-1] // 2
    lower = values[..., :half_dim]
    upper = values[..., half_dim:]
    return jnp.concatenate([lower * cosine - upper * sine, upper * cosine + lower * sine], axis=-1)


def rotate_back(grad_rot, cosine, sine):
    half_dim = grad_rot.shape[-1] // 2
    lower = grad_rot[..., :half_dim]
    upper = grad_rot[..., half_dim:]
    return jnp.concatenate([lower * cosine + upper * sine, upper * cosine - lower * sine], axis=-1)


def local(
    hidden_in,
    grad_out,
    lengths,
    attn_gain,
    w_qkv,
    w_head_gate,
    q_gain,
    k_gain,
    w_out,
    ffn_gain,
    w_gate,
    w_up,
    w_down,
):
    fsdp_count = lax.axis_size("fsdp")
    sp_count = lax.axis_size("sp")
    fsdp_rank = lax.axis_index("fsdp")
    sp_rank = lax.axis_index("sp")
    tok_rows = hidden_in.shape[0]
    model_width = hidden_in.shape[1]
    query_width = HEADS * HEAD_DIM
    kv_width = KV_HEADS * HEAD_DIM
    local_kv = KV_HEADS // sp_count
    head_group = HEADS // KV_HEADS
    score_scale = HEAD_DIM ** (-0.5)
    qkv_full, out_full, gate_full, attn_gain_full, q_gain_full, k_gain_full, ffn_gain_full = (
        lax.all_gather(w_qkv, "fsdp", axis=0, tiled=True),
        lax.all_gather(w_out, "fsdp", axis=0, tiled=True),
        lax.all_gather(w_head_gate, "fsdp", axis=0, tiled=True),
        lax.all_gather(attn_gain, "fsdp", axis=0, tiled=True),
        lax.all_gather(q_gain, "fsdp", axis=0, tiled=True),
        lax.all_gather(k_gain, "fsdp", axis=0, tiled=True),
        lax.all_gather(ffn_gain, "fsdp", axis=0, tiled=True),
    )
    attn_scale = attn_gain_full.astype(jnp.float32)
    query_scale = q_gain_full.astype(jnp.float32)
    key_scale = k_gain_full.astype(jnp.float32)
    ffn_scale = ffn_gain_full.astype(jnp.float32)
    token_first = (fsdp_rank * sp_count + sp_rank) * tok_rows
    own_tokens = token_first + jnp.arange(tok_rows, dtype=jnp.int32)
    cosine, sine = rope_tables(own_tokens - item_starts(own_tokens, lengths))
    inputs = hidden_in.astype(jnp.float32)
    inv_first = inv_rms(inputs)
    normed_a = (inputs * inv_first * attn_scale).astype(jnp.bfloat16)
    projected = mat_nt(normed_a, qkv_full)
    gate_logit = mat_nt(normed_a, gate_full)
    q_raw = projected[:, :query_width].reshape(tok_rows, HEADS, HEAD_DIM)
    k_raw = projected[:, query_width : query_width + kv_width].reshape(tok_rows, KV_HEADS, HEAD_DIM)
    q_inv = inv_rms(q_raw)
    k_inv = inv_rms(k_raw)
    query = (
        rotate(q_raw * q_inv * query_scale, cosine, sine)
        .reshape(tok_rows, query_width)
        .astype(jnp.bfloat16)
    )
    keys = (
        rotate(k_raw * k_inv * key_scale, cosine, sine)
        .reshape(tok_rows, kv_width)
        .astype(jnp.bfloat16)
    )
    values = projected[:, query_width + kv_width :].astype(jnp.bfloat16)
    query_heads, key_heads, value_heads = (
        lax.all_to_all(query, "sp", split_axis=1, concat_axis=0, tiled=True),
        lax.all_to_all(keys, "sp", split_axis=1, concat_axis=0, tiled=True),
        lax.all_to_all(values, "sp", split_axis=1, concat_axis=0, tiled=True),
    )
    key_all, value_all = (
        lax.all_gather(key_heads, "fsdp", axis=0, tiled=True),
        lax.all_gather(value_heads, "fsdp", axis=0, tiled=True),
    )
    span_rows = query_heads.shape[0]
    span_first = fsdp_rank * span_rows
    span_tokens = span_first + jnp.arange(span_rows, dtype=jnp.int32)
    span_starts = item_starts(span_tokens, lengths)
    query_four = query_heads.reshape(span_rows, local_kv, head_group, HEAD_DIM)
    key_total = key_all.shape[0]
    key_block = min(1024, key_total)
    block_count = key_total // key_block
    key_blocks = key_all.reshape(block_count, key_block, local_kv, HEAD_DIM)
    value_blocks = value_all.reshape(block_count, key_block, local_kv, HEAD_DIM)
    block_firsts = jnp.arange(block_count, dtype=jnp.int32) * key_block
    lowest_key = span_starts[0]
    highest_key = span_first + span_rows - 1

    def needed(block_first):
        return (block_first <= highest_key) & (block_first + key_block - 1 >= lowest_key)

    def block_weights(key_piece, block_first):
        scores = (
            jnp.einsum("qkgd,jkd->kgqj", query_four, key_piece, preferred_element_type=jnp.float32)
            * score_scale
        )
        columns = block_first + jnp.arange(key_block, dtype=jnp.int32)
        allowed = (columns[None, :] <= span_tokens[:, None]) & (
            columns[None, :] >= span_starts[:, None]
        )
        return jnp.where(allowed[None, None], jnp.exp(scores), 0.0)

    def forward_step(running, pieces):
        key_piece, value_piece, block_first = pieces

        def forward_compute(current):
            totals, unnormed = current
            weights = block_weights(key_piece, block_first)
            totals = totals + jnp.sum(weights, axis=3)
            unnormed = unnormed + jnp.einsum(
                "kgqj,jkd->qkgd",
                weights.astype(jnp.bfloat16),
                value_piece,
                preferred_element_type=jnp.float32,
            )
            return (totals, unnormed)

        return (
            lax.cond(needed(block_first), forward_compute, lambda current: current, running),
            None,
        )

    start_state = (
        jnp.zeros((local_kv, head_group, span_rows), jnp.float32),
        jnp.zeros((span_rows, local_kv, head_group, HEAD_DIM), jnp.float32),
    )
    scanned = lax.scan(forward_step, start_state, (key_blocks, value_blocks, block_firsts))[0]
    totals, unnormed = scanned
    totals_rows = jnp.transpose(totals, (2, 0, 1))[..., None]
    attended_heads = unnormed / totals_rows
    attended_send = attended_heads.reshape(span_rows, local_kv * head_group * HEAD_DIM).astype(
        jnp.bfloat16
    )
    returned = lax.all_to_all(attended_send, "sp", split_axis=0, concat_axis=1, tiled=True)
    gate_prob = jax.nn.sigmoid(gate_logit)
    attended_tok = returned.astype(jnp.float32).reshape(tok_rows, HEADS, HEAD_DIM)
    gated = (
        (attended_tok * gate_prob[:, :, None]).reshape(tok_rows, query_width).astype(jnp.bfloat16)
    )
    middle = inputs + jnp.dot(gated, out_full, preferred_element_type=jnp.float32)
    inv_second = inv_rms(middle)
    normed_b = (middle * inv_second * ffn_scale).astype(jnp.bfloat16)
    gate_piece = lax.all_gather(w_gate, "fsdp", axis=0, tiled=True)
    up_piece = lax.all_gather(w_up, "fsdp", axis=0, tiled=True)
    down_piece = lax.all_gather(w_down, "fsdp", axis=0, tiled=True)
    gate_pre = mat_nt(normed_b, gate_piece)
    up_pre = mat_nt(normed_b, up_piece)
    hidden = (jax.nn.silu(gate_pre) * up_pre).astype(jnp.bfloat16)
    ffn_part = jnp.dot(hidden, down_piece, preferred_element_type=jnp.float32)
    hidden_out = (middle + ffn_part).astype(jnp.bfloat16)
    gate_piece = lax.all_gather(w_gate, "fsdp", axis=0, tiled=True)
    up_piece = lax.all_gather(w_up, "fsdp", axis=0, tiled=True)
    down_piece = lax.all_gather(w_down, "fsdp", axis=0, tiled=True)
    gate_pre = mat_nt(normed_b, gate_piece)
    up_pre = mat_nt(normed_b, up_piece)
    sigma = jax.nn.sigmoid(gate_pre)
    swish = gate_pre * sigma
    hidden = (swish * up_pre).astype(jnp.bfloat16)
    grad_hidden = mat_nt(grad_out, down_piece)
    grad_gate = (grad_hidden * up_pre * sigma * (1.0 + gate_pre * (1.0 - sigma))).astype(
        jnp.bfloat16
    )
    grad_up = (grad_hidden * swish).astype(jnp.bfloat16)
    grad_acc = jnp.dot(grad_gate, gate_piece, preferred_element_type=jnp.float32) + jnp.dot(
        grad_up, up_piece, preferred_element_type=jnp.float32
    )
    grad_ffn_gain_local = jnp.sum(grad_acc * middle * inv_second, axis=0)
    grad_middle = grad_out.astype(jnp.float32) + norm_back(grad_acc, middle, inv_second, ffn_scale)
    grad_mid_b = grad_middle.astype(jnp.bfloat16)
    grad_gated = mat_nt(grad_mid_b, out_full).reshape(tok_rows, HEADS, HEAD_DIM)
    grad_attended = (
        (grad_gated * gate_prob[:, :, None]).reshape(tok_rows, query_width).astype(jnp.bfloat16)
    )
    gate_grad = (jnp.sum(grad_gated * attended_tok, axis=2) * gate_prob * (1.0 - gate_prob)).astype(
        jnp.bfloat16
    )
    grad_heads = lax.all_to_all(grad_attended, "sp", split_axis=1, concat_axis=0, tiled=True)
    grad_four = grad_heads.astype(jnp.float32).reshape(span_rows, local_kv, head_group, HEAD_DIM)
    grad_scaled = (grad_four / totals_rows).astype(jnp.bfloat16)
    delta_rows = jnp.sum(grad_four * attended_heads, axis=3) / totals_rows[..., 0]
    delta_heads = jnp.transpose(delta_rows, (1, 2, 0))

    def backward_step(grad_query, pieces):
        key_piece, value_piece, block_first = pieces

        def backward_compute(current):
            weights = block_weights(key_piece, block_first)
            grad_prob = jnp.einsum(
                "qkgd,jkd->kgqj", grad_scaled, value_piece, preferred_element_type=jnp.float32
            )
            grad_score = (weights * (grad_prob - delta_heads[..., None])).astype(jnp.bfloat16)
            current = (
                current
                + jnp.einsum(
                    "kgqj,jkd->qkgd", grad_score, key_piece, preferred_element_type=jnp.float32
                )
                * score_scale
            )
            grad_key = (
                jnp.einsum(
                    "kgqj,qkgd->jkd", grad_score, query_four, preferred_element_type=jnp.float32
                )
                * score_scale
            )
            grad_value = jnp.einsum(
                "kgqj,qkgd->jkd",
                weights.astype(jnp.bfloat16),
                grad_scaled,
                preferred_element_type=jnp.float32,
            )
            return (current, (grad_key, grad_value))

        def skip(current):
            nothing = jnp.zeros((key_block, local_kv, HEAD_DIM), jnp.float32)
            return (current, (nothing, nothing))

        return lax.cond(needed(block_first), backward_compute, skip, grad_query)

    grad_query, key_value_grads = lax.scan(
        backward_step,
        jnp.zeros((span_rows, local_kv, head_group, HEAD_DIM), jnp.float32),
        (key_blocks, value_blocks, block_firsts),
    )
    key_grads, value_grads = key_value_grads
    key_sum, value_sum = (
        lax.psum_scatter(
            key_grads.reshape(key_total, local_kv * HEAD_DIM),
            "fsdp",
            scatter_dimension=0,
            tiled=True,
        ),
        lax.psum_scatter(
            value_grads.reshape(key_total, local_kv * HEAD_DIM),
            "fsdp",
            scatter_dimension=0,
            tiled=True,
        ),
    )
    query_send = grad_query.reshape(span_rows, local_kv * head_group * HEAD_DIM).astype(
        jnp.bfloat16
    )
    back_query, back_key, back_value = (
        lax.all_to_all(query_send, "sp", split_axis=0, concat_axis=1, tiled=True),
        lax.all_to_all(key_sum.astype(jnp.bfloat16), "sp", split_axis=0, concat_axis=1, tiled=True),
        lax.all_to_all(
            value_sum.astype(jnp.bfloat16), "sp", split_axis=0, concat_axis=1, tiled=True
        ),
    )
    grad_qn = rotate_back(
        back_query.astype(jnp.float32).reshape(tok_rows, HEADS, HEAD_DIM), cosine, sine
    )
    grad_kn = rotate_back(
        back_key.astype(jnp.float32).reshape(tok_rows, KV_HEADS, HEAD_DIM), cosine, sine
    )
    grad_q_gain_local = jnp.sum(grad_qn * q_raw * q_inv, axis=(0, 1))
    grad_k_gain_local = jnp.sum(grad_kn * k_raw * k_inv, axis=(0, 1))
    grad_q_raw = norm_back(grad_qn, q_raw, q_inv, query_scale).reshape(tok_rows, query_width)
    grad_k_raw = norm_back(grad_kn, k_raw, k_inv, key_scale).reshape(tok_rows, kv_width)
    grad_proj = jnp.concatenate(
        [grad_q_raw.astype(jnp.bfloat16), grad_k_raw.astype(jnp.bfloat16), back_value], axis=1
    )
    grad_normed_a = jnp.dot(grad_proj, qkv_full, preferred_element_type=jnp.float32) + jnp.dot(
        gate_grad, gate_full, preferred_element_type=jnp.float32
    )
    grad_attn_gain_local = jnp.sum(grad_normed_a * inputs * inv_first, axis=0)
    grad_in = grad_middle + norm_back(grad_normed_a, inputs, inv_first, attn_scale)
    qkv_rows = w_qkv.shape[0]
    out_rows = w_out.shape[0]
    gate_rows = w_head_gate.shape[0]
    block_rows = qkv_rows + out_rows + gate_rows + 3
    small_rows = jnp.stack(
        [
            grad_attn_gain_local,
            grad_ffn_gain_local,
            jnp.concatenate(
                [
                    grad_q_gain_local,
                    grad_k_gain_local,
                    jnp.zeros((model_width - 2 * HEAD_DIM,), jnp.float32),
                ]
            ),
        ],
        axis=0,
    )
    ffn_partial = lax.psum_scatter(
        jnp.concatenate(
            [mat_tn(grad_gate, normed_b), mat_tn(grad_up, normed_b), mat_tn(hidden, grad_out)],
            axis=1,
        ).astype(jnp.bfloat16),
        "fsdp",
        scatter_dimension=0,
        tiled=True,
    ).astype(jnp.float32)
    proj_split = grad_proj.reshape(tok_rows, fsdp_count, qkv_rows)
    gated_split = gated.reshape(tok_rows, fsdp_count, out_rows)
    gate_split = gate_grad.reshape(tok_rows, fsdp_count, gate_rows)
    owners = block_rows * lax.axis_size("fsdp") // block_rows
    qkv_term = jnp.einsum("tor,td->ord", proj_split, normed_a, preferred_element_type=jnp.float32)
    out_term = jnp.einsum(
        "tor,td->ord", gated_split, grad_mid_b, preferred_element_type=jnp.float32
    )
    gate_term = jnp.einsum("tor,td->ord", gate_split, normed_a, preferred_element_type=jnp.float32)
    small_term = jnp.broadcast_to(small_rows[None], (owners, 3, model_width))
    joined = jnp.concatenate([qkv_term, out_term, gate_term, small_term], axis=1)
    attn_partial = lax.psum_scatter(
        joined.reshape(owners * block_rows, model_width), "fsdp", scatter_dimension=0, tiled=True
    )
    ffn_total, attn_total = lax.psum((ffn_partial, attn_partial), "sp")
    grad_w_gate = ffn_total[:, :model_width]
    grad_w_up = ffn_total[:, model_width : 2 * model_width]
    grad_w_down = ffn_total[:, 2 * model_width :]
    grad_w_qkv = attn_total[:qkv_rows]
    grad_w_out = attn_total[qkv_rows : qkv_rows + out_rows]
    grad_w_head_gate = attn_total[qkv_rows + out_rows : qkv_rows + out_rows + gate_rows]
    gain_sums = attn_total[qkv_rows + out_rows + gate_rows :]
    gain_part = model_width // fsdp_count
    head_part = HEAD_DIM // fsdp_count
    grad_attn_gain = lax.dynamic_slice_in_dim(gain_sums[0], fsdp_rank * gain_part, gain_part)
    grad_ffn_gain = lax.dynamic_slice_in_dim(gain_sums[1], fsdp_rank * gain_part, gain_part)
    grad_q_gain = lax.dynamic_slice_in_dim(gain_sums[2], fsdp_rank * head_part, head_part)
    grad_k_gain = lax.dynamic_slice_in_dim(
        gain_sums[2], HEAD_DIM + fsdp_rank * head_part, head_part
    )
    return (
        hidden_out,
        grad_in,
        grad_attn_gain,
        grad_w_qkv,
        grad_w_head_gate,
        grad_q_gain,
        grad_k_gain,
        grad_w_out,
        grad_ffn_gain,
        grad_w_gate,
        grad_w_up,
        grad_w_down,
    )


MESH = pl.DeviceIdType.MESH
VMEM_LIMIT = 62 * 1024 * 1024


def peer_copy(src, dst, send_sem, recv_sem, rank, plane):
    return pltpu.make_async_remote_copy(
        src_ref=src,
        dst_ref=dst,
        send_sem=send_sem,
        recv_sem=recv_sem,
        device_id=(rank, plane),
        device_id_type=MESH,
    )


def greet(peers):
    barrier = pltpu.get_barrier_semaphore()
    for peer in peers:
        pl.semaphore_signal(barrier, inc=1, device_id=peer, device_id_type=MESH)
    pl.semaphore_wait(barrier, len(peers))


def scatter_gains_kernel(
    p_ref, attn_ref, ffn_ref, head_ref, x_ref, scale_ref, dmid_ref, o_ref, so_ref, parts, small_buf, grad, small_send, small_recv, *rest
):
    rank, plane = lax.axis_index("fsdp"), lax.axis_index("sp")
    ranks = p_ref.shape[0]
    greet([(rank ^ k, plane) for k in range(1, 8)])
    for i in range(4):
        scatter_near(p_ref, i, rest[0], rest[3], rest[4]).start()
    for r in range(ranks):
        for i in range(2):
            columns = slice((2 * r + i) * HEAD_DIM, (2 * r + i + 1) * HEAD_DIM)
            parts[r, i : i + 1] = attn_ref[:, columns]
            parts[r, 2 + i : 3 + i] = ffn_ref[:, columns]
        parts[r, 4:5] = jnp.where(rank < ranks // 2, head_ref[...], 0.0)
        parts[r, 5:6] = jnp.where(
            (rank >= ranks // 2) & (rank < 3 * ranks // 4), head_ref[...], 0.0
        )
        parts[r, 6:8] = jnp.zeros((2, HEAD_DIM), jnp.float32)
    small = []
    for k in range(1, 8):
        copy = peer_copy(
            parts.at[rank ^ k],
            small_buf.at[k - 1],
            small_send.at[k - 1],
            small_recv.at[k - 1],
            rank ^ k,
            plane,
        )
        copy.start()
        small.append(copy)
    scatter_begin(p_ref, grad, *rest, started=True)
    total = parts[rank]
    for k in range(1, 8):
        small[k - 1].wait()
        total = total + small_buf[k - 1]
    so_ref[...] = total
    scatter_end(p_ref, grad, *rest)
    inputs = x_ref[...].astype(jnp.float32)
    o_ref[...] = dmid_ref[...] + norm_back(grad[...], inputs, inv_rms(inputs), scale_ref[...])


SCATTER_ORDER = (6, 2, 4, 0)


def scatter_far(i, out_buf, far_buf, send_sem, recv_sem):
    rank, plane = lax.axis_index("fsdp"), lax.axis_index("sp")
    return peer_copy(
        out_buf.at[i],
        far_buf.at[i],
        send_sem.at[i],
        recv_sem.at[i],
        rank ^ SCATTER_ORDER[i],
        plane,
    )


def scatter_near(p_ref, i, near_buf, sib_send, sib_recv):
    rank, plane = lax.axis_index("fsdp"), lax.axis_index("sp")
    return peer_copy(
        p_ref.at[rank ^ 1 ^ SCATTER_ORDER[i]],
        near_buf.at[i],
        sib_send.at[i],
        sib_recv.at[i],
        rank ^ 1,
        plane,
    )


def scatter_begin(p_ref, o_ref, near_buf, out_buf, far_buf, sib_send, sib_recv, send_sem, recv_sem, started=False):
    rank = lax.axis_index("fsdp")
    for i in range(0 if started else 4):
        scatter_near(p_ref, i, near_buf, sib_send, sib_recv).start()
    for i, k in enumerate(SCATTER_ORDER):
        scatter_near(p_ref, i, near_buf, sib_send, sib_recv).wait_recv()
        joined = p_ref[rank ^ k].astype(jnp.float32) + near_buf[i].astype(jnp.float32)
        if k:
            out_buf[i] = joined.astype(out_buf.dtype)
            scatter_far(i, out_buf, far_buf, send_sem, recv_sem).start()
        else:
            o_ref[...] = joined


def scatter_end(p_ref, o_ref, near_buf, out_buf, far_buf, sib_send, sib_recv, send_sem, recv_sem):
    for i in (1, 2, 0):
        scatter_far(i, out_buf, far_buf, send_sem, recv_sem).wait_recv()
        o_ref[...] += far_buf[i].astype(jnp.float32)
    for i in range(4):
        scatter_near(p_ref, i, near_buf, sib_send, sib_recv).wait_send()
    for i in range(3):
        scatter_far(i, out_buf, far_buf, send_sem, recv_sem).wait_send()


def scatter_scratch(rows, width, dtype):
    return [
        pltpu.VMEM((4, rows, width), dtype),
        pltpu.VMEM((3, rows, width), dtype),
        pltpu.VMEM((3, rows, width), dtype),
        pltpu.SemaphoreType.DMA((4,)),
        pltpu.SemaphoreType.DMA((4,)),
        pltpu.SemaphoreType.DMA((3,)),
        pltpu.SemaphoreType.DMA((3,)),
    ]


def scatter_gains(p, attn, ffn, head, x, scale, grad_middle, collective_id):
    ranks, rows, width = p.shape
    vmem = pl.BlockSpec(memory_space=pltpu.VMEM)
    small = (8, HEAD_DIM)
    return pl.pallas_call(
        scatter_gains_kernel,
        out_shape=(
            jax.ShapeDtypeStruct((rows, width), jnp.float32),
            jax.ShapeDtypeStruct(small, jnp.float32),
        ),
        in_specs=[vmem] * 7,
        out_specs=(vmem, vmem),
        scratch_shapes=[
            pltpu.VMEM((ranks,) + small, jnp.float32),
            pltpu.VMEM((7,) + small, jnp.float32),
            pltpu.VMEM((rows, width), jnp.float32),
            pltpu.SemaphoreType.DMA((7,)),
            pltpu.SemaphoreType.DMA((7,)),
        ]
        + scatter_scratch(rows, width, p.dtype),
        compiler_params=pltpu.CompilerParams(
            collective_id=collective_id, has_side_effects=True, vmem_limit_bytes=VMEM_LIMIT
        ),
        name="scatter_gains",
    )(p, attn, ffn, head, x, scale, grad_middle)


def projection_back_kernel(
    back_ref, raw_ref, cos_ref, sin_ref, xa_ref, x_ref, dgate_ref, w_ref, wg_ref, head_ref, blocks_ref, dxa_ref, qkv_ref, gate_ref, attn_ref, terms_ref, next_ref, sums, ag_send, ag_recv, own_sem
):
    rank, plane = lax.axis_index("fsdp"), lax.axis_index("sp")
    block = blocks_ref.at[1, 1]
    gather = (next_ref, ag_send, ag_recv)
    own = pltpu.make_async_copy(block, next_ref.at[rank], own_sem)
    group, rows, width = back_ref.shape

    @pl.when(pl.program_id(0) == 0)
    def _():
        greet([(rank ^ k, plane) for k in (1, 2, 4)])
        own.start()
        gather_start(*gather, own=block)
        for ref in (sums, gate_ref, attn_ref, terms_ref):
            ref[...] = jnp.zeros_like(ref)

    @pl.when(pl.program_id(0) == 2)
    def _():
        gather_pass(*gather, NEIGHBOURS_FIRST[:2])

    @pl.when(pl.program_id(0) == 3)
    def _():
        gather_pass(*gather, NEIGHBOURS_FIRST[2:])

    cosine, sine = cos_ref[...], sin_ref[...]
    columns = []
    for m in range(group):
        back = back_ref[m]
        grad = back.astype(jnp.float32)
        turned = grad * cosine - pltpu.roll(grad, width // 2, 1) * sine
        raw = raw_ref[:, m * width : (m + 1) * width]
        inverse = inv_rms(raw)
        terms_ref[...] += jnp.sum(turned * raw * inverse, axis=0, keepdims=True)
        grad_raw = norm_back(turned, raw, inverse, head_ref[...])
        columns.append(jnp.where(rank >= 6, grad, grad_raw).astype(jnp.bfloat16))
    grad_proj = jnp.concatenate(columns, axis=1)
    grad_a = jnp.dot(grad_proj, w_ref[...], preferred_element_type=jnp.float32)
    normed = xa_ref[...].reshape(rows, -1)
    normed32 = normed.astype(jnp.float32)
    for head in range(dgate_ref.shape[0]):
        gate = dgate_ref[head].astype(jnp.float32)
        grad_a = grad_a + gate * wg_ref[head : head + 1].astype(jnp.float32)
        gate_ref[head : head + 1] += jnp.sum(gate * normed32, axis=0, keepdims=True)
    inputs = x_ref[...].reshape(rows, -1).astype(jnp.float32)
    attn_ref[...] += jnp.sum(grad_a * inputs * inv_rms(inputs), axis=0, keepdims=True)
    dxa_ref[...] = grad_a.astype(jnp.bfloat16).reshape(dxa_ref.shape)
    sums[...] += mat_tn(grad_proj, normed)

    @pl.when(pl.program_id(0) == pl.num_programs(0) - 1)
    def _():
        qkv_ref[...] = sums[...].astype(jnp.bfloat16)
        gather_pass(*gather, DIAGONAL)
        gather_wait(*gather, FROM_SIBLING)
        gather_sent(*gather)
        own.wait()


def projection_back(back, raw, cosine, sine, normed, inputs, gate_grad, w_qkv, w_head_gate, head_scale, line_blocks, collective_id):
    ranks, rows, model_width = normed.shape
    group, tokens, width = back.shape
    pair = 2 * rows
    blocks = pl.BlockSpec((2, rows, model_width), lambda i: (i, 0, 0))
    thin = pl.BlockSpec((pair, width), lambda i: (i, 0))
    hbm = pl.BlockSpec(memory_space=pl.ANY)
    heads = gate_grad.shape[0]

    def still(shape):
        return pl.BlockSpec(shape, lambda i: (0, 0))

    return pl.pallas_call(
        projection_back_kernel,
        grid=(tokens // pair,),
        in_specs=[
            pl.BlockSpec((group, pair, width), lambda i: (0, i, 0)),
            pl.BlockSpec((pair, group * width), lambda i: (i, 0)),
            thin,
            thin,
            blocks,
            blocks,
            pl.BlockSpec((heads, pair, 1), lambda i: (0, i, 0)),
            still(w_qkv.shape),
            still(w_head_gate.shape),
            still(head_scale.shape),
            hbm,
        ],
        out_specs=(
            blocks,
            still(w_qkv.shape),
            still(w_head_gate.shape),
            still((1, model_width)),
            still((1, width)),
            hbm,
        ),
        out_shape=(
            jax.ShapeDtypeStruct(normed.shape, jnp.bfloat16),
            jax.ShapeDtypeStruct(w_qkv.shape, jnp.bfloat16),
            jax.ShapeDtypeStruct(w_head_gate.shape, jnp.float32),
            jax.ShapeDtypeStruct((1, model_width), jnp.float32),
            jax.ShapeDtypeStruct((1, width), jnp.float32),
            jax.ShapeDtypeStruct(normed.shape, line_blocks.dtype),
        ),
        scratch_shapes=[
            pltpu.VMEM(w_qkv.shape, jnp.float32),
            pltpu.SemaphoreType.DMA((GATHER_COPIES,)),
            pltpu.SemaphoreType.DMA((GATHER_COPIES,)),
            pltpu.SemaphoreType.DMA,
        ],
        compiler_params=pltpu.CompilerParams(
            collective_id=collective_id, has_side_effects=True, vmem_limit_bytes=VMEM_LIMIT
        ),
        name="projection_back",
    )(back, raw, cosine, sine, normed, inputs, gate_grad, w_qkv, w_head_gate, head_scale, line_blocks)


GATHER_COPIES = 13


def gather_copy(buf, i, send_sem, recv_sem, own=None):
    rank, plane = lax.axis_index("fsdp"), lax.axis_index("sp")
    rows = buf.shape[1]
    top, low = pl.ds(0, rows // 2), pl.ds(rows // 2, rows // 2)
    block, part, to = (
        (0, top, 2),
        (0, low, 2),
        (0, low, 4),
        (0, top, 4),
        (2, top, 4),
        (4, low, 2),
        (0, pl.ds(0, rows), 1),
        (2, top, 1),
        (2, low, 1),
        (4, low, 1),
        (4, top, 1),
        (6, top, 1),
        (6, low, 1),
    )[i]
    piece = buf.at[rank ^ block, part]
    source = piece if own is None or block else own.at[part]
    return peer_copy(source, piece, send_sem.at[i], recv_sem.at[i], rank ^ to, plane)


def gather_start(buf, send_sem, recv_sem, own=None):
    for i in (6, 0, 2, 1, 3):
        gather_copy(buf, i, send_sem, recv_sem, own).start()


def gather_pass(buf, send_sem, recv_sem, pairs):
    for arrived, onward in pairs:
        gather_copy(buf, arrived, send_sem, recv_sem).wait_recv()
        for i in onward:
            gather_copy(buf, i, send_sem, recv_sem).start()


def gather_wait(buf, send_sem, recv_sem, copies):
    for i in copies:
        gather_copy(buf, i, send_sem, recv_sem).wait_recv()


def gather_sent(buf, send_sem, recv_sem):
    for i in range(GATHER_COPIES):
        gather_copy(buf, i, send_sem, recv_sem).wait_send()


NEIGHBOURS_FIRST = ((0, (4, 7)), (2, (5, 9)), (1, (8,)), (3, (10,)))
DIAGONAL = ((4, (11,)), (5, (12,)))
FROM_SIBLING = (6, 7, 8, 9, 10, 11, 12)


def greet_line(ranks, planes):
    rank, plane = lax.axis_index("fsdp"), lax.axis_index("sp")
    barrier = pltpu.get_barrier_semaphore()
    for k in range(1, ranks):
        pl.semaphore_signal(
            barrier, inc=1, device_id=(rank ^ k, plane), device_id_type=MESH
        )

    @pl.when(plane > 0)
    def _():
        pl.semaphore_signal(barrier, inc=1, device_id=(rank, plane - 1), device_id_type=MESH)

    @pl.when(plane < planes - 1)
    def _():
        pl.semaphore_signal(barrier, inc=1, device_id=(rank, plane + 1), device_id_type=MESH)

    lower = (plane > 0).astype(jnp.int32)
    upper = (plane < planes - 1).astype(jnp.int32)
    pl.semaphore_wait(barrier, ranks - 1 + lower + upper)


def line_sends(planes, plane, j, side):
    if side == 0:
        return (plane >= j) & (plane < planes - 1)
    return (plane + j <= planes - 1) & (plane > 0)


def unheads_kernel(planes, dq_ref, dkv_ref, blocks_ref, n_ref, next_ref, ag_send, ag_recv, own_sem2, line_out, line_in, done, own_sem, q_send, q_recv, kv_send, kv_recv, line_send, line_recv):
    rank, plane = lax.axis_index("fsdp"), lax.axis_index("sp")
    greet_line(8, planes)
    gathers = [(next_ref.at[which], ag_send.at[which], ag_recv.at[which]) for which in range(2)]
    own_blocks = [
        pltpu.make_async_copy(blocks_ref.at[which, 0], next_ref.at[which, rank], own_sem2.at[which])
        for which in range(2)
    ]
    for copy in own_blocks:
        copy.start()

    def q_copy(m, to):
        return peer_copy(dq_ref, n_ref.at[pl.ds(2 * m, 2)], q_send, q_recv.at[m], to, plane)

    def kv_copy(m, which, to):
        return peer_copy(done.at[which], n_ref.at[m], kv_send.at[which], kv_recv.at[m], to, plane)

    def q_local():
        return pltpu.make_async_copy(dq_ref, n_ref.at[pl.ds(0, 2)], own_sem)

    def kv_local(m, which):
        return pltpu.make_async_copy(done.at[which], n_ref.at[m], own_sem)

    @pl.when(rank == 0)
    def _():
        q_local().start()

    for m in range(2):
        @pl.when((rank % 2 == m) & (rank != 0))
        def _():
            q_copy(m, rank // 2).start()

    def step_copy(j, which, side):
        to = plane + 1 if side == 0 else plane - 1
        return peer_copy(
            line_out.at[side, j, which],
            line_in.at[side, j, which],
            line_send.at[side, j, which],
            line_recv.at[side, j, which],
            rank,
            to,
        )

    def sends(j, side):
        return plane < planes - 1 - j if side == 0 else plane > j

    def target(j, side):
        return planes - 1 - j if side == 0 else j

    for which in range(2):
        gather_start(*gathers[which], own=blocks_ref.at[which, 0])

    for j in range(planes - 1):
        for which in range(2):
            for side in range(2):
                inner = plane > 0 if side == 0 else plane < planes - 1

                @pl.when(sends(j, side) & inner)
                def _():
                    step_copy(j, which, side).wait_recv()
                    total = dkv_ref[target(j, side), which].astype(jnp.float32) + line_in[
                        side, j, which
                    ].astype(jnp.float32)
                    line_out[side, j, which] = total.astype(line_out.dtype)

                @pl.when(sends(j, side) & jnp.logical_not(inner))
                def _():
                    line_out[side, j, which] = dkv_ref[target(j, side), which]

                @pl.when(sends(j, side))
                def _():
                    step_copy(j, which, side).start()

        if j == 1:
            gather_pass(*gathers[0], NEIGHBOURS_FIRST)
        if j == 2:
            gather_pass(*gathers[1], NEIGHBOURS_FIRST)
            gather_pass(*gathers[0], DIAGONAL)

    for which in range(2):
        total = dkv_ref[plane, which].astype(jnp.float32)
        done32 = total
        for j in range(planes - 1):
            for side in range(2):
                @pl.when(plane == target(j, side))
                def _():
                    step_copy(j, which, side).wait_recv()
        low = jnp.minimum(planes - 1 - plane, planes - 2)
        high = jnp.minimum(plane, planes - 2)
        below = line_in[0, low, which].astype(jnp.float32)
        above = line_in[1, high, which].astype(jnp.float32)
        done32 = done32 + jnp.where(plane > 0, below, 0.0) + jnp.where(plane < planes - 1, above, 0.0)
        done[which] = done32.astype(done.dtype)
        first = 4 + 2 * which
        to = first + rank // 4
        for m in range(4):
            @pl.when((rank % 4 == m) & (to != rank))
            def _():
                kv_copy(m, which, to).start()

            @pl.when((rank % 4 == m) & (to == rank))
            def _():
                kv_local(m, which).start()

    gather_pass(*gathers[1], DIAGONAL)
    for gather in gathers:
        gather_wait(*gather, FROM_SIBLING)
        gather_sent(*gather)
    for copy in own_blocks:
        copy.wait()

    @pl.when(rank < 4)
    def _():
        for m in range(2):
            @pl.when(2 * rank + m != rank)
            def _():
                q_copy(m, 0).wait_recv()

            @pl.when(2 * rank + m == rank)
            def _():
                q_local().wait()

    for which in range(2):
        first = 4 + 2 * which

        @pl.when((rank == first) | (rank == first + 1))
        def _():
            for m in range(4):
                @pl.when(4 * (rank - first) + m != rank)
                def _():
                    kv_copy(m, which, 0).wait_recv()

                @pl.when(4 * (rank - first) + m == rank)
                def _():
                    kv_local(m, which).wait()

    @pl.when(rank != 0)
    def _():
        q_copy(0, 0).wait_send()

    for which in range(2):
        @pl.when(4 + 2 * which + rank // 4 != rank)
        def _():
            kv_copy(0, which, 0).wait_send()

    for j in range(planes - 1):
        for which in range(2):
            for side in range(2):
                @pl.when(sends(j, side))
                def _():
                    step_copy(j, which, side).wait_send()


def return_heads(grad_query, grad_kv, line_blocks, collective_id):
    _, tokens, width = grad_query.shape
    planes = lax.axis_size("sp")
    ranks = lax.axis_size("fsdp")
    vmem = pl.BlockSpec(memory_space=pltpu.VMEM)
    hbm = pl.BlockSpec(memory_space=pl.ANY)
    return pl.pallas_call(
        functools.partial(unheads_kernel, planes),
        out_shape=(
            jax.ShapeDtypeStruct((4, tokens, width), grad_query.dtype),
            jax.ShapeDtypeStruct((2, ranks) + line_blocks.shape[2:], line_blocks.dtype),
        ),
        in_specs=[vmem, vmem, hbm],
        out_specs=(vmem, hbm),
        scratch_shapes=[
            pltpu.SemaphoreType.DMA((2, GATHER_COPIES)),
            pltpu.SemaphoreType.DMA((2, GATHER_COPIES)),
            pltpu.SemaphoreType.DMA((2,)),
            pltpu.VMEM((2, planes - 1, 2, tokens, width), grad_query.dtype),
            pltpu.VMEM((2, planes - 1, 2, tokens, width), grad_query.dtype),
            pltpu.VMEM((2, tokens, width), grad_query.dtype),
            pltpu.SemaphoreType.DMA,
            pltpu.SemaphoreType.DMA,
            pltpu.SemaphoreType.DMA((2,)),
            pltpu.SemaphoreType.DMA((2,)),
            pltpu.SemaphoreType.DMA((4,)),
            pltpu.SemaphoreType.DMA((2, planes - 1, 2)),
            pltpu.SemaphoreType.DMA((2, planes - 1, 2)),
        ],
        compiler_params=pltpu.CompilerParams(
            collective_id=collective_id, has_side_effects=True, vmem_limit_bytes=VMEM_LIMIT
        ),
        name="return_heads",
    )(grad_query, grad_kv, line_blocks)


def stack_heads(ref):
    return ref[...].reshape(ref.shape[0] * ref.shape[1], ref.shape[2])


def block_bounds(lengths_ref, ranks, planes, rows):
    block = pl.program_id(0)
    span = planes * rows
    first = block * span + lax.axis_index("sp") * rows
    start, end = jnp.int32(0), jnp.int32(0)
    for item in range(lengths_ref.shape[0]):
        end = end + lengths_ref[item]
        start = jnp.where(first >= end, end, start)
    return start // span, block, first


def row_starts(lengths_ref, tokens):
    start, end = jnp.zeros_like(tokens), jnp.int32(0)
    for item in range(lengths_ref.shape[0]):
        end = end + lengths_ref[item]
        start = jnp.where(tokens >= end, end, start)
    return start


def chunk_weights(query, key, scale, tokens, starts, first_key):
    scores = mat_nt(query, key) * scale
    columns = first_key + lax.broadcasted_iota(jnp.int32, scores.shape, 1)
    allowed = (columns <= tokens) & (columns >= starts)
    return jnp.where(allowed, jnp.exp(scores), 0.0)


def query_tokens(first, rows, group):
    row = lax.broadcasted_iota(jnp.int32, (group * rows, 1), 0)
    return first + lax.rem(row, rows)


def attend_kernel(ranks, planes, lengths_ref, q_ref, kv_ref, gate_ref, att_ref, total_ref, gated_ref):
    group, rows, width = q_ref.shape
    scale = HEAD_DIM ** (-0.5)
    low, high, first = block_bounds(lengths_ref, ranks, planes, rows)
    tokens = query_tokens(first, rows, group)
    starts = row_starts(lengths_ref, tokens)
    query = stack_heads(q_ref)
    span = planes * rows

    def step(chunk, running):
        total, unnorm = running
        key = kv_ref[:, 0, chunk].reshape(span, width)
        value = kv_ref[:, 1, chunk].reshape(span, width)
        weights = chunk_weights(query, key, scale, tokens, starts, chunk * span)
        total = total + jnp.sum(weights, axis=1, keepdims=True)
        unnorm = unnorm + jnp.dot(
            weights.astype(jnp.bfloat16), value, preferred_element_type=jnp.float32
        )
        return total, unnorm

    total, unnorm = lax.fori_loop(
        low,
        high + 1,
        step,
        (
            jnp.zeros((group * rows, 1), jnp.float32),
            jnp.zeros((group * rows, width), jnp.float32),
        ),
    )
    attended = unnorm / total
    att_ref[...] = attended.reshape(group, rows, width)
    total_ref[...] = total.reshape(group, rows, 1)
    sent = attended.astype(jnp.bfloat16).astype(jnp.float32)
    for head in range(group):
        gated = sent[head * rows : (head + 1) * rows] * jax.nn.sigmoid(gate_ref[head])
        gated_ref[:, head * width : (head + 1) * width] = gated.astype(jnp.bfloat16)


def attend(lengths, query, kv, gate_logit, rows):
    group, tokens, width = query.shape
    planes = kv.shape[0]
    ranks = tokens // rows
    kv_blocks = kv.reshape(planes, 2, ranks, rows, width)
    block = pl.BlockSpec((group, rows, width), lambda i, *_: (0, i, 0))
    thin = pl.BlockSpec((group, rows, 1), lambda i, *_: (0, i, 0))
    return pl.pallas_call(
        functools.partial(attend_kernel, ranks, planes),
        grid_spec=pltpu.PrefetchScalarGridSpec(
            num_scalar_prefetch=1,
            grid=(ranks,),
            in_specs=[
                block,
                pl.BlockSpec((planes, 2, ranks, rows, width), lambda i, *_: (0, 0, 0, 0, 0)),
                thin,
            ],
            out_specs=(
                block,
                thin,
                pl.BlockSpec((rows, group * width), lambda i, *_: (i, 0)),
            ),
        ),
        out_shape=(
            jax.ShapeDtypeStruct((group, tokens, width), jnp.float32),
            jax.ShapeDtypeStruct((group, tokens, 1), jnp.float32),
            jax.ShapeDtypeStruct((tokens, group * width), jnp.bfloat16),
        ),
        compiler_params=pltpu.CompilerParams(vmem_limit_bytes=VMEM_LIMIT),
        name="attend",
    )(lengths, query, kv_blocks, gate_logit)


def attend_back_kernel(
    ranks, planes, lengths_ref, q_ref, kv_ref, gate_ref, att_ref, total_ref, dgated_ref, dq_ref, dkv_ref, dgate_ref, sums
):
    group, rows, width = q_ref.shape
    scale = HEAD_DIM ** (-0.5)
    low, high, first = block_bounds(lengths_ref, ranks, planes, rows)
    tokens = query_tokens(first, rows, group)
    starts = row_starts(lengths_ref, tokens)
    query = stack_heads(q_ref)
    span = planes * rows

    @pl.when(pl.program_id(0) == 0)
    def _():
        sums[...] = jnp.zeros_like(sums)

    attended = stack_heads(att_ref)
    sent = attended.astype(jnp.bfloat16).astype(jnp.float32)
    total = stack_heads(total_ref)
    logit = stack_heads(gate_ref)
    prob = jax.nn.sigmoid(logit)
    dgated = jnp.concatenate(
        [dgated_ref[:, head * width : (head + 1) * width] for head in range(group)], axis=0
    )
    dattended = (dgated * prob).astype(jnp.bfloat16)
    dlogit = jnp.sum(dgated * sent, axis=1, keepdims=True) * prob * (1.0 - prob)
    dgate_ref[...] = dlogit.astype(jnp.bfloat16).reshape(group, rows, 1)
    dattended = dattended.astype(jnp.float32)
    scaled = (dattended / total).astype(jnp.bfloat16)
    delta = jnp.sum(dattended * attended, axis=1, keepdims=True) / total

    def step(chunk, dquery):
        key = kv_ref[:, 0, chunk].reshape(span, width)
        value = kv_ref[:, 1, chunk].reshape(span, width)
        weights = chunk_weights(query, key, scale, tokens, starts, chunk * span)
        dprob = mat_nt(scaled, value)
        dscore = (weights * (dprob - delta)).astype(jnp.bfloat16)
        dquery = dquery + jnp.dot(dscore, key, preferred_element_type=jnp.float32)
        dkey = mat_tn(dscore, query)
        dvalue = mat_tn(weights.astype(jnp.bfloat16), scaled)
        sums[:, 0, chunk] += dkey.reshape(planes, rows, width)
        sums[:, 1, chunk] += dvalue.reshape(planes, rows, width)
        return dquery

    dquery = lax.fori_loop(
        low, high + 1, step, jnp.zeros((group * rows, width), jnp.float32)
    )
    dq_ref[...] = (dquery * scale).astype(jnp.bfloat16).reshape(group, rows, width)

    @pl.when(pl.program_id(0) == ranks - 1)
    def _():
        for chunk in range(ranks):
            dkv_ref[:, 0, chunk] = (sums[:, 0, chunk] * scale).astype(jnp.bfloat16)
            dkv_ref[:, 1, chunk] = sums[:, 1, chunk].astype(jnp.bfloat16)


def attend_back(lengths, query, kv, gate_logit, attended, total, dgated, rows):
    group, tokens, width = query.shape
    planes = kv.shape[0]
    ranks = tokens // rows
    kv_blocks = kv.reshape(planes, 2, ranks, rows, width)
    block = pl.BlockSpec((group, rows, width), lambda i, *_: (0, i, 0))
    thin = pl.BlockSpec((group, rows, 1), lambda i, *_: (0, i, 0))
    whole = pl.BlockSpec((planes, 2, ranks, rows, width), lambda i, *_: (0, 0, 0, 0, 0))
    dquery, dkv, dgate = pl.pallas_call(
        functools.partial(attend_back_kernel, ranks, planes),
        grid_spec=pltpu.PrefetchScalarGridSpec(
            num_scalar_prefetch=1,
            grid=(ranks,),
            in_specs=[
                block,
                whole,
                thin,
                block,
                thin,
                pl.BlockSpec((rows, group * width), lambda i, *_: (i, 0)),
            ],
            out_specs=(block, whole, thin),
            scratch_shapes=[pltpu.VMEM((planes, 2, ranks, rows, width), jnp.float32)],
        ),
        out_shape=(
            jax.ShapeDtypeStruct((group, tokens, width), jnp.bfloat16),
            jax.ShapeDtypeStruct((planes, 2, ranks, rows, width), jnp.bfloat16),
            jax.ShapeDtypeStruct((group, tokens, 1), jnp.bfloat16),
        ),
        compiler_params=pltpu.CompilerParams(vmem_limit_bytes=VMEM_LIMIT),
        name="attend_back",
    )(lengths, query, kv_blocks, gate_logit, attended, total, dgated)
    return dquery, dkv.reshape(planes, 2, tokens, width), dgate


def middle_kernel(
    planes,
    gated_ref,
    wout_ref,
    x_ref,
    scale_ref,
    dy_hbm,
    wg_hbm,
    wu_hbm,
    wd_hbm,
    xg,
    line_hbm,
    down_hbm,
    mid_ref,
    dmid_ref,
    gain_ref,
    pm_ref,
    dgated_ref,
    act_ref,
    wg,
    wu,
    wd,
    dy,
    dhid,
    near_out,
    near_in,
    far_out,
    far_in,
    keep,
    down_buf,
    load_sem,
    dy_sem,
    down_sem,
    near_send,
    near_recv,
    far_send,
    far_recv,
    ag_send,
    ag_recv,
    line_send,
    line_recv,
):
    rank, plane = lax.axis_index("fsdp"), lax.axis_index("sp")
    ranks, rows, width = xg.shape
    loads = [
        pltpu.make_async_copy(wd_hbm, wd, load_sem.at[0]),
        pltpu.make_async_copy(wg_hbm, wg, load_sem.at[1]),
        pltpu.make_async_copy(wu_hbm, wu, load_sem.at[2]),
    ]
    dy_load = pltpu.make_async_copy(dy_hbm, dy, dy_sem)
    others = [lax.rem(plane + k, planes) for k in range(1, planes)]
    greet([(rank ^ k, plane) for k in (1, 2, 4, 6)] + [(rank, other) for other in others])

    def along(source, which):
        return [
            peer_copy(
                source,
                line_hbm.at[which, j - 1],
                line_send.at[which, j - 1],
                line_recv.at[which, j - 1],
                rank,
                lax.rem(plane + planes - j, planes),
            )
            for j in range(1, planes)
        ]

    def near(phase, i):
        return peer_copy(
            near_out.at[phase, i],
            near_in.at[phase, i],
            near_send.at[phase, i],
            near_recv.at[phase, i],
            rank ^ 1,
            plane,
        )

    def far(phase, i, k):
        return peer_copy(
            far_out.at[phase, i],
            far_in.at[phase, i],
            far_send.at[phase, i],
            far_recv.at[phase, i],
            rank ^ k,
            plane,
        )

    order = (6, 2, 4, 0)
    for i, k in enumerate(order):
        part = jnp.dot(
            gated_ref[rank ^ 1 ^ k], wout_ref[...], preferred_element_type=jnp.float32
        )
        near_out[0, i] = part.astype(jnp.bfloat16)
        near(0, i).start()
    dy_load.start()
    for copy in loads:
        copy.start()
    dy_line = along(dy_hbm.at[rank], 1)
    for copy in dy_line:
        copy.start()
    for i, k in enumerate(order):
        part = jnp.dot(gated_ref[rank ^ k], wout_ref[...], preferred_element_type=jnp.float32)
        near(0, i).wait_recv()
        part = part + near_in[0, i].astype(jnp.float32)
        if k:
            far_out[0, i] = part.astype(jnp.bfloat16)
            far(0, i, k).start()
        else:
            keep[...] = part

    dy_load.wait()
    loads[0].wait()

    @pl.loop(0, ranks // 2)
    def _(p):
        pair = dy[pl.ds(2 * p, 2)].reshape(2 * rows, width)
        dhid[p] = mat_nt(pair, wd[...])

    loads[1].wait()
    loads[2].wait()
    middle = x_ref[...].astype(jnp.float32) + keep[...]
    for i in (1, 2, 0):
        far(0, i, order[i]).wait_recv()
        middle = middle + far_in[0, i].astype(jnp.float32)
    inverse = inv_rms(middle)
    mid_ref[...] = middle
    normed = (middle * inverse * scale_ref[...]).astype(jnp.bfloat16)
    xg[rank] = normed
    sems = (ag_send.at[0], ag_recv.at[0])
    gather_start(xg, *sems)
    xb_line = along(xg.at[rank], 0)
    for copy in xb_line:
        copy.start()

    slots = {2: 0, 4: 1, 6: 2, 0: 3}

    def down_copy(p, slot):
        return pltpu.make_async_copy(
            down_buf.at[slot], down_hbm.at[pl.ds(2 * p, 2)], down_sem.at[slot]
        )

    def feed(k):
        p = (rank ^ k) // 2
        slot = (0, 2, 4, 6).index(k) % 2
        pair = xg[pl.ds(2 * p, 2)].reshape(2 * rows, width)
        gate_pre = mat_nt(pair, wg[...])
        up_pre = mat_nt(pair, wu[...])
        grad_hidden = dhid[p]
        sigma = jax.nn.sigmoid(gate_pre)
        swish = gate_pre * sigma
        grad_gate = (grad_hidden * up_pre * sigma * (1.0 + gate_pre * (1.0 - sigma))).astype(
            jnp.bfloat16
        )
        grad_up = (grad_hidden * swish).astype(jnp.bfloat16)
        part = jnp.dot(grad_gate, wg[...], preferred_element_type=jnp.float32) + jnp.dot(
            grad_up, wu[...], preferred_element_type=jnp.float32
        )
        i = slots[k]
        halves = part.reshape(2, rows, width)
        mine_first = lax.rem(rank, 2) == 0
        mine = jnp.where(mine_first, halves[0], halves[1])
        theirs = jnp.where(mine_first, halves[1], halves[0])
        near_out[1, i] = theirs.astype(jnp.bfloat16)
        near(1, i).start()
        hidden = (swish * up_pre).astype(jnp.bfloat16)
        for kept, value in enumerate((grad_gate, grad_up, hidden)):
            act_ref[kept, pl.ds(pl.multiple_of(2 * rows * p, 2 * rows), 2 * rows)] = value
        down = jnp.dot(hidden, wd[...], preferred_element_type=jnp.float32)
        if k in (4, 6):
            down_copy(p, slot).wait()
        down_buf[slot] = down.astype(jnp.bfloat16).reshape(2, rows, width)
        down_copy(p, slot).start()
        near(1, i).wait_recv()
        mine = mine + near_in[1, i].astype(jnp.float32)
        if k:
            far_out[1, i] = mine.astype(jnp.bfloat16)
            far(1, i, k).start()
        else:
            keep[...] = mine

    gather_wait(xg, *sems, (6,))
    feed(0)
    gather_pass(xg, *sems, NEIGHBOURS_FIRST)
    gather_wait(xg, *sems, (7, 8))
    feed(2)
    gather_pass(xg, *sems, DIAGONAL)
    gather_wait(xg, *sems, (9, 10))
    feed(4)
    gather_wait(xg, *sems, (11, 12))
    feed(6)

    grad = keep[...]
    for i, k in enumerate((2, 4, 6)):
        far(1, i, k).wait_recv()
        grad = grad + far_in[1, i].astype(jnp.float32)
    middle = mid_ref[...]
    inverse = inv_rms(middle)
    gain_ref[...] = jnp.sum(grad * middle * inverse, axis=0, keepdims=True)
    grad_middle = dy[rank].astype(jnp.float32) + norm_back(
        grad, middle, inverse, scale_ref[...]
    )
    dmid_ref[...] = grad_middle
    pm_ref[rank] = grad_middle.astype(jnp.bfloat16)
    sems2 = (ag_send.at[1], ag_recv.at[1])
    gather_start(pm_ref, *sems2)

    def gated_grad(k):
        p = (rank ^ k) // 2
        pair = pm_ref[pl.ds(2 * p, 2)].reshape(2 * rows, width)
        dgated_ref[pl.ds(2 * p, 2)] = mat_nt(pair, wout_ref[...]).reshape(
            2, rows, wout_ref.shape[0]
        )

    gather_wait(pm_ref, *sems2, (6,))
    gated_grad(0)
    gather_pass(pm_ref, *sems2, NEIGHBOURS_FIRST)
    gather_wait(pm_ref, *sems2, (7, 8))
    gated_grad(2)
    gather_wait(pm_ref, *sems2, (9, 10))
    gated_grad(4)
    gather_pass(pm_ref, *sems2, DIAGONAL)
    gather_wait(pm_ref, *sems2, (11, 12))
    gated_grad(6)

    gather_sent(xg, *sems)
    gather_sent(pm_ref, *sems2)
    for copy in dy_line + xb_line:
        copy.wait()
    for phase in range(2):
        for i in range(4):
            near(phase, i).wait_send()
        for i in range(3):
            far(phase, i, 2).wait_send()
    down_copy(0, 0).wait()
    down_copy(0, 1).wait()


def middle_layer(gated, w_out, x, scale, grad_plane, w_gate, w_up, w_down, collective_id):
    ranks, rows, _ = gated.shape
    planes = lax.axis_size("sp")
    width = x.shape[1]
    hidden = w_gate.shape[0]
    features = w_out.shape[0]
    vmem = pl.BlockSpec(memory_space=pltpu.VMEM)
    hbm = pl.BlockSpec(memory_space=pl.ANY)
    half, full = jnp.bfloat16, jnp.float32
    return pl.pallas_call(
        functools.partial(middle_kernel, planes),
        out_shape=(
            jax.ShapeDtypeStruct((ranks, rows, width), half),
            jax.ShapeDtypeStruct((2, planes - 1, rows, width), half),
            jax.ShapeDtypeStruct((ranks, rows, width), half),
            jax.ShapeDtypeStruct((rows, width), full),
            jax.ShapeDtypeStruct((rows, width), full),
            jax.ShapeDtypeStruct((1, width), full),
            jax.ShapeDtypeStruct((ranks, rows, width), half),
            jax.ShapeDtypeStruct((ranks, rows, features), full),
            jax.ShapeDtypeStruct((3, ranks * rows, hidden), half),
        ),
        in_specs=[vmem, vmem, vmem, vmem, hbm, hbm, hbm, hbm],
        out_specs=(vmem, hbm, hbm, vmem, vmem, vmem, vmem, vmem, vmem),
        scratch_shapes=[
            pltpu.VMEM((hidden, width), half),
            pltpu.VMEM((hidden, width), half),
            pltpu.VMEM((hidden, width), half),
            pltpu.VMEM((ranks, rows, width), half),
            pltpu.VMEM((ranks // 2, 2 * rows, hidden), full),
            pltpu.VMEM((2, 4, rows, width), half),
            pltpu.VMEM((2, 4, rows, width), half),
            pltpu.VMEM((2, 3, rows, width), half),
            pltpu.VMEM((2, 3, rows, width), half),
            pltpu.VMEM((rows, width), full),
            pltpu.VMEM((2, 2, rows, width), half),
            pltpu.SemaphoreType.DMA((3,)),
            pltpu.SemaphoreType.DMA,
            pltpu.SemaphoreType.DMA((2,)),
            pltpu.SemaphoreType.DMA((2, 4)),
            pltpu.SemaphoreType.DMA((2, 4)),
            pltpu.SemaphoreType.DMA((2, 3)),
            pltpu.SemaphoreType.DMA((2, 3)),
            pltpu.SemaphoreType.DMA((2, GATHER_COPIES)),
            pltpu.SemaphoreType.DMA((2, GATHER_COPIES)),
            pltpu.SemaphoreType.DMA((2, planes - 1)),
            pltpu.SemaphoreType.DMA((2, planes - 1)),
        ],
        compiler_params=pltpu.CompilerParams(
            collective_id=collective_id, has_side_effects=True, vmem_limit_bytes=VMEM_LIMIT
        ),
        name="middle_layer",
    )(gated, w_out, x, scale, grad_plane, w_gate, w_up, w_down)


def feed_weights_kernel(
    planes,
    xp_hbm,
    dp_hbm,
    act_hbm,
    blocks_hbm,
    first_hbm,
    second_hbm,
    down_hbm,
    mid_ref,
    small_ref,
    rows_ref,
    qkv_hbm,
    wg_ref,
    wu_ref,
    wd_ref,
    og_ref,
    ou_ref,
    od_ref,
    h_ref,
    so_ref,
    go_ref,
    sum_hbm,
    more_hbm,
    xbuf,
    dbuf,
    act,
    parts,
    small_buf,
    rows_buf,
    quarter,
    quarters,
    x_sem,
    d_sem,
    act_sem,
    part_sem,
    own_sem,
    ag_send,
    ag_recv,
    line_send,
    line_recv,
    part_send,
    part_recv,
    sum_send,
    sum_recv,
    quarter_sem,
    near_buf,
    out_buf,
    far_buf,
    sib_send,
    sib_recv,
    send_sem,
    recv_sem,
):
    rank, plane = lax.axis_index("fsdp"), lax.axis_index("sp")
    ranks, rows, width = xp_hbm.shape
    part = ranks // 2
    chunk = part * rows
    others = [lax.rem(plane + k, planes) for k in range(1, planes)]
    greet([(rank ^ k, plane) for k in (1, 2, 4, 6)] + [(rank, other) for other in others])

    picks = ((0, 1), (1, 2), (0, 2))
    gathers = [(more_hbm.at[g], ag_send.at[g], ag_recv.at[g]) for g in range(3)]
    own_blocks = [
        pltpu.make_async_copy(blocks_hbm.at[pick], more_hbm.at[g, rank], own_sem.at[g])
        for g, pick in enumerate(picks)
    ]

    def begin(g):
        gather_start(*gathers[g], own=blocks_hbm.at[picks[g]])

    def load(step, start):
        slot = lax.rem(step, 2)
        block = pl.ds(part * lax.rem(step, 2), part)
        group = step // 2
        sources = (
            (first_hbm.at[0, block], first_hbm.at[1, block]),
            (xp_hbm.at[block], dp_hbm.at[block]),
            (more_hbm.at[0, block], second_hbm.at[block]),
            (more_hbm.at[2, block], more_hbm.at[1, block]),
        )
        for index, (x_from, d_from) in enumerate(sources):
            @pl.when(group == index)
            def _():
                for copy in (
                    pltpu.make_async_copy(x_from, xbuf.at[slot], x_sem.at[slot]),
                    pltpu.make_async_copy(d_from, dbuf.at[slot], d_sem.at[slot]),
                ):
                    if start:
                        copy.start()
                    else:
                        copy.wait()

    def kept(step):
        where = pl.ds(pl.multiple_of(step * chunk, chunk), chunk)
        return pltpu.make_async_copy(act_hbm.at[:, where], act, act_sem)

    scatter = (near_buf, sib_send, sib_recv)
    own_parts = [
        pltpu.make_async_copy(down_hbm.at[rank ^ k], parts.at[i], part_sem.at[i])
        for i, k in enumerate(SCATTER_ORDER)
    ]
    small = [
        peer_copy(
            source,
            buffer.at[k],
            line_send.at[which, k],
            line_recv.at[which, k],
            rank,
            others[k],
        )
        for which, (source, buffer) in enumerate(((small_ref, small_buf), (rows_ref, rows_buf)))
        for k in range(planes - 1)
    ]

    quarter_rows = quarter.shape[0]

    def rows_of(index):
        return pl.ds(pl.multiple_of(index * quarter_rows, quarter_rows), quarter_rows)

    own_quarter = pltpu.make_async_copy(qkv_hbm.at[rows_of(plane)], quarter, quarter_sem.at[0])
    own_sum = pltpu.make_async_copy(quarter, sum_hbm.at[rows_of(plane)], quarter_sem.at[1])
    partials = [
        peer_copy(
            qkv_hbm.at[rows_of(others[k])],
            quarters.at[k],
            part_send.at[k],
            part_recv.at[k],
            rank,
            others[k],
        )
        for k in range(planes - 1)
    ]
    sums = [
        peer_copy(
            quarter,
            sum_hbm.at[rows_of(plane)],
            sum_send.at[k],
            sum_recv.at[k],
            rank,
            others[k],
        )
        for k in range(planes - 1)
    ]

    load(0, True)
    own_quarter.start()
    for copy in own_blocks + small + own_parts + partials:
        copy.start()
    begin(0)
    for i in range(4):
        scatter_near(down_hbm, i, *scatter).start()

    @pl.loop(0, 2 * planes)
    def _(step):
        @pl.when(step == 1)
        def _():
            gather_pass(*gathers[0], NEIGHBOURS_FIRST)
            begin(1)

        @pl.when(step == 2)
        def _():
            kept(0).start()
            gather_pass(*gathers[0], DIAGONAL)
            gather_pass(*gathers[1], NEIGHBOURS_FIRST)
            begin(2)

        @pl.when(step == 3)
        def _():
            kept(1).start()
            for i, k in enumerate(SCATTER_ORDER):
                own_parts[i].wait()
                scatter_near(down_hbm, i, *scatter).wait_recv()
                joined = parts[i].astype(jnp.float32) + near_buf[i].astype(jnp.float32)
                if k:
                    out_buf[i] = joined.astype(out_buf.dtype)
                else:
                    parts[i] = joined.astype(parts.dtype)

        @pl.when(step == 4)
        def _():
            gather_wait(*gathers[0], FROM_SIBLING)
            own_blocks[0].wait()
            load(step, True)
            gather_pass(*gathers[1], DIAGONAL)
            own_quarter.wait()
            total = quarter[...].astype(jnp.float32)
            for k in range(planes - 1):
                partials[k].wait()
                total = total + quarters[k].astype(jnp.float32)
            quarter[...] = total.astype(quarter.dtype)
            own_sum.start()
            for copy in sums:
                copy.start()

        @pl.when(step == 5)
        def _():
            gather_pass(*gathers[2], NEIGHBOURS_FIRST)
            for i in range(3):
                scatter_far(i, out_buf, far_buf, send_sem, recv_sem).start()

        @pl.when(step == 6)
        def _():
            gather_pass(*gathers[2], DIAGONAL)
            for g in (1, 2):
                gather_wait(*gathers[g], FROM_SIBLING)
                own_blocks[g].wait()
            load(step, True)

        load(step, False)

        @pl.when((lax.rem(step, 2) == 0) | (step == 1))
        def _():
            load(step + 1, True)

        slot = lax.rem(step, 2)
        normed = xbuf[slot].reshape(chunk, width)
        grad = dbuf[slot].reshape(chunk, width)

        own = step // 2 == 1

        @pl.when(own)
        def _():
            kept(0).wait()

        @pl.when(jnp.logical_not(own))
        def _():
            gate_pre = mat_nt(normed, wg_ref[...])
            up_pre = mat_nt(normed, wu_ref[...])
            grad_hidden = mat_nt(grad, wd_ref[...])
            sigma = jax.nn.sigmoid(gate_pre)
            swish = gate_pre * sigma
            act[0] = (grad_hidden * up_pre * sigma * (1.0 + gate_pre * (1.0 - sigma))).astype(
                jnp.bfloat16
            )
            act[1] = (grad_hidden * swish).astype(jnp.bfloat16)
            act[2] = (swish * up_pre).astype(jnp.bfloat16)

        @pl.when(step == 0)
        def _():
            for ref in (og_ref, ou_ref, od_ref):
                ref[...] = jnp.zeros_like(ref)

        og_ref[...] += mat_tn(act[0], normed)
        ou_ref[...] += mat_tn(act[1], normed)
        od_ref[...] += mat_tn(act[2], grad)

    output = mid_ref[...] + parts[3].astype(jnp.float32)
    for i in range(3):
        scatter_far(i, out_buf, far_buf, send_sem, recv_sem).wait()
        output = output + far_buf[i].astype(jnp.float32)
    h_ref[...] = output.astype(h_ref.dtype)
    for copy in small + sums:
        copy.wait()
    own_sum.wait()
    total, gate_rows = small_ref[...], rows_ref[...]
    for k in range(planes - 1):
        total = total + small_buf[k]
        gate_rows = gate_rows + rows_buf[k]
    so_ref[...] = total
    go_ref[...] = gate_rows
    for i in range(4):
        scatter_near(down_hbm, i, *scatter).wait_send()
    for gather in gathers:
        gather_sent(*gather)


def feed_weights(plane_x, plane_grad, acts, blocks, first, second, down, middle, small, gate_rows, qkv_part, w_gate, w_up, w_down, collective_id):
    ranks, rows, width = plane_x.shape
    planes = lax.axis_size("sp")
    hidden = w_gate.shape[0]
    vmem = pl.BlockSpec(memory_space=pltpu.VMEM)
    hbm = pl.BlockSpec(memory_space=pl.ANY)
    tokens = planes * ranks * rows
    half, full = plane_x.dtype, jnp.float32
    return pl.pallas_call(
        functools.partial(feed_weights_kernel, planes),
        in_specs=[hbm] * 7 + [vmem] * 3 + [hbm] + [vmem] * 3,
        out_specs=(vmem,) * 6 + (hbm, hbm),
        out_shape=[jax.ShapeDtypeStruct(w_gate.shape, full)] * 3
        + [
            jax.ShapeDtypeStruct((rows, width), half),
            jax.ShapeDtypeStruct(small.shape, full),
            jax.ShapeDtypeStruct(gate_rows.shape, full),
            jax.ShapeDtypeStruct(qkv_part.shape, half),
            jax.ShapeDtypeStruct((3, ranks, rows, width), half),
        ],
        scratch_shapes=[
            pltpu.VMEM((2, ranks // 2, rows, width), half),
            pltpu.VMEM((2, ranks // 2, rows, width), half),
            pltpu.VMEM((3, ranks // 2 * rows, hidden), half),
            pltpu.VMEM((4, rows, width), half),
            pltpu.VMEM((planes - 1,) + small.shape, full),
            pltpu.VMEM((planes - 1,) + gate_rows.shape, full),
            pltpu.VMEM((qkv_part.shape[0] // planes, width), half),
            pltpu.VMEM((planes - 1, qkv_part.shape[0] // planes, width), half),
            pltpu.SemaphoreType.DMA((2,)),
            pltpu.SemaphoreType.DMA((2,)),
            pltpu.SemaphoreType.DMA,
            pltpu.SemaphoreType.DMA((4,)),
            pltpu.SemaphoreType.DMA((3,)),
            pltpu.SemaphoreType.DMA((3, GATHER_COPIES)),
            pltpu.SemaphoreType.DMA((3, GATHER_COPIES)),
            pltpu.SemaphoreType.DMA((2, planes - 1)),
            pltpu.SemaphoreType.DMA((2, planes - 1)),
        ]
        + [pltpu.SemaphoreType.DMA((planes - 1,))] * 4
        + [
            pltpu.SemaphoreType.DMA((2,)),
        ]
        + scatter_scratch(rows, width, half),
        cost_estimate=pl.CostEstimate(
            flops=12 * tokens * w_gate.size,
            bytes_accessed=4 * tokens * width + 18 * w_gate.size,
            transcendentals=tokens * w_gate.shape[0],
        ),
        compiler_params=pltpu.CompilerParams(
            collective_id=collective_id, has_side_effects=True, vmem_limit_bytes=VMEM_LIMIT
        ),
        name="feed_weights",
    )(plane_x, plane_grad, acts, blocks, first, second, down, middle, small, gate_rows, qkv_part, w_gate, w_up, w_down)[:7]


def front_kernel(
    planes,
    lengths_ref,
    x_ref,
    small_ref,
    w_ref,
    wg_ref,
    dyo_ref,
    q_ref,
    kv_ref,
    dy_ref,
    xg,
    xa_ref,
    raw_ref,
    gate_ref,
    attn_ref,
    ffn_ref,
    head_ref,
    cos_ref,
    sin_ref,
    nat,
    gains,
    small_send,
    small_recv,
    ag_send,
    ag_recv,
    own_sem,
    local_sem,
    q_send,
    q_recv,
    kv_send,
    kv_recv,
    line_send,
    line_recv,
):
    rank, plane = lax.axis_index("fsdp"), lax.axis_index("sp")
    ranks, rows, width = xg.shape
    pair_rows = 2 * rows
    chip = rank // 2
    greet_line(ranks, planes)
    own_block = pltpu.make_async_copy(dyo_ref, dy_ref.at[rank], own_sem)
    own_block.start()
    small = []
    for k in range(1, ranks):
        copy = peer_copy(
            small_ref, gains.at[rank], small_send.at[k - 1], small_recv.at[k - 1], rank ^ k, plane
        )
        copy.start()
        small.append(copy)
    sems = (ag_send.at[0], ag_recv.at[0])
    gather_start(xg, *sems, own=x_ref)
    xg[rank] = x_ref[...]
    gains[rank] = small_ref[...]

    half = HEAD_DIM // 2
    lane = lax.broadcasted_iota(jnp.int32, (1, HEAD_DIM), 1)
    step = lax.rem(lane, half).astype(jnp.float32)
    frequency = jnp.exp(-math.log(ROPE_BASE) * 2.0 * step / HEAD_DIM)
    sign = jnp.where(lane < half, -1.0, 1.0)

    @pl.loop(0, ranks)
    def _(block):
        tokens = (block * planes + plane) * rows + lax.broadcasted_iota(jnp.int32, (rows, 1), 0)
        position = tokens - row_starts(lengths_ref, tokens)
        angles = position.astype(jnp.float32) * frequency
        where = pl.ds(pl.multiple_of(block * rows, rows), rows)
        cos_ref[where] = jnp.cos(angles)
        sin_ref[where] = jnp.sin(angles) * sign

    for copy in small:
        copy.wait_recv()
    head_q, head_k = gains[0, 4:5], gains[0, 5:6]
    for r in range(1, ranks):
        head_q = head_q + gains[r, 4:5]
        head_k = head_k + gains[r, 5:6]
    head_ref[...] = jnp.where(rank < ranks // 2, head_q, head_k)
    for r in range(ranks):
        for i in range(2):
            columns = slice((2 * r + i) * HEAD_DIM, (2 * r + i + 1) * HEAD_DIM)
            attn_ref[:, columns] = gains[r, i : i + 1]
            ffn_ref[:, columns] = gains[r, 2 + i : 3 + i]

    def token_rows(p):
        return pl.ds(pl.multiple_of(p * pair_rows, pair_rows), pair_rows)

    def q_copy(m, p, to):
        return peer_copy(
            nat.at[pl.ds(2 * m, 2), token_rows(p)],
            q_ref.at[:, token_rows(p)],
            q_send.at[m, p],
            q_recv.at[p],
            to,
            plane,
        )

    def kv_copy(m, which, p, to):
        return peer_copy(
            nat.at[m, token_rows(p)],
            kv_ref.at[plane, which, token_rows(p)],
            kv_send.at[m, p],
            kv_recv.at[which, p],
            to,
            plane,
        )

    def q_local(p):
        return pltpu.make_async_copy(
            nat.at[pl.ds(0, 2), token_rows(p)], q_ref.at[:, token_rows(p)], local_sem.at[p]
        )

    def kv_local(m, which, p):
        return pltpu.make_async_copy(
            nat.at[m, token_rows(p)], kv_ref.at[plane, which, token_rows(p)], local_sem.at[p]
        )

    def process(k):
        p = chip ^ (k // 2)
        inputs = xg[pl.ds(2 * p, 2)].reshape(pair_rows, width).astype(jnp.float32)
        normed = (inputs * inv_rms(inputs) * attn_ref[...]).astype(jnp.bfloat16)
        xa_ref[pl.ds(2 * p, 2)] = normed.reshape(2, rows, width)
        projected = mat_nt(normed, w_ref[...])
        raw_ref[token_rows(p)] = projected
        logits = mat_nt(normed, wg_ref[...])
        for head in range(gate_ref.shape[0]):
            gate_ref[head, token_rows(p)] = logits[:, head : head + 1]
        cosine, sine = cos_ref[token_rows(p)], sin_ref[token_rows(p)]
        for m in range(4):
            head = projected[:, m * HEAD_DIM : (m + 1) * HEAD_DIM]
            scaled = head * inv_rms(head) * head_ref[...]
            turned = scaled * cosine + pltpu.roll(scaled, half, 1) * sine
            nat[m, token_rows(p)] = jnp.where(rank >= 6, head, turned).astype(jnp.bfloat16)

        @pl.when(rank < 4)
        def _():
            for m in range(2):
                @pl.when(2 * rank + m != rank)
                def _():
                    q_copy(m, p, 2 * rank + m).start()

        @pl.when(rank == 0)
        def _():
            q_local(p).start()

        for which in range(2):
            first = 4 + 2 * which

            @pl.when((rank == first) | (rank == first + 1))
            def _():
                for m in range(4):
                    to = 4 * (rank - first) + m

                    @pl.when(to != rank)
                    def _():
                        kv_copy(m, which, p, to).start()

            @pl.when(rank == first + 1)
            def _():
                kv_local((first + 1) % 4, which, p).start()

    def line_piece(origin, which, p, side, j, to):
        piece = kv_ref.at[origin, which, token_rows(p)]
        return peer_copy(
            piece,
            piece,
            line_send.at[side, j, which, p],
            line_recv.at[side, j, which, p],
            rank,
            to,
        )

    def origin_of(side, j):
        return plane - j if side == 0 else plane + j

    def next_of(side):
        return plane + 1 if side == 0 else plane - 1

    def line_go(which, p, j):
        if j == 0:
            @pl.when(rank == 5 + 2 * which)
            def _():
                kv_local((5 + 2 * which) % 4, which, p).wait()

            @pl.when(rank != 5 + 2 * which)
            def _():
                kv_copy(0, which, p, 0).wait_recv()

        for side in range(2):
            if j:
                arrives = (plane >= j) if side == 0 else (plane + j <= planes - 1)

                @pl.when(arrives)
                def _():
                    line_piece(origin_of(side, j), which, p, side, j - 1, plane).wait_recv()

            if j < planes - 1:
                @pl.when(line_sends(planes, plane, j, side))
                def _():
                    line_piece(origin_of(side, j), which, p, side, j, next_of(side)).start()

    slots = (((0, 2), (1, 3)), ((0, 3), (1, 2)), ((0, 0), (1, 1)), ((0, 1), (1, 0)))

    def slot_go(slot, j):
        for which, p in slots[slot]:
            line_go(which, p, j)

    gather_wait(xg, *sems, (6,))
    process(0)
    slot_go(0, 0)
    gather_pass(xg, *sems, NEIGHBOURS_FIRST)
    gather_wait(xg, *sems, (7, 8))
    process(2)
    slot_go(0, 1)
    gather_wait(xg, *sems, (9, 10))
    process(4)
    gather_pass(xg, *sems, DIAGONAL)
    slot_go(1, 0)
    slot_go(0, 2)
    gather_wait(xg, *sems, (11, 12))
    process(6)
    sems2 = (ag_send.at[1], ag_recv.at[1])
    slot_go(2, 0)
    slot_go(1, 1)
    slot_go(3, 0)
    gather_start(dy_ref, *sems2, own=dyo_ref)
    slot_go(0, 3)
    slot_go(1, 2)
    slot_go(2, 1)
    slot_go(3, 1)
    slot_go(1, 3)
    slot_go(2, 2)
    gather_pass(dy_ref, *sems2, NEIGHBOURS_FIRST)
    slot_go(3, 2)
    slot_go(2, 3)
    gather_pass(dy_ref, *sems2, DIAGONAL)
    slot_go(3, 3)
    gather_wait(dy_ref, *sems2, FROM_SIBLING)

    for p in range(ranks // 2):
        @pl.when(rank == 0)
        def _():
            q_local(p).wait()

        @pl.when(rank != 0)
        def _():
            q_copy(0, p, 0).wait_recv()

    for copy in small:
        copy.wait_send()
    gather_sent(xg, *sems)
    gather_sent(dy_ref, *sems2)
    own_block.wait()
    for p in range(ranks // 2):
        @pl.when(rank < 4)
        def _():
            for m in range(2):
                @pl.when(2 * rank + m != rank)
                def _():
                    q_copy(m, p, 0).wait_send()

        for which in range(2):
            first = 4 + 2 * which

            @pl.when((rank == first) | (rank == first + 1))
            def _():
                for m in range(4):
                    @pl.when(4 * (rank - first) + m != rank)
                    def _():
                        kv_copy(m, which, p, 0).wait_send()

            for j in range(planes - 1):
                for side in range(2):
                    @pl.when(line_sends(planes, plane, j, side))
                    def _():
                        line_piece(0, which, p, side, j, next_of(side)).wait_send()


def front(lengths, x, small, w_qkv, w_head_gate, grad, collective_id):
    rows, width = x.shape
    ranks, planes = lax.axis_size("fsdp"), lax.axis_size("sp")
    tokens = ranks * rows
    heads = w_head_gate.shape[0]
    vmem = pl.BlockSpec(memory_space=pltpu.VMEM)
    hbm = pl.BlockSpec(memory_space=pl.ANY)
    half, full = jnp.bfloat16, jnp.float32
    pairs = ranks // 2
    return pl.pallas_call(
        functools.partial(front_kernel, planes),
        out_shape=(
            jax.ShapeDtypeStruct((2, tokens, HEAD_DIM), half),
            jax.ShapeDtypeStruct((planes, 2, tokens, HEAD_DIM), half),
            jax.ShapeDtypeStruct((ranks, rows, width), half),
            jax.ShapeDtypeStruct((ranks, rows, width), half),
            jax.ShapeDtypeStruct((ranks, rows, width), half),
            jax.ShapeDtypeStruct((tokens, w_qkv.shape[0]), full),
            jax.ShapeDtypeStruct((heads, tokens, 1), full),
            jax.ShapeDtypeStruct((1, width), full),
            jax.ShapeDtypeStruct((1, width), full),
            jax.ShapeDtypeStruct((1, HEAD_DIM), full),
            jax.ShapeDtypeStruct((tokens, HEAD_DIM), full),
            jax.ShapeDtypeStruct((tokens, HEAD_DIM), full),
        ),
        in_specs=[pl.BlockSpec(memory_space=pltpu.SMEM), vmem, vmem, vmem, vmem, hbm],
        out_specs=(hbm, hbm, hbm) + (vmem,) * 9,
        scratch_shapes=[
            pltpu.VMEM((4, tokens, HEAD_DIM), half),
            pltpu.VMEM((ranks,) + small.shape, small.dtype),
            pltpu.SemaphoreType.DMA((ranks - 1,)),
            pltpu.SemaphoreType.DMA((ranks - 1,)),
            pltpu.SemaphoreType.DMA((2, GATHER_COPIES)),
            pltpu.SemaphoreType.DMA((2, GATHER_COPIES)),
            pltpu.SemaphoreType.DMA,
            pltpu.SemaphoreType.DMA((pairs,)),
            pltpu.SemaphoreType.DMA((2, pairs)),
            pltpu.SemaphoreType.DMA((pairs,)),
            pltpu.SemaphoreType.DMA((4, pairs)),
            pltpu.SemaphoreType.DMA((2, pairs)),
            pltpu.SemaphoreType.DMA((2, planes - 1, 2, pairs)),
            pltpu.SemaphoreType.DMA((2, planes - 1, 2, pairs)),
        ],
        compiler_params=pltpu.CompilerParams(
            collective_id=collective_id, has_side_effects=True, vmem_limit_bytes=VMEM_LIMIT
        ),
        name="front",
    )(lengths, x, small, w_qkv, w_head_gate, grad)


def local_planes(
    hidden_in,
    grad_out,
    lengths,
    attn_gain,
    w_qkv,
    w_head_gate,
    q_gain,
    k_gain,
    w_out,
    ffn_gain,
    w_gate,
    w_up,
    w_down,
):
    ranks, planes = lax.axis_size("fsdp"), lax.axis_size("sp")
    rank, plane = lax.axis_index("fsdp"), lax.axis_index("sp")
    rows, model_width = hidden_in.shape
    tokens = ranks * rows
    own_heads = w_qkv.shape[0] // HEAD_DIM
    local_heads = HEADS // ranks

    thin = q_gain.shape[0]
    spread = jnp.zeros((2, HEAD_DIM), attn_gain.dtype)
    spread = lax.dynamic_update_slice(
        spread, jnp.stack([q_gain, k_gain]), (jnp.int32(0), rank * thin)
    )
    own_gains = jnp.concatenate(
        [
            attn_gain.reshape(-1, HEAD_DIM),
            ffn_gain.reshape(-1, HEAD_DIM),
            spread,
            jnp.zeros((2, HEAD_DIM), attn_gain.dtype),
        ],
        axis=0,
    ).astype(jnp.float32)
    (
        query,
        kv,
        plane_grad,
        gathered,
        normed_a,
        projected,
        gate_logit,
        attn_scale,
        ffn_scale,
        head_scale,
        cosine,
        sine,
    ) = front(lengths, hidden_in, own_gains, w_qkv, w_head_gate, grad_out, 0)
    attended, total, gated = attend(lengths, query, kv, gate_logit, rows)
    plane_b, line_blocks, down_part, middle, grad_middle, grad_ffn_gain_local, plane_mid, grad_gated, acts = middle_layer(
        gated.reshape(ranks, rows, -1),
        w_out,
        hidden_in,
        ffn_scale,
        plane_grad,
        w_gate,
        w_up,
        w_down,
        2,
    )
    grad_gated = grad_gated.reshape(tokens, -1)
    out_part = mat_tn(gated, plane_mid.reshape(tokens, model_width)).astype(jnp.bfloat16)
    reduced = lax.psum_scatter(out_part, "sp", scatter_dimension=0, tiled=True)
    grad_query, grad_kv, gate_grad = attend_back(
        lengths, query, kv, gate_logit, attended, total, grad_gated, rows
    )
    back, first_plane = return_heads(grad_query, grad_kv, line_blocks, 6)
    grad_a_part, qkv_part, gate_rows, attn_terms, head_terms, second_grad = projection_back(
        back,
        projected,
        cosine,
        sine,
        normed_a,
        gathered,
        gate_grad,
        w_qkv,
        w_head_gate,
        head_scale,
        line_blocks,
        8,
    )
    reduced, grad_a_part = lax.optimization_barrier((reduced, grad_a_part))
    out_sum = lax.all_gather(reduced, "sp", axis=0, tiled=True)
    grad_in, gain_sums = scatter_gains(
        grad_a_part,
        attn_terms,
        grad_ffn_gain_local,
        head_terms,
        hidden_in,
        attn_scale,
        grad_middle,
        7,
    )
    out_sum, gain_sums = lax.optimization_barrier((out_sum, gain_sums))
    grad_w_out = out_sum.astype(jnp.float32)
    grad_w_gate, grad_w_up, grad_w_down, hidden_out, gain_total, grad_w_head_gate, qkv_total = feed_weights(
        plane_b,
        plane_grad,
        acts,
        line_blocks,
        first_plane,
        second_grad,
        down_part,
        middle,
        gain_sums,
        gate_rows,
        qkv_part,
        w_gate,
        w_up,
        w_down,
        4,
    )
    grad_w_qkv = qkv_total.astype(jnp.float32)
    grad_attn_gain = gain_total[:2].reshape(-1)
    grad_ffn_gain = gain_total[2:4].reshape(-1)
    grad_q_gain = lax.dynamic_slice_in_dim(gain_total[4], rank * thin, thin)
    grad_k_gain = lax.dynamic_slice_in_dim(gain_total[5], rank * thin, thin)
    return (
        hidden_out,
        grad_in,
        grad_attn_gain,
        grad_w_qkv,
        grad_w_head_gate,
        grad_q_gain,
        grad_k_gain,
        grad_w_out,
        grad_ffn_gain,
        grad_w_gate,
        grad_w_up,
        grad_w_down,
    )


def solution(mesh):
    planar = mesh.shape["fsdp"] == 8 and mesh.shape["sp"] == 4
    return jax.shard_map(
        local_planes if planar else local,
        mesh=mesh,
        in_specs=(
            P(("fsdp", "sp"), None),
            P(("fsdp", "sp"), None),
            P(),
            P("fsdp"),
            P("fsdp", None),
            P("fsdp", None),
            P("fsdp"),
            P("fsdp"),
            P("fsdp", None),
            P("fsdp"),
            P("fsdp", None),
            P("fsdp", None),
            P("fsdp", None),
        ),
        out_specs=(
            P(("fsdp", "sp"), None),
            P(("fsdp", "sp"), None),
            P("fsdp"),
            P("fsdp", None),
            P("fsdp", None),
            P("fsdp"),
            P("fsdp"),
            P("fsdp", None),
            P("fsdp"),
            P("fsdp", None),
            P("fsdp", None),
            P("fsdp", None),
        ),
        check_vma=False,
    )
```

```python
import functools
import math

import jax
import jax.numpy as jnp
from jax import lax
from jax.experimental import pallas as pl
from jax.experimental.pallas import tpu as pltpu
from jax.sharding import PartitionSpec as P

HEADS = 16
KV_HEADS = 8
HEAD_DIM = 128


EPS = 1e-06
ROPE_BASE = 1000000.0


def mat_nt(factor, others):
    return lax.dot_general(
        factor, others, (((1,), (1,)), ((), ())), preferred_element_type=jnp.float32
    )


def mat_tn(factor, others):
    return lax.dot_general(
        factor, others, (((0,), (0,)), ((), ())), preferred_element_type=jnp.float32
    )


def inv_rms(values):
    return lax.rsqrt(jnp.mean(values * values, axis=-1, keepdims=True) + EPS)


def norm_back(grad_norm, values, inverse, scaling):
    scaled = grad_norm * scaling
    cubed = inverse * inverse * inverse
    return inverse * scaled - values * cubed * jnp.mean(scaled * values, axis=-1, keepdims=True)


def item_starts(token_index, lengths):
    ends = jnp.cumsum(lengths)
    starts = ends - lengths
    inside = (token_index[:, None] >= starts[None, :]) & (token_index[:, None] < ends[None, :])
    return jnp.sum(jnp.where(inside, starts[None, :], 0), axis=1)


def rope_tables(position):
    half_dim = HEAD_DIM // 2
    freq_steps = jnp.arange(half_dim, dtype=jnp.float32)
    frequency = jnp.exp(-math.log(ROPE_BASE) * 2.0 * freq_steps / HEAD_DIM)
    angles = position.astype(jnp.float32)[:, None] * frequency[None, :]
    return (jnp.cos(angles)[:, None, :], jnp.sin(angles)[:, None, :])


def rotate(values, cosine, sine):
    half_dim = values.shape[-1] // 2
    lower = values[..., :half_dim]
    upper = values[..., half_dim:]
    return jnp.concatenate([lower * cosine - upper * sine, upper * cosine + lower * sine], axis=-1)


def rotate_back(grad_rot, cosine, sine):
    half_dim = grad_rot.shape[-1] // 2
    lower = grad_rot[..., :half_dim]
    upper = grad_rot[..., half_dim:]
    return jnp.concatenate([lower * cosine + upper * sine, upper * cosine - lower * sine], axis=-1)


def local(
    hidden_in,
    grad_out,
    lengths,
    attn_gain,
    w_qkv,
    w_head_gate,
    q_gain,
    k_gain,
    w_out,
    ffn_gain,
    w_gate,
    w_up,
    w_down,
):
    fsdp_count = lax.axis_size("fsdp")
    sp_count = lax.axis_size("sp")
    fsdp_rank = lax.axis_index("fsdp")
    sp_rank = lax.axis_index("sp")
    tok_rows = hidden_in.shape[0]
    model_width = hidden_in.shape[1]
    query_width = HEADS * HEAD_DIM
    kv_width = KV_HEADS * HEAD_DIM
    local_kv = KV_HEADS // sp_count
    head_group = HEADS // KV_HEADS
    score_scale = HEAD_DIM ** (-0.5)
    qkv_full, out_full, gate_full, attn_gain_full, q_gain_full, k_gain_full, ffn_gain_full = (
        lax.all_gather(w_qkv, "fsdp", axis=0, tiled=True),
        lax.all_gather(w_out, "fsdp", axis=0, tiled=True),
        lax.all_gather(w_head_gate, "fsdp", axis=0, tiled=True),
        lax.all_gather(attn_gain, "fsdp", axis=0, tiled=True),
        lax.all_gather(q_gain, "fsdp", axis=0, tiled=True),
        lax.all_gather(k_gain, "fsdp", axis=0, tiled=True),
        lax.all_gather(ffn_gain, "fsdp", axis=0, tiled=True),
    )
    attn_scale = attn_gain_full.astype(jnp.float32)
    query_scale = q_gain_full.astype(jnp.float32)
    key_scale = k_gain_full.astype(jnp.float32)
    ffn_scale = ffn_gain_full.astype(jnp.float32)
    token_first = (fsdp_rank * sp_count + sp_rank) * tok_rows
    own_tokens = token_first + jnp.arange(tok_rows, dtype=jnp.int32)
    cosine, sine = rope_tables(own_tokens - item_starts(own_tokens, lengths))
    inputs = hidden_in.astype(jnp.float32)
    inv_first = inv_rms(inputs)
    normed_a = (inputs * inv_first * attn_scale).astype(jnp.bfloat16)
    projected = mat_nt(normed_a, qkv_full)
    gate_logit = mat_nt(normed_a, gate_full)
    q_raw = projected[:, :query_width].reshape(tok_rows, HEADS, HEAD_DIM)
    k_raw = projected[:, query_width : query_width + kv_width].reshape(tok_rows, KV_HEADS, HEAD_DIM)
    q_inv = inv_rms(q_raw)
    k_inv = inv_rms(k_raw)
    query = (
        rotate(q_raw * q_inv * query_scale, cosine, sine)
        .reshape(tok_rows, query_width)
        .astype(jnp.bfloat16)
    )
    keys = (
        rotate(k_raw * k_inv * key_scale, cosine, sine)
        .reshape(tok_rows, kv_width)
        .astype(jnp.bfloat16)
    )
    values = projected[:, query_width + kv_width :].astype(jnp.bfloat16)
    query_heads, key_heads, value_heads = (
        lax.all_to_all(query, "sp", split_axis=1, concat_axis=0, tiled=True),
        lax.all_to_all(keys, "sp", split_axis=1, concat_axis=0, tiled=True),
        lax.all_to_all(values, "sp", split_axis=1, concat_axis=0, tiled=True),
    )
    key_all, value_all = (
        lax.all_gather(key_heads, "fsdp", axis=0, tiled=True),
        lax.all_gather(value_heads, "fsdp", axis=0, tiled=True),
    )
    span_rows = query_heads.shape[0]
    span_first = fsdp_rank * span_rows
    span_tokens = span_first + jnp.arange(span_rows, dtype=jnp.int32)
    span_starts = item_starts(span_tokens, lengths)
    query_four = query_heads.reshape(span_rows, local_kv, head_group, HEAD_DIM)
    key_total = key_all.shape[0]
    key_block = min(1024, key_total)
    block_count = key_total // key_block
    key_blocks = key_all.reshape(block_count, key_block, local_kv, HEAD_DIM)
    value_blocks = value_all.reshape(block_count, key_block, local_kv, HEAD_DIM)
    block_firsts = jnp.arange(block_count, dtype=jnp.int32) * key_block
    lowest_key = span_starts[0]
    highest_key = span_first + span_rows - 1

    def needed(block_first):
        return (block_first <= highest_key) & (block_first + key_block - 1 >= lowest_key)

    def block_weights(key_piece, block_first):
        scores = (
            jnp.einsum("qkgd,jkd->kgqj", query_four, key_piece, preferred_element_type=jnp.float32)
            * score_scale
        )
        columns = block_first + jnp.arange(key_block, dtype=jnp.int32)
        allowed = (columns[None, :] <= span_tokens[:, None]) & (
            columns[None, :] >= span_starts[:, None]
        )
        return jnp.where(allowed[None, None], jnp.exp(scores), 0.0)

    def forward_step(running, pieces):
        key_piece, value_piece, block_first = pieces

        def forward_compute(current):
            totals, unnormed = current
            weights = block_weights(key_piece, block_first)
            totals = totals + jnp.sum(weights, axis=3)
            unnormed = unnormed + jnp.einsum(
                "kgqj,jkd->qkgd",
                weights.astype(jnp.bfloat16),
                value_piece,
                preferred_element_type=jnp.float32,
            )
            return (totals, unnormed)

        return (
            lax.cond(needed(block_first), forward_compute, lambda current: current, running),
            None,
        )

    start_state = (
        jnp.zeros((local_kv, head_group, span_rows), jnp.float32),
        jnp.zeros((span_rows, local_kv, head_group, HEAD_DIM), jnp.float32),
    )
    scanned = lax.scan(forward_step, start_state, (key_blocks, value_blocks, block_firsts))[0]
    totals, unnormed = scanned
    totals_rows = jnp.transpose(totals, (2, 0, 1))[..., None]
    attended_heads = unnormed / totals_rows
    attended_send = attended_heads.reshape(span_rows, local_kv * head_group * HEAD_DIM).astype(
        jnp.bfloat16
    )
    returned = lax.all_to_all(attended_send, "sp", split_axis=0, concat_axis=1, tiled=True)
    gate_prob = jax.nn.sigmoid(gate_logit)
    attended_tok = returned.astype(jnp.float32).reshape(tok_rows, HEADS, HEAD_DIM)
    gated = (
        (attended_tok * gate_prob[:, :, None]).reshape(tok_rows, query_width).astype(jnp.bfloat16)
    )
    middle = inputs + jnp.dot(gated, out_full, preferred_element_type=jnp.float32)
    inv_second = inv_rms(middle)
    normed_b = (middle * inv_second * ffn_scale).astype(jnp.bfloat16)
    gate_piece = lax.all_gather(w_gate, "fsdp", axis=0, tiled=True)
    up_piece = lax.all_gather(w_up, "fsdp", axis=0, tiled=True)
    down_piece = lax.all_gather(w_down, "fsdp", axis=0, tiled=True)
    gate_pre = mat_nt(normed_b, gate_piece)
    up_pre = mat_nt(normed_b, up_piece)
    hidden = (jax.nn.silu(gate_pre) * up_pre).astype(jnp.bfloat16)
    ffn_part = jnp.dot(hidden, down_piece, preferred_element_type=jnp.float32)
    hidden_out = (middle + ffn_part).astype(jnp.bfloat16)
    gate_piece = lax.all_gather(w_gate, "fsdp", axis=0, tiled=True)
    up_piece = lax.all_gather(w_up, "fsdp", axis=0, tiled=True)
    down_piece = lax.all_gather(w_down, "fsdp", axis=0, tiled=True)
    gate_pre = mat_nt(normed_b, gate_piece)
    up_pre = mat_nt(normed_b, up_piece)
    sigma = jax.nn.sigmoid(gate_pre)
    swish = gate_pre * sigma
    hidden = (swish * up_pre).astype(jnp.bfloat16)
    grad_hidden = mat_nt(grad_out, down_piece)
    grad_gate = (grad_hidden * up_pre * sigma * (1.0 + gate_pre * (1.0 - sigma))).astype(
        jnp.bfloat16
    )
    grad_up = (grad_hidden * swish).astype(jnp.bfloat16)
    grad_acc = jnp.dot(grad_gate, gate_piece, preferred_element_type=jnp.float32) + jnp.dot(
        grad_up, up_piece, preferred_element_type=jnp.float32
    )
    grad_ffn_gain_local = jnp.sum(grad_acc * middle * inv_second, axis=0)
    grad_middle = grad_out.astype(jnp.float32) + norm_back(grad_acc, middle, inv_second, ffn_scale)
    grad_mid_b = grad_middle.astype(jnp.bfloat16)
    grad_gated = mat_nt(grad_mid_b, out_full).reshape(tok_rows, HEADS, HEAD_DIM)
    grad_attended = (
        (grad_gated * gate_prob[:, :, None]).reshape(tok_rows, query_width).astype(jnp.bfloat16)
    )
    gate_grad = (jnp.sum(grad_gated * attended_tok, axis=2) * gate_prob * (1.0 - gate_prob)).astype(
        jnp.bfloat16
    )
    grad_heads = lax.all_to_all(grad_attended, "sp", split_axis=1, concat_axis=0, tiled=True)
    grad_four = grad_heads.astype(jnp.float32).reshape(span_rows, local_kv, head_group, HEAD_DIM)
    grad_scaled = (grad_four / totals_rows).astype(jnp.bfloat16)
    delta_rows = jnp.sum(grad_four * attended_heads, axis=3) / totals_rows[..., 0]
    delta_heads = jnp.transpose(delta_rows, (1, 2, 0))

    def backward_step(grad_query, pieces):
        key_piece, value_piece, block_first = pieces

        def backward_compute(current):
            weights = block_weights(key_piece, block_first)
            grad_prob = jnp.einsum(
                "qkgd,jkd->kgqj", grad_scaled, value_piece, preferred_element_type=jnp.float32
            )
            grad_score = (weights * (grad_prob - delta_heads[..., None])).astype(jnp.bfloat16)
            current = (
                current
                + jnp.einsum(
                    "kgqj,jkd->qkgd", grad_score, key_piece, preferred_element_type=jnp.float32
                )
                * score_scale
            )
            grad_key = (
                jnp.einsum(
                    "kgqj,qkgd->jkd", grad_score, query_four, preferred_element_type=jnp.float32
                )
                * score_scale
            )
            grad_value = jnp.einsum(
                "kgqj,qkgd->jkd",
                weights.astype(jnp.bfloat16),
                grad_scaled,
                preferred_element_type=jnp.float32,
            )
            return (current, (grad_key, grad_value))

        def skip(current):
            nothing = jnp.zeros((key_block, local_kv, HEAD_DIM), jnp.float32)
            return (current, (nothing, nothing))

        return lax.cond(needed(block_first), backward_compute, skip, grad_query)

    grad_query, key_value_grads = lax.scan(
        backward_step,
        jnp.zeros((span_rows, local_kv, head_group, HEAD_DIM), jnp.float32),
        (key_blocks, value_blocks, block_firsts),
    )
    key_grads, value_grads = key_value_grads
    key_sum, value_sum = (
        lax.psum_scatter(
            key_grads.reshape(key_total, local_kv * HEAD_DIM),
            "fsdp",
            scatter_dimension=0,
            tiled=True,
        ),
        lax.psum_scatter(
            value_grads.reshape(key_total, local_kv * HEAD_DIM),
            "fsdp",
            scatter_dimension=0,
            tiled=True,
        ),
    )
    query_send = grad_query.reshape(span_rows, local_kv * head_group * HEAD_DIM).astype(
        jnp.bfloat16
    )
    back_query, back_key, back_value = (
        lax.all_to_all(query_send, "sp", split_axis=0, concat_axis=1, tiled=True),
        lax.all_to_all(key_sum.astype(jnp.bfloat16), "sp", split_axis=0, concat_axis=1, tiled=True),
        lax.all_to_all(
            value_sum.astype(jnp.bfloat16), "sp", split_axis=0, concat_axis=1, tiled=True
        ),
    )
    grad_qn = rotate_back(
        back_query.astype(jnp.float32).reshape(tok_rows, HEADS, HEAD_DIM), cosine, sine
    )
    grad_kn = rotate_back(
        back_key.astype(jnp.float32).reshape(tok_rows, KV_HEADS, HEAD_DIM), cosine, sine
    )
    grad_q_gain_local = jnp.sum(grad_qn * q_raw * q_inv, axis=(0, 1))
    grad_k_gain_local = jnp.sum(grad_kn * k_raw * k_inv, axis=(0, 1))
    grad_q_raw = norm_back(grad_qn, q_raw, q_inv, query_scale).reshape(tok_rows, query_width)
    grad_k_raw = norm_back(grad_kn, k_raw, k_inv, key_scale).reshape(tok_rows, kv_width)
    grad_proj = jnp.concatenate(
        [grad_q_raw.astype(jnp.bfloat16), grad_k_raw.astype(jnp.bfloat16), back_value], axis=1
    )
    grad_normed_a = jnp.dot(grad_proj, qkv_full, preferred_element_type=jnp.float32) + jnp.dot(
        gate_grad, gate_full, preferred_element_type=jnp.float32
    )
    grad_attn_gain_local = jnp.sum(grad_normed_a * inputs * inv_first, axis=0)
    grad_in = grad_middle + norm_back(grad_normed_a, inputs, inv_first, attn_scale)
    qkv_rows = w_qkv.shape[0]
    out_rows = w_out.shape[0]
    gate_rows = w_head_gate.shape[0]
    block_rows = qkv_rows + out_rows + gate_rows + 3
    small_rows = jnp.stack(
        [
            grad_attn_gain_local,
            grad_ffn_gain_local,
            jnp.concatenate(
                [
                    grad_q_gain_local,
                    grad_k_gain_local,
                    jnp.zeros((model_width - 2 * HEAD_DIM,), jnp.float32),
                ]
            ),
        ],
        axis=0,
    )
    ffn_partial = lax.psum_scatter(
        jnp.concatenate(
            [mat_tn(grad_gate, normed_b), mat_tn(grad_up, normed_b), mat_tn(hidden, grad_out)],
            axis=1,
        ).astype(jnp.bfloat16),
        "fsdp",
        scatter_dimension=0,
        tiled=True,
    ).astype(jnp.float32)
    proj_split = grad_proj.reshape(tok_rows, fsdp_count, qkv_rows)
    gated_split = gated.reshape(tok_rows, fsdp_count, out_rows)
    gate_split = gate_grad.reshape(tok_rows, fsdp_count, gate_rows)
    owners = block_rows * lax.axis_size("fsdp") // block_rows
    qkv_term = jnp.einsum("tor,td->ord", proj_split, normed_a, preferred_element_type=jnp.float32)
    out_term = jnp.einsum(
        "tor,td->ord", gated_split, grad_mid_b, preferred_element_type=jnp.float32
    )
    gate_term = jnp.einsum("tor,td->ord", gate_split, normed_a, preferred_element_type=jnp.float32)
    small_term = jnp.broadcast_to(small_rows[None], (owners, 3, model_width))
    joined = jnp.concatenate([qkv_term, out_term, gate_term, small_term], axis=1)
    attn_partial = lax.psum_scatter(
        joined.reshape(owners * block_rows, model_width), "fsdp", scatter_dimension=0, tiled=True
    )
    ffn_total, attn_total = lax.psum((ffn_partial, attn_partial), "sp")
    grad_w_gate = ffn_total[:, :model_width]
    grad_w_up = ffn_total[:, model_width : 2 * model_width]
    grad_w_down = ffn_total[:, 2 * model_width :]
    grad_w_qkv = attn_total[:qkv_rows]
    grad_w_out = attn_total[qkv_rows : qkv_rows + out_rows]
    grad_w_head_gate = attn_total[qkv_rows + out_rows : qkv_rows + out_rows + gate_rows]
    gain_sums = attn_total[qkv_rows + out_rows + gate_rows :]
    gain_part = model_width // fsdp_count
    head_part = HEAD_DIM // fsdp_count
    grad_attn_gain = lax.dynamic_slice_in_dim(gain_sums[0], fsdp_rank * gain_part, gain_part)
    grad_ffn_gain = lax.dynamic_slice_in_dim(gain_sums[1], fsdp_rank * gain_part, gain_part)
    grad_q_gain = lax.dynamic_slice_in_dim(gain_sums[2], fsdp_rank * head_part, head_part)
    grad_k_gain = lax.dynamic_slice_in_dim(
        gain_sums[2], HEAD_DIM + fsdp_rank * head_part, head_part
    )
    return (
        hidden_out,
        grad_in,
        grad_attn_gain,
        grad_w_qkv,
        grad_w_head_gate,
        grad_q_gain,
        grad_k_gain,
        grad_w_out,
        grad_ffn_gain,
        grad_w_gate,
        grad_w_up,
        grad_w_down,
    )


MESH = pl.DeviceIdType.MESH
VMEM_LIMIT = 62 * 1024 * 1024


def peer_copy(src, dst, send_sem, recv_sem, rank, plane):
    return pltpu.make_async_remote_copy(
        src_ref=src,
        dst_ref=dst,
        send_sem=send_sem,
        recv_sem=recv_sem,
        device_id=(rank, plane),
        device_id_type=MESH,
    )


def greet(peers):
    barrier = pltpu.get_barrier_semaphore()
    for peer in peers:
        pl.semaphore_signal(barrier, inc=1, device_id=peer, device_id_type=MESH)
    pl.semaphore_wait(barrier, len(peers))


def scatter_gains_kernel(
    p_ref, attn_ref, ffn_ref, head_ref, x_ref, scale_ref, dmid_ref, o_ref, so_ref, parts, small_buf, grad, small_send, small_recv, near_buf, out_buf, far_buf, sib_send, sib_recv, send_sem, recv_sem
):
    rank, plane = lax.axis_index("fsdp"), lax.axis_index("sp")
    ranks = p_ref.shape[0]
    greet([(rank ^ k, plane) for k in range(1, 8)])
    for i in range(4):
        scatter_near(p_ref, i, near_buf, sib_send, sib_recv).start()
    for r in range(ranks):
        for i in range(2):
            columns = slice((2 * r + i) * HEAD_DIM, (2 * r + i + 1) * HEAD_DIM)
            parts[r, i : i + 1] = attn_ref[:, columns]
            parts[r, 2 + i : 3 + i] = ffn_ref[:, columns]
        parts[r, 4:5] = jnp.where(rank < ranks // 2, head_ref[...], 0.0)
        parts[r, 5:6] = jnp.where(
            (rank >= ranks // 2) & (rank < 3 * ranks // 4), head_ref[...], 0.0
        )
        parts[r, 6:8] = jnp.zeros((2, HEAD_DIM), jnp.float32)
    small = []
    for k in range(1, 8):
        copy = peer_copy(
            parts.at[rank ^ k],
            small_buf.at[k - 1],
            small_send.at[k - 1],
            small_recv.at[k - 1],
            rank ^ k,
            plane,
        )
        copy.start()
        small.append(copy)
    sems = (send_sem, recv_sem)

    def block_of(i):
        scatter_near(p_ref, i, near_buf, sib_send, sib_recv).wait_recv()
        return p_ref[rank ^ SCATTER_ORDER[i]].astype(jnp.float32) + near_buf[i].astype(jnp.float32)

    def own_block():
        grad[...] = block_of(3)

    relay_blocks(out_buf, far_buf, sems, block_of, own_block)
    total = parts[rank]
    for k in range(1, 8):
        small[k - 1].wait()
        total = total + small_buf[k - 1]
    so_ref[...] = total
    grad[...] = relay_sum(out_buf, far_buf, sems, grad[...])
    inputs = x_ref[...].astype(jnp.float32)
    o_ref[...] = dmid_ref[...] + norm_back(grad[...], inputs, inv_rms(inputs), scale_ref[...])
    for i in range(4):
        scatter_near(p_ref, i, near_buf, sib_send, sib_recv).wait_send()
    relay_sent(out_buf, far_buf, sems)


SCATTER_ORDER = (6, 2, 4, 0)


def scatter_far(i, out_buf, far_buf, send_sem, recv_sem):
    rank, plane = lax.axis_index("fsdp"), lax.axis_index("sp")
    return peer_copy(
        out_buf.at[i],
        far_buf.at[i],
        send_sem.at[i],
        recv_sem.at[i],
        rank ^ SCATTER_ORDER[i],
        plane,
    )


def scatter_near(p_ref, i, near_buf, sib_send, sib_recv):
    rank, plane = lax.axis_index("fsdp"), lax.axis_index("sp")
    return peer_copy(
        p_ref.at[rank ^ 1 ^ SCATTER_ORDER[i]],
        near_buf.at[i],
        sib_send.at[i],
        sib_recv.at[i],
        rank ^ 1,
        plane,
    )


def relay_copy(i, out_buf, far_buf, send_sem, recv_sem):
    rank, plane = lax.axis_index("fsdp"), lax.axis_index("sp")
    half = out_buf.shape[1] // 2
    top, low = pl.ds(0, half), pl.ds(half, half)
    slot, part, to = (
        (0, top, 2),
        (0, low, 4),
        (1, top, 2),
        (2, low, 4),
        (1, low, 2),
        (2, top, 4),
    )[i]
    return peer_copy(
        out_buf.at[slot, part],
        far_buf.at[slot, part],
        send_sem.at[i],
        recv_sem.at[i],
        rank ^ to,
        plane,
    )


def relay_blocks(out_buf, far_buf, sems, block_of, own_block):
    half = out_buf.shape[1] // 2
    copies = [relay_copy(i, out_buf, far_buf, *sems) for i in range(6)]
    for slot, ready in ((0, (0, 1)), (1, (2,)), (2, (3,))):
        out_buf[slot] = block_of(slot).astype(out_buf.dtype)
        for i in ready:
            copies[i].start()
    own_block()
    for arrived, slot, onward, rows in ((0, 2, 5, slice(0, half)), (1, 1, 4, slice(half, 2 * half))):
        copies[arrived].wait_recv()
        joined = out_buf[slot, rows].astype(jnp.float32) + far_buf[0, rows].astype(jnp.float32)
        out_buf[slot, rows] = joined.astype(out_buf.dtype)
        copies[onward].start()


def relay_sum(out_buf, far_buf, sems, total):
    for i in (2, 3, 5, 4):
        relay_copy(i, out_buf, far_buf, *sems).wait_recv()
    return total + far_buf[1].astype(jnp.float32) + far_buf[2].astype(jnp.float32)


def relay_sent(out_buf, far_buf, sems):
    for i in range(6):
        relay_copy(i, out_buf, far_buf, *sems).wait_send()


def scatter_scratch(rows, width, dtype):
    return [
        pltpu.VMEM((4, rows, width), dtype),
        pltpu.VMEM((3, rows, width), dtype),
        pltpu.VMEM((3, rows, width), dtype),
        pltpu.SemaphoreType.DMA((4,)),
        pltpu.SemaphoreType.DMA((4,)),
        pltpu.SemaphoreType.DMA((3,)),
        pltpu.SemaphoreType.DMA((3,)),
    ]


def scatter_gains(p, attn, ffn, head, x, scale, grad_middle, collective_id):
    ranks, rows, width = p.shape
    vmem = pl.BlockSpec(memory_space=pltpu.VMEM)
    small = (8, HEAD_DIM)
    return pl.pallas_call(
        scatter_gains_kernel,
        out_shape=(
            jax.ShapeDtypeStruct((rows, width), jnp.float32),
            jax.ShapeDtypeStruct(small, jnp.float32),
        ),
        in_specs=[vmem] * 7,
        out_specs=(vmem, vmem),
        scratch_shapes=[
            pltpu.VMEM((ranks,) + small, jnp.float32),
            pltpu.VMEM((7,) + small, jnp.float32),
            pltpu.VMEM((rows, width), jnp.float32),
            pltpu.SemaphoreType.DMA((7,)),
            pltpu.SemaphoreType.DMA((7,)),
        ]
        + scatter_scratch(rows, width, p.dtype)[:-2]
        + [pltpu.SemaphoreType.DMA((6,)), pltpu.SemaphoreType.DMA((6,))],
        compiler_params=pltpu.CompilerParams(
            collective_id=collective_id, has_side_effects=True, vmem_limit_bytes=VMEM_LIMIT
        ),
        name="scatter_gains",
    )(p, attn, ffn, head, x, scale, grad_middle)


def projection_back_kernel(
    back_ref, raw_ref, cos_ref, sin_ref, xa_ref, x_ref, dgate_ref, w_ref, wg_ref, head_ref, blocks_ref, dxa_ref, qkv_ref, gate_ref, attn_ref, terms_ref, next_ref, sums, ag_send, ag_recv, own_sem
):
    rank, plane = lax.axis_index("fsdp"), lax.axis_index("sp")
    block = blocks_ref.at[0, 0]
    gather = (next_ref, ag_send, ag_recv)
    own = pltpu.make_async_copy(block, next_ref.at[rank], own_sem)
    group, rows, width = back_ref.shape

    @pl.when(pl.program_id(0) == 0)
    def _():
        greet([(rank ^ k, plane) for k in (1, 2, 4)])
        own.start()
        gather_start(*gather, own=block)
        for ref in (sums, gate_ref, attn_ref, terms_ref):
            ref[...] = jnp.zeros_like(ref)

    @pl.when(pl.program_id(0) == 2)
    def _():
        gather_pass(*gather, NEIGHBOURS_FIRST[:2])

    @pl.when(pl.program_id(0) == 3)
    def _():
        gather_pass(*gather, NEIGHBOURS_FIRST[2:])

    cosine, sine = cos_ref[...], sin_ref[...]
    columns = []
    for m in range(group):
        back = back_ref[m]
        grad = back.astype(jnp.float32)
        turned = grad * cosine - pltpu.roll(grad, width // 2, 1) * sine
        raw = raw_ref[:, m * width : (m + 1) * width]
        inverse = inv_rms(raw)
        terms_ref[...] += jnp.sum(turned * raw * inverse, axis=0, keepdims=True)
        grad_raw = norm_back(turned, raw, inverse, head_ref[...])
        columns.append(jnp.where(rank >= 6, grad, grad_raw).astype(jnp.bfloat16))
    grad_proj = jnp.concatenate(columns, axis=1)
    grad_a = jnp.dot(grad_proj, w_ref[...], preferred_element_type=jnp.float32)
    normed = xa_ref[...].reshape(rows, -1)
    normed32 = normed.astype(jnp.float32)
    for head in range(dgate_ref.shape[0]):
        gate = dgate_ref[head].astype(jnp.float32)
        grad_a = grad_a + gate * wg_ref[head : head + 1].astype(jnp.float32)
        gate_ref[head : head + 1] += jnp.sum(gate * normed32, axis=0, keepdims=True)
    inputs = x_ref[...].reshape(rows, -1).astype(jnp.float32)
    attn_ref[...] += jnp.sum(grad_a * inputs * inv_rms(inputs), axis=0, keepdims=True)
    dxa_ref[...] = grad_a.astype(jnp.bfloat16).reshape(dxa_ref.shape)
    sums[...] += mat_tn(grad_proj, normed)

    @pl.when(pl.program_id(0) == pl.num_programs(0) - 1)
    def _():
        qkv_ref[...] = sums[...].astype(jnp.bfloat16)
        gather_pass(*gather, DIAGONAL)
        gather_wait(*gather, FROM_SIBLING)
        gather_sent(*gather)
        own.wait()


def projection_back(back, raw, cosine, sine, normed, inputs, gate_grad, w_qkv, w_head_gate, head_scale, line_blocks, collective_id):
    ranks, rows, model_width = normed.shape
    group, tokens, width = back.shape
    pair = 2 * rows
    blocks = pl.BlockSpec((2, rows, model_width), lambda i: (i, 0, 0))
    thin = pl.BlockSpec((pair, width), lambda i: (i, 0))
    hbm = pl.BlockSpec(memory_space=pl.ANY)
    heads = gate_grad.shape[0]

    def still(shape):
        return pl.BlockSpec(shape, lambda i: (0, 0))

    return pl.pallas_call(
        projection_back_kernel,
        grid=(tokens // pair,),
        in_specs=[
            pl.BlockSpec((group, pair, width), lambda i: (0, i, 0)),
            pl.BlockSpec((pair, group * width), lambda i: (i, 0)),
            thin,
            thin,
            blocks,
            blocks,
            pl.BlockSpec((heads, pair, 1), lambda i: (0, i, 0)),
            still(w_qkv.shape),
            still(w_head_gate.shape),
            still(head_scale.shape),
            hbm,
        ],
        out_specs=(
            blocks,
            still(w_qkv.shape),
            still(w_head_gate.shape),
            still((1, model_width)),
            still((1, width)),
            hbm,
        ),
        out_shape=(
            jax.ShapeDtypeStruct(normed.shape, jnp.bfloat16),
            jax.ShapeDtypeStruct(w_qkv.shape, jnp.bfloat16),
            jax.ShapeDtypeStruct(w_head_gate.shape, jnp.float32),
            jax.ShapeDtypeStruct((1, model_width), jnp.float32),
            jax.ShapeDtypeStruct((1, width), jnp.float32),
            jax.ShapeDtypeStruct(normed.shape, line_blocks.dtype),
        ),
        scratch_shapes=[
            pltpu.VMEM(w_qkv.shape, jnp.float32),
            pltpu.SemaphoreType.DMA((GATHER_COPIES,)),
            pltpu.SemaphoreType.DMA((GATHER_COPIES,)),
            pltpu.SemaphoreType.DMA,
        ],
        compiler_params=pltpu.CompilerParams(
            collective_id=collective_id, has_side_effects=True, vmem_limit_bytes=VMEM_LIMIT
        ),
        name="projection_back",
    )(back, raw, cosine, sine, normed, inputs, gate_grad, w_qkv, w_head_gate, head_scale, line_blocks)


GATHER_COPIES = 13


def gather_copy(buf, i, send_sem, recv_sem, own=None):
    rank, plane = lax.axis_index("fsdp"), lax.axis_index("sp")
    rows = buf.shape[1]
    top, low = pl.ds(0, rows // 2), pl.ds(rows // 2, rows // 2)
    block, part, to = (
        (0, top, 2),
        (0, low, 2),
        (0, low, 4),
        (0, top, 4),
        (2, top, 4),
        (4, low, 2),
        (0, pl.ds(0, rows), 1),
        (2, top, 1),
        (2, low, 1),
        (4, low, 1),
        (4, top, 1),
        (6, top, 1),
        (6, low, 1),
    )[i]
    piece = buf.at[rank ^ block, part]
    source = piece if own is None or block else own.at[part]
    return peer_copy(source, piece, send_sem.at[i], recv_sem.at[i], rank ^ to, plane)


def gather_start(buf, send_sem, recv_sem, own=None):
    for i in (6, 0, 2, 1, 3):
        gather_copy(buf, i, send_sem, recv_sem, own).start()


def gather_pass(buf, send_sem, recv_sem, pairs):
    for arrived, onward in pairs:
        gather_copy(buf, arrived, send_sem, recv_sem).wait_recv()
        for i in onward:
            gather_copy(buf, i, send_sem, recv_sem).start()


def gather_wait(buf, send_sem, recv_sem, copies):
    for i in copies:
        gather_copy(buf, i, send_sem, recv_sem).wait_recv()


def gather_sent(buf, send_sem, recv_sem):
    for i in range(GATHER_COPIES):
        gather_copy(buf, i, send_sem, recv_sem).wait_send()


NEIGHBOURS_FIRST = ((0, (4, 7)), (2, (5, 9)), (1, (8,)), (3, (10,)))
DIAGONAL = ((4, (11,)), (5, (12,)))
FROM_SIBLING = (6, 7, 8, 9, 10, 11, 12)


def greet_line(ranks, planes):
    rank, plane = lax.axis_index("fsdp"), lax.axis_index("sp")
    barrier = pltpu.get_barrier_semaphore()
    for k in range(1, ranks):
        pl.semaphore_signal(
            barrier, inc=1, device_id=(rank ^ k, plane), device_id_type=MESH
        )

    @pl.when(plane > 0)
    def _():
        pl.semaphore_signal(barrier, inc=1, device_id=(rank, plane - 1), device_id_type=MESH)

    @pl.when(plane < planes - 1)
    def _():
        pl.semaphore_signal(barrier, inc=1, device_id=(rank, plane + 1), device_id_type=MESH)

    lower = (plane > 0).astype(jnp.int32)
    upper = (plane < planes - 1).astype(jnp.int32)
    pl.semaphore_wait(barrier, ranks - 1 + lower + upper)


def line_sends(planes, plane, j, side):
    if side == 0:
        return (plane >= j) & (plane < planes - 1)
    return (plane + j <= planes - 1) & (plane > 0)


def unheads_kernel(planes, dq_ref, dkv_ref, gated_ref, pm_hbm, blocks_ref, n_ref, wout_ref, next_ref, pm, pm_sem, ag_send, ag_recv, own_sem2, line_out, line_in, done, own_sem, q_send, q_recv, kv_send, kv_recv, line_send, line_recv):
    rank, plane = lax.axis_index("fsdp"), lax.axis_index("sp")
    greet_line(8, planes)
    block = blocks_ref.at[1, 0]
    gather = (next_ref, ag_send, ag_recv)
    own_block = pltpu.make_async_copy(block, next_ref.at[rank], own_sem2)
    own_block.start()
    mid_load = pltpu.make_async_copy(pm_hbm, pm, pm_sem)
    mid_load.start()

    def q_copy(m, to):
        return peer_copy(dq_ref, n_ref.at[pl.ds(2 * m, 2)], q_send, q_recv.at[m], to, plane)

    def kv_copy(m, which, to):
        return peer_copy(done.at[which], n_ref.at[m], kv_send.at[which], kv_recv.at[m], to, plane)

    def q_local():
        return pltpu.make_async_copy(dq_ref, n_ref.at[pl.ds(0, 2)], own_sem)

    def kv_local(m, which):
        return pltpu.make_async_copy(done.at[which], n_ref.at[m], own_sem)

    @pl.when(rank == 0)
    def _():
        q_local().start()

    for m in range(2):
        @pl.when((rank % 2 == m) & (rank != 0))
        def _():
            q_copy(m, rank // 2).start()

    def step_copy(j, which, side):
        to = plane + 1 if side == 0 else plane - 1
        return peer_copy(
            line_out.at[side, j, which],
            line_in.at[side, j, which],
            line_send.at[side, j, which],
            line_recv.at[side, j, which],
            rank,
            to,
        )

    def sends(j, side):
        return plane < planes - 1 - j if side == 0 else plane > j

    def target(j, side):
        return planes - 1 - j if side == 0 else j

    gather_start(*gather, own=block)

    for j in range(planes - 1):
        for which in range(2):
            for side in range(2):
                inner = plane > 0 if side == 0 else plane < planes - 1

                @pl.when(sends(j, side) & inner)
                def _():
                    step_copy(j, which, side).wait_recv()
                    total = dkv_ref[target(j, side), which].astype(jnp.float32) + line_in[
                        side, j, which
                    ].astype(jnp.float32)
                    line_out[side, j, which] = total.astype(line_out.dtype)

                @pl.when(sends(j, side) & jnp.logical_not(inner))
                def _():
                    line_out[side, j, which] = dkv_ref[target(j, side), which]

                @pl.when(sends(j, side))
                def _():
                    step_copy(j, which, side).start()

        if j == 0:
            mid_load.wait()
            wout_ref[...] = mat_tn(gated_ref[...], pm[...].reshape(-1, pm.shape[-1])).astype(
                wout_ref.dtype
            )
        if j == 1:
            gather_pass(*gather, NEIGHBOURS_FIRST)
        if j == 2:
            gather_pass(*gather, DIAGONAL)

    for which in range(2):
        total = dkv_ref[plane, which].astype(jnp.float32)
        done32 = total
        for j in range(planes - 1):
            for side in range(2):
                @pl.when(plane == target(j, side))
                def _():
                    step_copy(j, which, side).wait_recv()
        low = jnp.minimum(planes - 1 - plane, planes - 2)
        high = jnp.minimum(plane, planes - 2)
        below = line_in[0, low, which].astype(jnp.float32)
        above = line_in[1, high, which].astype(jnp.float32)
        done32 = done32 + jnp.where(plane > 0, below, 0.0) + jnp.where(plane < planes - 1, above, 0.0)
        done[which] = done32.astype(done.dtype)
        first = 4 + 2 * which
        to = first + rank // 4
        for m in range(4):
            @pl.when((rank % 4 == m) & (to != rank))
            def _():
                kv_copy(m, which, to).start()

            @pl.when((rank % 4 == m) & (to == rank))
            def _():
                kv_local(m, which).start()

    gather_wait(*gather, FROM_SIBLING)
    gather_sent(*gather)
    own_block.wait()

    @pl.when(rank < 4)
    def _():
        for m in range(2):
            @pl.when(2 * rank + m != rank)
            def _():
                q_copy(m, 0).wait_recv()

            @pl.when(2 * rank + m == rank)
            def _():
                q_local().wait()

    for which in range(2):
        first = 4 + 2 * which

        @pl.when((rank == first) | (rank == first + 1))
        def _():
            for m in range(4):
                @pl.when(4 * (rank - first) + m != rank)
                def _():
                    kv_copy(m, which, 0).wait_recv()

                @pl.when(4 * (rank - first) + m == rank)
                def _():
                    kv_local(m, which).wait()

    @pl.when(rank != 0)
    def _():
        q_copy(0, 0).wait_send()

    for which in range(2):
        @pl.when(4 + 2 * which + rank // 4 != rank)
        def _():
            kv_copy(0, which, 0).wait_send()

    for j in range(planes - 1):
        for which in range(2):
            for side in range(2):
                @pl.when(sends(j, side))
                def _():
                    step_copy(j, which, side).wait_send()


def return_heads(grad_query, grad_kv, gated, plane_mid, line_blocks, collective_id):
    _, tokens, width = grad_query.shape
    planes = lax.axis_size("sp")
    ranks = lax.axis_size("fsdp")
    vmem = pl.BlockSpec(memory_space=pltpu.VMEM)
    hbm = pl.BlockSpec(memory_space=pl.ANY)
    return pl.pallas_call(
        functools.partial(unheads_kernel, planes),
        out_shape=(
            jax.ShapeDtypeStruct((4, tokens, width), grad_query.dtype),
            jax.ShapeDtypeStruct((gated.shape[1], plane_mid.shape[-1]), gated.dtype),
            jax.ShapeDtypeStruct((ranks,) + line_blocks.shape[2:], line_blocks.dtype),
        ),
        in_specs=[vmem, vmem, vmem, hbm, hbm],
        out_specs=(vmem, vmem, hbm),
        scratch_shapes=[
            pltpu.VMEM(plane_mid.shape, plane_mid.dtype),
            pltpu.SemaphoreType.DMA,
            pltpu.SemaphoreType.DMA((GATHER_COPIES,)),
            pltpu.SemaphoreType.DMA((GATHER_COPIES,)),
            pltpu.SemaphoreType.DMA,
            pltpu.VMEM((2, planes - 1, 2, tokens, width), grad_query.dtype),
            pltpu.VMEM((2, planes - 1, 2, tokens, width), grad_query.dtype),
            pltpu.VMEM((2, tokens, width), grad_query.dtype),
            pltpu.SemaphoreType.DMA,
            pltpu.SemaphoreType.DMA,
            pltpu.SemaphoreType.DMA((2,)),
            pltpu.SemaphoreType.DMA((2,)),
            pltpu.SemaphoreType.DMA((4,)),
            pltpu.SemaphoreType.DMA((2, planes - 1, 2)),
            pltpu.SemaphoreType.DMA((2, planes - 1, 2)),
        ],
        compiler_params=pltpu.CompilerParams(
            collective_id=collective_id, has_side_effects=True, vmem_limit_bytes=VMEM_LIMIT
        ),
        name="return_heads",
    )(grad_query, grad_kv, gated, plane_mid, line_blocks)


def stack_heads(ref):
    return ref[...].reshape(ref.shape[0] * ref.shape[1], ref.shape[2])


def block_bounds(lengths_ref, ranks, planes, rows):
    block = pl.program_id(0)
    span = planes * rows
    first = block * span + lax.axis_index("sp") * rows
    start, end = jnp.int32(0), jnp.int32(0)
    for item in range(lengths_ref.shape[0]):
        end = end + lengths_ref[item]
        start = jnp.where(first >= end, end, start)
    return start // span, block, first


def row_starts(lengths_ref, tokens):
    start, end = jnp.zeros_like(tokens), jnp.int32(0)
    for item in range(lengths_ref.shape[0]):
        end = end + lengths_ref[item]
        start = jnp.where(tokens >= end, end, start)
    return start


def chunk_weights(query, key, scale, tokens, starts, first_key):
    scores = mat_nt(query, key) * scale
    columns = first_key + lax.broadcasted_iota(jnp.int32, scores.shape, 1)
    allowed = (columns <= tokens) & (columns >= starts)
    return jnp.where(allowed, jnp.exp(scores), 0.0)


def query_tokens(first, rows, group):
    row = lax.broadcasted_iota(jnp.int32, (group * rows, 1), 0)
    return first + lax.rem(row, rows)


def attend_kernel(ranks, planes, lengths_ref, q_ref, kv_ref, gate_ref, att_ref, total_ref, gated_ref):
    group, rows, width = q_ref.shape
    scale = HEAD_DIM ** (-0.5)
    low, high, first = block_bounds(lengths_ref, ranks, planes, rows)
    tokens = query_tokens(first, rows, group)
    starts = row_starts(lengths_ref, tokens)
    query = stack_heads(q_ref)
    span = planes * rows

    def step(chunk, running):
        total, unnorm = running
        key = kv_ref[:, 0, chunk].reshape(span, width)
        value = kv_ref[:, 1, chunk].reshape(span, width)
        weights = chunk_weights(query, key, scale, tokens, starts, chunk * span)
        total = total + jnp.sum(weights, axis=1, keepdims=True)
        unnorm = unnorm + jnp.dot(
            weights.astype(jnp.bfloat16), value, preferred_element_type=jnp.float32
        )
        return total, unnorm

    total, unnorm = lax.fori_loop(
        low,
        high + 1,
        step,
        (
            jnp.zeros((group * rows, 1), jnp.float32),
            jnp.zeros((group * rows, width), jnp.float32),
        ),
    )
    attended = unnorm / total
    att_ref[...] = attended.reshape(group, rows, width)
    total_ref[...] = total.reshape(group, rows, 1)
    sent = attended.astype(jnp.bfloat16).astype(jnp.float32)
    for head in range(group):
        gated = sent[head * rows : (head + 1) * rows] * jax.nn.sigmoid(gate_ref[head])
        gated_ref[:, head * width : (head + 1) * width] = gated.astype(jnp.bfloat16)


def attend(lengths, query, kv, gate_logit, rows):
    group, tokens, width = query.shape
    planes = kv.shape[0]
    ranks = tokens // rows
    kv_blocks = kv.reshape(planes, 2, ranks, rows, width)
    block = pl.BlockSpec((group, rows, width), lambda i, *_: (0, i, 0))
    thin = pl.BlockSpec((group, rows, 1), lambda i, *_: (0, i, 0))
    return pl.pallas_call(
        functools.partial(attend_kernel, ranks, planes),
        grid_spec=pltpu.PrefetchScalarGridSpec(
            num_scalar_prefetch=1,
            grid=(ranks,),
            in_specs=[
                block,
                pl.BlockSpec((planes, 2, ranks, rows, width), lambda i, *_: (0, 0, 0, 0, 0)),
                thin,
            ],
            out_specs=(
                block,
                thin,
                pl.BlockSpec((rows, group * width), lambda i, *_: (i, 0)),
            ),
        ),
        out_shape=(
            jax.ShapeDtypeStruct((group, tokens, width), jnp.float32),
            jax.ShapeDtypeStruct((group, tokens, 1), jnp.float32),
            jax.ShapeDtypeStruct((tokens, group * width), jnp.bfloat16),
        ),
        compiler_params=pltpu.CompilerParams(vmem_limit_bytes=VMEM_LIMIT),
        name="attend",
    )(lengths, query, kv_blocks, gate_logit)


def attend_back_kernel(
    ranks, planes, lengths_ref, q_ref, kv_ref, gate_ref, att_ref, total_ref, dgated_ref, dq_ref, dkv_ref, dgate_ref, sums
):
    group, rows, width = q_ref.shape
    scale = HEAD_DIM ** (-0.5)
    low, high, first = block_bounds(lengths_ref, ranks, planes, rows)
    tokens = query_tokens(first, rows, group)
    starts = row_starts(lengths_ref, tokens)
    query = stack_heads(q_ref)
    span = planes * rows

    @pl.when(pl.program_id(0) == 0)
    def _():
        sums[...] = jnp.zeros_like(sums)

    attended = stack_heads(att_ref)
    sent = attended.astype(jnp.bfloat16).astype(jnp.float32)
    total = stack_heads(total_ref)
    logit = stack_heads(gate_ref)
    prob = jax.nn.sigmoid(logit)
    dgated = jnp.concatenate(
        [dgated_ref[:, head * width : (head + 1) * width] for head in range(group)], axis=0
    )
    dattended = (dgated * prob).astype(jnp.bfloat16)
    dlogit = jnp.sum(dgated * sent, axis=1, keepdims=True) * prob * (1.0 - prob)
    dgate_ref[...] = dlogit.astype(jnp.bfloat16).reshape(group, rows, 1)
    dattended = dattended.astype(jnp.float32)
    scaled = (dattended / total).astype(jnp.bfloat16)
    delta = jnp.sum(dattended * attended, axis=1, keepdims=True) / total

    def step(chunk, dquery):
        key = kv_ref[:, 0, chunk].reshape(span, width)
        value = kv_ref[:, 1, chunk].reshape(span, width)
        weights = chunk_weights(query, key, scale, tokens, starts, chunk * span)
        dprob = mat_nt(scaled, value)
        dscore = (weights * (dprob - delta)).astype(jnp.bfloat16)
        dquery = dquery + jnp.dot(dscore, key, preferred_element_type=jnp.float32)
        dkey = mat_tn(dscore, query)
        dvalue = mat_tn(weights.astype(jnp.bfloat16), scaled)
        sums[:, 0, chunk] += dkey.reshape(planes, rows, width)
        sums[:, 1, chunk] += dvalue.reshape(planes, rows, width)
        return dquery

    dquery = lax.fori_loop(
        low, high + 1, step, jnp.zeros((group * rows, width), jnp.float32)
    )
    dq_ref[...] = (dquery * scale).astype(jnp.bfloat16).reshape(group, rows, width)

    @pl.when(pl.program_id(0) == ranks - 1)
    def _():
        for chunk in range(ranks):
            dkv_ref[:, 0, chunk] = (sums[:, 0, chunk] * scale).astype(jnp.bfloat16)
            dkv_ref[:, 1, chunk] = sums[:, 1, chunk].astype(jnp.bfloat16)


def attend_back(lengths, query, kv, gate_logit, attended, total, dgated, rows):
    group, tokens, width = query.shape
    planes = kv.shape[0]
    ranks = tokens // rows
    kv_blocks = kv.reshape(planes, 2, ranks, rows, width)
    block = pl.BlockSpec((group, rows, width), lambda i, *_: (0, i, 0))
    thin = pl.BlockSpec((group, rows, 1), lambda i, *_: (0, i, 0))
    whole = pl.BlockSpec((planes, 2, ranks, rows, width), lambda i, *_: (0, 0, 0, 0, 0))
    dquery, dkv, dgate = pl.pallas_call(
        functools.partial(attend_back_kernel, ranks, planes),
        grid_spec=pltpu.PrefetchScalarGridSpec(
            num_scalar_prefetch=1,
            grid=(ranks,),
            in_specs=[
                block,
                whole,
                thin,
                block,
                thin,
                pl.BlockSpec((rows, group * width), lambda i, *_: (i, 0)),
            ],
            out_specs=(block, whole, thin),
            scratch_shapes=[pltpu.VMEM((planes, 2, ranks, rows, width), jnp.float32)],
        ),
        out_shape=(
            jax.ShapeDtypeStruct((group, tokens, width), jnp.bfloat16),
            jax.ShapeDtypeStruct((planes, 2, ranks, rows, width), jnp.bfloat16),
            jax.ShapeDtypeStruct((group, tokens, 1), jnp.bfloat16),
        ),
        compiler_params=pltpu.CompilerParams(vmem_limit_bytes=VMEM_LIMIT),
        name="attend_back",
    )(lengths, query, kv_blocks, gate_logit, attended, total, dgated)
    return dquery, dkv.reshape(planes, 2, tokens, width), dgate


def middle_kernel(
    planes,
    gated_ref,
    wout_ref,
    x_ref,
    scale_ref,
    dy_hbm,
    wg_hbm,
    wu_hbm,
    wd_hbm,
    xg,
    line_hbm,
    down_hbm,
    mid_ref,
    dmid_ref,
    gain_ref,
    pm_ref,
    dgated_ref,
    act_ref,
    wg,
    wu,
    wd,
    dy,
    dhid,
    near_out,
    near_in,
    far_out,
    far_in,
    keep,
    down_buf,
    load_sem,
    dy_sem,
    down_sem,
    near_send,
    near_recv,
    far_send,
    far_recv,
    ag_send,
    ag_recv,
    line_send,
    line_recv,
):
    rank, plane = lax.axis_index("fsdp"), lax.axis_index("sp")
    ranks, rows, width = xg.shape
    loads = [
        pltpu.make_async_copy(wd_hbm, wd, load_sem.at[0]),
        pltpu.make_async_copy(wg_hbm, wg, load_sem.at[1]),
        pltpu.make_async_copy(wu_hbm, wu, load_sem.at[2]),
    ]
    dy_load = pltpu.make_async_copy(dy_hbm, dy, dy_sem)
    others = [lax.rem(plane + k, planes) for k in range(1, planes)]
    greet([(rank ^ k, plane) for k in (1, 2, 4, 6)] + [(rank, other) for other in others])

    def along(source, which):
        return [
            peer_copy(
                source,
                line_hbm.at[which, j - 1],
                line_send.at[which, j - 1],
                line_recv.at[which, j - 1],
                rank,
                lax.rem(plane + planes - j, planes),
            )
            for j in range(1, planes)
        ]

    def near(phase, i):
        return peer_copy(
            near_out.at[phase, i],
            near_in.at[phase, i],
            near_send.at[phase, i],
            near_recv.at[phase, i],
            rank ^ 1,
            plane,
        )

    def far(phase, i, k):
        return peer_copy(
            far_out.at[phase, i],
            far_in.at[phase, i],
            far_send.at[phase, i],
            far_recv.at[phase, i],
            rank ^ k,
            plane,
        )

    order = (6, 2, 4, 0)
    for i, k in enumerate(order):
        part = jnp.dot(
            gated_ref[rank ^ 1 ^ k], wout_ref[...], preferred_element_type=jnp.float32
        )
        near_out[0, i] = part.astype(jnp.bfloat16)
        near(0, i).start()
    dy_load.start()
    for copy in loads:
        copy.start()
    dy_line = along(dy_hbm.at[rank], 1)
    for copy in dy_line:
        copy.start()
    for i, k in enumerate(order):
        part = jnp.dot(gated_ref[rank ^ k], wout_ref[...], preferred_element_type=jnp.float32)
        near(0, i).wait_recv()
        part = part + near_in[0, i].astype(jnp.float32)
        if k:
            far_out[0, i] = part.astype(jnp.bfloat16)
            far(0, i, k).start()
        else:
            keep[...] = part

    dy_load.wait()
    loads[0].wait()

    @pl.loop(0, ranks // 2)
    def _(p):
        pair = dy[pl.ds(2 * p, 2)].reshape(2 * rows, width)
        dhid[p] = mat_nt(pair, wd[...])

    loads[1].wait()
    loads[2].wait()
    middle = x_ref[...].astype(jnp.float32) + keep[...]
    for i in (1, 2, 0):
        far(0, i, order[i]).wait_recv()
        middle = middle + far_in[0, i].astype(jnp.float32)
    inverse = inv_rms(middle)
    mid_ref[...] = middle
    normed = (middle * inverse * scale_ref[...]).astype(jnp.bfloat16)
    xg[rank] = normed
    sems = (ag_send.at[0], ag_recv.at[0])
    gather_start(xg, *sems)
    xb_line = along(xg.at[rank], 0)
    for copy in xb_line:
        copy.start()

    slots = {2: 0, 4: 1, 6: 2, 0: 3}

    def down_copy(p, slot):
        return pltpu.make_async_copy(
            down_buf.at[slot], down_hbm.at[pl.ds(2 * p, 2)], down_sem.at[slot]
        )

    def feed(k):
        p = (rank ^ k) // 2
        slot = (0, 2, 4, 6).index(k) % 2
        pair = xg[pl.ds(2 * p, 2)].reshape(2 * rows, width)
        gate_pre = mat_nt(pair, wg[...])
        up_pre = mat_nt(pair, wu[...])
        grad_hidden = dhid[p]
        sigma = jax.nn.sigmoid(gate_pre)
        swish = gate_pre * sigma
        grad_gate = (grad_hidden * up_pre * sigma * (1.0 + gate_pre * (1.0 - sigma))).astype(
            jnp.bfloat16
        )
        grad_up = (grad_hidden * swish).astype(jnp.bfloat16)
        part = jnp.dot(grad_gate, wg[...], preferred_element_type=jnp.float32) + jnp.dot(
            grad_up, wu[...], preferred_element_type=jnp.float32
        )
        i = slots[k]
        halves = part.reshape(2, rows, width)
        mine_first = lax.rem(rank, 2) == 0
        mine = jnp.where(mine_first, halves[0], halves[1])
        theirs = jnp.where(mine_first, halves[1], halves[0])
        near_out[1, i] = theirs.astype(jnp.bfloat16)
        near(1, i).start()
        hidden = (swish * up_pre).astype(jnp.bfloat16)
        for kept, value in enumerate((grad_gate, grad_up, hidden)):
            act_ref[kept, pl.ds(pl.multiple_of(2 * rows * p, 2 * rows), 2 * rows)] = value
        down = jnp.dot(hidden, wd[...], preferred_element_type=jnp.float32)
        if k in (4, 6):
            down_copy(p, slot).wait()
        down_buf[slot] = down.astype(jnp.bfloat16).reshape(2, rows, width)
        down_copy(p, slot).start()
        near(1, i).wait_recv()
        mine = mine + near_in[1, i].astype(jnp.float32)
        if k:
            far_out[1, i] = mine.astype(jnp.bfloat16)
            far(1, i, k).start()
        else:
            keep[...] = mine

    gather_wait(xg, *sems, (6,))
    feed(0)
    gather_pass(xg, *sems, NEIGHBOURS_FIRST)
    gather_wait(xg, *sems, (7, 8))
    feed(2)
    gather_pass(xg, *sems, DIAGONAL)
    gather_wait(xg, *sems, (9, 10))
    feed(4)
    gather_wait(xg, *sems, (11, 12))
    feed(6)

    grad = keep[...]
    for i, k in enumerate((2, 4, 6)):
        far(1, i, k).wait_recv()
        grad = grad + far_in[1, i].astype(jnp.float32)
    middle = mid_ref[...]
    inverse = inv_rms(middle)
    gain_ref[...] = jnp.sum(grad * middle * inverse, axis=0, keepdims=True)
    grad_middle = dy[rank].astype(jnp.float32) + norm_back(
        grad, middle, inverse, scale_ref[...]
    )
    dmid_ref[...] = grad_middle
    pm_ref[rank] = grad_middle.astype(jnp.bfloat16)
    sems2 = (ag_send.at[1], ag_recv.at[1])
    gather_start(pm_ref, *sems2)

    def gated_grad(k):
        p = (rank ^ k) // 2
        pair = pm_ref[pl.ds(2 * p, 2)].reshape(2 * rows, width)
        dgated_ref[pl.ds(2 * p, 2)] = mat_nt(pair, wout_ref[...]).reshape(
            2, rows, wout_ref.shape[0]
        )

    gather_wait(pm_ref, *sems2, (6,))
    gated_grad(0)
    gather_pass(pm_ref, *sems2, NEIGHBOURS_FIRST)
    gather_wait(pm_ref, *sems2, (7, 8))
    gated_grad(2)
    gather_wait(pm_ref, *sems2, (9, 10))
    gated_grad(4)
    gather_pass(pm_ref, *sems2, DIAGONAL)
    gather_wait(pm_ref, *sems2, (11, 12))
    gated_grad(6)

    gather_sent(xg, *sems)
    gather_sent(pm_ref, *sems2)
    for copy in dy_line + xb_line:
        copy.wait()
    for phase in range(2):
        for i in range(4):
            near(phase, i).wait_send()
        for i in range(3):
            far(phase, i, 2).wait_send()
    down_copy(0, 0).wait()
    down_copy(0, 1).wait()


def middle_layer(gated, w_out, x, scale, grad_plane, w_gate, w_up, w_down, collective_id):
    ranks, rows, _ = gated.shape
    planes = lax.axis_size("sp")
    width = x.shape[1]
    hidden = w_gate.shape[0]
    features = w_out.shape[0]
    vmem = pl.BlockSpec(memory_space=pltpu.VMEM)
    hbm = pl.BlockSpec(memory_space=pl.ANY)
    half, full = jnp.bfloat16, jnp.float32
    return pl.pallas_call(
        functools.partial(middle_kernel, planes),
        out_shape=(
            jax.ShapeDtypeStruct((ranks, rows, width), half),
            jax.ShapeDtypeStruct((2, planes - 1, rows, width), half),
            jax.ShapeDtypeStruct((ranks, rows, width), half),
            jax.ShapeDtypeStruct((rows, width), full),
            jax.ShapeDtypeStruct((rows, width), full),
            jax.ShapeDtypeStruct((1, width), full),
            jax.ShapeDtypeStruct((ranks, rows, width), half),
            jax.ShapeDtypeStruct((ranks, rows, features), full),
            jax.ShapeDtypeStruct((3, ranks * rows, hidden), half),
        ),
        in_specs=[vmem, vmem, vmem, vmem, hbm, hbm, hbm, hbm],
        out_specs=(vmem, hbm, hbm, vmem, vmem, vmem, vmem, vmem, vmem),
        scratch_shapes=[
            pltpu.VMEM((hidden, width), half),
            pltpu.VMEM((hidden, width), half),
            pltpu.VMEM((hidden, width), half),
            pltpu.VMEM((ranks, rows, width), half),
            pltpu.VMEM((ranks // 2, 2 * rows, hidden), full),
            pltpu.VMEM((2, 4, rows, width), half),
            pltpu.VMEM((2, 4, rows, width), half),
            pltpu.VMEM((2, 3, rows, width), half),
            pltpu.VMEM((2, 3, rows, width), half),
            pltpu.VMEM((rows, width), full),
            pltpu.VMEM((2, 2, rows, width), half),
            pltpu.SemaphoreType.DMA((3,)),
            pltpu.SemaphoreType.DMA,
            pltpu.SemaphoreType.DMA((2,)),
            pltpu.SemaphoreType.DMA((2, 4)),
            pltpu.SemaphoreType.DMA((2, 4)),
            pltpu.SemaphoreType.DMA((2, 3)),
            pltpu.SemaphoreType.DMA((2, 3)),
            pltpu.SemaphoreType.DMA((2, GATHER_COPIES)),
            pltpu.SemaphoreType.DMA((2, GATHER_COPIES)),
            pltpu.SemaphoreType.DMA((2, planes - 1)),
            pltpu.SemaphoreType.DMA((2, planes - 1)),
        ],
        compiler_params=pltpu.CompilerParams(
            collective_id=collective_id, has_side_effects=True, vmem_limit_bytes=VMEM_LIMIT
        ),
        name="middle_layer",
    )(gated, w_out, x, scale, grad_plane, w_gate, w_up, w_down)


def feed_weights_kernel(
    planes,
    xp_hbm,
    dp_hbm,
    act_hbm,
    blocks_hbm,
    first_hbm,
    second_hbm,
    down_hbm,
    mid_ref,
    small_ref,
    rows_ref,
    qkv_hbm,
    wg_hbm,
    wu_hbm,
    wd_hbm,
    og_ref,
    ou_ref,
    od_ref,
    h_ref,
    so_ref,
    go_ref,
    sum_hbm,
    more_hbm,
    wg_ref,
    wu_ref,
    wd_ref,
    w_sem,
    xbuf,
    dbuf,
    act,
    parts,
    small_buf,
    rows_buf,
    quarter,
    quarters,
    x_sem,
    d_sem,
    act_sem,
    part_sem,
    own_sem,
    ag_send,
    ag_recv,
    line_send,
    line_recv,
    part_send,
    part_recv,
    sum_send,
    sum_recv,
    quarter_sem,
    near_buf,
    out_buf,
    far_buf,
    sib_send,
    sib_recv,
    send_sem,
    recv_sem,
):
    rank, plane = lax.axis_index("fsdp"), lax.axis_index("sp")
    ranks, rows, width = xp_hbm.shape
    part = ranks // 2
    chunk = part * rows
    others = [lax.rem(plane + k, planes) for k in range(1, planes)]
    greet([(rank ^ k, plane) for k in (1, 2, 4, 6)] + [(rank, other) for other in others])

    picks = ((0, 1), (1, 1), (1, 2), (0, 2))
    gathers = [(more_hbm.at[g], ag_send.at[g], ag_recv.at[g]) for g in range(4)]
    own_blocks = [
        pltpu.make_async_copy(blocks_hbm.at[pick], more_hbm.at[g, rank], own_sem.at[g])
        for g, pick in enumerate(picks)
    ]

    def begin(g):
        gather_start(*gathers[g], own=blocks_hbm.at[picks[g]])

    def load(step, start):
        slot = lax.rem(step, 2)
        block = pl.ds(part * lax.rem(step, 2), part)
        group = step // 2
        sources = (
            (xp_hbm.at[block], dp_hbm.at[block]),
            (first_hbm.at[block], second_hbm.at[block]),
            (more_hbm.at[0, block], more_hbm.at[1, block]),
            (more_hbm.at[3, block], more_hbm.at[2, block]),
        )
        for index, (x_from, d_from) in enumerate(sources):
            @pl.when(group == index)
            def _():
                for copy in (
                    pltpu.make_async_copy(x_from, xbuf.at[slot], x_sem.at[slot]),
                    pltpu.make_async_copy(d_from, dbuf.at[slot], d_sem.at[slot]),
                ):
                    if start:
                        copy.start()
                    else:
                        copy.wait()

    def kept(step):
        where = pl.ds(pl.multiple_of(step * chunk, chunk), chunk)
        return pltpu.make_async_copy(act_hbm.at[:, where], act, act_sem)

    scatter = (near_buf, sib_send, sib_recv)
    own_parts = [
        pltpu.make_async_copy(down_hbm.at[rank ^ k], parts.at[i], part_sem.at[i])
        for i, k in enumerate(SCATTER_ORDER)
    ]
    small = [
        peer_copy(
            source,
            buffer.at[k],
            line_send.at[which, k],
            line_recv.at[which, k],
            rank,
            others[k],
        )
        for which, (source, buffer) in enumerate(((small_ref, small_buf), (rows_ref, rows_buf)))
        for k in range(planes - 1)
    ]

    quarter_rows = quarter.shape[0]

    def rows_of(index):
        return pl.ds(pl.multiple_of(index * quarter_rows, quarter_rows), quarter_rows)

    own_quarter = pltpu.make_async_copy(qkv_hbm.at[rows_of(plane)], quarter, quarter_sem.at[0])
    own_sum = pltpu.make_async_copy(quarter, sum_hbm.at[rows_of(plane)], quarter_sem.at[1])
    partials = [
        peer_copy(
            qkv_hbm.at[rows_of(others[k])],
            quarters.at[k],
            part_send.at[k],
            part_recv.at[k],
            rank,
            others[k],
        )
        for k in range(planes - 1)
    ]
    sums = [
        peer_copy(
            quarter,
            sum_hbm.at[rows_of(plane)],
            sum_send.at[k],
            sum_recv.at[k],
            rank,
            others[k],
        )
        for k in range(planes - 1)
    ]

    load(0, True)
    kept(0).start()
    weights = [
        pltpu.make_async_copy(source, target, w_sem.at[index])
        for index, (source, target) in enumerate(
            ((wg_hbm, wg_ref), (wu_hbm, wu_ref), (wd_hbm, wd_ref))
        )
    ]
    for copy in weights:
        copy.start()
    own_quarter.start()
    for copy in own_blocks + small + own_parts + partials:
        copy.start()
    begin(0)
    for i in range(4):
        scatter_near(down_hbm, i, *scatter).start()

    @pl.loop(0, 2 * planes)
    def _(step):
        @pl.when(step == 1)
        def _():
            kept(1).start()
            begin(1)

        @pl.when(step == 2)
        def _():
            for copy in weights:
                copy.wait()
            gather_pass(*gathers[0], NEIGHBOURS_FIRST)

        @pl.when(step == 3)
        def _():
            gather_pass(*gathers[0], DIAGONAL)
            gather_pass(*gathers[1], NEIGHBOURS_FIRST)
            begin(2)
            for i, k in enumerate(SCATTER_ORDER):
                own_parts[i].wait()
                scatter_near(down_hbm, i, *scatter).wait_recv()
                joined = parts[i].astype(jnp.float32) + near_buf[i].astype(jnp.float32)
                if k:
                    out_buf[i] = joined.astype(out_buf.dtype)
                else:
                    parts[i] = joined.astype(parts.dtype)

        @pl.when(step == 4)
        def _():
            gather_pass(*gathers[1], DIAGONAL)
            begin(3)
            for g in (0, 1):
                gather_wait(*gathers[g], FROM_SIBLING)
                own_blocks[g].wait()
            load(step, True)
            own_quarter.wait()
            total = quarter[...].astype(jnp.float32)
            for k in range(planes - 1):
                partials[k].wait()
                total = total + quarters[k].astype(jnp.float32)
            quarter[...] = total.astype(quarter.dtype)
            own_sum.start()
            for copy in sums:
                copy.start()

        @pl.when(step == 5)
        def _():
            gather_pass(*gathers[2], NEIGHBOURS_FIRST)
            gather_pass(*gathers[3], NEIGHBOURS_FIRST)

        @pl.when(step == 6)
        def _():
            for g in (2, 3):
                gather_pass(*gathers[g], DIAGONAL)
            for i in range(3):
                scatter_far(i, out_buf, far_buf, send_sem, recv_sem).start()
            for g in (2, 3):
                gather_wait(*gathers[g], FROM_SIBLING)
                own_blocks[g].wait()
            load(step, True)

        load(step, False)

        @pl.when((lax.rem(step, 2) == 0) | (step == 1))
        def _():
            load(step + 1, True)

        slot = lax.rem(step, 2)
        normed = xbuf[slot].reshape(chunk, width)
        grad = dbuf[slot].reshape(chunk, width)

        own = step < 2

        @pl.when(own)
        def _():
            kept(0).wait()

        @pl.when(jnp.logical_not(own))
        def _():
            gate_pre = mat_nt(normed, wg_ref[...])
            up_pre = mat_nt(normed, wu_ref[...])
            grad_hidden = mat_nt(grad, wd_ref[...])
            sigma = jax.nn.sigmoid(gate_pre)
            swish = gate_pre * sigma
            act[0] = (grad_hidden * up_pre * sigma * (1.0 + gate_pre * (1.0 - sigma))).astype(
                jnp.bfloat16
            )
            act[1] = (grad_hidden * swish).astype(jnp.bfloat16)
            act[2] = (swish * up_pre).astype(jnp.bfloat16)

        @pl.when(step == 0)
        def _():
            for ref in (og_ref, ou_ref, od_ref):
                ref[...] = jnp.zeros_like(ref)

        og_ref[...] += mat_tn(act[0], normed)
        ou_ref[...] += mat_tn(act[1], normed)
        od_ref[...] += mat_tn(act[2], grad)

    output = mid_ref[...] + parts[3].astype(jnp.float32)
    for i in range(3):
        scatter_far(i, out_buf, far_buf, send_sem, recv_sem).wait()
        output = output + far_buf[i].astype(jnp.float32)
    h_ref[...] = output.astype(h_ref.dtype)
    for copy in small + sums:
        copy.wait()
    own_sum.wait()
    total, gate_rows = small_ref[...], rows_ref[...]
    for k in range(planes - 1):
        total = total + small_buf[k]
        gate_rows = gate_rows + rows_buf[k]
    so_ref[...] = total
    go_ref[...] = gate_rows
    for i in range(4):
        scatter_near(down_hbm, i, *scatter).wait_send()
    for gather in gathers:
        gather_sent(*gather)


def feed_weights(plane_x, plane_grad, acts, blocks, first, second, down, middle, small, gate_rows, qkv_part, w_gate, w_up, w_down, collective_id):
    ranks, rows, width = plane_x.shape
    planes = lax.axis_size("sp")
    hidden = w_gate.shape[0]
    vmem = pl.BlockSpec(memory_space=pltpu.VMEM)
    hbm = pl.BlockSpec(memory_space=pl.ANY)
    tokens = planes * ranks * rows
    half, full = plane_x.dtype, jnp.float32
    return pl.pallas_call(
        functools.partial(feed_weights_kernel, planes),
        in_specs=[hbm] * 7 + [vmem] * 3 + [hbm] * 4,
        out_specs=(vmem,) * 6 + (hbm, hbm),
        out_shape=[jax.ShapeDtypeStruct(w_gate.shape, full)] * 3
        + [
            jax.ShapeDtypeStruct((rows, width), half),
            jax.ShapeDtypeStruct(small.shape, full),
            jax.ShapeDtypeStruct(gate_rows.shape, full),
            jax.ShapeDtypeStruct(qkv_part.shape, half),
            jax.ShapeDtypeStruct((4, ranks, rows, width), half),
        ],
        scratch_shapes=[pltpu.VMEM(w_gate.shape, half)] * 3
        + [
            pltpu.SemaphoreType.DMA((3,)),
            pltpu.VMEM((2, ranks // 2, rows, width), half),
            pltpu.VMEM((2, ranks // 2, rows, width), half),
            pltpu.VMEM((3, ranks // 2 * rows, hidden), half),
            pltpu.VMEM((4, rows, width), half),
            pltpu.VMEM((planes - 1,) + small.shape, full),
            pltpu.VMEM((planes - 1,) + gate_rows.shape, full),
            pltpu.VMEM((qkv_part.shape[0] // planes, width), half),
            pltpu.VMEM((planes - 1, qkv_part.shape[0] // planes, width), half),
            pltpu.SemaphoreType.DMA((2,)),
            pltpu.SemaphoreType.DMA((2,)),
            pltpu.SemaphoreType.DMA,
            pltpu.SemaphoreType.DMA((4,)),
            pltpu.SemaphoreType.DMA((4,)),
            pltpu.SemaphoreType.DMA((4, GATHER_COPIES)),
            pltpu.SemaphoreType.DMA((4, GATHER_COPIES)),
            pltpu.SemaphoreType.DMA((2, planes - 1)),
            pltpu.SemaphoreType.DMA((2, planes - 1)),
        ]
        + [pltpu.SemaphoreType.DMA((planes - 1,))] * 4
        + [
            pltpu.SemaphoreType.DMA((2,)),
        ]
        + scatter_scratch(rows, width, half),
        cost_estimate=pl.CostEstimate(
            flops=12 * tokens * w_gate.size,
            bytes_accessed=4 * tokens * width + 18 * w_gate.size,
            transcendentals=tokens * w_gate.shape[0],
        ),
        compiler_params=pltpu.CompilerParams(
            collective_id=collective_id, has_side_effects=True, vmem_limit_bytes=VMEM_LIMIT
        ),
        name="feed_weights",
    )(plane_x, plane_grad, acts, blocks, first, second, down, middle, small, gate_rows, qkv_part, w_gate, w_up, w_down)[:7]


def front_kernel(
    planes,
    lengths_ref,
    x_ref,
    small_ref,
    w_ref,
    wg_ref,
    dyo_ref,
    q_ref,
    kv_ref,
    dy_ref,
    xg,
    xa_ref,
    raw_ref,
    gate_ref,
    attn_ref,
    ffn_ref,
    head_ref,
    cos_ref,
    sin_ref,
    nat,
    gains,
    small_send,
    small_recv,
    ag_send,
    ag_recv,
    own_sem,
    local_sem,
    q_send,
    q_recv,
    kv_send,
    kv_recv,
    line_send,
    line_recv,
):
    rank, plane = lax.axis_index("fsdp"), lax.axis_index("sp")
    ranks, rows, width = xg.shape
    pair_rows = 2 * rows
    chip = rank // 2
    greet_line(ranks, planes)
    own_block = pltpu.make_async_copy(dyo_ref, dy_ref.at[rank], own_sem)
    own_block.start()
    small = []
    for k in range(1, ranks):
        copy = peer_copy(
            small_ref, gains.at[rank], small_send.at[k - 1], small_recv.at[k - 1], rank ^ k, plane
        )
        copy.start()
        small.append(copy)
    sems = (ag_send.at[0], ag_recv.at[0])
    gather_start(xg, *sems, own=x_ref)
    xg[rank] = x_ref[...]
    gains[rank] = small_ref[...]

    half = HEAD_DIM // 2
    lane = lax.broadcasted_iota(jnp.int32, (1, HEAD_DIM), 1)
    step = lax.rem(lane, half).astype(jnp.float32)
    frequency = jnp.exp(-math.log(ROPE_BASE) * 2.0 * step / HEAD_DIM)
    sign = jnp.where(lane < half, -1.0, 1.0)

    @pl.loop(0, ranks)
    def _(block):
        tokens = (block * planes + plane) * rows + lax.broadcasted_iota(jnp.int32, (rows, 1), 0)
        position = tokens - row_starts(lengths_ref, tokens)
        angles = position.astype(jnp.float32) * frequency
        where = pl.ds(pl.multiple_of(block * rows, rows), rows)
        cos_ref[where] = jnp.cos(angles)
        sin_ref[where] = jnp.sin(angles) * sign

    for copy in small:
        copy.wait_recv()
    head_q, head_k = gains[0, 4:5], gains[0, 5:6]
    for r in range(1, ranks):
        head_q = head_q + gains[r, 4:5]
        head_k = head_k + gains[r, 5:6]
    head_ref[...] = jnp.where(rank < ranks // 2, head_q, head_k)
    for r in range(ranks):
        for i in range(2):
            columns = slice((2 * r + i) * HEAD_DIM, (2 * r + i + 1) * HEAD_DIM)
            attn_ref[:, columns] = gains[r, i : i + 1]
            ffn_ref[:, columns] = gains[r, 2 + i : 3 + i]

    def token_rows(p):
        return pl.ds(pl.multiple_of(p * pair_rows, pair_rows), pair_rows)

    def q_copy(m, p, to):
        return peer_copy(
            nat.at[pl.ds(2 * m, 2), token_rows(p)],
            q_ref.at[:, token_rows(p)],
            q_send.at[m, p],
            q_recv.at[p],
            to,
            plane,
        )

    def kv_copy(m, which, p, to):
        return peer_copy(
            nat.at[m, token_rows(p)],
            kv_ref.at[plane, which, token_rows(p)],
            kv_send.at[m, p],
            kv_recv.at[which, p],
            to,
            plane,
        )

    def q_local(p):
        return pltpu.make_async_copy(
            nat.at[pl.ds(0, 2), token_rows(p)], q_ref.at[:, token_rows(p)], local_sem.at[p]
        )

    def kv_local(m, which, p):
        return pltpu.make_async_copy(
            nat.at[m, token_rows(p)], kv_ref.at[plane, which, token_rows(p)], local_sem.at[p]
        )

    def process(k):
        p = chip ^ (k // 2)
        inputs = xg[pl.ds(2 * p, 2)].reshape(pair_rows, width).astype(jnp.float32)
        normed = (inputs * inv_rms(inputs) * attn_ref[...]).astype(jnp.bfloat16)
        xa_ref[pl.ds(2 * p, 2)] = normed.reshape(2, rows, width)
        projected = mat_nt(normed, w_ref[...])
        raw_ref[token_rows(p)] = projected
        logits = mat_nt(normed, wg_ref[...])
        for head in range(gate_ref.shape[0]):
            gate_ref[head, token_rows(p)] = logits[:, head : head + 1]
        cosine, sine = cos_ref[token_rows(p)], sin_ref[token_rows(p)]
        for m in range(4):
            head = projected[:, m * HEAD_DIM : (m + 1) * HEAD_DIM]
            scaled = head * inv_rms(head) * head_ref[...]
            turned = scaled * cosine + pltpu.roll(scaled, half, 1) * sine
            nat[m, token_rows(p)] = jnp.where(rank >= 6, head, turned).astype(jnp.bfloat16)

        @pl.when(rank < 4)
        def _():
            for m in range(2):
                @pl.when(2 * rank + m != rank)
                def _():
                    q_copy(m, p, 2 * rank + m).start()

        @pl.when(rank == 0)
        def _():
            q_local(p).start()

        for which in range(2):
            first = 4 + 2 * which

            @pl.when((rank == first) | (rank == first + 1))
            def _():
                for m in range(4):
                    to = 4 * (rank - first) + m

                    @pl.when(to != rank)
                    def _():
                        kv_copy(m, which, p, to).start()

            @pl.when(rank == first + 1)
            def _():
                kv_local((first + 1) % 4, which, p).start()

    def line_piece(origin, which, p, side, j, to):
        piece = kv_ref.at[origin, which, token_rows(p)]
        return peer_copy(
            piece,
            piece,
            line_send.at[side, j, which, p],
            line_recv.at[side, j, which, p],
            rank,
            to,
        )

    def origin_of(side, j):
        return plane - j if side == 0 else plane + j

    def next_of(side):
        return plane + 1 if side == 0 else plane - 1

    def line_go(which, p, j):
        if j == 0:
            @pl.when(rank == 5 + 2 * which)
            def _():
                kv_local((5 + 2 * which) % 4, which, p).wait()

            @pl.when(rank != 5 + 2 * which)
            def _():
                kv_copy(0, which, p, 0).wait_recv()

        for side in range(2):
            if j:
                arrives = (plane >= j) if side == 0 else (plane + j <= planes - 1)

                @pl.when(arrives)
                def _():
                    line_piece(origin_of(side, j), which, p, side, j - 1, plane).wait_recv()

            if j < planes - 1:
                @pl.when(line_sends(planes, plane, j, side))
                def _():
                    line_piece(origin_of(side, j), which, p, side, j, next_of(side)).start()

    slots = (((0, 2), (1, 3)), ((0, 3), (1, 2)), ((0, 0), (1, 1)), ((0, 1), (1, 0)))

    def slot_go(slot, j):
        for which, p in slots[slot]:
            line_go(which, p, j)

    gather_wait(xg, *sems, (6,))
    process(0)
    slot_go(0, 0)
    gather_pass(xg, *sems, NEIGHBOURS_FIRST)
    gather_wait(xg, *sems, (7, 8))
    process(2)
    slot_go(0, 1)
    gather_wait(xg, *sems, (9, 10))
    process(4)
    gather_pass(xg, *sems, DIAGONAL)
    slot_go(1, 0)
    slot_go(0, 2)
    gather_wait(xg, *sems, (11, 12))
    process(6)
    sems2 = (ag_send.at[1], ag_recv.at[1])
    slot_go(2, 0)
    slot_go(1, 1)
    slot_go(3, 0)
    gather_start(dy_ref, *sems2, own=dyo_ref)
    slot_go(0, 3)
    slot_go(1, 2)
    slot_go(2, 1)
    slot_go(3, 1)
    slot_go(1, 3)
    slot_go(2, 2)
    gather_pass(dy_ref, *sems2, NEIGHBOURS_FIRST)
    slot_go(3, 2)
    slot_go(2, 3)
    gather_pass(dy_ref, *sems2, DIAGONAL)
    slot_go(3, 3)
    gather_wait(dy_ref, *sems2, FROM_SIBLING)

    for p in range(ranks // 2):
        @pl.when(rank == 0)
        def _():
            q_local(p).wait()

        @pl.when(rank != 0)
        def _():
            q_copy(0, p, 0).wait_recv()

    for copy in small:
        copy.wait_send()
    gather_sent(xg, *sems)
    gather_sent(dy_ref, *sems2)
    own_block.wait()
    for p in range(ranks // 2):
        @pl.when(rank < 4)
        def _():
            for m in range(2):
                @pl.when(2 * rank + m != rank)
                def _():
                    q_copy(m, p, 0).wait_send()

        for which in range(2):
            first = 4 + 2 * which

            @pl.when((rank == first) | (rank == first + 1))
            def _():
                for m in range(4):
                    @pl.when(4 * (rank - first) + m != rank)
                    def _():
                        kv_copy(m, which, p, 0).wait_send()

            for j in range(planes - 1):
                for side in range(2):
                    @pl.when(line_sends(planes, plane, j, side))
                    def _():
                        line_piece(0, which, p, side, j, next_of(side)).wait_send()


def front(lengths, x, small, w_qkv, w_head_gate, grad, collective_id):
    rows, width = x.shape
    ranks, planes = lax.axis_size("fsdp"), lax.axis_size("sp")
    tokens = ranks * rows
    heads = w_head_gate.shape[0]
    vmem = pl.BlockSpec(memory_space=pltpu.VMEM)
    hbm = pl.BlockSpec(memory_space=pl.ANY)
    half, full = jnp.bfloat16, jnp.float32
    pairs = ranks // 2
    return pl.pallas_call(
        functools.partial(front_kernel, planes),
        out_shape=(
            jax.ShapeDtypeStruct((2, tokens, HEAD_DIM), half),
            jax.ShapeDtypeStruct((planes, 2, tokens, HEAD_DIM), half),
            jax.ShapeDtypeStruct((ranks, rows, width), half),
            jax.ShapeDtypeStruct((ranks, rows, width), half),
            jax.ShapeDtypeStruct((ranks, rows, width), half),
            jax.ShapeDtypeStruct((tokens, w_qkv.shape[0]), full),
            jax.ShapeDtypeStruct((heads, tokens, 1), full),
            jax.ShapeDtypeStruct((1, width), full),
            jax.ShapeDtypeStruct((1, width), full),
            jax.ShapeDtypeStruct((1, HEAD_DIM), full),
            jax.ShapeDtypeStruct((tokens, HEAD_DIM), full),
            jax.ShapeDtypeStruct((tokens, HEAD_DIM), full),
        ),
        in_specs=[pl.BlockSpec(memory_space=pltpu.SMEM), vmem, vmem, vmem, vmem, hbm],
        out_specs=(hbm, hbm, hbm) + (vmem,) * 9,
        scratch_shapes=[
            pltpu.VMEM((4, tokens, HEAD_DIM), half),
            pltpu.VMEM((ranks,) + small.shape, small.dtype),
            pltpu.SemaphoreType.DMA((ranks - 1,)),
            pltpu.SemaphoreType.DMA((ranks - 1,)),
            pltpu.SemaphoreType.DMA((2, GATHER_COPIES)),
            pltpu.SemaphoreType.DMA((2, GATHER_COPIES)),
            pltpu.SemaphoreType.DMA,
            pltpu.SemaphoreType.DMA((pairs,)),
            pltpu.SemaphoreType.DMA((2, pairs)),
            pltpu.SemaphoreType.DMA((pairs,)),
            pltpu.SemaphoreType.DMA((4, pairs)),
            pltpu.SemaphoreType.DMA((2, pairs)),
            pltpu.SemaphoreType.DMA((2, planes - 1, 2, pairs)),
            pltpu.SemaphoreType.DMA((2, planes - 1, 2, pairs)),
        ],
        compiler_params=pltpu.CompilerParams(
            collective_id=collective_id, has_side_effects=True, vmem_limit_bytes=VMEM_LIMIT
        ),
        name="front",
    )(lengths, x, small, w_qkv, w_head_gate, grad)


def local_planes(
    hidden_in,
    grad_out,
    lengths,
    attn_gain,
    w_qkv,
    w_head_gate,
    q_gain,
    k_gain,
    w_out,
    ffn_gain,
    w_gate,
    w_up,
    w_down,
):
    ranks, planes = lax.axis_size("fsdp"), lax.axis_size("sp")
    rank, plane = lax.axis_index("fsdp"), lax.axis_index("sp")
    rows, model_width = hidden_in.shape
    tokens = ranks * rows
    own_heads = w_qkv.shape[0] // HEAD_DIM
    local_heads = HEADS // ranks

    thin = q_gain.shape[0]
    spread = jnp.zeros((2, HEAD_DIM), attn_gain.dtype)
    spread = lax.dynamic_update_slice(
        spread, jnp.stack([q_gain, k_gain]), (jnp.int32(0), rank * thin)
    )
    own_gains = jnp.concatenate(
        [
            attn_gain.reshape(-1, HEAD_DIM),
            ffn_gain.reshape(-1, HEAD_DIM),
            spread,
            jnp.zeros((2, HEAD_DIM), attn_gain.dtype),
        ],
        axis=0,
    ).astype(jnp.float32)
    (
        query,
        kv,
        plane_grad,
        gathered,
        normed_a,
        projected,
        gate_logit,
        attn_scale,
        ffn_scale,
        head_scale,
        cosine,
        sine,
    ) = front(lengths, hidden_in, own_gains, w_qkv, w_head_gate, grad_out, 0)
    attended, total, gated = attend(lengths, query, kv, gate_logit, rows)
    plane_b, line_blocks, down_part, middle, grad_middle, grad_ffn_gain_local, plane_mid, grad_gated, acts = middle_layer(
        gated.reshape(ranks, rows, -1),
        w_out,
        hidden_in,
        ffn_scale,
        plane_grad,
        w_gate,
        w_up,
        w_down,
        2,
    )
    grad_gated = grad_gated.reshape(tokens, -1)
    grad_query, grad_kv, gate_grad = attend_back(
        lengths, query, kv, gate_logit, attended, total, grad_gated, rows
    )
    back, out_part, first_grad = return_heads(
        grad_query, grad_kv, gated, plane_mid, line_blocks, 6
    )
    reduced = lax.psum_scatter(out_part, "sp", scatter_dimension=0, tiled=True)
    grad_a_part, qkv_part, gate_rows, attn_terms, head_terms, first_b = projection_back(
        back,
        projected,
        cosine,
        sine,
        normed_a,
        gathered,
        gate_grad,
        w_qkv,
        w_head_gate,
        head_scale,
        line_blocks,
        8,
    )
    reduced, grad_a_part = lax.optimization_barrier((reduced, grad_a_part))
    out_sum = lax.all_gather(reduced, "sp", axis=0, tiled=True)
    grad_in, gain_sums = scatter_gains(
        grad_a_part,
        attn_terms,
        grad_ffn_gain_local,
        head_terms,
        hidden_in,
        attn_scale,
        grad_middle,
        7,
    )
    out_sum, gain_sums = lax.optimization_barrier((out_sum, gain_sums))
    grad_w_out = out_sum.astype(jnp.float32)
    grad_w_gate, grad_w_up, grad_w_down, hidden_out, gain_total, grad_w_head_gate, qkv_total = feed_weights(
        plane_b,
        plane_grad,
        acts,
        line_blocks,
        first_b,
        first_grad,
        down_part,
        middle,
        gain_sums,
        gate_rows,
        qkv_part,
        w_gate,
        w_up,
        w_down,
        4,
    )
    grad_w_qkv = qkv_total.astype(jnp.float32)
    grad_attn_gain = gain_total[:2].reshape(-1)
    grad_ffn_gain = gain_total[2:4].reshape(-1)
    grad_q_gain = lax.dynamic_slice_in_dim(gain_total[4], rank * thin, thin)
    grad_k_gain = lax.dynamic_slice_in_dim(gain_total[5], rank * thin, thin)
    return (
        hidden_out,
        grad_in,
        grad_attn_gain,
        grad_w_qkv,
        grad_w_head_gate,
        grad_q_gain,
        grad_k_gain,
        grad_w_out,
        grad_ffn_gain,
        grad_w_gate,
        grad_w_up,
        grad_w_down,
    )


def solution(mesh):
    planar = mesh.shape["fsdp"] == 8 and mesh.shape["sp"] == 4
    return jax.shard_map(
        local_planes if planar else local,
        mesh=mesh,
        in_specs=(
            P(("fsdp", "sp"), None),
            P(("fsdp", "sp"), None),
            P(),
            P("fsdp"),
            P("fsdp", None),
            P("fsdp", None),
            P("fsdp"),
            P("fsdp"),
            P("fsdp", None),
            P("fsdp"),
            P("fsdp", None),
            P("fsdp", None),
            P("fsdp", None),
        ),
        out_specs=(
            P(("fsdp", "sp"), None),
            P(("fsdp", "sp"), None),
            P("fsdp"),
            P("fsdp", None),
            P("fsdp", None),
            P("fsdp"),
            P("fsdp"),
            P("fsdp", None),
            P("fsdp"),
            P("fsdp", None),
            P("fsdp", None),
            P("fsdp", None),
        ),
        check_vma=False,
    )
```

```python
import functools
import math

import jax
import jax.numpy as jnp
from jax import lax
from jax.experimental import pallas as pl
from jax.experimental.pallas import tpu as pltpu
from jax.sharding import PartitionSpec as P

HEADS = 16
KV_HEADS = 8
HEAD_DIM = 128


EPS = 1e-06
ROPE_BASE = 1000000.0


def mat_nt(factor, others):
    return lax.dot_general(
        factor, others, (((1,), (1,)), ((), ())), preferred_element_type=jnp.float32
    )


def mat_tn(factor, others):
    return lax.dot_general(
        factor, others, (((0,), (0,)), ((), ())), preferred_element_type=jnp.float32
    )


def inv_rms(values):
    return lax.rsqrt(jnp.mean(values * values, axis=-1, keepdims=True) + EPS)


def norm_back(grad_norm, values, inverse, scaling):
    scaled = grad_norm * scaling
    cubed = inverse * inverse * inverse
    return inverse * scaled - values * cubed * jnp.mean(scaled * values, axis=-1, keepdims=True)


def item_starts(token_index, lengths):
    ends = jnp.cumsum(lengths)
    starts = ends - lengths
    inside = (token_index[:, None] >= starts[None, :]) & (token_index[:, None] < ends[None, :])
    return jnp.sum(jnp.where(inside, starts[None, :], 0), axis=1)


def rope_tables(position):
    half_dim = HEAD_DIM // 2
    freq_steps = jnp.arange(half_dim, dtype=jnp.float32)
    frequency = jnp.exp(-math.log(ROPE_BASE) * 2.0 * freq_steps / HEAD_DIM)
    angles = position.astype(jnp.float32)[:, None] * frequency[None, :]
    return (jnp.cos(angles)[:, None, :], jnp.sin(angles)[:, None, :])


def rotate(values, cosine, sine):
    half_dim = values.shape[-1] // 2
    lower = values[..., :half_dim]
    upper = values[..., half_dim:]
    return jnp.concatenate([lower * cosine - upper * sine, upper * cosine + lower * sine], axis=-1)


def rotate_back(grad_rot, cosine, sine):
    half_dim = grad_rot.shape[-1] // 2
    lower = grad_rot[..., :half_dim]
    upper = grad_rot[..., half_dim:]
    return jnp.concatenate([lower * cosine + upper * sine, upper * cosine - lower * sine], axis=-1)


def local(
    hidden_in,
    grad_out,
    lengths,
    attn_gain,
    w_qkv,
    w_head_gate,
    q_gain,
    k_gain,
    w_out,
    ffn_gain,
    w_gate,
    w_up,
    w_down,
):
    fsdp_count = lax.axis_size("fsdp")
    sp_count = lax.axis_size("sp")
    fsdp_rank = lax.axis_index("fsdp")
    sp_rank = lax.axis_index("sp")
    tok_rows = hidden_in.shape[0]
    model_width = hidden_in.shape[1]
    query_width = HEADS * HEAD_DIM
    kv_width = KV_HEADS * HEAD_DIM
    local_kv = KV_HEADS // sp_count
    head_group = HEADS // KV_HEADS
    score_scale = HEAD_DIM ** (-0.5)
    qkv_full, out_full, gate_full, attn_gain_full, q_gain_full, k_gain_full, ffn_gain_full = (
        lax.all_gather(w_qkv, "fsdp", axis=0, tiled=True),
        lax.all_gather(w_out, "fsdp", axis=0, tiled=True),
        lax.all_gather(w_head_gate, "fsdp", axis=0, tiled=True),
        lax.all_gather(attn_gain, "fsdp", axis=0, tiled=True),
        lax.all_gather(q_gain, "fsdp", axis=0, tiled=True),
        lax.all_gather(k_gain, "fsdp", axis=0, tiled=True),
        lax.all_gather(ffn_gain, "fsdp", axis=0, tiled=True),
    )
    attn_scale = attn_gain_full.astype(jnp.float32)
    query_scale = q_gain_full.astype(jnp.float32)
    key_scale = k_gain_full.astype(jnp.float32)
    ffn_scale = ffn_gain_full.astype(jnp.float32)
    token_first = (fsdp_rank * sp_count + sp_rank) * tok_rows
    own_tokens = token_first + jnp.arange(tok_rows, dtype=jnp.int32)
    cosine, sine = rope_tables(own_tokens - item_starts(own_tokens, lengths))
    inputs = hidden_in.astype(jnp.float32)
    inv_first = inv_rms(inputs)
    normed_a = (inputs * inv_first * attn_scale).astype(jnp.bfloat16)
    projected = mat_nt(normed_a, qkv_full)
    gate_logit = mat_nt(normed_a, gate_full)
    q_raw = projected[:, :query_width].reshape(tok_rows, HEADS, HEAD_DIM)
    k_raw = projected[:, query_width : query_width + kv_width].reshape(tok_rows, KV_HEADS, HEAD_DIM)
    q_inv = inv_rms(q_raw)
    k_inv = inv_rms(k_raw)
    query = (
        rotate(q_raw * q_inv * query_scale, cosine, sine)
        .reshape(tok_rows, query_width)
        .astype(jnp.bfloat16)
    )
    keys = (
        rotate(k_raw * k_inv * key_scale, cosine, sine)
        .reshape(tok_rows, kv_width)
        .astype(jnp.bfloat16)
    )
    values = projected[:, query_width + kv_width :].astype(jnp.bfloat16)
    query_heads, key_heads, value_heads = (
        lax.all_to_all(query, "sp", split_axis=1, concat_axis=0, tiled=True),
        lax.all_to_all(keys, "sp", split_axis=1, concat_axis=0, tiled=True),
        lax.all_to_all(values, "sp", split_axis=1, concat_axis=0, tiled=True),
    )
    key_all, value_all = (
        lax.all_gather(key_heads, "fsdp", axis=0, tiled=True),
        lax.all_gather(value_heads, "fsdp", axis=0, tiled=True),
    )
    span_rows = query_heads.shape[0]
    span_first = fsdp_rank * span_rows
    span_tokens = span_first + jnp.arange(span_rows, dtype=jnp.int32)
    span_starts = item_starts(span_tokens, lengths)
    query_four = query_heads.reshape(span_rows, local_kv, head_group, HEAD_DIM)
    key_total = key_all.shape[0]
    key_block = min(1024, key_total)
    block_count = key_total // key_block
    key_blocks = key_all.reshape(block_count, key_block, local_kv, HEAD_DIM)
    value_blocks = value_all.reshape(block_count, key_block, local_kv, HEAD_DIM)
    block_firsts = jnp.arange(block_count, dtype=jnp.int32) * key_block
    lowest_key = span_starts[0]
    highest_key = span_first + span_rows - 1

    def needed(block_first):
        return (block_first <= highest_key) & (block_first + key_block - 1 >= lowest_key)

    def block_weights(key_piece, block_first):
        scores = (
            jnp.einsum("qkgd,jkd->kgqj", query_four, key_piece, preferred_element_type=jnp.float32)
            * score_scale
        )
        columns = block_first + jnp.arange(key_block, dtype=jnp.int32)
        allowed = (columns[None, :] <= span_tokens[:, None]) & (
            columns[None, :] >= span_starts[:, None]
        )
        return jnp.where(allowed[None, None], jnp.exp(scores), 0.0)

    def forward_step(running, pieces):
        key_piece, value_piece, block_first = pieces

        def forward_compute(current):
            totals, unnormed = current
            weights = block_weights(key_piece, block_first)
            totals = totals + jnp.sum(weights, axis=3)
            unnormed = unnormed + jnp.einsum(
                "kgqj,jkd->qkgd",
                weights.astype(jnp.bfloat16),
                value_piece,
                preferred_element_type=jnp.float32,
            )
            return (totals, unnormed)

        return (
            lax.cond(needed(block_first), forward_compute, lambda current: current, running),
            None,
        )

    start_state = (
        jnp.zeros((local_kv, head_group, span_rows), jnp.float32),
        jnp.zeros((span_rows, local_kv, head_group, HEAD_DIM), jnp.float32),
    )
    scanned = lax.scan(forward_step, start_state, (key_blocks, value_blocks, block_firsts))[0]
    totals, unnormed = scanned
    totals_rows = jnp.transpose(totals, (2, 0, 1))[..., None]
    attended_heads = unnormed / totals_rows
    attended_send = attended_heads.reshape(span_rows, local_kv * head_group * HEAD_DIM).astype(
        jnp.bfloat16
    )
    returned = lax.all_to_all(attended_send, "sp", split_axis=0, concat_axis=1, tiled=True)
    gate_prob = jax.nn.sigmoid(gate_logit)
    attended_tok = returned.astype(jnp.float32).reshape(tok_rows, HEADS, HEAD_DIM)
    gated = (
        (attended_tok * gate_prob[:, :, None]).reshape(tok_rows, query_width).astype(jnp.bfloat16)
    )
    middle = inputs + jnp.dot(gated, out_full, preferred_element_type=jnp.float32)
    inv_second = inv_rms(middle)
    normed_b = (middle * inv_second * ffn_scale).astype(jnp.bfloat16)
    gate_piece = lax.all_gather(w_gate, "fsdp", axis=0, tiled=True)
    up_piece = lax.all_gather(w_up, "fsdp", axis=0, tiled=True)
    down_piece = lax.all_gather(w_down, "fsdp", axis=0, tiled=True)
    gate_pre = mat_nt(normed_b, gate_piece)
    up_pre = mat_nt(normed_b, up_piece)
    hidden = (jax.nn.silu(gate_pre) * up_pre).astype(jnp.bfloat16)
    ffn_part = jnp.dot(hidden, down_piece, preferred_element_type=jnp.float32)
    hidden_out = (middle + ffn_part).astype(jnp.bfloat16)
    gate_piece = lax.all_gather(w_gate, "fsdp", axis=0, tiled=True)
    up_piece = lax.all_gather(w_up, "fsdp", axis=0, tiled=True)
    down_piece = lax.all_gather(w_down, "fsdp", axis=0, tiled=True)
    gate_pre = mat_nt(normed_b, gate_piece)
    up_pre = mat_nt(normed_b, up_piece)
    sigma = jax.nn.sigmoid(gate_pre)
    swish = gate_pre * sigma
    hidden = (swish * up_pre).astype(jnp.bfloat16)
    grad_hidden = mat_nt(grad_out, down_piece)
    grad_gate = (grad_hidden * up_pre * sigma * (1.0 + gate_pre * (1.0 - sigma))).astype(
        jnp.bfloat16
    )
    grad_up = (grad_hidden * swish).astype(jnp.bfloat16)
    grad_acc = jnp.dot(grad_gate, gate_piece, preferred_element_type=jnp.float32) + jnp.dot(
        grad_up, up_piece, preferred_element_type=jnp.float32
    )
    grad_ffn_gain_local = jnp.sum(grad_acc * middle * inv_second, axis=0)
    grad_middle = grad_out.astype(jnp.float32) + norm_back(grad_acc, middle, inv_second, ffn_scale)
    grad_mid_b = grad_middle.astype(jnp.bfloat16)
    grad_gated = mat_nt(grad_mid_b, out_full).reshape(tok_rows, HEADS, HEAD_DIM)
    grad_attended = (
        (grad_gated * gate_prob[:, :, None]).reshape(tok_rows, query_width).astype(jnp.bfloat16)
    )
    gate_grad = (jnp.sum(grad_gated * attended_tok, axis=2) * gate_prob * (1.0 - gate_prob)).astype(
        jnp.bfloat16
    )
    grad_heads = lax.all_to_all(grad_attended, "sp", split_axis=1, concat_axis=0, tiled=True)
    grad_four = grad_heads.astype(jnp.float32).reshape(span_rows, local_kv, head_group, HEAD_DIM)
    grad_scaled = (grad_four / totals_rows).astype(jnp.bfloat16)
    delta_rows = jnp.sum(grad_four * attended_heads, axis=3) / totals_rows[..., 0]
    delta_heads = jnp.transpose(delta_rows, (1, 2, 0))

    def backward_step(grad_query, pieces):
        key_piece, value_piece, block_first = pieces

        def backward_compute(current):
            weights = block_weights(key_piece, block_first)
            grad_prob = jnp.einsum(
                "qkgd,jkd->kgqj", grad_scaled, value_piece, preferred_element_type=jnp.float32
            )
            grad_score = (weights * (grad_prob - delta_heads[..., None])).astype(jnp.bfloat16)
            current = (
                current
                + jnp.einsum(
                    "kgqj,jkd->qkgd", grad_score, key_piece, preferred_element_type=jnp.float32
                )
                * score_scale
            )
            grad_key = (
                jnp.einsum(
                    "kgqj,qkgd->jkd", grad_score, query_four, preferred_element_type=jnp.float32
                )
                * score_scale
            )
            grad_value = jnp.einsum(
                "kgqj,qkgd->jkd",
                weights.astype(jnp.bfloat16),
                grad_scaled,
                preferred_element_type=jnp.float32,
            )
            return (current, (grad_key, grad_value))

        def skip(current):
            nothing = jnp.zeros((key_block, local_kv, HEAD_DIM), jnp.float32)
            return (current, (nothing, nothing))

        return lax.cond(needed(block_first), backward_compute, skip, grad_query)

    grad_query, key_value_grads = lax.scan(
        backward_step,
        jnp.zeros((span_rows, local_kv, head_group, HEAD_DIM), jnp.float32),
        (key_blocks, value_blocks, block_firsts),
    )
    key_grads, value_grads = key_value_grads
    key_sum, value_sum = (
        lax.psum_scatter(
            key_grads.reshape(key_total, local_kv * HEAD_DIM),
            "fsdp",
            scatter_dimension=0,
            tiled=True,
        ),
        lax.psum_scatter(
            value_grads.reshape(key_total, local_kv * HEAD_DIM),
            "fsdp",
            scatter_dimension=0,
            tiled=True,
        ),
    )
    query_send = grad_query.reshape(span_rows, local_kv * head_group * HEAD_DIM).astype(
        jnp.bfloat16
    )
    back_query, back_key, back_value = (
        lax.all_to_all(query_send, "sp", split_axis=0, concat_axis=1, tiled=True),
        lax.all_to_all(key_sum.astype(jnp.bfloat16), "sp", split_axis=0, concat_axis=1, tiled=True),
        lax.all_to_all(
            value_sum.astype(jnp.bfloat16), "sp", split_axis=0, concat_axis=1, tiled=True
        ),
    )
    grad_qn = rotate_back(
        back_query.astype(jnp.float32).reshape(tok_rows, HEADS, HEAD_DIM), cosine, sine
    )
    grad_kn = rotate_back(
        back_key.astype(jnp.float32).reshape(tok_rows, KV_HEADS, HEAD_DIM), cosine, sine
    )
    grad_q_gain_local = jnp.sum(grad_qn * q_raw * q_inv, axis=(0, 1))
    grad_k_gain_local = jnp.sum(grad_kn * k_raw * k_inv, axis=(0, 1))
    grad_q_raw = norm_back(grad_qn, q_raw, q_inv, query_scale).reshape(tok_rows, query_width)
    grad_k_raw = norm_back(grad_kn, k_raw, k_inv, key_scale).reshape(tok_rows, kv_width)
    grad_proj = jnp.concatenate(
        [grad_q_raw.astype(jnp.bfloat16), grad_k_raw.astype(jnp.bfloat16), back_value], axis=1
    )
    grad_normed_a = jnp.dot(grad_proj, qkv_full, preferred_element_type=jnp.float32) + jnp.dot(
        gate_grad, gate_full, preferred_element_type=jnp.float32
    )
    grad_attn_gain_local = jnp.sum(grad_normed_a * inputs * inv_first, axis=0)
    grad_in = grad_middle + norm_back(grad_normed_a, inputs, inv_first, attn_scale)
    qkv_rows = w_qkv.shape[0]
    out_rows = w_out.shape[0]
    gate_rows = w_head_gate.shape[0]
    block_rows = qkv_rows + out_rows + gate_rows + 3
    small_rows = jnp.stack(
        [
            grad_attn_gain_local,
            grad_ffn_gain_local,
            jnp.concatenate(
                [
                    grad_q_gain_local,
                    grad_k_gain_local,
                    jnp.zeros((model_width - 2 * HEAD_DIM,), jnp.float32),
                ]
            ),
        ],
        axis=0,
    )
    ffn_partial = lax.psum_scatter(
        jnp.concatenate(
            [mat_tn(grad_gate, normed_b), mat_tn(grad_up, normed_b), mat_tn(hidden, grad_out)],
            axis=1,
        ).astype(jnp.bfloat16),
        "fsdp",
        scatter_dimension=0,
        tiled=True,
    ).astype(jnp.float32)
    proj_split = grad_proj.reshape(tok_rows, fsdp_count, qkv_rows)
    gated_split = gated.reshape(tok_rows, fsdp_count, out_rows)
    gate_split = gate_grad.reshape(tok_rows, fsdp_count, gate_rows)
    owners = block_rows * lax.axis_size("fsdp") // block_rows
    qkv_term = jnp.einsum("tor,td->ord", proj_split, normed_a, preferred_element_type=jnp.float32)
    out_term = jnp.einsum(
        "tor,td->ord", gated_split, grad_mid_b, preferred_element_type=jnp.float32
    )
    gate_term = jnp.einsum("tor,td->ord", gate_split, normed_a, preferred_element_type=jnp.float32)
    small_term = jnp.broadcast_to(small_rows[None], (owners, 3, model_width))
    joined = jnp.concatenate([qkv_term, out_term, gate_term, small_term], axis=1)
    attn_partial = lax.psum_scatter(
        joined.reshape(owners * block_rows, model_width), "fsdp", scatter_dimension=0, tiled=True
    )
    ffn_total, attn_total = lax.psum((ffn_partial, attn_partial), "sp")
    grad_w_gate = ffn_total[:, :model_width]
    grad_w_up = ffn_total[:, model_width : 2 * model_width]
    grad_w_down = ffn_total[:, 2 * model_width :]
    grad_w_qkv = attn_total[:qkv_rows]
    grad_w_out = attn_total[qkv_rows : qkv_rows + out_rows]
    grad_w_head_gate = attn_total[qkv_rows + out_rows : qkv_rows + out_rows + gate_rows]
    gain_sums = attn_total[qkv_rows + out_rows + gate_rows :]
    gain_part = model_width // fsdp_count
    head_part = HEAD_DIM // fsdp_count
    grad_attn_gain = lax.dynamic_slice_in_dim(gain_sums[0], fsdp_rank * gain_part, gain_part)
    grad_ffn_gain = lax.dynamic_slice_in_dim(gain_sums[1], fsdp_rank * gain_part, gain_part)
    grad_q_gain = lax.dynamic_slice_in_dim(gain_sums[2], fsdp_rank * head_part, head_part)
    grad_k_gain = lax.dynamic_slice_in_dim(
        gain_sums[2], HEAD_DIM + fsdp_rank * head_part, head_part
    )
    return (
        hidden_out,
        grad_in,
        grad_attn_gain,
        grad_w_qkv,
        grad_w_head_gate,
        grad_q_gain,
        grad_k_gain,
        grad_w_out,
        grad_ffn_gain,
        grad_w_gate,
        grad_w_up,
        grad_w_down,
    )


MESH = pl.DeviceIdType.MESH
VMEM_LIMIT = 62 * 1024 * 1024


def peer_copy(src, dst, send_sem, recv_sem, rank, plane):
    return pltpu.make_async_remote_copy(
        src_ref=src,
        dst_ref=dst,
        send_sem=send_sem,
        recv_sem=recv_sem,
        device_id=(rank, plane),
        device_id_type=MESH,
    )


def greet(peers):
    barrier = pltpu.get_barrier_semaphore()
    for peer in peers:
        pl.semaphore_signal(barrier, inc=1, device_id=peer, device_id_type=MESH)
    pl.semaphore_wait(barrier, len(peers))


def scatter_gains_kernel(
    p_ref, attn_ref, ffn_ref, head_ref, x_ref, scale_ref, dmid_ref, o_ref, so_ref, parts, small_buf, grad, small_send, small_recv, near_buf, out_buf, far_buf, sib_send, sib_recv, send_sem, recv_sem
):
    rank, plane = lax.axis_index("fsdp"), lax.axis_index("sp")
    ranks = p_ref.shape[0]
    greet([(rank ^ k, plane) for k in range(1, 8)])
    for i in range(4):
        scatter_near(p_ref, i, near_buf, sib_send, sib_recv).start()
    for r in range(ranks):
        for i in range(2):
            columns = slice((2 * r + i) * HEAD_DIM, (2 * r + i + 1) * HEAD_DIM)
            parts[r, i : i + 1] = attn_ref[:, columns]
            parts[r, 2 + i : 3 + i] = ffn_ref[:, columns]
        parts[r, 4:5] = jnp.where(rank < ranks // 2, head_ref[...], 0.0)
        parts[r, 5:6] = jnp.where(
            (rank >= ranks // 2) & (rank < 3 * ranks // 4), head_ref[...], 0.0
        )
        parts[r, 6:8] = jnp.zeros((2, HEAD_DIM), jnp.float32)
    small = []
    for k in range(1, 8):
        copy = peer_copy(
            parts.at[rank ^ k],
            small_buf.at[k - 1],
            small_send.at[k - 1],
            small_recv.at[k - 1],
            rank ^ k,
            plane,
        )
        copy.start()
        small.append(copy)
    sems = (send_sem, recv_sem)

    def block_of(i):
        scatter_near(p_ref, i, near_buf, sib_send, sib_recv).wait_recv()
        return p_ref[rank ^ SCATTER_ORDER[i]].astype(jnp.float32) + near_buf[i].astype(jnp.float32)

    def own_block():
        grad[...] = block_of(3)

    relay_blocks(out_buf, far_buf, sems, block_of, own_block)
    total = parts[rank]
    for k in range(1, 8):
        small[k - 1].wait()
        total = total + small_buf[k - 1]
    so_ref[...] = total
    grad[...] = relay_sum(out_buf, far_buf, sems, grad[...])
    inputs = x_ref[...].astype(jnp.float32)
    o_ref[...] = dmid_ref[...] + norm_back(grad[...], inputs, inv_rms(inputs), scale_ref[...])
    for i in range(4):
        scatter_near(p_ref, i, near_buf, sib_send, sib_recv).wait_send()
    relay_sent(out_buf, far_buf, sems)


SCATTER_ORDER = (6, 2, 4, 0)


def scatter_far(i, out_buf, far_buf, send_sem, recv_sem):
    rank, plane = lax.axis_index("fsdp"), lax.axis_index("sp")
    return peer_copy(
        out_buf.at[i],
        far_buf.at[i],
        send_sem.at[i],
        recv_sem.at[i],
        rank ^ SCATTER_ORDER[i],
        plane,
    )


def scatter_near(p_ref, i, near_buf, sib_send, sib_recv):
    rank, plane = lax.axis_index("fsdp"), lax.axis_index("sp")
    return peer_copy(
        p_ref.at[rank ^ 1 ^ SCATTER_ORDER[i]],
        near_buf.at[i],
        sib_send.at[i],
        sib_recv.at[i],
        rank ^ 1,
        plane,
    )


def relay_copy(i, out_buf, far_buf, send_sem, recv_sem):
    rank, plane = lax.axis_index("fsdp"), lax.axis_index("sp")
    half = out_buf.shape[1] // 2
    top, low = pl.ds(0, half), pl.ds(half, half)
    slot, part, to = (
        (0, top, 2),
        (0, low, 4),
        (1, top, 2),
        (2, low, 4),
        (1, low, 2),
        (2, top, 4),
    )[i]
    return peer_copy(
        out_buf.at[slot, part],
        far_buf.at[slot, part],
        send_sem.at[i],
        recv_sem.at[i],
        rank ^ to,
        plane,
    )


def relay_blocks(out_buf, far_buf, sems, block_of, own_block):
    half = out_buf.shape[1] // 2
    copies = [relay_copy(i, out_buf, far_buf, *sems) for i in range(6)]
    for slot, ready in ((0, (0, 1)), (1, (2,)), (2, (3,))):
        out_buf[slot] = block_of(slot).astype(out_buf.dtype)
        for i in ready:
            copies[i].start()
    own_block()
    for arrived, slot, onward, rows in ((0, 2, 5, slice(0, half)), (1, 1, 4, slice(half, 2 * half))):
        copies[arrived].wait_recv()
        joined = out_buf[slot, rows].astype(jnp.float32) + far_buf[0, rows].astype(jnp.float32)
        out_buf[slot, rows] = joined.astype(out_buf.dtype)
        copies[onward].start()


def relay_sum(out_buf, far_buf, sems, total):
    for i in (2, 3, 5, 4):
        relay_copy(i, out_buf, far_buf, *sems).wait_recv()
    return total + far_buf[1].astype(jnp.float32) + far_buf[2].astype(jnp.float32)


def relay_sent(out_buf, far_buf, sems):
    for i in range(6):
        relay_copy(i, out_buf, far_buf, *sems).wait_send()


def scatter_scratch(rows, width, dtype):
    return [
        pltpu.VMEM((4, rows, width), dtype),
        pltpu.VMEM((3, rows, width), dtype),
        pltpu.VMEM((3, rows, width), dtype),
        pltpu.SemaphoreType.DMA((4,)),
        pltpu.SemaphoreType.DMA((4,)),
        pltpu.SemaphoreType.DMA((3,)),
        pltpu.SemaphoreType.DMA((3,)),
    ]


def scatter_gains(p, attn, ffn, head, x, scale, grad_middle, collective_id):
    ranks, rows, width = p.shape
    vmem = pl.BlockSpec(memory_space=pltpu.VMEM)
    small = (8, HEAD_DIM)
    return pl.pallas_call(
        scatter_gains_kernel,
        out_shape=(
            jax.ShapeDtypeStruct((rows, width), jnp.float32),
            jax.ShapeDtypeStruct(small, jnp.float32),
        ),
        in_specs=[vmem] * 7,
        out_specs=(vmem, vmem),
        scratch_shapes=[
            pltpu.VMEM((ranks,) + small, jnp.float32),
            pltpu.VMEM((7,) + small, jnp.float32),
            pltpu.VMEM((rows, width), jnp.float32),
            pltpu.SemaphoreType.DMA((7,)),
            pltpu.SemaphoreType.DMA((7,)),
        ]
        + scatter_scratch(rows, width, p.dtype)[:-2]
        + [pltpu.SemaphoreType.DMA((6,)), pltpu.SemaphoreType.DMA((6,))],
        compiler_params=pltpu.CompilerParams(
            collective_id=collective_id, has_side_effects=True, vmem_limit_bytes=VMEM_LIMIT
        ),
        name="scatter_gains",
    )(p, attn, ffn, head, x, scale, grad_middle)


def projection_back_kernel(
    back_ref, raw_ref, cos_ref, sin_ref, xa_ref, x_ref, dgate_ref, w_ref, wg_ref, head_ref, blocks_ref, dxa_ref, qkv_ref, gate_ref, attn_ref, terms_ref, next_ref, sums, ag_send, ag_recv, own_sem
):
    rank, plane = lax.axis_index("fsdp"), lax.axis_index("sp")
    block = blocks_ref.at[0, 0]
    gather = (next_ref, ag_send, ag_recv)
    own = pltpu.make_async_copy(block, next_ref.at[rank], own_sem)
    group, rows, width = back_ref.shape

    @pl.when(pl.program_id(0) == 0)
    def _():
        greet([(rank ^ k, plane) for k in (1, 2, 4)])
        own.start()
        gather_start(*gather, own=block)
        for ref in (sums, gate_ref, attn_ref, terms_ref):
            ref[...] = jnp.zeros_like(ref)

    @pl.when(pl.program_id(0) == 2)
    def _():
        gather_pass(*gather, NEIGHBOURS_FIRST[:2])

    @pl.when(pl.program_id(0) == 3)
    def _():
        gather_pass(*gather, NEIGHBOURS_FIRST[2:])

    cosine, sine = cos_ref[...], sin_ref[...]
    columns = []
    for m in range(group):
        back = back_ref[m]
        grad = back.astype(jnp.float32)
        turned = grad * cosine - pltpu.roll(grad, width // 2, 1) * sine
        raw = raw_ref[:, m * width : (m + 1) * width]
        inverse = inv_rms(raw)
        terms_ref[...] += jnp.sum(turned * raw * inverse, axis=0, keepdims=True)
        grad_raw = norm_back(turned, raw, inverse, head_ref[...])
        columns.append(jnp.where(rank >= 6, grad, grad_raw).astype(jnp.bfloat16))
    grad_proj = jnp.concatenate(columns, axis=1)
    grad_a = jnp.dot(grad_proj, w_ref[...], preferred_element_type=jnp.float32)
    normed = xa_ref[...].reshape(rows, -1)
    normed32 = normed.astype(jnp.float32)
    for head in range(dgate_ref.shape[0]):
        gate = dgate_ref[head].astype(jnp.float32)
        grad_a = grad_a + gate * wg_ref[head : head + 1].astype(jnp.float32)
        gate_ref[head : head + 1] += jnp.sum(gate * normed32, axis=0, keepdims=True)
    inputs = x_ref[...].reshape(rows, -1).astype(jnp.float32)
    attn_ref[...] += jnp.sum(grad_a * inputs * inv_rms(inputs), axis=0, keepdims=True)
    dxa_ref[...] = grad_a.astype(jnp.bfloat16).reshape(dxa_ref.shape)
    sums[...] += mat_tn(grad_proj, normed)

    @pl.when(pl.program_id(0) == pl.num_programs(0) - 1)
    def _():
        qkv_ref[...] = sums[...].astype(jnp.bfloat16)
        gather_pass(*gather, DIAGONAL)
        gather_wait(*gather, FROM_SIBLING)
        gather_sent(*gather)
        own.wait()


def projection_back(back, raw, cosine, sine, normed, inputs, gate_grad, w_qkv, w_head_gate, head_scale, line_blocks, collective_id):
    ranks, rows, model_width = normed.shape
    group, tokens, width = back.shape
    pair = 2 * rows
    blocks = pl.BlockSpec((2, rows, model_width), lambda i: (i, 0, 0))
    thin = pl.BlockSpec((pair, width), lambda i: (i, 0))
    hbm = pl.BlockSpec(memory_space=pl.ANY)
    heads = gate_grad.shape[0]

    def still(shape):
        return pl.BlockSpec(shape, lambda i: (0, 0))

    return pl.pallas_call(
        projection_back_kernel,
        grid=(tokens // pair,),
        in_specs=[
            pl.BlockSpec((group, pair, width), lambda i: (0, i, 0)),
            pl.BlockSpec((pair, group * width), lambda i: (i, 0)),
            thin,
            thin,
            blocks,
            blocks,
            pl.BlockSpec((heads, pair, 1), lambda i: (0, i, 0)),
            still(w_qkv.shape),
            still(w_head_gate.shape),
            still(head_scale.shape),
            hbm,
        ],
        out_specs=(
            blocks,
            still(w_qkv.shape),
            still(w_head_gate.shape),
            still((1, model_width)),
            still((1, width)),
            hbm,
        ),
        out_shape=(
            jax.ShapeDtypeStruct(normed.shape, jnp.bfloat16),
            jax.ShapeDtypeStruct(w_qkv.shape, jnp.bfloat16),
            jax.ShapeDtypeStruct(w_head_gate.shape, jnp.float32),
            jax.ShapeDtypeStruct((1, model_width), jnp.float32),
            jax.ShapeDtypeStruct((1, width), jnp.float32),
            jax.ShapeDtypeStruct(normed.shape, line_blocks.dtype),
        ),
        scratch_shapes=[
            pltpu.VMEM(w_qkv.shape, jnp.float32),
            pltpu.SemaphoreType.DMA((GATHER_COPIES,)),
            pltpu.SemaphoreType.DMA((GATHER_COPIES,)),
            pltpu.SemaphoreType.DMA,
        ],
        compiler_params=pltpu.CompilerParams(
            collective_id=collective_id, has_side_effects=True, vmem_limit_bytes=VMEM_LIMIT
        ),
        name="projection_back",
    )(back, raw, cosine, sine, normed, inputs, gate_grad, w_qkv, w_head_gate, head_scale, line_blocks)


GATHER_COPIES = 13


def gather_copy(buf, i, send_sem, recv_sem, own=None):
    rank, plane = lax.axis_index("fsdp"), lax.axis_index("sp")
    rows = buf.shape[1]
    top, low = pl.ds(0, rows // 2), pl.ds(rows // 2, rows // 2)
    block, part, to = (
        (0, top, 2),
        (0, low, 2),
        (0, low, 4),
        (0, top, 4),
        (2, top, 4),
        (4, low, 2),
        (0, pl.ds(0, rows), 1),
        (2, top, 1),
        (2, low, 1),
        (4, low, 1),
        (4, top, 1),
        (6, top, 1),
        (6, low, 1),
    )[i]
    piece = buf.at[rank ^ block, part]
    source = piece if own is None or block else own.at[part]
    return peer_copy(source, piece, send_sem.at[i], recv_sem.at[i], rank ^ to, plane)


def gather_start(buf, send_sem, recv_sem, own=None):
    for i in (6, 0, 2, 1, 3):
        gather_copy(buf, i, send_sem, recv_sem, own).start()


def gather_pass(buf, send_sem, recv_sem, pairs):
    for arrived, onward in pairs:
        gather_copy(buf, arrived, send_sem, recv_sem).wait_recv()
        for i in onward:
            gather_copy(buf, i, send_sem, recv_sem).start()


def gather_wait(buf, send_sem, recv_sem, copies):
    for i in copies:
        gather_copy(buf, i, send_sem, recv_sem).wait_recv()


def gather_sent(buf, send_sem, recv_sem):
    for i in range(GATHER_COPIES):
        gather_copy(buf, i, send_sem, recv_sem).wait_send()


NEIGHBOURS_FIRST = ((0, (4, 7)), (2, (5, 9)), (1, (8,)), (3, (10,)))
DIAGONAL = ((4, (11,)), (5, (12,)))
FROM_SIBLING = (6, 7, 8, 9, 10, 11, 12)


def greet_line(ranks, planes):
    rank, plane = lax.axis_index("fsdp"), lax.axis_index("sp")
    barrier = pltpu.get_barrier_semaphore()
    for k in range(1, ranks):
        pl.semaphore_signal(
            barrier, inc=1, device_id=(rank ^ k, plane), device_id_type=MESH
        )

    @pl.when(plane > 0)
    def _():
        pl.semaphore_signal(barrier, inc=1, device_id=(rank, plane - 1), device_id_type=MESH)

    @pl.when(plane < planes - 1)
    def _():
        pl.semaphore_signal(barrier, inc=1, device_id=(rank, plane + 1), device_id_type=MESH)

    lower = (plane > 0).astype(jnp.int32)
    upper = (plane < planes - 1).astype(jnp.int32)
    pl.semaphore_wait(barrier, ranks - 1 + lower + upper)


def line_sends(planes, plane, j, side):
    if side == 0:
        return (plane >= j) & (plane < planes - 1)
    return (plane + j <= planes - 1) & (plane > 0)


def unheads_kernel(planes, dq_ref, dkv_ref, gated_ref, pm_hbm, blocks_ref, n_ref, wout_ref, next_ref, pm, pm_sem, ag_send, ag_recv, own_sem2, line_out, line_in, done, own_sem, q_send, q_recv, kv_send, kv_recv, line_send, line_recv):
    rank, plane = lax.axis_index("fsdp"), lax.axis_index("sp")
    greet_line(8, planes)
    block = blocks_ref.at[1, 0]
    gather = (next_ref, ag_send, ag_recv)
    own_block = pltpu.make_async_copy(block, next_ref.at[rank], own_sem2)
    own_block.start()
    mid_load = pltpu.make_async_copy(pm_hbm, pm, pm_sem)
    mid_load.start()

    def q_copy(m, to):
        return peer_copy(dq_ref, n_ref.at[pl.ds(2 * m, 2)], q_send, q_recv.at[m], to, plane)

    def kv_copy(m, which, to):
        return peer_copy(done.at[which], n_ref.at[m], kv_send.at[which], kv_recv.at[m], to, plane)

    def q_local():
        return pltpu.make_async_copy(dq_ref, n_ref.at[pl.ds(0, 2)], own_sem)

    def kv_local(m, which):
        return pltpu.make_async_copy(done.at[which], n_ref.at[m], own_sem)

    @pl.when(rank == 0)
    def _():
        q_local().start()

    for m in range(2):
        @pl.when((rank % 2 == m) & (rank != 0))
        def _():
            q_copy(m, rank // 2).start()

    def step_copy(j, which, side):
        to = plane + 1 if side == 0 else plane - 1
        return peer_copy(
            line_out.at[side, j, which],
            line_in.at[side, j, which],
            line_send.at[side, j, which],
            line_recv.at[side, j, which],
            rank,
            to,
        )

    def sends(j, side):
        return plane < planes - 1 - j if side == 0 else plane > j

    def target(j, side):
        return planes - 1 - j if side == 0 else j

    gather_start(*gather, own=block)

    for j in range(planes - 1):
        for which in range(2):
            for side in range(2):
                inner = plane > 0 if side == 0 else plane < planes - 1

                @pl.when(sends(j, side) & inner)
                def _():
                    step_copy(j, which, side).wait_recv()
                    total = dkv_ref[target(j, side), which].astype(jnp.float32) + line_in[
                        side, j, which
                    ].astype(jnp.float32)
                    line_out[side, j, which] = total.astype(line_out.dtype)

                @pl.when(sends(j, side) & jnp.logical_not(inner))
                def _():
                    line_out[side, j, which] = dkv_ref[target(j, side), which]

                @pl.when(sends(j, side))
                def _():
                    step_copy(j, which, side).start()

        if j == 0:
            mid_load.wait()
            wout_ref[...] = mat_tn(gated_ref[...], pm[...].reshape(-1, pm.shape[-1])).astype(
                wout_ref.dtype
            )
        if j == 1:
            gather_pass(*gather, NEIGHBOURS_FIRST)
        if j == 2:
            gather_pass(*gather, DIAGONAL)

    for which in range(2):
        total = dkv_ref[plane, which].astype(jnp.float32)
        done32 = total
        for j in range(planes - 1):
            for side in range(2):
                @pl.when(plane == target(j, side))
                def _():
                    step_copy(j, which, side).wait_recv()
        low = jnp.minimum(planes - 1 - plane, planes - 2)
        high = jnp.minimum(plane, planes - 2)
        below = line_in[0, low, which].astype(jnp.float32)
        above = line_in[1, high, which].astype(jnp.float32)
        done32 = done32 + jnp.where(plane > 0, below, 0.0) + jnp.where(plane < planes - 1, above, 0.0)
        done[which] = done32.astype(done.dtype)
        first = 4 + 2 * which
        to = first + rank // 4
        for m in range(4):
            @pl.when((rank % 4 == m) & (to != rank))
            def _():
                kv_copy(m, which, to).start()

            @pl.when((rank % 4 == m) & (to == rank))
            def _():
                kv_local(m, which).start()

    gather_wait(*gather, FROM_SIBLING)
    gather_sent(*gather)
    own_block.wait()

    @pl.when(rank < 4)
    def _():
        for m in range(2):
            @pl.when(2 * rank + m != rank)
            def _():
                q_copy(m, 0).wait_recv()

            @pl.when(2 * rank + m == rank)
            def _():
                q_local().wait()

    for which in range(2):
        first = 4 + 2 * which

        @pl.when((rank == first) | (rank == first + 1))
        def _():
            for m in range(4):
                @pl.when(4 * (rank - first) + m != rank)
                def _():
                    kv_copy(m, which, 0).wait_recv()

                @pl.when(4 * (rank - first) + m == rank)
                def _():
                    kv_local(m, which).wait()

    @pl.when(rank != 0)
    def _():
        q_copy(0, 0).wait_send()

    for which in range(2):
        @pl.when(4 + 2 * which + rank // 4 != rank)
        def _():
            kv_copy(0, which, 0).wait_send()

    for j in range(planes - 1):
        for which in range(2):
            for side in range(2):
                @pl.when(sends(j, side))
                def _():
                    step_copy(j, which, side).wait_send()


def return_heads(grad_query, grad_kv, gated, plane_mid, line_blocks, collective_id):
    _, tokens, width = grad_query.shape
    planes = lax.axis_size("sp")
    ranks = lax.axis_size("fsdp")
    vmem = pl.BlockSpec(memory_space=pltpu.VMEM)
    hbm = pl.BlockSpec(memory_space=pl.ANY)
    return pl.pallas_call(
        functools.partial(unheads_kernel, planes),
        out_shape=(
            jax.ShapeDtypeStruct((4, tokens, width), grad_query.dtype),
            jax.ShapeDtypeStruct((gated.shape[1], plane_mid.shape[-1]), gated.dtype),
            jax.ShapeDtypeStruct((ranks,) + line_blocks.shape[2:], line_blocks.dtype),
        ),
        in_specs=[vmem, vmem, vmem, hbm, hbm],
        out_specs=(vmem, vmem, hbm),
        scratch_shapes=[
            pltpu.VMEM(plane_mid.shape, plane_mid.dtype),
            pltpu.SemaphoreType.DMA,
            pltpu.SemaphoreType.DMA((GATHER_COPIES,)),
            pltpu.SemaphoreType.DMA((GATHER_COPIES,)),
            pltpu.SemaphoreType.DMA,
            pltpu.VMEM((2, planes - 1, 2, tokens, width), grad_query.dtype),
            pltpu.VMEM((2, planes - 1, 2, tokens, width), grad_query.dtype),
            pltpu.VMEM((2, tokens, width), grad_query.dtype),
            pltpu.SemaphoreType.DMA,
            pltpu.SemaphoreType.DMA,
            pltpu.SemaphoreType.DMA((2,)),
            pltpu.SemaphoreType.DMA((2,)),
            pltpu.SemaphoreType.DMA((4,)),
            pltpu.SemaphoreType.DMA((2, planes - 1, 2)),
            pltpu.SemaphoreType.DMA((2, planes - 1, 2)),
        ],
        compiler_params=pltpu.CompilerParams(
            collective_id=collective_id, has_side_effects=True, vmem_limit_bytes=VMEM_LIMIT
        ),
        name="return_heads",
    )(grad_query, grad_kv, gated, plane_mid, line_blocks)


def stack_heads(ref):
    return ref[...].reshape(ref.shape[0] * ref.shape[1], ref.shape[2])


def block_bounds(lengths_ref, ranks, planes, rows):
    block = pl.program_id(0)
    span = planes * rows
    first = block * span + lax.axis_index("sp") * rows
    start, end = jnp.int32(0), jnp.int32(0)
    for item in range(lengths_ref.shape[0]):
        end = end + lengths_ref[item]
        start = jnp.where(first >= end, end, start)
    return start // span, block, first


def row_starts(lengths_ref, tokens):
    start, end = jnp.zeros_like(tokens), jnp.int32(0)
    for item in range(lengths_ref.shape[0]):
        end = end + lengths_ref[item]
        start = jnp.where(tokens >= end, end, start)
    return start


def chunk_weights(query, key, scale, tokens, starts, first_key):
    scores = mat_nt(query, key) * scale
    columns = first_key + lax.broadcasted_iota(jnp.int32, scores.shape, 1)
    allowed = (columns <= tokens) & (columns >= starts)
    return jnp.where(allowed, jnp.exp(scores), 0.0)


def query_tokens(first, rows, group):
    row = lax.broadcasted_iota(jnp.int32, (group * rows, 1), 0)
    return first + lax.rem(row, rows)


def attend_kernel(ranks, planes, lengths_ref, q_ref, kv_ref, gate_ref, att_ref, total_ref, gated_ref):
    group, rows, width = q_ref.shape
    scale = HEAD_DIM ** (-0.5)
    low, high, first = block_bounds(lengths_ref, ranks, planes, rows)
    tokens = query_tokens(first, rows, group)
    starts = row_starts(lengths_ref, tokens)
    query = stack_heads(q_ref)
    span = planes * rows

    def step(chunk, running):
        total, unnorm = running
        key = kv_ref[:, 0, chunk].reshape(span, width)
        value = kv_ref[:, 1, chunk].reshape(span, width)
        weights = chunk_weights(query, key, scale, tokens, starts, chunk * span)
        total = total + jnp.sum(weights, axis=1, keepdims=True)
        unnorm = unnorm + jnp.dot(
            weights.astype(jnp.bfloat16), value, preferred_element_type=jnp.float32
        )
        return total, unnorm

    total, unnorm = lax.fori_loop(
        low,
        high + 1,
        step,
        (
            jnp.zeros((group * rows, 1), jnp.float32),
            jnp.zeros((group * rows, width), jnp.float32),
        ),
    )
    attended = unnorm / total
    att_ref[...] = attended.reshape(group, rows, width)
    total_ref[...] = total.reshape(group, rows, 1)
    sent = attended.astype(jnp.bfloat16).astype(jnp.float32)
    for head in range(group):
        gated = sent[head * rows : (head + 1) * rows] * jax.nn.sigmoid(gate_ref[head])
        gated_ref[:, head * width : (head + 1) * width] = gated.astype(jnp.bfloat16)


def attend(lengths, query, kv, gate_logit, rows):
    group, tokens, width = query.shape
    planes = kv.shape[0]
    ranks = tokens // rows
    kv_blocks = kv.reshape(planes, 2, ranks, rows, width)
    block = pl.BlockSpec((group, rows, width), lambda i, *_: (0, i, 0))
    thin = pl.BlockSpec((group, rows, 1), lambda i, *_: (0, i, 0))
    return pl.pallas_call(
        functools.partial(attend_kernel, ranks, planes),
        grid_spec=pltpu.PrefetchScalarGridSpec(
            num_scalar_prefetch=1,
            grid=(ranks,),
            in_specs=[
                block,
                pl.BlockSpec((planes, 2, ranks, rows, width), lambda i, *_: (0, 0, 0, 0, 0)),
                thin,
            ],
            out_specs=(
                block,
                thin,
                pl.BlockSpec((rows, group * width), lambda i, *_: (i, 0)),
            ),
        ),
        out_shape=(
            jax.ShapeDtypeStruct((group, tokens, width), jnp.float32),
            jax.ShapeDtypeStruct((group, tokens, 1), jnp.float32),
            jax.ShapeDtypeStruct((tokens, group * width), jnp.bfloat16),
        ),
        compiler_params=pltpu.CompilerParams(vmem_limit_bytes=VMEM_LIMIT),
        name="attend",
    )(lengths, query, kv_blocks, gate_logit)


def attend_back_kernel(
    ranks, planes, lengths_ref, q_ref, kv_ref, gate_ref, att_ref, total_ref, dgated_ref, dq_ref, dkv_ref, dgate_ref, sums
):
    group, rows, width = q_ref.shape
    scale = HEAD_DIM ** (-0.5)
    low, high, first = block_bounds(lengths_ref, ranks, planes, rows)
    tokens = query_tokens(first, rows, group)
    starts = row_starts(lengths_ref, tokens)
    query = stack_heads(q_ref)
    span = planes * rows

    @pl.when(pl.program_id(0) == 0)
    def _():
        sums[...] = jnp.zeros_like(sums)

    attended = stack_heads(att_ref)
    sent = attended.astype(jnp.bfloat16).astype(jnp.float32)
    total = stack_heads(total_ref)
    logit = stack_heads(gate_ref)
    prob = jax.nn.sigmoid(logit)
    dgated = jnp.concatenate(
        [dgated_ref[:, head * width : (head + 1) * width] for head in range(group)], axis=0
    )
    dattended = (dgated * prob).astype(jnp.bfloat16)
    dlogit = jnp.sum(dgated * sent, axis=1, keepdims=True) * prob * (1.0 - prob)
    dgate_ref[...] = dlogit.astype(jnp.bfloat16).reshape(group, rows, 1)
    dattended = dattended.astype(jnp.float32)
    scaled = (dattended / total).astype(jnp.bfloat16)
    delta = jnp.sum(dattended * attended, axis=1, keepdims=True) / total

    def step(chunk, dquery):
        key = kv_ref[:, 0, chunk].reshape(span, width)
        value = kv_ref[:, 1, chunk].reshape(span, width)
        weights = chunk_weights(query, key, scale, tokens, starts, chunk * span)
        dprob = mat_nt(scaled, value)
        dscore = (weights * (dprob - delta)).astype(jnp.bfloat16)
        dquery = dquery + jnp.dot(dscore, key, preferred_element_type=jnp.float32)
        dkey = mat_tn(dscore, query)
        dvalue = mat_tn(weights.astype(jnp.bfloat16), scaled)
        sums[:, 0, chunk] += dkey.reshape(planes, rows, width)
        sums[:, 1, chunk] += dvalue.reshape(planes, rows, width)
        return dquery

    dquery = lax.fori_loop(
        low, high + 1, step, jnp.zeros((group * rows, width), jnp.float32)
    )
    dq_ref[...] = (dquery * scale).astype(jnp.bfloat16).reshape(group, rows, width)

    @pl.when(pl.program_id(0) == ranks - 1)
    def _():
        for chunk in range(ranks):
            dkv_ref[:, 0, chunk] = (sums[:, 0, chunk] * scale).astype(jnp.bfloat16)
            dkv_ref[:, 1, chunk] = sums[:, 1, chunk].astype(jnp.bfloat16)


def attend_back(lengths, query, kv, gate_logit, attended, total, dgated, rows):
    group, tokens, width = query.shape
    planes = kv.shape[0]
    ranks = tokens // rows
    kv_blocks = kv.reshape(planes, 2, ranks, rows, width)
    block = pl.BlockSpec((group, rows, width), lambda i, *_: (0, i, 0))
    thin = pl.BlockSpec((group, rows, 1), lambda i, *_: (0, i, 0))
    whole = pl.BlockSpec((planes, 2, ranks, rows, width), lambda i, *_: (0, 0, 0, 0, 0))
    dquery, dkv, dgate = pl.pallas_call(
        functools.partial(attend_back_kernel, ranks, planes),
        grid_spec=pltpu.PrefetchScalarGridSpec(
            num_scalar_prefetch=1,
            grid=(ranks,),
            in_specs=[
                block,
                whole,
                thin,
                block,
                thin,
                pl.BlockSpec((rows, group * width), lambda i, *_: (i, 0)),
            ],
            out_specs=(block, whole, thin),
            scratch_shapes=[pltpu.VMEM((planes, 2, ranks, rows, width), jnp.float32)],
        ),
        out_shape=(
            jax.ShapeDtypeStruct((group, tokens, width), jnp.bfloat16),
            jax.ShapeDtypeStruct((planes, 2, ranks, rows, width), jnp.bfloat16),
            jax.ShapeDtypeStruct((group, tokens, 1), jnp.bfloat16),
        ),
        compiler_params=pltpu.CompilerParams(vmem_limit_bytes=VMEM_LIMIT),
        name="attend_back",
    )(lengths, query, kv_blocks, gate_logit, attended, total, dgated)
    return dquery, dkv.reshape(planes, 2, tokens, width), dgate


def middle_kernel(
    planes,
    gated_ref,
    wout_ref,
    x_ref,
    scale_ref,
    dy_hbm,
    wg_hbm,
    wu_hbm,
    wd_hbm,
    xg_hbm,
    line_hbm,
    down_hbm,
    mid_ref,
    dmid_ref,
    gain_ref,
    pm_ref,
    dgated_ref,
    act_hbm,
    xg,
    act_ref,
    flush_sem,
    wg,
    wu,
    wd,
    dy,
    dhid,
    near_out,
    near_in,
    far_out,
    far_in,
    keep,
    down_buf,
    load_sem,
    dy_sem,
    down_sem,
    near_send,
    near_recv,
    far_send,
    far_recv,
    ag_send,
    ag_recv,
    line_send,
    line_recv,
):
    rank, plane = lax.axis_index("fsdp"), lax.axis_index("sp")
    ranks, rows, width = xg.shape
    loads = [
        pltpu.make_async_copy(wd_hbm, wd, load_sem.at[0]),
        pltpu.make_async_copy(wg_hbm, wg, load_sem.at[1]),
        pltpu.make_async_copy(wu_hbm, wu, load_sem.at[2]),
    ]
    dy_load = pltpu.make_async_copy(dy_hbm, dy, dy_sem)
    others = [lax.rem(plane + k, planes) for k in range(1, planes)]
    greet([(rank ^ k, plane) for k in (1, 2, 4, 6)] + [(rank, other) for other in others])

    def along(source, which):
        return [
            peer_copy(
                source,
                line_hbm.at[which, j - 1],
                line_send.at[which, j - 1],
                line_recv.at[which, j - 1],
                rank,
                lax.rem(plane + planes - j, planes),
            )
            for j in range(1, planes)
        ]

    def near(phase, i):
        return peer_copy(
            near_out.at[phase, i],
            near_in.at[phase, i],
            near_send.at[phase, i],
            near_recv.at[phase, i],
            rank ^ 1,
            plane,
        )

    def far(phase, i, k):
        return peer_copy(
            far_out.at[phase, i],
            far_in.at[phase, i],
            far_send.at[phase, i],
            far_recv.at[phase, i],
            rank ^ k,
            plane,
        )

    order = (6, 2, 4, 0)
    for i, k in enumerate(order):
        part = jnp.dot(
            gated_ref[rank ^ 1 ^ k], wout_ref[...], preferred_element_type=jnp.float32
        )
        near_out[0, i] = part.astype(jnp.bfloat16)
        near(0, i).start()
    dy_load.start()
    for copy in loads:
        copy.start()
    dy_line = along(dy_hbm.at[rank], 1)
    for copy in dy_line:
        copy.start()
    for i, k in enumerate(order):
        part = jnp.dot(gated_ref[rank ^ k], wout_ref[...], preferred_element_type=jnp.float32)
        near(0, i).wait_recv()
        part = part + near_in[0, i].astype(jnp.float32)
        if k:
            far_out[0, i] = part.astype(jnp.bfloat16)
            far(0, i, k).start()
        else:
            keep[...] = part

    dy_load.wait()
    loads[0].wait()

    @pl.loop(0, ranks // 2)
    def _(p):
        pair = dy[pl.ds(2 * p, 2)].reshape(2 * rows, width)
        dhid[p] = mat_nt(pair, wd[...])

    loads[1].wait()
    loads[2].wait()
    middle = x_ref[...].astype(jnp.float32) + keep[...]
    for i in (1, 2, 0):
        far(0, i, order[i]).wait_recv()
        middle = middle + far_in[0, i].astype(jnp.float32)
    inverse = inv_rms(middle)
    mid_ref[...] = middle
    normed = (middle * inverse * scale_ref[...]).astype(jnp.bfloat16)
    xg[rank] = normed
    sems = (ag_send.at[0], ag_recv.at[0])
    gather_start(xg, *sems)
    xb_line = along(xg.at[rank], 0)
    for copy in xb_line:
        copy.start()

    slots = {2: 0, 4: 1, 6: 2, 0: 3}

    def down_copy(p, slot):
        return pltpu.make_async_copy(
            down_buf.at[slot], down_hbm.at[pl.ds(2 * p, 2)], down_sem.at[slot]
        )

    def act_copy(p):
        where = pl.ds(pl.multiple_of(2 * rows * p, 2 * rows), 2 * rows)
        return pltpu.make_async_copy(
            act_ref.at[:, where], act_hbm.at[:, where], flush_sem.at[p]
        )

    def feed(k):
        p = (rank ^ k) // 2
        slot = (0, 2, 4, 6).index(k) % 2
        pair = xg[pl.ds(2 * p, 2)].reshape(2 * rows, width)
        gate_pre = mat_nt(pair, wg[...])
        up_pre = mat_nt(pair, wu[...])
        grad_hidden = dhid[p]
        sigma = jax.nn.sigmoid(gate_pre)
        swish = gate_pre * sigma
        grad_gate = (grad_hidden * up_pre * sigma * (1.0 + gate_pre * (1.0 - sigma))).astype(
            jnp.bfloat16
        )
        grad_up = (grad_hidden * swish).astype(jnp.bfloat16)
        part = jnp.dot(grad_gate, wg[...], preferred_element_type=jnp.float32) + jnp.dot(
            grad_up, wu[...], preferred_element_type=jnp.float32
        )
        i = slots[k]
        halves = part.reshape(2, rows, width)
        mine_first = lax.rem(rank, 2) == 0
        mine = jnp.where(mine_first, halves[0], halves[1])
        theirs = jnp.where(mine_first, halves[1], halves[0])
        near_out[1, i] = theirs.astype(jnp.bfloat16)
        near(1, i).start()
        hidden = (swish * up_pre).astype(jnp.bfloat16)
        for kept, value in enumerate((grad_gate, grad_up, hidden)):
            act_ref[kept, pl.ds(pl.multiple_of(2 * rows * p, 2 * rows), 2 * rows)] = value
        act_copy(p).start()
        down = jnp.dot(hidden, wd[...], preferred_element_type=jnp.float32)
        if k in (4, 6):
            down_copy(p, slot).wait()
        down_buf[slot] = down.astype(jnp.bfloat16).reshape(2, rows, width)
        down_copy(p, slot).start()
        near(1, i).wait_recv()
        mine = mine + near_in[1, i].astype(jnp.float32)
        if k:
            far_out[1, i] = mine.astype(jnp.bfloat16)
            far(1, i, k).start()
        else:
            keep[...] = mine

    gather_wait(xg, *sems, (6,))
    feed(0)
    gather_pass(xg, *sems, NEIGHBOURS_FIRST)
    gather_wait(xg, *sems, (7, 8))
    feed(2)
    gather_pass(xg, *sems, DIAGONAL)
    gather_wait(xg, *sems, (9, 10))
    feed(4)
    gather_wait(xg, *sems, (11, 12))
    feed(6)
    xg_copy = pltpu.make_async_copy(xg, xg_hbm, flush_sem.at[ranks // 2])
    xg_copy.start()

    grad = keep[...]
    for i, k in enumerate((2, 4, 6)):
        far(1, i, k).wait_recv()
        grad = grad + far_in[1, i].astype(jnp.float32)
    middle = mid_ref[...]
    inverse = inv_rms(middle)
    gain_ref[...] = jnp.sum(grad * middle * inverse, axis=0, keepdims=True)
    grad_middle = dy[rank].astype(jnp.float32) + norm_back(
        grad, middle, inverse, scale_ref[...]
    )
    dmid_ref[...] = grad_middle
    pm_ref[rank] = grad_middle.astype(jnp.bfloat16)
    sems2 = (ag_send.at[1], ag_recv.at[1])
    gather_start(pm_ref, *sems2)

    def gated_grad(k):
        p = (rank ^ k) // 2
        pair = pm_ref[pl.ds(2 * p, 2)].reshape(2 * rows, width)
        dgated_ref[pl.ds(2 * p, 2)] = mat_nt(pair, wout_ref[...]).reshape(
            2, rows, wout_ref.shape[0]
        )

    gather_wait(pm_ref, *sems2, (6,))
    gated_grad(0)
    gather_pass(pm_ref, *sems2, NEIGHBOURS_FIRST)
    gather_wait(pm_ref, *sems2, (7, 8))
    gated_grad(2)
    gather_wait(pm_ref, *sems2, (9, 10))
    gated_grad(4)
    gather_pass(pm_ref, *sems2, DIAGONAL)
    gather_wait(pm_ref, *sems2, (11, 12))
    gated_grad(6)

    gather_sent(xg, *sems)
    xg_copy.wait()
    for p in range(ranks // 2):
        act_copy(p).wait()
    gather_sent(pm_ref, *sems2)
    for copy in dy_line + xb_line:
        copy.wait()
    for phase in range(2):
        for i in range(4):
            near(phase, i).wait_send()
        for i in range(3):
            far(phase, i, 2).wait_send()
    down_copy(0, 0).wait()
    down_copy(0, 1).wait()


def middle_layer(gated, w_out, x, scale, grad_plane, w_gate, w_up, w_down, collective_id):
    ranks, rows, _ = gated.shape
    planes = lax.axis_size("sp")
    width = x.shape[1]
    hidden = w_gate.shape[0]
    features = w_out.shape[0]
    vmem = pl.BlockSpec(memory_space=pltpu.VMEM)
    hbm = pl.BlockSpec(memory_space=pl.ANY)
    half, full = jnp.bfloat16, jnp.float32
    return pl.pallas_call(
        functools.partial(middle_kernel, planes),
        out_shape=(
            jax.ShapeDtypeStruct((ranks, rows, width), half),
            jax.ShapeDtypeStruct((2, planes - 1, rows, width), half),
            jax.ShapeDtypeStruct((ranks, rows, width), half),
            jax.ShapeDtypeStruct((rows, width), full),
            jax.ShapeDtypeStruct((rows, width), full),
            jax.ShapeDtypeStruct((1, width), full),
            jax.ShapeDtypeStruct((ranks, rows, width), half),
            jax.ShapeDtypeStruct((ranks, rows, features), full),
            jax.ShapeDtypeStruct((3, ranks * rows, hidden), half),
        ),
        in_specs=[vmem, vmem, vmem, vmem, hbm, hbm, hbm, hbm],
        out_specs=(hbm, hbm, hbm, vmem, vmem, vmem, vmem, vmem, hbm),
        scratch_shapes=[
            pltpu.VMEM((ranks, rows, width), half),
            pltpu.VMEM((3, ranks * rows, hidden), half),
            pltpu.SemaphoreType.DMA((ranks // 2 + 1,)),
            pltpu.VMEM((hidden, width), half),
            pltpu.VMEM((hidden, width), half),
            pltpu.VMEM((hidden, width), half),
            pltpu.VMEM((ranks, rows, width), half),
            pltpu.VMEM((ranks // 2, 2 * rows, hidden), full),
            pltpu.VMEM((2, 4, rows, width), half),
            pltpu.VMEM((2, 4, rows, width), half),
            pltpu.VMEM((2, 3, rows, width), half),
            pltpu.VMEM((2, 3, rows, width), half),
            pltpu.VMEM((rows, width), full),
            pltpu.VMEM((2, 2, rows, width), half),
            pltpu.SemaphoreType.DMA((3,)),
            pltpu.SemaphoreType.DMA,
            pltpu.SemaphoreType.DMA((2,)),
            pltpu.SemaphoreType.DMA((2, 4)),
            pltpu.SemaphoreType.DMA((2, 4)),
            pltpu.SemaphoreType.DMA((2, 3)),
            pltpu.SemaphoreType.DMA((2, 3)),
            pltpu.SemaphoreType.DMA((2, GATHER_COPIES)),
            pltpu.SemaphoreType.DMA((2, GATHER_COPIES)),
            pltpu.SemaphoreType.DMA((2, planes - 1)),
            pltpu.SemaphoreType.DMA((2, planes - 1)),
        ],
        compiler_params=pltpu.CompilerParams(
            collective_id=collective_id, has_side_effects=True, vmem_limit_bytes=VMEM_LIMIT
        ),
        name="middle_layer",
    )(gated, w_out, x, scale, grad_plane, w_gate, w_up, w_down)


def feed_weights_kernel(
    planes,
    xp_hbm,
    dp_hbm,
    act_hbm,
    blocks_hbm,
    first_hbm,
    second_hbm,
    down_hbm,
    mid_ref,
    small_ref,
    rows_ref,
    qkv_hbm,
    wg_hbm,
    wu_hbm,
    wd_hbm,
    og_hbm,
    ou_hbm,
    od_hbm,
    h_ref,
    so_ref,
    go_ref,
    sum_hbm,
    more_hbm,
    wg_ref,
    wu_ref,
    wd_ref,
    w_sem,
    og_ref,
    ou_ref,
    od_ref,
    o_sem,
    xbuf,
    dbuf,
    act,
    parts,
    small_buf,
    rows_buf,
    quarter,
    quarters,
    x_sem,
    d_sem,
    act_sem,
    part_sem,
    own_sem,
    ag_send,
    ag_recv,
    line_send,
    line_recv,
    part_send,
    part_recv,
    sum_send,
    sum_recv,
    quarter_sem,
    near_buf,
    out_buf,
    far_buf,
    sib_send,
    sib_recv,
    send_sem,
    recv_sem,
):
    rank, plane = lax.axis_index("fsdp"), lax.axis_index("sp")
    ranks, rows, width = xp_hbm.shape
    part = ranks // 2
    chunk = part * rows
    others = [lax.rem(plane + k, planes) for k in range(1, planes)]
    greet([(rank ^ k, plane) for k in (1, 2, 4, 6)] + [(rank, other) for other in others])

    picks = ((0, 1), (1, 1), (1, 2), (0, 2))
    gathers = [(more_hbm.at[g], ag_send.at[g], ag_recv.at[g]) for g in range(4)]
    own_blocks = [
        pltpu.make_async_copy(blocks_hbm.at[pick], more_hbm.at[g, rank], own_sem.at[g])
        for g, pick in enumerate(picks)
    ]

    def begin(g):
        gather_start(*gathers[g], own=blocks_hbm.at[picks[g]])

    def load(step, start):
        slot = lax.rem(step, 2)
        block = pl.ds(part * lax.rem(step, 2), part)
        group = step // 2
        sources = (
            (xp_hbm.at[block], dp_hbm.at[block]),
            (first_hbm.at[block], second_hbm.at[block]),
            (more_hbm.at[0, block], more_hbm.at[1, block]),
            (more_hbm.at[3, block], more_hbm.at[2, block]),
        )
        for index, (x_from, d_from) in enumerate(sources):
            @pl.when(group == index)
            def _():
                for copy in (
                    pltpu.make_async_copy(x_from, xbuf.at[slot], x_sem.at[slot]),
                    pltpu.make_async_copy(d_from, dbuf.at[slot], d_sem.at[slot]),
                ):
                    if start:
                        copy.start()
                    else:
                        copy.wait()

    def kept(step):
        where = pl.ds(pl.multiple_of(step * chunk, chunk), chunk)
        return pltpu.make_async_copy(act_hbm.at[:, where], act, act_sem)

    scatter = (near_buf, sib_send, sib_recv)
    own_parts = [
        pltpu.make_async_copy(down_hbm.at[rank ^ k], parts.at[i], part_sem.at[i])
        for i, k in enumerate(SCATTER_ORDER)
    ]
    small = [
        peer_copy(
            source,
            buffer.at[k],
            line_send.at[which, k],
            line_recv.at[which, k],
            rank,
            others[k],
        )
        for which, (source, buffer) in enumerate(((small_ref, small_buf), (rows_ref, rows_buf)))
        for k in range(planes - 1)
    ]

    quarter_rows = quarter.shape[0]

    def rows_of(index):
        return pl.ds(pl.multiple_of(index * quarter_rows, quarter_rows), quarter_rows)

    own_quarter = pltpu.make_async_copy(qkv_hbm.at[rows_of(plane)], quarter, quarter_sem.at[0])
    own_sum = pltpu.make_async_copy(quarter, sum_hbm.at[rows_of(plane)], quarter_sem.at[1])
    partials = [
        peer_copy(
            qkv_hbm.at[rows_of(others[k])],
            quarters.at[k],
            part_send.at[k],
            part_recv.at[k],
            rank,
            others[k],
        )
        for k in range(planes - 1)
    ]
    sums = [
        peer_copy(
            quarter,
            sum_hbm.at[rows_of(plane)],
            sum_send.at[k],
            sum_recv.at[k],
            rank,
            others[k],
        )
        for k in range(planes - 1)
    ]

    totals = ((og_ref, og_hbm), (ou_ref, ou_hbm), (od_ref, od_hbm))
    load(0, True)
    kept(0).start()
    weights = [
        pltpu.make_async_copy(source, target, w_sem.at[index])
        for index, (source, target) in enumerate(
            ((wg_hbm, wg_ref), (wu_hbm, wu_ref), (wd_hbm, wd_ref))
        )
    ]
    for copy in weights:
        copy.start()
    own_quarter.start()
    for copy in own_blocks + small + own_parts + partials:
        copy.start()
    begin(0)
    for i in range(4):
        scatter_near(down_hbm, i, *scatter).start()

    @pl.loop(0, 2 * planes)
    def _(step):
        @pl.when(step == 1)
        def _():
            kept(1).start()
            begin(1)

        @pl.when(step == 2)
        def _():
            for copy in weights:
                copy.wait()
            gather_pass(*gathers[0], NEIGHBOURS_FIRST)

        @pl.when(step == 3)
        def _():
            gather_pass(*gathers[0], DIAGONAL)
            gather_pass(*gathers[1], NEIGHBOURS_FIRST)
            begin(2)
            for i, k in enumerate(SCATTER_ORDER):
                own_parts[i].wait()
                scatter_near(down_hbm, i, *scatter).wait_recv()
                joined = parts[i].astype(jnp.float32) + near_buf[i].astype(jnp.float32)
                if k:
                    out_buf[i] = joined.astype(out_buf.dtype)
                else:
                    parts[i] = joined.astype(parts.dtype)

        @pl.when(step == 4)
        def _():
            gather_pass(*gathers[1], DIAGONAL)
            begin(3)
            for g in (0, 1):
                gather_wait(*gathers[g], FROM_SIBLING)
                own_blocks[g].wait()
            load(step, True)
            own_quarter.wait()
            total = quarter[...].astype(jnp.float32)
            for k in range(planes - 1):
                partials[k].wait()
                total = total + quarters[k].astype(jnp.float32)
            quarter[...] = total.astype(quarter.dtype)
            own_sum.start()
            for copy in sums:
                copy.start()

        @pl.when(step == 5)
        def _():
            gather_pass(*gathers[2], NEIGHBOURS_FIRST)
            gather_pass(*gathers[3], NEIGHBOURS_FIRST)

        @pl.when(step == 6)
        def _():
            for g in (2, 3):
                gather_pass(*gathers[g], DIAGONAL)
            for i in range(3):
                scatter_far(i, out_buf, far_buf, send_sem, recv_sem).start()
            for g in (2, 3):
                gather_wait(*gathers[g], FROM_SIBLING)
                own_blocks[g].wait()
            load(step, True)

        load(step, False)

        @pl.when((lax.rem(step, 2) == 0) | (step == 1))
        def _():
            load(step + 1, True)

        slot = lax.rem(step, 2)
        normed = xbuf[slot].reshape(chunk, width)
        grad = dbuf[slot].reshape(chunk, width)

        own = step < 2

        @pl.when(own)
        def _():
            kept(0).wait()

        @pl.when(jnp.logical_not(own))
        def _():
            gate_pre = mat_nt(normed, wg_ref[...])
            up_pre = mat_nt(normed, wu_ref[...])
            grad_hidden = mat_nt(grad, wd_ref[...])
            sigma = jax.nn.sigmoid(gate_pre)
            swish = gate_pre * sigma
            act[0] = (grad_hidden * up_pre * sigma * (1.0 + gate_pre * (1.0 - sigma))).astype(
                jnp.bfloat16
            )
            act[1] = (grad_hidden * swish).astype(jnp.bfloat16)
            act[2] = (swish * up_pre).astype(jnp.bfloat16)

        @pl.when(step == 0)
        def _():
            for ref in (og_ref, ou_ref, od_ref):
                ref[...] = jnp.zeros_like(ref)

        for index, other in ((0, normed), (1, normed), (2, grad)):
            source, target = totals[index]
            source[...] += mat_tn(act[index], other)

            @pl.when(step == 2 * planes - 1)
            def _():
                pltpu.make_async_copy(source, target, o_sem.at[index]).start()

    output = mid_ref[...] + parts[3].astype(jnp.float32)
    for i in range(3):
        scatter_far(i, out_buf, far_buf, send_sem, recv_sem).wait()
        output = output + far_buf[i].astype(jnp.float32)
    h_ref[...] = output.astype(h_ref.dtype)
    for copy in small + sums:
        copy.wait()
    own_sum.wait()
    total, gate_rows = small_ref[...], rows_ref[...]
    for k in range(planes - 1):
        total = total + small_buf[k]
        gate_rows = gate_rows + rows_buf[k]
    so_ref[...] = total
    go_ref[...] = gate_rows
    for i in range(4):
        scatter_near(down_hbm, i, *scatter).wait_send()
    for gather in gathers:
        gather_sent(*gather)
    for index, (source, target) in enumerate(totals):
        pltpu.make_async_copy(source, target, o_sem.at[index]).wait()


def feed_weights(plane_x, plane_grad, acts, blocks, first, second, down, middle, small, gate_rows, qkv_part, w_gate, w_up, w_down, collective_id):
    ranks, rows, width = plane_x.shape
    planes = lax.axis_size("sp")
    hidden = w_gate.shape[0]
    vmem = pl.BlockSpec(memory_space=pltpu.VMEM)
    hbm = pl.BlockSpec(memory_space=pl.ANY)
    tokens = planes * ranks * rows
    half, full = plane_x.dtype, jnp.float32
    return pl.pallas_call(
        functools.partial(feed_weights_kernel, planes),
        in_specs=[hbm] * 7 + [vmem] * 3 + [hbm] * 4,
        out_specs=(hbm,) * 3 + (vmem,) * 3 + (hbm, hbm),
        out_shape=[jax.ShapeDtypeStruct(w_gate.shape, full)] * 3
        + [
            jax.ShapeDtypeStruct((rows, width), half),
            jax.ShapeDtypeStruct(small.shape, full),
            jax.ShapeDtypeStruct(gate_rows.shape, full),
            jax.ShapeDtypeStruct(qkv_part.shape, half),
            jax.ShapeDtypeStruct((4, ranks, rows, width), half),
        ],
        scratch_shapes=[pltpu.VMEM(w_gate.shape, half)] * 3
        + [
            pltpu.SemaphoreType.DMA((3,)),
        ]
        + [pltpu.VMEM(w_gate.shape, full)] * 3
        + [
            pltpu.SemaphoreType.DMA((3,)),
            pltpu.VMEM((2, ranks // 2, rows, width), half),
            pltpu.VMEM((2, ranks // 2, rows, width), half),
            pltpu.VMEM((3, ranks // 2 * rows, hidden), half),
            pltpu.VMEM((4, rows, width), half),
            pltpu.VMEM((planes - 1,) + small.shape, full),
            pltpu.VMEM((planes - 1,) + gate_rows.shape, full),
            pltpu.VMEM((qkv_part.shape[0] // planes, width), half),
            pltpu.VMEM((planes - 1, qkv_part.shape[0] // planes, width), half),
            pltpu.SemaphoreType.DMA((2,)),
            pltpu.SemaphoreType.DMA((2,)),
            pltpu.SemaphoreType.DMA,
            pltpu.SemaphoreType.DMA((4,)),
            pltpu.SemaphoreType.DMA((4,)),
            pltpu.SemaphoreType.DMA((4, GATHER_COPIES)),
            pltpu.SemaphoreType.DMA((4, GATHER_COPIES)),
            pltpu.SemaphoreType.DMA((2, planes - 1)),
            pltpu.SemaphoreType.DMA((2, planes - 1)),
        ]
        + [pltpu.SemaphoreType.DMA((planes - 1,))] * 4
        + [
            pltpu.SemaphoreType.DMA((2,)),
        ]
        + scatter_scratch(rows, width, half),
        cost_estimate=pl.CostEstimate(
            flops=12 * tokens * w_gate.size,
            bytes_accessed=4 * tokens * width + 18 * w_gate.size,
            transcendentals=tokens * w_gate.shape[0],
        ),
        compiler_params=pltpu.CompilerParams(
            collective_id=collective_id, has_side_effects=True, vmem_limit_bytes=VMEM_LIMIT
        ),
        name="feed_weights",
    )(plane_x, plane_grad, acts, blocks, first, second, down, middle, small, gate_rows, qkv_part, w_gate, w_up, w_down)[:7]


def front_kernel(
    planes,
    lengths_ref,
    x_ref,
    small_ref,
    w_ref,
    wg_ref,
    dyo_ref,
    q_ref,
    kv_ref,
    dy_ref,
    xg_hbm,
    xa_hbm,
    raw_hbm,
    gate_ref,
    attn_ref,
    ffn_ref,
    head_ref,
    cos_ref,
    sin_ref,
    xg,
    xa_ref,
    raw_ref,
    flush_sem,
    nat,
    gains,
    small_send,
    small_recv,
    ag_send,
    ag_recv,
    own_sem,
    local_sem,
    q_send,
    q_recv,
    kv_send,
    kv_recv,
    line_send,
    line_recv,
):
    rank, plane = lax.axis_index("fsdp"), lax.axis_index("sp")
    ranks, rows, width = xg.shape
    pair_rows = 2 * rows
    chip = rank // 2
    greet_line(ranks, planes)
    own_block = pltpu.make_async_copy(dyo_ref, dy_ref.at[rank], own_sem)
    own_block.start()
    small = []
    for k in range(1, ranks):
        copy = peer_copy(
            small_ref, gains.at[rank], small_send.at[k - 1], small_recv.at[k - 1], rank ^ k, plane
        )
        copy.start()
        small.append(copy)
    sems = (ag_send.at[0], ag_recv.at[0])
    gather_start(xg, *sems, own=x_ref)
    xg[rank] = x_ref[...]
    gains[rank] = small_ref[...]

    half = HEAD_DIM // 2
    lane = lax.broadcasted_iota(jnp.int32, (1, HEAD_DIM), 1)
    step = lax.rem(lane, half).astype(jnp.float32)
    frequency = jnp.exp(-math.log(ROPE_BASE) * 2.0 * step / HEAD_DIM)
    sign = jnp.where(lane < half, -1.0, 1.0)

    @pl.loop(0, ranks)
    def _(block):
        tokens = (block * planes + plane) * rows + lax.broadcasted_iota(jnp.int32, (rows, 1), 0)
        position = tokens - row_starts(lengths_ref, tokens)
        angles = position.astype(jnp.float32) * frequency
        where = pl.ds(pl.multiple_of(block * rows, rows), rows)
        cos_ref[where] = jnp.cos(angles)
        sin_ref[where] = jnp.sin(angles) * sign

    for copy in small:
        copy.wait_recv()
    head_q, head_k = gains[0, 4:5], gains[0, 5:6]
    for r in range(1, ranks):
        head_q = head_q + gains[r, 4:5]
        head_k = head_k + gains[r, 5:6]
    head_ref[...] = jnp.where(rank < ranks // 2, head_q, head_k)
    for r in range(ranks):
        for i in range(2):
            columns = slice((2 * r + i) * HEAD_DIM, (2 * r + i + 1) * HEAD_DIM)
            attn_ref[:, columns] = gains[r, i : i + 1]
            ffn_ref[:, columns] = gains[r, 2 + i : 3 + i]

    def token_rows(p):
        return pl.ds(pl.multiple_of(p * pair_rows, pair_rows), pair_rows)

    def q_copy(m, p, to):
        return peer_copy(
            nat.at[pl.ds(2 * m, 2), token_rows(p)],
            q_ref.at[:, token_rows(p)],
            q_send.at[m, p],
            q_recv.at[p],
            to,
            plane,
        )

    def kv_copy(m, which, p, to):
        return peer_copy(
            nat.at[m, token_rows(p)],
            kv_ref.at[plane, which, token_rows(p)],
            kv_send.at[m, p],
            kv_recv.at[which, p],
            to,
            plane,
        )

    def q_local(p):
        return pltpu.make_async_copy(
            nat.at[pl.ds(0, 2), token_rows(p)], q_ref.at[:, token_rows(p)], local_sem.at[p]
        )

    def kv_local(m, which, p):
        return pltpu.make_async_copy(
            nat.at[m, token_rows(p)], kv_ref.at[plane, which, token_rows(p)], local_sem.at[p]
        )

    def flush(p):
        pair = pl.ds(2 * p, 2)
        return [
            pltpu.make_async_copy(xg.at[pair], xg_hbm.at[pair], flush_sem.at[0, p]),
            pltpu.make_async_copy(xa_ref.at[pair], xa_hbm.at[pair], flush_sem.at[1, p]),
            pltpu.make_async_copy(
                raw_ref.at[token_rows(p)], raw_hbm.at[token_rows(p)], flush_sem.at[2, p]
            ),
        ]

    def process(k):
        p = chip ^ (k // 2)
        inputs = xg[pl.ds(2 * p, 2)].reshape(pair_rows, width).astype(jnp.float32)
        normed = (inputs * inv_rms(inputs) * attn_ref[...]).astype(jnp.bfloat16)
        xa_ref[pl.ds(2 * p, 2)] = normed.reshape(2, rows, width)
        projected = mat_nt(normed, w_ref[...])
        raw_ref[token_rows(p)] = projected
        for copy in flush(p):
            copy.start()
        logits = mat_nt(normed, wg_ref[...])
        for head in range(gate_ref.shape[0]):
            gate_ref[head, token_rows(p)] = logits[:, head : head + 1]
        cosine, sine = cos_ref[token_rows(p)], sin_ref[token_rows(p)]
        for m in range(4):
            head = projected[:, m * HEAD_DIM : (m + 1) * HEAD_DIM]
            scaled = head * inv_rms(head) * head_ref[...]
            turned = scaled * cosine + pltpu.roll(scaled, half, 1) * sine
            nat[m, token_rows(p)] = jnp.where(rank >= 6, head, turned).astype(jnp.bfloat16)

        @pl.when(rank < 4)
        def _():
            for m in range(2):
                @pl.when(2 * rank + m != rank)
                def _():
                    q_copy(m, p, 2 * rank + m).start()

        @pl.when(rank == 0)
        def _():
            q_local(p).start()

        for which in range(2):
            first = 4 + 2 * which

            @pl.when((rank == first) | (rank == first + 1))
            def _():
                for m in range(4):
                    to = 4 * (rank - first) + m

                    @pl.when(to != rank)
                    def _():
                        kv_copy(m, which, p, to).start()

            @pl.when(rank == first + 1)
            def _():
                kv_local((first + 1) % 4, which, p).start()

    def line_piece(origin, which, p, side, j, to):
        piece = kv_ref.at[origin, which, token_rows(p)]
        return peer_copy(
            piece,
            piece,
            line_send.at[side, j, which, p],
            line_recv.at[side, j, which, p],
            rank,
            to,
        )

    def origin_of(side, j):
        return plane - j if side == 0 else plane + j

    def next_of(side):
        return plane + 1 if side == 0 else plane - 1

    def line_go(which, p, j):
        if j == 0:
            @pl.when(rank == 5 + 2 * which)
            def _():
                kv_local((5 + 2 * which) % 4, which, p).wait()

            @pl.when(rank != 5 + 2 * which)
            def _():
                kv_copy(0, which, p, 0).wait_recv()

        for side in range(2):
            if j:
                arrives = (plane >= j) if side == 0 else (plane + j <= planes - 1)

                @pl.when(arrives)
                def _():
                    line_piece(origin_of(side, j), which, p, side, j - 1, plane).wait_recv()

            if j < planes - 1:
                @pl.when(line_sends(planes, plane, j, side))
                def _():
                    line_piece(origin_of(side, j), which, p, side, j, next_of(side)).start()

    slots = (((0, 2), (1, 3)), ((0, 3), (1, 2)), ((0, 0), (1, 1)), ((0, 1), (1, 0)))

    def slot_go(slot, j):
        for which, p in slots[slot]:
            line_go(which, p, j)

    gather_wait(xg, *sems, (6,))
    process(0)
    slot_go(0, 0)
    gather_pass(xg, *sems, NEIGHBOURS_FIRST)
    gather_wait(xg, *sems, (7, 8))
    process(2)
    slot_go(0, 1)
    gather_wait(xg, *sems, (9, 10))
    process(4)
    gather_pass(xg, *sems, DIAGONAL)
    slot_go(1, 0)
    slot_go(0, 2)
    gather_wait(xg, *sems, (11, 12))
    process(6)
    sems2 = (ag_send.at[1], ag_recv.at[1])
    slot_go(2, 0)
    slot_go(1, 1)
    slot_go(3, 0)
    gather_start(dy_ref, *sems2, own=dyo_ref)
    slot_go(0, 3)
    slot_go(1, 2)
    slot_go(2, 1)
    slot_go(3, 1)
    slot_go(1, 3)
    slot_go(2, 2)
    gather_pass(dy_ref, *sems2, NEIGHBOURS_FIRST)
    slot_go(3, 2)
    slot_go(2, 3)
    gather_pass(dy_ref, *sems2, DIAGONAL)
    slot_go(3, 3)
    gather_wait(dy_ref, *sems2, FROM_SIBLING)

    for p in range(ranks // 2):
        @pl.when(rank == 0)
        def _():
            q_local(p).wait()

        @pl.when(rank != 0)
        def _():
            q_copy(0, p, 0).wait_recv()

    for p in range(ranks // 2):
        for copy in flush(p):
            copy.wait()
    for copy in small:
        copy.wait_send()
    gather_sent(xg, *sems)
    gather_sent(dy_ref, *sems2)
    own_block.wait()
    for p in range(ranks // 2):
        @pl.when(rank < 4)
        def _():
            for m in range(2):
                @pl.when(2 * rank + m != rank)
                def _():
                    q_copy(m, p, 0).wait_send()

        for which in range(2):
            first = 4 + 2 * which

            @pl.when((rank == first) | (rank == first + 1))
            def _():
                for m in range(4):
                    @pl.when(4 * (rank - first) + m != rank)
                    def _():
                        kv_copy(m, which, p, 0).wait_send()

            for j in range(planes - 1):
                for side in range(2):
                    @pl.when(line_sends(planes, plane, j, side))
                    def _():
                        line_piece(0, which, p, side, j, next_of(side)).wait_send()


def front(lengths, x, small, w_qkv, w_head_gate, grad, collective_id):
    rows, width = x.shape
    ranks, planes = lax.axis_size("fsdp"), lax.axis_size("sp")
    tokens = ranks * rows
    heads = w_head_gate.shape[0]
    vmem = pl.BlockSpec(memory_space=pltpu.VMEM)
    hbm = pl.BlockSpec(memory_space=pl.ANY)
    half, full = jnp.bfloat16, jnp.float32
    pairs = ranks // 2
    return pl.pallas_call(
        functools.partial(front_kernel, planes),
        out_shape=(
            jax.ShapeDtypeStruct((2, tokens, HEAD_DIM), half),
            jax.ShapeDtypeStruct((planes, 2, tokens, HEAD_DIM), half),
            jax.ShapeDtypeStruct((ranks, rows, width), half),
            jax.ShapeDtypeStruct((ranks, rows, width), half),
            jax.ShapeDtypeStruct((ranks, rows, width), half),
            jax.ShapeDtypeStruct((tokens, w_qkv.shape[0]), full),
            jax.ShapeDtypeStruct((heads, tokens, 1), full),
            jax.ShapeDtypeStruct((1, width), full),
            jax.ShapeDtypeStruct((1, width), full),
            jax.ShapeDtypeStruct((1, HEAD_DIM), full),
            jax.ShapeDtypeStruct((tokens, HEAD_DIM), full),
            jax.ShapeDtypeStruct((tokens, HEAD_DIM), full),
        ),
        in_specs=[pl.BlockSpec(memory_space=pltpu.SMEM), vmem, vmem, vmem, vmem, hbm],
        out_specs=(hbm,) * 6 + (vmem,) * 6,
        scratch_shapes=[
            pltpu.VMEM((ranks, rows, width), half),
            pltpu.VMEM((ranks, rows, width), half),
            pltpu.VMEM((tokens, w_qkv.shape[0]), full),
            pltpu.SemaphoreType.DMA((3, pairs)),
            pltpu.VMEM((4, tokens, HEAD_DIM), half),
            pltpu.VMEM((ranks,) + small.shape, small.dtype),
            pltpu.SemaphoreType.DMA((ranks - 1,)),
            pltpu.SemaphoreType.DMA((ranks - 1,)),
            pltpu.SemaphoreType.DMA((2, GATHER_COPIES)),
            pltpu.SemaphoreType.DMA((2, GATHER_COPIES)),
            pltpu.SemaphoreType.DMA,
            pltpu.SemaphoreType.DMA((pairs,)),
            pltpu.SemaphoreType.DMA((2, pairs)),
            pltpu.SemaphoreType.DMA((pairs,)),
            pltpu.SemaphoreType.DMA((4, pairs)),
            pltpu.SemaphoreType.DMA((2, pairs)),
            pltpu.SemaphoreType.DMA((2, planes - 1, 2, pairs)),
            pltpu.SemaphoreType.DMA((2, planes - 1, 2, pairs)),
        ],
        compiler_params=pltpu.CompilerParams(
            collective_id=collective_id, has_side_effects=True, vmem_limit_bytes=VMEM_LIMIT
        ),
        name="front",
    )(lengths, x, small, w_qkv, w_head_gate, grad)


def local_planes(
    hidden_in,
    grad_out,
    lengths,
    attn_gain,
    w_qkv,
    w_head_gate,
    q_gain,
    k_gain,
    w_out,
    ffn_gain,
    w_gate,
    w_up,
    w_down,
):
    ranks, planes = lax.axis_size("fsdp"), lax.axis_size("sp")
    rank, plane = lax.axis_index("fsdp"), lax.axis_index("sp")
    rows, model_width = hidden_in.shape
    tokens = ranks * rows
    own_heads = w_qkv.shape[0] // HEAD_DIM
    local_heads = HEADS // ranks

    thin = q_gain.shape[0]
    spread = jnp.zeros((2, HEAD_DIM), attn_gain.dtype)
    spread = lax.dynamic_update_slice(
        spread, jnp.stack([q_gain, k_gain]), (jnp.int32(0), rank * thin)
    )
    own_gains = jnp.concatenate(
        [
            attn_gain.reshape(-1, HEAD_DIM),
            ffn_gain.reshape(-1, HEAD_DIM),
            spread,
            jnp.zeros((2, HEAD_DIM), attn_gain.dtype),
        ],
        axis=0,
    ).astype(jnp.float32)
    (
        query,
        kv,
        plane_grad,
        gathered,
        normed_a,
        projected,
        gate_logit,
        attn_scale,
        ffn_scale,
        head_scale,
        cosine,
        sine,
    ) = front(lengths, hidden_in, own_gains, w_qkv, w_head_gate, grad_out, 0)
    attended, total, gated = attend(lengths, query, kv, gate_logit, rows)
    plane_b, line_blocks, down_part, middle, grad_middle, grad_ffn_gain_local, plane_mid, grad_gated, acts = middle_layer(
        gated.reshape(ranks, rows, -1),
        w_out,
        hidden_in,
        ffn_scale,
        plane_grad,
        w_gate,
        w_up,
        w_down,
        2,
    )
    grad_gated = grad_gated.reshape(tokens, -1)
    grad_query, grad_kv, gate_grad = attend_back(
        lengths, query, kv, gate_logit, attended, total, grad_gated, rows
    )
    back, out_part, first_grad = return_heads(
        grad_query, grad_kv, gated, plane_mid, line_blocks, 6
    )
    reduced = lax.psum_scatter(out_part, "sp", scatter_dimension=0, tiled=True)
    grad_a_part, qkv_part, gate_rows, attn_terms, head_terms, first_b = projection_back(
        back,
        projected,
        cosine,
        sine,
        normed_a,
        gathered,
        gate_grad,
        w_qkv,
        w_head_gate,
        head_scale,
        line_blocks,
        8,
    )
    reduced, grad_a_part = lax.optimization_barrier((reduced, grad_a_part))
    out_sum = lax.all_gather(reduced, "sp", axis=0, tiled=True)
    grad_in, gain_sums = scatter_gains(
        grad_a_part,
        attn_terms,
        grad_ffn_gain_local,
        head_terms,
        hidden_in,
        attn_scale,
        grad_middle,
        7,
    )
    out_sum, gain_sums = lax.optimization_barrier((out_sum, gain_sums))
    grad_w_out = out_sum.astype(jnp.float32)
    grad_w_gate, grad_w_up, grad_w_down, hidden_out, gain_total, grad_w_head_gate, qkv_total = feed_weights(
        plane_b,
        plane_grad,
        acts,
        line_blocks,
        first_b,
        first_grad,
        down_part,
        middle,
        gain_sums,
        gate_rows,
        qkv_part,
        w_gate,
        w_up,
        w_down,
        4,
    )
    grad_w_qkv = qkv_total.astype(jnp.float32)
    grad_attn_gain = gain_total[:2].reshape(-1)
    grad_ffn_gain = gain_total[2:4].reshape(-1)
    grad_q_gain = lax.dynamic_slice_in_dim(gain_total[4], rank * thin, thin)
    grad_k_gain = lax.dynamic_slice_in_dim(gain_total[5], rank * thin, thin)
    return (
        hidden_out,
        grad_in,
        grad_attn_gain,
        grad_w_qkv,
        grad_w_head_gate,
        grad_q_gain,
        grad_k_gain,
        grad_w_out,
        grad_ffn_gain,
        grad_w_gate,
        grad_w_up,
        grad_w_down,
    )


def solution(mesh):
    planar = mesh.shape["fsdp"] == 8 and mesh.shape["sp"] == 4
    return jax.shard_map(
        local_planes if planar else local,
        mesh=mesh,
        in_specs=(
            P(("fsdp", "sp"), None),
            P(("fsdp", "sp"), None),
            P(),
            P("fsdp"),
            P("fsdp", None),
            P("fsdp", None),
            P("fsdp"),
            P("fsdp"),
            P("fsdp", None),
            P("fsdp"),
            P("fsdp", None),
            P("fsdp", None),
            P("fsdp", None),
        ),
        out_specs=(
            P(("fsdp", "sp"), None),
            P(("fsdp", "sp"), None),
            P("fsdp"),
            P("fsdp", None),
            P("fsdp", None),
            P("fsdp"),
            P("fsdp"),
            P("fsdp", None),
            P("fsdp"),
            P("fsdp", None),
            P("fsdp", None),
            P("fsdp", None),
        ),
        check_vma=False,
    )
```

```python
import functools
import math

import jax
import jax.numpy as jnp
from jax import lax
from jax.experimental import pallas as pl
from jax.experimental.pallas import tpu as pltpu
from jax.sharding import PartitionSpec as P

HEADS = 16
KV_HEADS = 8
HEAD_DIM = 128


EPS = 1e-06
ROPE_BASE = 1000000.0


def mat_nt(factor, others):
    return lax.dot_general(
        factor, others, (((1,), (1,)), ((), ())), preferred_element_type=jnp.float32
    )


def mat_tn(factor, others):
    return lax.dot_general(
        factor, others, (((0,), (0,)), ((), ())), preferred_element_type=jnp.float32
    )


def inv_rms(values):
    return lax.rsqrt(jnp.mean(values * values, axis=-1, keepdims=True) + EPS)


def norm_back(grad_norm, values, inverse, scaling):
    scaled = grad_norm * scaling
    cubed = inverse * inverse * inverse
    return inverse * scaled - values * cubed * jnp.mean(scaled * values, axis=-1, keepdims=True)


def item_starts(token_index, lengths):
    ends = jnp.cumsum(lengths)
    starts = ends - lengths
    inside = (token_index[:, None] >= starts[None, :]) & (token_index[:, None] < ends[None, :])
    return jnp.sum(jnp.where(inside, starts[None, :], 0), axis=1)


def rope_tables(position):
    half_dim = HEAD_DIM // 2
    freq_steps = jnp.arange(half_dim, dtype=jnp.float32)
    frequency = jnp.exp(-math.log(ROPE_BASE) * 2.0 * freq_steps / HEAD_DIM)
    angles = position.astype(jnp.float32)[:, None] * frequency[None, :]
    return (jnp.cos(angles)[:, None, :], jnp.sin(angles)[:, None, :])


def rotate(values, cosine, sine):
    half_dim = values.shape[-1] // 2
    lower = values[..., :half_dim]
    upper = values[..., half_dim:]
    return jnp.concatenate([lower * cosine - upper * sine, upper * cosine + lower * sine], axis=-1)


def rotate_back(grad_rot, cosine, sine):
    half_dim = grad_rot.shape[-1] // 2
    lower = grad_rot[..., :half_dim]
    upper = grad_rot[..., half_dim:]
    return jnp.concatenate([lower * cosine + upper * sine, upper * cosine - lower * sine], axis=-1)


def local(
    hidden_in,
    grad_out,
    lengths,
    attn_gain,
    w_qkv,
    w_head_gate,
    q_gain,
    k_gain,
    w_out,
    ffn_gain,
    w_gate,
    w_up,
    w_down,
):
    fsdp_count = lax.axis_size("fsdp")
    sp_count = lax.axis_size("sp")
    fsdp_rank = lax.axis_index("fsdp")
    sp_rank = lax.axis_index("sp")
    tok_rows = hidden_in.shape[0]
    model_width = hidden_in.shape[1]
    query_width = HEADS * HEAD_DIM
    kv_width = KV_HEADS * HEAD_DIM
    local_kv = KV_HEADS // sp_count
    head_group = HEADS // KV_HEADS
    score_scale = HEAD_DIM ** (-0.5)
    qkv_full, out_full, gate_full, attn_gain_full, q_gain_full, k_gain_full, ffn_gain_full = (
        lax.all_gather(w_qkv, "fsdp", axis=0, tiled=True),
        lax.all_gather(w_out, "fsdp", axis=0, tiled=True),
        lax.all_gather(w_head_gate, "fsdp", axis=0, tiled=True),
        lax.all_gather(attn_gain, "fsdp", axis=0, tiled=True),
        lax.all_gather(q_gain, "fsdp", axis=0, tiled=True),
        lax.all_gather(k_gain, "fsdp", axis=0, tiled=True),
        lax.all_gather(ffn_gain, "fsdp", axis=0, tiled=True),
    )
    attn_scale = attn_gain_full.astype(jnp.float32)
    query_scale = q_gain_full.astype(jnp.float32)
    key_scale = k_gain_full.astype(jnp.float32)
    ffn_scale = ffn_gain_full.astype(jnp.float32)
    token_first = (fsdp_rank * sp_count + sp_rank) * tok_rows
    own_tokens = token_first + jnp.arange(tok_rows, dtype=jnp.int32)
    cosine, sine = rope_tables(own_tokens - item_starts(own_tokens, lengths))
    inputs = hidden_in.astype(jnp.float32)
    inv_first = inv_rms(inputs)
    normed_a = (inputs * inv_first * attn_scale).astype(jnp.bfloat16)
    projected = mat_nt(normed_a, qkv_full)
    gate_logit = mat_nt(normed_a, gate_full)
    q_raw = projected[:, :query_width].reshape(tok_rows, HEADS, HEAD_DIM)
    k_raw = projected[:, query_width : query_width + kv_width].reshape(tok_rows, KV_HEADS, HEAD_DIM)
    q_inv = inv_rms(q_raw)
    k_inv = inv_rms(k_raw)
    query = (
        rotate(q_raw * q_inv * query_scale, cosine, sine)
        .reshape(tok_rows, query_width)
        .astype(jnp.bfloat16)
    )
    keys = (
        rotate(k_raw * k_inv * key_scale, cosine, sine)
        .reshape(tok_rows, kv_width)
        .astype(jnp.bfloat16)
    )
    values = projected[:, query_width + kv_width :].astype(jnp.bfloat16)
    query_heads, key_heads, value_heads = (
        lax.all_to_all(query, "sp", split_axis=1, concat_axis=0, tiled=True),
        lax.all_to_all(keys, "sp", split_axis=1, concat_axis=0, tiled=True),
        lax.all_to_all(values, "sp", split_axis=1, concat_axis=0, tiled=True),
    )
    key_all, value_all = (
        lax.all_gather(key_heads, "fsdp", axis=0, tiled=True),
        lax.all_gather(value_heads, "fsdp", axis=0, tiled=True),
    )
    span_rows = query_heads.shape[0]
    span_first = fsdp_rank * span_rows
    span_tokens = span_first + jnp.arange(span_rows, dtype=jnp.int32)
    span_starts = item_starts(span_tokens, lengths)
    query_four = query_heads.reshape(span_rows, local_kv, head_group, HEAD_DIM)
    key_total = key_all.shape[0]
    key_block = min(1024, key_total)
    block_count = key_total // key_block
    key_blocks = key_all.reshape(block_count, key_block, local_kv, HEAD_DIM)
    value_blocks = value_all.reshape(block_count, key_block, local_kv, HEAD_DIM)
    block_firsts = jnp.arange(block_count, dtype=jnp.int32) * key_block
    lowest_key = span_starts[0]
    highest_key = span_first + span_rows - 1

    def needed(block_first):
        return (block_first <= highest_key) & (block_first + key_block - 1 >= lowest_key)

    def block_weights(key_piece, block_first):
        scores = (
            jnp.einsum("qkgd,jkd->kgqj", query_four, key_piece, preferred_element_type=jnp.float32)
            * score_scale
        )
        columns = block_first + jnp.arange(key_block, dtype=jnp.int32)
        allowed = (columns[None, :] <= span_tokens[:, None]) & (
            columns[None, :] >= span_starts[:, None]
        )
        return jnp.where(allowed[None, None], jnp.exp(scores), 0.0)

    def forward_step(running, pieces):
        key_piece, value_piece, block_first = pieces

        def forward_compute(current):
            totals, unnormed = current
            weights = block_weights(key_piece, block_first)
            totals = totals + jnp.sum(weights, axis=3)
            unnormed = unnormed + jnp.einsum(
                "kgqj,jkd->qkgd",
                weights.astype(jnp.bfloat16),
                value_piece,
                preferred_element_type=jnp.float32,
            )
            return (totals, unnormed)

        return (
            lax.cond(needed(block_first), forward_compute, lambda current: current, running),
            None,
        )

    start_state = (
        jnp.zeros((local_kv, head_group, span_rows), jnp.float32),
        jnp.zeros((span_rows, local_kv, head_group, HEAD_DIM), jnp.float32),
    )
    scanned = lax.scan(forward_step, start_state, (key_blocks, value_blocks, block_firsts))[0]
    totals, unnormed = scanned
    totals_rows = jnp.transpose(totals, (2, 0, 1))[..., None]
    attended_heads = unnormed / totals_rows
    attended_send = attended_heads.reshape(span_rows, local_kv * head_group * HEAD_DIM).astype(
        jnp.bfloat16
    )
    returned = lax.all_to_all(attended_send, "sp", split_axis=0, concat_axis=1, tiled=True)
    gate_prob = jax.nn.sigmoid(gate_logit)
    attended_tok = returned.astype(jnp.float32).reshape(tok_rows, HEADS, HEAD_DIM)
    gated = (
        (attended_tok * gate_prob[:, :, None]).reshape(tok_rows, query_width).astype(jnp.bfloat16)
    )
    middle = inputs + jnp.dot(gated, out_full, preferred_element_type=jnp.float32)
    inv_second = inv_rms(middle)
    normed_b = (middle * inv_second * ffn_scale).astype(jnp.bfloat16)
    gate_piece = lax.all_gather(w_gate, "fsdp", axis=0, tiled=True)
    up_piece = lax.all_gather(w_up, "fsdp", axis=0, tiled=True)
    down_piece = lax.all_gather(w_down, "fsdp", axis=0, tiled=True)
    gate_pre = mat_nt(normed_b, gate_piece)
    up_pre = mat_nt(normed_b, up_piece)
    hidden = (jax.nn.silu(gate_pre) * up_pre).astype(jnp.bfloat16)
    ffn_part = jnp.dot(hidden, down_piece, preferred_element_type=jnp.float32)
    hidden_out = (middle + ffn_part).astype(jnp.bfloat16)
    gate_piece = lax.all_gather(w_gate, "fsdp", axis=0, tiled=True)
    up_piece = lax.all_gather(w_up, "fsdp", axis=0, tiled=True)
    down_piece = lax.all_gather(w_down, "fsdp", axis=0, tiled=True)
    gate_pre = mat_nt(normed_b, gate_piece)
    up_pre = mat_nt(normed_b, up_piece)
    sigma = jax.nn.sigmoid(gate_pre)
    swish = gate_pre * sigma
    hidden = (swish * up_pre).astype(jnp.bfloat16)
    grad_hidden = mat_nt(grad_out, down_piece)
    grad_gate = (grad_hidden * up_pre * sigma * (1.0 + gate_pre * (1.0 - sigma))).astype(
        jnp.bfloat16
    )
    grad_up = (grad_hidden * swish).astype(jnp.bfloat16)
    grad_acc = jnp.dot(grad_gate, gate_piece, preferred_element_type=jnp.float32) + jnp.dot(
        grad_up, up_piece, preferred_element_type=jnp.float32
    )
    grad_ffn_gain_local = jnp.sum(grad_acc * middle * inv_second, axis=0)
    grad_middle = grad_out.astype(jnp.float32) + norm_back(grad_acc, middle, inv_second, ffn_scale)
    grad_mid_b = grad_middle.astype(jnp.bfloat16)
    grad_gated = mat_nt(grad_mid_b, out_full).reshape(tok_rows, HEADS, HEAD_DIM)
    grad_attended = (
        (grad_gated * gate_prob[:, :, None]).reshape(tok_rows, query_width).astype(jnp.bfloat16)
    )
    gate_grad = (jnp.sum(grad_gated * attended_tok, axis=2) * gate_prob * (1.0 - gate_prob)).astype(
        jnp.bfloat16
    )
    grad_heads = lax.all_to_all(grad_attended, "sp", split_axis=1, concat_axis=0, tiled=True)
    grad_four = grad_heads.astype(jnp.float32).reshape(span_rows, local_kv, head_group, HEAD_DIM)
    grad_scaled = (grad_four / totals_rows).astype(jnp.bfloat16)
    delta_rows = jnp.sum(grad_four * attended_heads, axis=3) / totals_rows[..., 0]
    delta_heads = jnp.transpose(delta_rows, (1, 2, 0))

    def backward_step(grad_query, pieces):
        key_piece, value_piece, block_first = pieces

        def backward_compute(current):
            weights = block_weights(key_piece, block_first)
            grad_prob = jnp.einsum(
                "qkgd,jkd->kgqj", grad_scaled, value_piece, preferred_element_type=jnp.float32
            )
            grad_score = (weights * (grad_prob - delta_heads[..., None])).astype(jnp.bfloat16)
            current = (
                current
                + jnp.einsum(
                    "kgqj,jkd->qkgd", grad_score, key_piece, preferred_element_type=jnp.float32
                )
                * score_scale
            )
            grad_key = (
                jnp.einsum(
                    "kgqj,qkgd->jkd", grad_score, query_four, preferred_element_type=jnp.float32
                )
                * score_scale
            )
            grad_value = jnp.einsum(
                "kgqj,qkgd->jkd",
                weights.astype(jnp.bfloat16),
                grad_scaled,
                preferred_element_type=jnp.float32,
            )
            return (current, (grad_key, grad_value))

        def skip(current):
            nothing = jnp.zeros((key_block, local_kv, HEAD_DIM), jnp.float32)
            return (current, (nothing, nothing))

        return lax.cond(needed(block_first), backward_compute, skip, grad_query)

    grad_query, key_value_grads = lax.scan(
        backward_step,
        jnp.zeros((span_rows, local_kv, head_group, HEAD_DIM), jnp.float32),
        (key_blocks, value_blocks, block_firsts),
    )
    key_grads, value_grads = key_value_grads
    key_sum, value_sum = (
        lax.psum_scatter(
            key_grads.reshape(key_total, local_kv * HEAD_DIM),
            "fsdp",
            scatter_dimension=0,
            tiled=True,
        ),
        lax.psum_scatter(
            value_grads.reshape(key_total, local_kv * HEAD_DIM),
            "fsdp",
            scatter_dimension=0,
            tiled=True,
        ),
    )
    query_send = grad_query.reshape(span_rows, local_kv * head_group * HEAD_DIM).astype(
        jnp.bfloat16
    )
    back_query, back_key, back_value = (
        lax.all_to_all(query_send, "sp", split_axis=0, concat_axis=1, tiled=True),
        lax.all_to_all(key_sum.astype(jnp.bfloat16), "sp", split_axis=0, concat_axis=1, tiled=True),
        lax.all_to_all(
            value_sum.astype(jnp.bfloat16), "sp", split_axis=0, concat_axis=1, tiled=True
        ),
    )
    grad_qn = rotate_back(
        back_query.astype(jnp.float32).reshape(tok_rows, HEADS, HEAD_DIM), cosine, sine
    )
    grad_kn = rotate_back(
        back_key.astype(jnp.float32).reshape(tok_rows, KV_HEADS, HEAD_DIM), cosine, sine
    )
    grad_q_gain_local = jnp.sum(grad_qn * q_raw * q_inv, axis=(0, 1))
    grad_k_gain_local = jnp.sum(grad_kn * k_raw * k_inv, axis=(0, 1))
    grad_q_raw = norm_back(grad_qn, q_raw, q_inv, query_scale).reshape(tok_rows, query_width)
    grad_k_raw = norm_back(grad_kn, k_raw, k_inv, key_scale).reshape(tok_rows, kv_width)
    grad_proj = jnp.concatenate(
        [grad_q_raw.astype(jnp.bfloat16), grad_k_raw.astype(jnp.bfloat16), back_value], axis=1
    )
    grad_normed_a = jnp.dot(grad_proj, qkv_full, preferred_element_type=jnp.float32) + jnp.dot(
        gate_grad, gate_full, preferred_element_type=jnp.float32
    )
    grad_attn_gain_local = jnp.sum(grad_normed_a * inputs * inv_first, axis=0)
    grad_in = grad_middle + norm_back(grad_normed_a, inputs, inv_first, attn_scale)
    qkv_rows = w_qkv.shape[0]
    out_rows = w_out.shape[0]
    gate_rows = w_head_gate.shape[0]
    block_rows = qkv_rows + out_rows + gate_rows + 3
    small_rows = jnp.stack(
        [
            grad_attn_gain_local,
            grad_ffn_gain_local,
            jnp.concatenate(
                [
                    grad_q_gain_local,
                    grad_k_gain_local,
                    jnp.zeros((model_width - 2 * HEAD_DIM,), jnp.float32),
                ]
            ),
        ],
        axis=0,
    )
    ffn_partial = lax.psum_scatter(
        jnp.concatenate(
            [mat_tn(grad_gate, normed_b), mat_tn(grad_up, normed_b), mat_tn(hidden, grad_out)],
            axis=1,
        ).astype(jnp.bfloat16),
        "fsdp",
        scatter_dimension=0,
        tiled=True,
    ).astype(jnp.float32)
    proj_split = grad_proj.reshape(tok_rows, fsdp_count, qkv_rows)
    gated_split = gated.reshape(tok_rows, fsdp_count, out_rows)
    gate_split = gate_grad.reshape(tok_rows, fsdp_count, gate_rows)
    owners = block_rows * lax.axis_size("fsdp") // block_rows
    qkv_term = jnp.einsum("tor,td->ord", proj_split, normed_a, preferred_element_type=jnp.float32)
    out_term = jnp.einsum(
        "tor,td->ord", gated_split, grad_mid_b, preferred_element_type=jnp.float32
    )
    gate_term = jnp.einsum("tor,td->ord", gate_split, normed_a, preferred_element_type=jnp.float32)
    small_term = jnp.broadcast_to(small_rows[None], (owners, 3, model_width))
    joined = jnp.concatenate([qkv_term, out_term, gate_term, small_term], axis=1)
    attn_partial = lax.psum_scatter(
        joined.reshape(owners * block_rows, model_width), "fsdp", scatter_dimension=0, tiled=True
    )
    ffn_total, attn_total = lax.psum((ffn_partial, attn_partial), "sp")
    grad_w_gate = ffn_total[:, :model_width]
    grad_w_up = ffn_total[:, model_width : 2 * model_width]
    grad_w_down = ffn_total[:, 2 * model_width :]
    grad_w_qkv = attn_total[:qkv_rows]
    grad_w_out = attn_total[qkv_rows : qkv_rows + out_rows]
    grad_w_head_gate = attn_total[qkv_rows + out_rows : qkv_rows + out_rows + gate_rows]
    gain_sums = attn_total[qkv_rows + out_rows + gate_rows :]
    gain_part = model_width // fsdp_count
    head_part = HEAD_DIM // fsdp_count
    grad_attn_gain = lax.dynamic_slice_in_dim(gain_sums[0], fsdp_rank * gain_part, gain_part)
    grad_ffn_gain = lax.dynamic_slice_in_dim(gain_sums[1], fsdp_rank * gain_part, gain_part)
    grad_q_gain = lax.dynamic_slice_in_dim(gain_sums[2], fsdp_rank * head_part, head_part)
    grad_k_gain = lax.dynamic_slice_in_dim(
        gain_sums[2], HEAD_DIM + fsdp_rank * head_part, head_part
    )
    return (
        hidden_out,
        grad_in,
        grad_attn_gain,
        grad_w_qkv,
        grad_w_head_gate,
        grad_q_gain,
        grad_k_gain,
        grad_w_out,
        grad_ffn_gain,
        grad_w_gate,
        grad_w_up,
        grad_w_down,
    )


MESH = pl.DeviceIdType.MESH
VMEM_LIMIT = 62 * 1024 * 1024


def peer_copy(src, dst, send_sem, recv_sem, rank, plane):
    return pltpu.make_async_remote_copy(
        src_ref=src,
        dst_ref=dst,
        send_sem=send_sem,
        recv_sem=recv_sem,
        device_id=(rank, plane),
        device_id_type=MESH,
    )


def greet(peers):
    barrier = pltpu.get_barrier_semaphore()
    for peer in peers:
        pl.semaphore_signal(barrier, inc=1, device_id=peer, device_id_type=MESH)
    pl.semaphore_wait(barrier, len(peers))


def scatter_gains_kernel(
    p_ref, attn_ref, ffn_ref, head_ref, x_ref, scale_ref, dmid_ref, o_ref, so_ref, parts, small_buf, grad, small_send, small_recv, near_buf, out_buf, far_buf, sib_send, sib_recv, send_sem, recv_sem
):
    rank, plane = lax.axis_index("fsdp"), lax.axis_index("sp")
    ranks = p_ref.shape[0]
    greet([(rank ^ k, plane) for k in range(1, 8)])
    for i in range(4):
        scatter_near(p_ref, i, near_buf, sib_send, sib_recv).start()
    for r in range(ranks):
        for i in range(2):
            columns = slice((2 * r + i) * HEAD_DIM, (2 * r + i + 1) * HEAD_DIM)
            parts[r, i : i + 1] = attn_ref[:, columns]
            parts[r, 2 + i : 3 + i] = ffn_ref[:, columns]
        parts[r, 4:5] = jnp.where(rank < ranks // 2, head_ref[...], 0.0)
        parts[r, 5:6] = jnp.where(
            (rank >= ranks // 2) & (rank < 3 * ranks // 4), head_ref[...], 0.0
        )
        parts[r, 6:8] = jnp.zeros((2, HEAD_DIM), jnp.float32)
    small = []
    for k in range(1, 8):
        copy = peer_copy(
            parts.at[rank ^ k],
            small_buf.at[k - 1],
            small_send.at[k - 1],
            small_recv.at[k - 1],
            rank ^ k,
            plane,
        )
        copy.start()
        small.append(copy)
    sems = (send_sem, recv_sem)

    def block_of(i):
        scatter_near(p_ref, i, near_buf, sib_send, sib_recv).wait_recv()
        return p_ref[rank ^ SCATTER_ORDER[i]].astype(jnp.float32) + near_buf[i].astype(jnp.float32)

    def own_block():
        grad[...] = block_of(3)

    relay_blocks(out_buf, far_buf, sems, block_of, own_block)
    total = parts[rank]
    for k in range(1, 8):
        small[k - 1].wait()
        total = total + small_buf[k - 1]
    so_ref[...] = total
    grad[...] = relay_sum(out_buf, far_buf, sems, grad[...])
    inputs = x_ref[...].astype(jnp.float32)
    o_ref[...] = dmid_ref[...] + norm_back(grad[...], inputs, inv_rms(inputs), scale_ref[...])
    for i in range(4):
        scatter_near(p_ref, i, near_buf, sib_send, sib_recv).wait_send()
    relay_sent(out_buf, far_buf, sems)


SCATTER_ORDER = (6, 2, 4, 0)


def scatter_far(i, out_buf, far_buf, send_sem, recv_sem):
    rank, plane = lax.axis_index("fsdp"), lax.axis_index("sp")
    return peer_copy(
        out_buf.at[i],
        far_buf.at[i],
        send_sem.at[i],
        recv_sem.at[i],
        rank ^ SCATTER_ORDER[i],
        plane,
    )


def scatter_near(p_ref, i, near_buf, sib_send, sib_recv):
    rank, plane = lax.axis_index("fsdp"), lax.axis_index("sp")
    return peer_copy(
        p_ref.at[rank ^ 1 ^ SCATTER_ORDER[i]],
        near_buf.at[i],
        sib_send.at[i],
        sib_recv.at[i],
        rank ^ 1,
        plane,
    )


def relay_copy(i, out_buf, far_buf, send_sem, recv_sem):
    rank, plane = lax.axis_index("fsdp"), lax.axis_index("sp")
    half = out_buf.shape[1] // 2
    top, low = pl.ds(0, half), pl.ds(half, half)
    slot, part, to = (
        (0, top, 2),
        (0, low, 4),
        (1, top, 2),
        (2, low, 4),
        (1, low, 2),
        (2, top, 4),
    )[i]
    return peer_copy(
        out_buf.at[slot, part],
        far_buf.at[slot, part],
        send_sem.at[i],
        recv_sem.at[i],
        rank ^ to,
        plane,
    )


def relay_blocks(out_buf, far_buf, sems, block_of, own_block):
    half = out_buf.shape[1] // 2
    copies = [relay_copy(i, out_buf, far_buf, *sems) for i in range(6)]
    for slot, ready in ((0, (0, 1)), (1, (2,)), (2, (3,))):
        out_buf[slot] = block_of(slot).astype(out_buf.dtype)
        for i in ready:
            copies[i].start()
    own_block()
    for arrived, slot, onward, rows in ((0, 2, 5, slice(0, half)), (1, 1, 4, slice(half, 2 * half))):
        copies[arrived].wait_recv()
        joined = out_buf[slot, rows].astype(jnp.float32) + far_buf[0, rows].astype(jnp.float32)
        out_buf[slot, rows] = joined.astype(out_buf.dtype)
        copies[onward].start()


def relay_sum(out_buf, far_buf, sems, total):
    for i in (2, 3, 5, 4):
        relay_copy(i, out_buf, far_buf, *sems).wait_recv()
    return total + far_buf[1].astype(jnp.float32) + far_buf[2].astype(jnp.float32)


def relay_sent(out_buf, far_buf, sems):
    for i in range(6):
        relay_copy(i, out_buf, far_buf, *sems).wait_send()


def scatter_scratch(rows, width, dtype):
    return [
        pltpu.VMEM((4, rows, width), dtype),
        pltpu.VMEM((3, rows, width), dtype),
        pltpu.VMEM((3, rows, width), dtype),
        pltpu.SemaphoreType.DMA((4,)),
        pltpu.SemaphoreType.DMA((4,)),
        pltpu.SemaphoreType.DMA((3,)),
        pltpu.SemaphoreType.DMA((3,)),
    ]


def scatter_gains(p, attn, ffn, head, x, scale, grad_middle, collective_id):
    ranks, rows, width = p.shape
    vmem = pl.BlockSpec(memory_space=pltpu.VMEM)
    small = (8, HEAD_DIM)
    return pl.pallas_call(
        scatter_gains_kernel,
        out_shape=(
            jax.ShapeDtypeStruct((rows, width), jnp.float32),
            jax.ShapeDtypeStruct(small, jnp.float32),
        ),
        in_specs=[vmem] * 7,
        out_specs=(vmem, vmem),
        scratch_shapes=[
            pltpu.VMEM((ranks,) + small, jnp.float32),
            pltpu.VMEM((7,) + small, jnp.float32),
            pltpu.VMEM((rows, width), jnp.float32),
            pltpu.SemaphoreType.DMA((7,)),
            pltpu.SemaphoreType.DMA((7,)),
        ]
        + scatter_scratch(rows, width, p.dtype)[:-2]
        + [pltpu.SemaphoreType.DMA((6,)), pltpu.SemaphoreType.DMA((6,))],
        compiler_params=pltpu.CompilerParams(
            collective_id=collective_id, has_side_effects=True, vmem_limit_bytes=VMEM_LIMIT
        ),
        name="scatter_gains",
    )(p, attn, ffn, head, x, scale, grad_middle)


def projection_back_kernel(
    back_ref, raw_ref, cos_ref, sin_ref, xa_ref, x_ref, dgate_ref, w_ref, wg_ref, head_ref, blocks_ref, dxa_ref, qkv_ref, gate_ref, attn_ref, terms_ref, next_ref, sums, ag_send, ag_recv, own_sem
):
    rank, plane = lax.axis_index("fsdp"), lax.axis_index("sp")
    block = blocks_ref.at[0, 0]
    gather = (next_ref, ag_send, ag_recv)
    own = pltpu.make_async_copy(block, next_ref.at[rank], own_sem)
    group, rows, width = back_ref.shape

    @pl.when(pl.program_id(0) == 0)
    def _():
        greet([(rank ^ k, plane) for k in (1, 2, 4)])
        own.start()
        gather_start(*gather, own=block)
        for ref in (sums, gate_ref, attn_ref, terms_ref):
            ref[...] = jnp.zeros_like(ref)

    @pl.when(pl.program_id(0) == 2)
    def _():
        gather_pass(*gather, NEIGHBOURS_FIRST[:2])

    @pl.when(pl.program_id(0) == 3)
    def _():
        gather_pass(*gather, NEIGHBOURS_FIRST[2:])

    cosine, sine = cos_ref[...], sin_ref[...]
    columns = []
    for m in range(group):
        back = back_ref[m]
        grad = back.astype(jnp.float32)
        turned = grad * cosine - pltpu.roll(grad, width // 2, 1) * sine
        raw = raw_ref[:, m * width : (m + 1) * width]
        inverse = inv_rms(raw)
        terms_ref[...] += jnp.sum(turned * raw * inverse, axis=0, keepdims=True)
        grad_raw = norm_back(turned, raw, inverse, head_ref[...])
        columns.append(jnp.where(rank >= 6, grad, grad_raw).astype(jnp.bfloat16))
    grad_proj = jnp.concatenate(columns, axis=1)
    grad_a = jnp.dot(grad_proj, w_ref[...], preferred_element_type=jnp.float32)
    normed = xa_ref[...].reshape(rows, -1)
    normed32 = normed.astype(jnp.float32)
    for head in range(dgate_ref.shape[0]):
        gate = dgate_ref[head].astype(jnp.float32)
        grad_a = grad_a + gate * wg_ref[head : head + 1].astype(jnp.float32)
        gate_ref[head : head + 1] += jnp.sum(gate * normed32, axis=0, keepdims=True)
    inputs = x_ref[...].reshape(rows, -1).astype(jnp.float32)
    attn_ref[...] += jnp.sum(grad_a * inputs * inv_rms(inputs), axis=0, keepdims=True)
    dxa_ref[...] = grad_a.astype(jnp.bfloat16).reshape(dxa_ref.shape)
    sums[...] += mat_tn(grad_proj, normed)

    @pl.when(pl.program_id(0) == pl.num_programs(0) - 1)
    def _():
        qkv_ref[...] = sums[...].astype(jnp.bfloat16)
        gather_pass(*gather, DIAGONAL)
        gather_wait(*gather, FROM_SIBLING)
        gather_sent(*gather)
        own.wait()


def projection_back(back, raw, cosine, sine, normed, inputs, gate_grad, w_qkv, w_head_gate, head_scale, line_blocks, collective_id):
    ranks, rows, model_width = normed.shape
    group, tokens, width = back.shape
    pair = 2 * rows
    blocks = pl.BlockSpec((2, rows, model_width), lambda i: (i, 0, 0))
    thin = pl.BlockSpec((pair, width), lambda i: (i, 0))
    hbm = pl.BlockSpec(memory_space=pl.ANY)
    heads = gate_grad.shape[0]

    def still(shape):
        return pl.BlockSpec(shape, lambda i: (0, 0))

    return pl.pallas_call(
        projection_back_kernel,
        grid=(tokens // pair,),
        in_specs=[
            pl.BlockSpec((group, pair, width), lambda i: (0, i, 0)),
            pl.BlockSpec((pair, group * width), lambda i: (i, 0)),
            thin,
            thin,
            blocks,
            blocks,
            pl.BlockSpec((heads, pair, 1), lambda i: (0, i, 0)),
            still(w_qkv.shape),
            still(w_head_gate.shape),
            still(head_scale.shape),
            hbm,
        ],
        out_specs=(
            blocks,
            still(w_qkv.shape),
            still(w_head_gate.shape),
            still((1, model_width)),
            still((1, width)),
            hbm,
        ),
        out_shape=(
            jax.ShapeDtypeStruct(normed.shape, jnp.bfloat16),
            jax.ShapeDtypeStruct(w_qkv.shape, jnp.bfloat16),
            jax.ShapeDtypeStruct(w_head_gate.shape, jnp.float32),
            jax.ShapeDtypeStruct((1, model_width), jnp.float32),
            jax.ShapeDtypeStruct((1, width), jnp.float32),
            jax.ShapeDtypeStruct(normed.shape, line_blocks.dtype),
        ),
        scratch_shapes=[
            pltpu.VMEM(w_qkv.shape, jnp.float32),
            pltpu.SemaphoreType.DMA((GATHER_COPIES,)),
            pltpu.SemaphoreType.DMA((GATHER_COPIES,)),
            pltpu.SemaphoreType.DMA,
        ],
        compiler_params=pltpu.CompilerParams(
            collective_id=collective_id, has_side_effects=True, vmem_limit_bytes=VMEM_LIMIT
        ),
        name="projection_back",
    )(back, raw, cosine, sine, normed, inputs, gate_grad, w_qkv, w_head_gate, head_scale, line_blocks)


GATHER_COPIES = 13


def gather_copy(buf, i, send_sem, recv_sem, own=None):
    rank, plane = lax.axis_index("fsdp"), lax.axis_index("sp")
    rows = buf.shape[1]
    top, low = pl.ds(0, rows // 2), pl.ds(rows // 2, rows // 2)
    block, part, to = (
        (0, top, 2),
        (0, low, 2),
        (0, low, 4),
        (0, top, 4),
        (2, top, 4),
        (4, low, 2),
        (0, pl.ds(0, rows), 1),
        (2, top, 1),
        (2, low, 1),
        (4, low, 1),
        (4, top, 1),
        (6, top, 1),
        (6, low, 1),
    )[i]
    piece = buf.at[rank ^ block, part]
    source = piece if own is None or block else own.at[part]
    return peer_copy(source, piece, send_sem.at[i], recv_sem.at[i], rank ^ to, plane)


def gather_start(buf, send_sem, recv_sem, own=None):
    for i in (6, 0, 2, 1, 3):
        gather_copy(buf, i, send_sem, recv_sem, own).start()


def gather_pass(buf, send_sem, recv_sem, pairs):
    for arrived, onward in pairs:
        gather_copy(buf, arrived, send_sem, recv_sem).wait_recv()
        for i in onward:
            gather_copy(buf, i, send_sem, recv_sem).start()


def gather_wait(buf, send_sem, recv_sem, copies):
    for i in copies:
        gather_copy(buf, i, send_sem, recv_sem).wait_recv()


def gather_sent(buf, send_sem, recv_sem):
    for i in range(GATHER_COPIES):
        gather_copy(buf, i, send_sem, recv_sem).wait_send()


NEIGHBOURS_FIRST = ((0, (4, 7)), (2, (5, 9)), (1, (8,)), (3, (10,)))
DIAGONAL = ((4, (11,)), (5, (12,)))
FROM_SIBLING = (6, 7, 8, 9, 10, 11, 12)


def greet_line(ranks, planes):
    rank, plane = lax.axis_index("fsdp"), lax.axis_index("sp")
    barrier = pltpu.get_barrier_semaphore()
    for k in range(1, ranks):
        pl.semaphore_signal(
            barrier, inc=1, device_id=(rank ^ k, plane), device_id_type=MESH
        )

    @pl.when(plane > 0)
    def _():
        pl.semaphore_signal(barrier, inc=1, device_id=(rank, plane - 1), device_id_type=MESH)

    @pl.when(plane < planes - 1)
    def _():
        pl.semaphore_signal(barrier, inc=1, device_id=(rank, plane + 1), device_id_type=MESH)

    lower = (plane > 0).astype(jnp.int32)
    upper = (plane < planes - 1).astype(jnp.int32)
    pl.semaphore_wait(barrier, ranks - 1 + lower + upper)


def line_sends(planes, plane, j, side):
    if side == 0:
        return (plane >= j) & (plane < planes - 1)
    return (plane + j <= planes - 1) & (plane > 0)


def unheads_kernel(planes, dq_ref, dkv_ref, gated_ref, pm_hbm, blocks_ref, n_ref, wout_ref, next_ref, pm, pm_sem, ag_send, ag_recv, own_sem2, line_out, line_in, done, own_sem, q_send, q_recv, kv_send, kv_recv, line_send, line_recv):
    rank, plane = lax.axis_index("fsdp"), lax.axis_index("sp")
    greet_line(8, planes)
    block = blocks_ref.at[1, 0]
    gather = (next_ref, ag_send, ag_recv)
    own_block = pltpu.make_async_copy(block, next_ref.at[rank], own_sem2)
    own_block.start()
    mid_load = pltpu.make_async_copy(pm_hbm, pm, pm_sem)
    mid_load.start()

    def q_copy(m, to):
        return peer_copy(dq_ref, n_ref.at[pl.ds(2 * m, 2)], q_send, q_recv.at[m], to, plane)

    def kv_copy(m, which, to):
        return peer_copy(done.at[which], n_ref.at[m], kv_send.at[which], kv_recv.at[m], to, plane)

    def q_local():
        return pltpu.make_async_copy(dq_ref, n_ref.at[pl.ds(0, 2)], own_sem)

    def kv_local(m, which):
        return pltpu.make_async_copy(done.at[which], n_ref.at[m], own_sem)

    @pl.when(rank == 0)
    def _():
        q_local().start()

    for m in range(2):
        @pl.when((rank % 2 == m) & (rank != 0))
        def _():
            q_copy(m, rank // 2).start()

    def step_copy(j, which, side):
        to = plane + 1 if side == 0 else plane - 1
        return peer_copy(
            line_out.at[side, j, which],
            line_in.at[side, j, which],
            line_send.at[side, j, which],
            line_recv.at[side, j, which],
            rank,
            to,
        )

    def sends(j, side):
        return plane < planes - 1 - j if side == 0 else plane > j

    def target(j, side):
        return planes - 1 - j if side == 0 else j

    gather_start(*gather, own=block)

    for j in range(planes - 1):
        for which in range(2):
            for side in range(2):
                inner = plane > 0 if side == 0 else plane < planes - 1

                @pl.when(sends(j, side) & inner)
                def _():
                    step_copy(j, which, side).wait_recv()
                    total = dkv_ref[target(j, side), which].astype(jnp.float32) + line_in[
                        side, j, which
                    ].astype(jnp.float32)
                    line_out[side, j, which] = total.astype(line_out.dtype)

                @pl.when(sends(j, side) & jnp.logical_not(inner))
                def _():
                    line_out[side, j, which] = dkv_ref[target(j, side), which]

                @pl.when(sends(j, side))
                def _():
                    step_copy(j, which, side).start()

        if j == 0:
            mid_load.wait()
            wout_ref[...] = mat_tn(gated_ref[...], pm[...].reshape(-1, pm.shape[-1])).astype(
                wout_ref.dtype
            )
        if j == 1:
            gather_pass(*gather, NEIGHBOURS_FIRST)
        if j == 2:
            gather_pass(*gather, DIAGONAL)

    for which in range(2):
        total = dkv_ref[plane, which].astype(jnp.float32)
        done32 = total
        for j in range(planes - 1):
            for side in range(2):
                @pl.when(plane == target(j, side))
                def _():
                    step_copy(j, which, side).wait_recv()
        low = jnp.minimum(planes - 1 - plane, planes - 2)
        high = jnp.minimum(plane, planes - 2)
        below = line_in[0, low, which].astype(jnp.float32)
        above = line_in[1, high, which].astype(jnp.float32)
        done32 = done32 + jnp.where(plane > 0, below, 0.0) + jnp.where(plane < planes - 1, above, 0.0)
        done[which] = done32.astype(done.dtype)
        first = 4 + 2 * which
        to = first + rank // 4
        for m in range(4):
            @pl.when((rank % 4 == m) & (to != rank))
            def _():
                kv_copy(m, which, to).start()

            @pl.when((rank % 4 == m) & (to == rank))
            def _():
                kv_local(m, which).start()

    gather_wait(*gather, FROM_SIBLING)
    gather_sent(*gather)
    own_block.wait()

    @pl.when(rank < 4)
    def _():
        for m in range(2):
            @pl.when(2 * rank + m != rank)
            def _():
                q_copy(m, 0).wait_recv()

            @pl.when(2 * rank + m == rank)
            def _():
                q_local().wait()

    for which in range(2):
        first = 4 + 2 * which

        @pl.when((rank == first) | (rank == first + 1))
        def _():
            for m in range(4):
                @pl.when(4 * (rank - first) + m != rank)
                def _():
                    kv_copy(m, which, 0).wait_recv()

                @pl.when(4 * (rank - first) + m == rank)
                def _():
                    kv_local(m, which).wait()

    @pl.when(rank != 0)
    def _():
        q_copy(0, 0).wait_send()

    for which in range(2):
        @pl.when(4 + 2 * which + rank // 4 != rank)
        def _():
            kv_copy(0, which, 0).wait_send()

    for j in range(planes - 1):
        for which in range(2):
            for side in range(2):
                @pl.when(sends(j, side))
                def _():
                    step_copy(j, which, side).wait_send()


def return_heads(grad_query, grad_kv, gated, plane_mid, line_blocks, collective_id):
    _, tokens, width = grad_query.shape
    planes = lax.axis_size("sp")
    ranks = lax.axis_size("fsdp")
    vmem = pl.BlockSpec(memory_space=pltpu.VMEM)
    hbm = pl.BlockSpec(memory_space=pl.ANY)
    return pl.pallas_call(
        functools.partial(unheads_kernel, planes),
        out_shape=(
            jax.ShapeDtypeStruct((4, tokens, width), grad_query.dtype),
            jax.ShapeDtypeStruct((gated.shape[1], plane_mid.shape[-1]), gated.dtype),
            jax.ShapeDtypeStruct((ranks,) + line_blocks.shape[2:], line_blocks.dtype),
        ),
        in_specs=[vmem, vmem, vmem, hbm, hbm],
        out_specs=(vmem, vmem, hbm),
        scratch_shapes=[
            pltpu.VMEM(plane_mid.shape, plane_mid.dtype),
            pltpu.SemaphoreType.DMA,
            pltpu.SemaphoreType.DMA((GATHER_COPIES,)),
            pltpu.SemaphoreType.DMA((GATHER_COPIES,)),
            pltpu.SemaphoreType.DMA,
            pltpu.VMEM((2, planes - 1, 2, tokens, width), grad_query.dtype),
            pltpu.VMEM((2, planes - 1, 2, tokens, width), grad_query.dtype),
            pltpu.VMEM((2, tokens, width), grad_query.dtype),
            pltpu.SemaphoreType.DMA,
            pltpu.SemaphoreType.DMA,
            pltpu.SemaphoreType.DMA((2,)),
            pltpu.SemaphoreType.DMA((2,)),
            pltpu.SemaphoreType.DMA((4,)),
            pltpu.SemaphoreType.DMA((2, planes - 1, 2)),
            pltpu.SemaphoreType.DMA((2, planes - 1, 2)),
        ],
        compiler_params=pltpu.CompilerParams(
            collective_id=collective_id, has_side_effects=True, vmem_limit_bytes=VMEM_LIMIT
        ),
        name="return_heads",
    )(grad_query, grad_kv, gated, plane_mid, line_blocks)


def stack_heads(ref):
    return ref[...].reshape(ref.shape[0] * ref.shape[1], ref.shape[2])


def block_bounds(lengths_ref, ranks, planes, rows):
    block = pl.program_id(0)
    span = planes * rows
    first = block * span + lax.axis_index("sp") * rows
    start, last_start, end = jnp.int32(0), jnp.int32(0), jnp.int32(0)
    for item in range(lengths_ref.shape[0]):
        end = end + lengths_ref[item]
        start = jnp.where(first >= end, end, start)
        last_start = jnp.where(first + rows - 1 >= end, end, last_start)
    low = start // span
    inner = jnp.clip((last_start + span - 1) // span, low, block)
    return low, inner, block, first


def sweep(low, inner, high, step, running):
    running = lax.fori_loop(low, inner, functools.partial(step, True), running)
    running = lax.fori_loop(inner, high, functools.partial(step, False), running)
    return step(True, high, running)


def row_starts(lengths_ref, tokens):
    start, end = jnp.zeros_like(tokens), jnp.int32(0)
    for item in range(lengths_ref.shape[0]):
        end = end + lengths_ref[item]
        start = jnp.where(tokens >= end, end, start)
    return start


def chunk_weights(masked, query, key, scale, tokens, starts, first_key):
    scores = mat_nt(query, key) * (scale * math.log2(math.e))
    if not masked:
        return jnp.exp2(scores)
    columns = first_key + lax.broadcasted_iota(jnp.int32, scores.shape, 1)
    allowed = (columns <= tokens) & (columns >= starts)
    return jnp.where(allowed, jnp.exp2(scores), 0.0)


def query_tokens(first, rows, group):
    row = lax.broadcasted_iota(jnp.int32, (group * rows, 1), 0)
    return first + lax.rem(row, rows)


def attend_kernel(ranks, planes, lengths_ref, q_ref, kv_ref, gate_ref, att_ref, total_ref, gated_ref):
    group, rows, width = q_ref.shape
    scale = HEAD_DIM ** (-0.5)
    low, inner, high, first = block_bounds(lengths_ref, ranks, planes, rows)
    tokens = query_tokens(first, rows, group)
    starts = row_starts(lengths_ref, tokens)
    query = stack_heads(q_ref)
    span = planes * rows

    def step(masked, chunk, running):
        total, unnorm = running
        key = kv_ref[:, 0, chunk].reshape(span, width)
        value = kv_ref[:, 1, chunk].reshape(span, width)
        weights = chunk_weights(masked, query, key, scale, tokens, starts, chunk * span)
        total = total + jnp.sum(weights, axis=1, keepdims=True)
        unnorm = unnorm + jnp.dot(
            weights.astype(jnp.bfloat16), value, preferred_element_type=jnp.float32
        )
        return total, unnorm

    total, unnorm = sweep(
        low,
        inner,
        high,
        step,
        (
            jnp.zeros((group * rows, 1), jnp.float32),
            jnp.zeros((group * rows, width), jnp.float32),
        ),
    )
    attended = unnorm / total
    att_ref[...] = attended.reshape(group, rows, width)
    total_ref[...] = total.reshape(group, rows, 1)
    sent = attended.astype(jnp.bfloat16).astype(jnp.float32)
    for head in range(group):
        gated = sent[head * rows : (head + 1) * rows] * jax.nn.sigmoid(gate_ref[head])
        gated_ref[:, head * width : (head + 1) * width] = gated.astype(jnp.bfloat16)


def attend(lengths, query, kv, gate_logit, rows):
    group, tokens, width = query.shape
    planes = kv.shape[0]
    ranks = tokens // rows
    kv_blocks = kv.reshape(planes, 2, ranks, rows, width)
    block = pl.BlockSpec((group, rows, width), lambda i, *_: (0, i, 0))
    thin = pl.BlockSpec((group, rows, 1), lambda i, *_: (0, i, 0))
    return pl.pallas_call(
        functools.partial(attend_kernel, ranks, planes),
        grid_spec=pltpu.PrefetchScalarGridSpec(
            num_scalar_prefetch=1,
            grid=(ranks,),
            in_specs=[
                block,
                pl.BlockSpec((planes, 2, ranks, rows, width), lambda i, *_: (0, 0, 0, 0, 0)),
                thin,
            ],
            out_specs=(
                block,
                thin,
                pl.BlockSpec((rows, group * width), lambda i, *_: (i, 0)),
            ),
        ),
        out_shape=(
            jax.ShapeDtypeStruct((group, tokens, width), jnp.float32),
            jax.ShapeDtypeStruct((group, tokens, 1), jnp.float32),
            jax.ShapeDtypeStruct((tokens, group * width), jnp.bfloat16),
        ),
        compiler_params=pltpu.CompilerParams(vmem_limit_bytes=VMEM_LIMIT),
        name="attend",
    )(lengths, query, kv_blocks, gate_logit)


def attend_back_kernel(
    ranks, planes, lengths_ref, q_ref, kv_ref, gate_ref, att_ref, total_ref, dgated_ref, dq_ref, dkv_ref, dgate_ref, sums
):
    group, rows, width = q_ref.shape
    scale = HEAD_DIM ** (-0.5)
    low, inner, high, first = block_bounds(lengths_ref, ranks, planes, rows)
    tokens = query_tokens(first, rows, group)
    starts = row_starts(lengths_ref, tokens)
    query = stack_heads(q_ref)
    span = planes * rows

    @pl.when(pl.program_id(0) == 0)
    def _():
        sums[...] = jnp.zeros_like(sums)

    attended = stack_heads(att_ref)
    sent = attended.astype(jnp.bfloat16).astype(jnp.float32)
    total = stack_heads(total_ref)
    logit = stack_heads(gate_ref)
    prob = jax.nn.sigmoid(logit)
    dgated = jnp.concatenate(
        [dgated_ref[:, head * width : (head + 1) * width] for head in range(group)], axis=0
    )
    dattended = (dgated * prob).astype(jnp.bfloat16)
    dlogit = jnp.sum(dgated * sent, axis=1, keepdims=True) * prob * (1.0 - prob)
    dgate_ref[...] = dlogit.astype(jnp.bfloat16).reshape(group, rows, 1)
    dattended = dattended.astype(jnp.float32)
    scaled = (dattended / total).astype(jnp.bfloat16)
    delta = jnp.sum(dattended * attended, axis=1, keepdims=True) / total

    def step(masked, chunk, dquery):
        key = kv_ref[:, 0, chunk].reshape(span, width)
        value = kv_ref[:, 1, chunk].reshape(span, width)
        weights = chunk_weights(masked, query, key, scale, tokens, starts, chunk * span)
        dprob = mat_nt(scaled, value)
        dscore = (weights * (dprob - delta)).astype(jnp.bfloat16)
        dquery = dquery + jnp.dot(dscore, key, preferred_element_type=jnp.float32)
        dkey = mat_tn(dscore, query)
        dvalue = mat_tn(weights.astype(jnp.bfloat16), scaled)
        sums[:, 0, chunk] += dkey.reshape(planes, rows, width)
        sums[:, 1, chunk] += dvalue.reshape(planes, rows, width)
        return dquery

    dquery = sweep(
        low, inner, high, step, jnp.zeros((group * rows, width), jnp.float32)
    )
    dq_ref[...] = (dquery * scale).astype(jnp.bfloat16).reshape(group, rows, width)

    @pl.when(pl.program_id(0) == ranks - 1)
    def _():
        for chunk in range(ranks):
            dkv_ref[:, 0, chunk] = (sums[:, 0, chunk] * scale).astype(jnp.bfloat16)
            dkv_ref[:, 1, chunk] = sums[:, 1, chunk].astype(jnp.bfloat16)


def attend_back(lengths, query, kv, gate_logit, attended, total, dgated, rows):
    group, tokens, width = query.shape
    planes = kv.shape[0]
    ranks = tokens // rows
    kv_blocks = kv.reshape(planes, 2, ranks, rows, width)
    block = pl.BlockSpec((group, rows, width), lambda i, *_: (0, i, 0))
    thin = pl.BlockSpec((group, rows, 1), lambda i, *_: (0, i, 0))
    whole = pl.BlockSpec((planes, 2, ranks, rows, width), lambda i, *_: (0, 0, 0, 0, 0))
    dquery, dkv, dgate = pl.pallas_call(
        functools.partial(attend_back_kernel, ranks, planes),
        grid_spec=pltpu.PrefetchScalarGridSpec(
            num_scalar_prefetch=1,
            grid=(ranks,),
            in_specs=[
                block,
                whole,
                thin,
                block,
                thin,
                pl.BlockSpec((rows, group * width), lambda i, *_: (i, 0)),
            ],
            out_specs=(block, whole, thin),
            scratch_shapes=[pltpu.VMEM((planes, 2, ranks, rows, width), jnp.float32)],
        ),
        out_shape=(
            jax.ShapeDtypeStruct((group, tokens, width), jnp.bfloat16),
            jax.ShapeDtypeStruct((planes, 2, ranks, rows, width), jnp.bfloat16),
            jax.ShapeDtypeStruct((group, tokens, 1), jnp.bfloat16),
        ),
        compiler_params=pltpu.CompilerParams(vmem_limit_bytes=VMEM_LIMIT),
        name="attend_back",
    )(lengths, query, kv_blocks, gate_logit, attended, total, dgated)
    return dquery, dkv.reshape(planes, 2, tokens, width), dgate


def middle_kernel(
    planes,
    gated_ref,
    wout_ref,
    x_ref,
    scale_ref,
    dy_hbm,
    wg_hbm,
    wu_hbm,
    wd_hbm,
    xg_hbm,
    line_hbm,
    down_hbm,
    mid_ref,
    dmid_ref,
    gain_ref,
    pm_ref,
    dgated_ref,
    act_hbm,
    xg,
    act_ref,
    flush_sem,
    wg,
    wu,
    wd,
    dy,
    dhid,
    near_out,
    near_in,
    far_out,
    far_in,
    keep,
    down_buf,
    load_sem,
    dy_sem,
    down_sem,
    near_send,
    near_recv,
    far_send,
    far_recv,
    ag_send,
    ag_recv,
    line_send,
    line_recv,
):
    rank, plane = lax.axis_index("fsdp"), lax.axis_index("sp")
    ranks, rows, width = xg.shape
    loads = [
        pltpu.make_async_copy(wd_hbm, wd, load_sem.at[0]),
        pltpu.make_async_copy(wg_hbm, wg, load_sem.at[1]),
        pltpu.make_async_copy(wu_hbm, wu, load_sem.at[2]),
    ]
    dy_load = pltpu.make_async_copy(dy_hbm, dy, dy_sem)
    others = [lax.rem(plane + k, planes) for k in range(1, planes)]
    greet([(rank ^ k, plane) for k in (1, 2, 4, 6)] + [(rank, other) for other in others])

    def along(source, which):
        return [
            peer_copy(
                source,
                line_hbm.at[which, j - 1],
                line_send.at[which, j - 1],
                line_recv.at[which, j - 1],
                rank,
                lax.rem(plane + planes - j, planes),
            )
            for j in range(1, planes)
        ]

    def near(phase, i):
        return peer_copy(
            near_out.at[phase, i],
            near_in.at[phase, i],
            near_send.at[phase, i],
            near_recv.at[phase, i],
            rank ^ 1,
            plane,
        )

    def far(phase, i, k):
        return peer_copy(
            far_out.at[phase, i],
            far_in.at[phase, i],
            far_send.at[phase, i],
            far_recv.at[phase, i],
            rank ^ k,
            plane,
        )

    order = (6, 2, 4, 0)
    for i, k in enumerate(order):
        part = jnp.dot(
            gated_ref[rank ^ 1 ^ k], wout_ref[...], preferred_element_type=jnp.float32
        )
        near_out[0, i] = part.astype(jnp.bfloat16)
        near(0, i).start()
    dy_load.start()
    for copy in loads:
        copy.start()
    dy_line = along(dy_hbm.at[rank], 1)
    for copy in dy_line:
        copy.start()
    for i, k in enumerate(order):
        part = jnp.dot(gated_ref[rank ^ k], wout_ref[...], preferred_element_type=jnp.float32)
        near(0, i).wait_recv()
        part = part + near_in[0, i].astype(jnp.float32)
        if k:
            far_out[0, i] = part.astype(jnp.bfloat16)
            far(0, i, k).start()
        else:
            keep[...] = part

    dy_load.wait()
    loads[0].wait()

    @pl.loop(0, ranks // 2)
    def _(p):
        pair = dy[pl.ds(2 * p, 2)].reshape(2 * rows, width)
        dhid[p] = mat_nt(pair, wd[...])

    loads[1].wait()
    loads[2].wait()
    middle = x_ref[...].astype(jnp.float32) + keep[...]
    for i in (1, 2, 0):
        far(0, i, order[i]).wait_recv()
        middle = middle + far_in[0, i].astype(jnp.float32)
    inverse = inv_rms(middle)
    mid_ref[...] = middle
    normed = (middle * inverse * scale_ref[...]).astype(jnp.bfloat16)
    xg[rank] = normed
    sems = (ag_send.at[0], ag_recv.at[0])
    gather_start(xg, *sems)
    xb_line = along(xg.at[rank], 0)
    for copy in xb_line:
        copy.start()

    slots = {2: 0, 4: 1, 6: 2, 0: 3}

    def down_copy(p, slot):
        return pltpu.make_async_copy(
            down_buf.at[slot], down_hbm.at[pl.ds(2 * p, 2)], down_sem.at[slot]
        )

    def act_copy(p):
        where = pl.ds(pl.multiple_of(2 * rows * p, 2 * rows), 2 * rows)
        return pltpu.make_async_copy(
            act_ref.at[:, where], act_hbm.at[:, where], flush_sem.at[p]
        )

    def feed(k):
        p = (rank ^ k) // 2
        slot = (0, 2, 4, 6).index(k) % 2
        pair = xg[pl.ds(2 * p, 2)].reshape(2 * rows, width)
        gate_pre = mat_nt(pair, wg[...])
        up_pre = mat_nt(pair, wu[...])
        grad_hidden = dhid[p]
        sigma = jax.nn.sigmoid(gate_pre)
        swish = gate_pre * sigma
        grad_gate = (grad_hidden * up_pre * sigma * (1.0 + gate_pre * (1.0 - sigma))).astype(
            jnp.bfloat16
        )
        grad_up = (grad_hidden * swish).astype(jnp.bfloat16)
        part = jnp.dot(grad_gate, wg[...], preferred_element_type=jnp.float32) + jnp.dot(
            grad_up, wu[...], preferred_element_type=jnp.float32
        )
        i = slots[k]
        halves = part.reshape(2, rows, width)
        mine_first = lax.rem(rank, 2) == 0
        mine = jnp.where(mine_first, halves[0], halves[1])
        theirs = jnp.where(mine_first, halves[1], halves[0])
        near_out[1, i] = theirs.astype(jnp.bfloat16)
        near(1, i).start()
        hidden = (swish * up_pre).astype(jnp.bfloat16)
        for kept, value in enumerate((grad_gate, grad_up, hidden)):
            act_ref[kept, pl.ds(pl.multiple_of(2 * rows * p, 2 * rows), 2 * rows)] = value
        act_copy(p).start()
        down = jnp.dot(hidden, wd[...], preferred_element_type=jnp.float32)
        if k in (4, 6):
            down_copy(p, slot).wait()
        down_buf[slot] = down.astype(jnp.bfloat16).reshape(2, rows, width)
        down_copy(p, slot).start()
        near(1, i).wait_recv()
        mine = mine + near_in[1, i].astype(jnp.float32)
        if k:
            far_out[1, i] = mine.astype(jnp.bfloat16)
            far(1, i, k).start()
        else:
            keep[...] = mine

    gather_wait(xg, *sems, (6,))
    feed(0)
    gather_pass(xg, *sems, NEIGHBOURS_FIRST)
    gather_wait(xg, *sems, (7, 8))
    feed(2)
    gather_pass(xg, *sems, DIAGONAL)
    gather_wait(xg, *sems, (9, 10))
    feed(4)
    gather_wait(xg, *sems, (11, 12))
    feed(6)
    xg_copy = pltpu.make_async_copy(xg, xg_hbm, flush_sem.at[ranks // 2])
    xg_copy.start()

    grad = keep[...]
    for i, k in enumerate((2, 4, 6)):
        far(1, i, k).wait_recv()
        grad = grad + far_in[1, i].astype(jnp.float32)
    middle = mid_ref[...]
    inverse = inv_rms(middle)
    gain_ref[...] = jnp.sum(grad * middle * inverse, axis=0, keepdims=True)
    grad_middle = dy[rank].astype(jnp.float32) + norm_back(
        grad, middle, inverse, scale_ref[...]
    )
    dmid_ref[...] = grad_middle
    pm_ref[rank] = grad_middle.astype(jnp.bfloat16)
    sems2 = (ag_send.at[1], ag_recv.at[1])
    gather_start(pm_ref, *sems2)

    def gated_grad(k):
        p = (rank ^ k) // 2
        pair = pm_ref[pl.ds(2 * p, 2)].reshape(2 * rows, width)
        dgated_ref[pl.ds(2 * p, 2)] = mat_nt(pair, wout_ref[...]).reshape(
            2, rows, wout_ref.shape[0]
        )

    gather_wait(pm_ref, *sems2, (6,))
    gated_grad(0)
    gather_pass(pm_ref, *sems2, NEIGHBOURS_FIRST)
    gather_wait(pm_ref, *sems2, (7, 8))
    gated_grad(2)
    gather_wait(pm_ref, *sems2, (9, 10))
    gated_grad(4)
    gather_pass(pm_ref, *sems2, DIAGONAL)
    gather_wait(pm_ref, *sems2, (11, 12))
    gated_grad(6)

    gather_sent(xg, *sems)
    xg_copy.wait()
    for p in range(ranks // 2):
        act_copy(p).wait()
    gather_sent(pm_ref, *sems2)
    for copy in dy_line + xb_line:
        copy.wait()
    for phase in range(2):
        for i in range(4):
            near(phase, i).wait_send()
        for i in range(3):
            far(phase, i, 2).wait_send()
    down_copy(0, 0).wait()
    down_copy(0, 1).wait()


def middle_layer(gated, w_out, x, scale, grad_plane, w_gate, w_up, w_down, collective_id):
    ranks, rows, _ = gated.shape
    planes = lax.axis_size("sp")
    width = x.shape[1]
    hidden = w_gate.shape[0]
    features = w_out.shape[0]
    vmem = pl.BlockSpec(memory_space=pltpu.VMEM)
    hbm = pl.BlockSpec(memory_space=pl.ANY)
    half, full = jnp.bfloat16, jnp.float32
    return pl.pallas_call(
        functools.partial(middle_kernel, planes),
        out_shape=(
            jax.ShapeDtypeStruct((ranks, rows, width), half),
            jax.ShapeDtypeStruct((2, planes - 1, rows, width), half),
            jax.ShapeDtypeStruct((ranks, rows, width), half),
            jax.ShapeDtypeStruct((rows, width), full),
            jax.ShapeDtypeStruct((rows, width), full),
            jax.ShapeDtypeStruct((1, width), full),
            jax.ShapeDtypeStruct((ranks, rows, width), half),
            jax.ShapeDtypeStruct((ranks, rows, features), full),
            jax.ShapeDtypeStruct((3, ranks * rows, hidden), half),
        ),
        in_specs=[vmem, vmem, vmem, vmem, hbm, hbm, hbm, hbm],
        out_specs=(hbm, hbm, hbm, vmem, vmem, vmem, vmem, vmem, hbm),
        scratch_shapes=[
            pltpu.VMEM((ranks, rows, width), half),
            pltpu.VMEM((3, ranks * rows, hidden), half),
            pltpu.SemaphoreType.DMA((ranks // 2 + 1,)),
            pltpu.VMEM((hidden, width), half),
            pltpu.VMEM((hidden, width), half),
            pltpu.VMEM((hidden, width), half),
            pltpu.VMEM((ranks, rows, width), half),
            pltpu.VMEM((ranks // 2, 2 * rows, hidden), full),
            pltpu.VMEM((2, 4, rows, width), half),
            pltpu.VMEM((2, 4, rows, width), half),
            pltpu.VMEM((2, 3, rows, width), half),
            pltpu.VMEM((2, 3, rows, width), half),
            pltpu.VMEM((rows, width), full),
            pltpu.VMEM((2, 2, rows, width), half),
            pltpu.SemaphoreType.DMA((3,)),
            pltpu.SemaphoreType.DMA,
            pltpu.SemaphoreType.DMA((2,)),
            pltpu.SemaphoreType.DMA((2, 4)),
            pltpu.SemaphoreType.DMA((2, 4)),
            pltpu.SemaphoreType.DMA((2, 3)),
            pltpu.SemaphoreType.DMA((2, 3)),
            pltpu.SemaphoreType.DMA((2, GATHER_COPIES)),
            pltpu.SemaphoreType.DMA((2, GATHER_COPIES)),
            pltpu.SemaphoreType.DMA((2, planes - 1)),
            pltpu.SemaphoreType.DMA((2, planes - 1)),
        ],
        compiler_params=pltpu.CompilerParams(
            collective_id=collective_id, has_side_effects=True, vmem_limit_bytes=VMEM_LIMIT
        ),
        name="middle_layer",
    )(gated, w_out, x, scale, grad_plane, w_gate, w_up, w_down)


def feed_weights_kernel(
    planes,
    xp_hbm,
    dp_hbm,
    act_hbm,
    blocks_hbm,
    first_hbm,
    second_hbm,
    down_hbm,
    mid_ref,
    small_ref,
    rows_ref,
    qkv_hbm,
    wg_hbm,
    wu_hbm,
    wd_hbm,
    og_hbm,
    ou_hbm,
    od_hbm,
    h_ref,
    so_ref,
    go_ref,
    sum_hbm,
    more_hbm,
    wg_ref,
    wu_ref,
    wd_ref,
    w_sem,
    og_ref,
    ou_ref,
    od_ref,
    o_sem,
    xbuf,
    dbuf,
    act,
    parts,
    small_buf,
    rows_buf,
    quarter,
    quarters,
    x_sem,
    d_sem,
    act_sem,
    part_sem,
    own_sem,
    ag_send,
    ag_recv,
    line_send,
    line_recv,
    part_send,
    part_recv,
    sum_send,
    sum_recv,
    quarter_sem,
    near_buf,
    out_buf,
    far_buf,
    sib_send,
    sib_recv,
    send_sem,
    recv_sem,
):
    rank, plane = lax.axis_index("fsdp"), lax.axis_index("sp")
    ranks, rows, width = xp_hbm.shape
    part = ranks // 2
    chunk = part * rows
    others = [lax.rem(plane + k, planes) for k in range(1, planes)]
    greet([(rank ^ k, plane) for k in (1, 2, 4, 6)] + [(rank, other) for other in others])

    picks = ((0, 1), (1, 1), (1, 2), (0, 2))
    gathers = [(more_hbm.at[g], ag_send.at[g], ag_recv.at[g]) for g in range(4)]
    own_blocks = [
        pltpu.make_async_copy(blocks_hbm.at[pick], more_hbm.at[g, rank], own_sem.at[g])
        for g, pick in enumerate(picks)
    ]

    def begin(g):
        gather_start(*gathers[g], own=blocks_hbm.at[picks[g]])

    def load(step, start):
        slot = lax.rem(step, 2)
        block = pl.ds(part * lax.rem(step, 2), part)
        group = step // 2
        sources = (
            (xp_hbm.at[block], dp_hbm.at[block]),
            (first_hbm.at[block], second_hbm.at[block]),
            (more_hbm.at[0, block], more_hbm.at[1, block]),
            (more_hbm.at[3, block], more_hbm.at[2, block]),
        )
        for index, (x_from, d_from) in enumerate(sources):
            @pl.when(group == index)
            def _():
                for copy in (
                    pltpu.make_async_copy(x_from, xbuf.at[slot], x_sem.at[slot]),
                    pltpu.make_async_copy(d_from, dbuf.at[slot], d_sem.at[slot]),
                ):
                    if start:
                        copy.start()
                    else:
                        copy.wait()

    def kept(step):
        where = pl.ds(pl.multiple_of(step * chunk, chunk), chunk)
        return pltpu.make_async_copy(act_hbm.at[:, where], act, act_sem)

    scatter = (near_buf, sib_send, sib_recv)
    own_parts = [
        pltpu.make_async_copy(down_hbm.at[rank ^ k], parts.at[i], part_sem.at[i])
        for i, k in enumerate(SCATTER_ORDER)
    ]
    small = [
        peer_copy(
            source,
            buffer.at[k],
            line_send.at[which, k],
            line_recv.at[which, k],
            rank,
            others[k],
        )
        for which, (source, buffer) in enumerate(((small_ref, small_buf), (rows_ref, rows_buf)))
        for k in range(planes - 1)
    ]

    quarter_rows = quarter.shape[0]

    def rows_of(index):
        return pl.ds(pl.multiple_of(index * quarter_rows, quarter_rows), quarter_rows)

    own_quarter = pltpu.make_async_copy(qkv_hbm.at[rows_of(plane)], quarter, quarter_sem.at[0])
    own_sum = pltpu.make_async_copy(quarter, sum_hbm.at[rows_of(plane)], quarter_sem.at[1])
    partials = [
        peer_copy(
            qkv_hbm.at[rows_of(others[k])],
            quarters.at[k],
            part_send.at[k],
            part_recv.at[k],
            rank,
            others[k],
        )
        for k in range(planes - 1)
    ]
    sums = [
        peer_copy(
            quarter,
            sum_hbm.at[rows_of(plane)],
            sum_send.at[k],
            sum_recv.at[k],
            rank,
            others[k],
        )
        for k in range(planes - 1)
    ]

    totals = ((og_ref, og_hbm), (ou_ref, ou_hbm), (od_ref, od_hbm))
    load(0, True)
    kept(0).start()
    weights = [
        pltpu.make_async_copy(source, target, w_sem.at[index])
        for index, (source, target) in enumerate(
            ((wg_hbm, wg_ref), (wu_hbm, wu_ref), (wd_hbm, wd_ref))
        )
    ]
    for copy in weights:
        copy.start()
    own_quarter.start()
    for copy in own_blocks + small + own_parts + partials:
        copy.start()
    begin(0)
    for i in range(4):
        scatter_near(down_hbm, i, *scatter).start()

    @pl.loop(0, 2 * planes)
    def _(step):
        @pl.when(step == 1)
        def _():
            kept(1).start()
            begin(1)

        @pl.when(step == 2)
        def _():
            for copy in weights:
                copy.wait()
            gather_pass(*gathers[0], NEIGHBOURS_FIRST)

        @pl.when(step == 3)
        def _():
            gather_pass(*gathers[0], DIAGONAL)
            gather_pass(*gathers[1], NEIGHBOURS_FIRST)
            begin(2)
            for i, k in enumerate(SCATTER_ORDER):
                own_parts[i].wait()
                scatter_near(down_hbm, i, *scatter).wait_recv()
                joined = parts[i].astype(jnp.float32) + near_buf[i].astype(jnp.float32)
                if k:
                    out_buf[i] = joined.astype(out_buf.dtype)
                else:
                    parts[i] = joined.astype(parts.dtype)

        @pl.when(step == 4)
        def _():
            gather_pass(*gathers[1], DIAGONAL)
            begin(3)
            for g in (0, 1):
                gather_wait(*gathers[g], FROM_SIBLING)
                own_blocks[g].wait()
            load(step, True)
            own_quarter.wait()
            total = quarter[...].astype(jnp.float32)
            for k in range(planes - 1):
                partials[k].wait()
                total = total + quarters[k].astype(jnp.float32)
            quarter[...] = total.astype(quarter.dtype)
            own_sum.start()
            for copy in sums:
                copy.start()

        @pl.when(step == 5)
        def _():
            gather_pass(*gathers[2], NEIGHBOURS_FIRST)
            gather_pass(*gathers[3], NEIGHBOURS_FIRST)

        @pl.when(step == 6)
        def _():
            for g in (2, 3):
                gather_pass(*gathers[g], DIAGONAL)
            for i in range(3):
                scatter_far(i, out_buf, far_buf, send_sem, recv_sem).start()
            for g in (2, 3):
                gather_wait(*gathers[g], FROM_SIBLING)
                own_blocks[g].wait()
            load(step, True)

        load(step, False)

        @pl.when((lax.rem(step, 2) == 0) | (step == 1))
        def _():
            load(step + 1, True)

        slot = lax.rem(step, 2)
        normed = xbuf[slot].reshape(chunk, width)
        grad = dbuf[slot].reshape(chunk, width)

        own = step < 2

        @pl.when(own)
        def _():
            kept(0).wait()

        @pl.when(jnp.logical_not(own))
        def _():
            gate_pre = mat_nt(normed, wg_ref[...])
            up_pre = mat_nt(normed, wu_ref[...])
            grad_hidden = mat_nt(grad, wd_ref[...])
            sigma = jax.nn.sigmoid(gate_pre)
            swish = gate_pre * sigma
            act[0] = (grad_hidden * up_pre * sigma * (1.0 + gate_pre * (1.0 - sigma))).astype(
                jnp.bfloat16
            )
            act[1] = (grad_hidden * swish).astype(jnp.bfloat16)
            act[2] = (swish * up_pre).astype(jnp.bfloat16)

        @pl.when(step == 0)
        def _():
            for ref in (og_ref, ou_ref, od_ref):
                ref[...] = jnp.zeros_like(ref)

        for index, other in ((0, normed), (1, normed), (2, grad)):
            source, target = totals[index]
            source[...] += mat_tn(act[index], other)

            @pl.when(step == 2 * planes - 1)
            def _():
                pltpu.make_async_copy(source, target, o_sem.at[index]).start()

    output = mid_ref[...] + parts[3].astype(jnp.float32)
    for i in range(3):
        scatter_far(i, out_buf, far_buf, send_sem, recv_sem).wait()
        output = output + far_buf[i].astype(jnp.float32)
    h_ref[...] = output.astype(h_ref.dtype)
    for copy in small + sums:
        copy.wait()
    own_sum.wait()
    total, gate_rows = small_ref[...], rows_ref[...]
    for k in range(planes - 1):
        total = total + small_buf[k]
        gate_rows = gate_rows + rows_buf[k]
    so_ref[...] = total
    go_ref[...] = gate_rows
    for i in range(4):
        scatter_near(down_hbm, i, *scatter).wait_send()
    for gather in gathers:
        gather_sent(*gather)
    for index, (source, target) in enumerate(totals):
        pltpu.make_async_copy(source, target, o_sem.at[index]).wait()


def feed_weights(plane_x, plane_grad, acts, blocks, first, second, down, middle, small, gate_rows, qkv_part, w_gate, w_up, w_down, collective_id):
    ranks, rows, width = plane_x.shape
    planes = lax.axis_size("sp")
    hidden = w_gate.shape[0]
    vmem = pl.BlockSpec(memory_space=pltpu.VMEM)
    hbm = pl.BlockSpec(memory_space=pl.ANY)
    tokens = planes * ranks * rows
    half, full = plane_x.dtype, jnp.float32
    return pl.pallas_call(
        functools.partial(feed_weights_kernel, planes),
        in_specs=[hbm] * 7 + [vmem] * 3 + [hbm] * 4,
        out_specs=(hbm,) * 3 + (vmem,) * 3 + (hbm, hbm),
        out_shape=[jax.ShapeDtypeStruct(w_gate.shape, full)] * 3
        + [
            jax.ShapeDtypeStruct((rows, width), half),
            jax.ShapeDtypeStruct(small.shape, full),
            jax.ShapeDtypeStruct(gate_rows.shape, full),
            jax.ShapeDtypeStruct(qkv_part.shape, half),
            jax.ShapeDtypeStruct((4, ranks, rows, width), half),
        ],
        scratch_shapes=[pltpu.VMEM(w_gate.shape, half)] * 3
        + [
            pltpu.SemaphoreType.DMA((3,)),
        ]
        + [pltpu.VMEM(w_gate.shape, full)] * 3
        + [
            pltpu.SemaphoreType.DMA((3,)),
            pltpu.VMEM((2, ranks // 2, rows, width), half),
            pltpu.VMEM((2, ranks // 2, rows, width), half),
            pltpu.VMEM((3, ranks // 2 * rows, hidden), half),
            pltpu.VMEM((4, rows, width), half),
            pltpu.VMEM((planes - 1,) + small.shape, full),
            pltpu.VMEM((planes - 1,) + gate_rows.shape, full),
            pltpu.VMEM((qkv_part.shape[0] // planes, width), half),
            pltpu.VMEM((planes - 1, qkv_part.shape[0] // planes, width), half),
            pltpu.SemaphoreType.DMA((2,)),
            pltpu.SemaphoreType.DMA((2,)),
            pltpu.SemaphoreType.DMA,
            pltpu.SemaphoreType.DMA((4,)),
            pltpu.SemaphoreType.DMA((4,)),
            pltpu.SemaphoreType.DMA((4, GATHER_COPIES)),
            pltpu.SemaphoreType.DMA((4, GATHER_COPIES)),
            pltpu.SemaphoreType.DMA((2, planes - 1)),
            pltpu.SemaphoreType.DMA((2, planes - 1)),
        ]
        + [pltpu.SemaphoreType.DMA((planes - 1,))] * 4
        + [
            pltpu.SemaphoreType.DMA((2,)),
        ]
        + scatter_scratch(rows, width, half),
        cost_estimate=pl.CostEstimate(
            flops=12 * tokens * w_gate.size,
            bytes_accessed=4 * tokens * width + 18 * w_gate.size,
            transcendentals=tokens * w_gate.shape[0],
        ),
        compiler_params=pltpu.CompilerParams(
            collective_id=collective_id, has_side_effects=True, vmem_limit_bytes=VMEM_LIMIT
        ),
        name="feed_weights",
    )(plane_x, plane_grad, acts, blocks, first, second, down, middle, small, gate_rows, qkv_part, w_gate, w_up, w_down)[:7]


def front_kernel(
    planes,
    lengths_ref,
    x_ref,
    small_ref,
    w_ref,
    wg_ref,
    dyo_ref,
    q_ref,
    kv_ref,
    dy_ref,
    xg_hbm,
    xa_hbm,
    raw_hbm,
    gate_ref,
    attn_ref,
    ffn_ref,
    head_ref,
    cos_ref,
    sin_ref,
    xg,
    xa_ref,
    raw_ref,
    flush_sem,
    nat,
    gains,
    small_send,
    small_recv,
    ag_send,
    ag_recv,
    own_sem,
    local_sem,
    q_send,
    q_recv,
    kv_send,
    kv_recv,
    line_send,
    line_recv,
):
    rank, plane = lax.axis_index("fsdp"), lax.axis_index("sp")
    ranks, rows, width = xg.shape
    pair_rows = 2 * rows
    chip = rank // 2
    greet_line(ranks, planes)
    own_block = pltpu.make_async_copy(dyo_ref, dy_ref.at[rank], own_sem)
    own_block.start()
    small = []
    for k in range(1, ranks):
        copy = peer_copy(
            small_ref, gains.at[rank], small_send.at[k - 1], small_recv.at[k - 1], rank ^ k, plane
        )
        copy.start()
        small.append(copy)
    sems = (ag_send.at[0], ag_recv.at[0])
    gather_start(xg, *sems, own=x_ref)
    xg[rank] = x_ref[...]
    gains[rank] = small_ref[...]

    half = HEAD_DIM // 2
    lane = lax.broadcasted_iota(jnp.int32, (1, HEAD_DIM), 1)
    step = lax.rem(lane, half).astype(jnp.float32)
    frequency = jnp.exp(-math.log(ROPE_BASE) * 2.0 * step / HEAD_DIM)
    sign = jnp.where(lane < half, -1.0, 1.0)

    @pl.loop(0, ranks)
    def _(block):
        tokens = (block * planes + plane) * rows + lax.broadcasted_iota(jnp.int32, (rows, 1), 0)
        position = tokens - row_starts(lengths_ref, tokens)
        angles = position.astype(jnp.float32) * frequency
        where = pl.ds(pl.multiple_of(block * rows, rows), rows)
        cos_ref[where] = jnp.cos(angles)
        sin_ref[where] = jnp.sin(angles) * sign

    for copy in small:
        copy.wait_recv()
    head_q, head_k = gains[0, 4:5], gains[0, 5:6]
    for r in range(1, ranks):
        head_q = head_q + gains[r, 4:5]
        head_k = head_k + gains[r, 5:6]
    head_ref[...] = jnp.where(rank < ranks // 2, head_q, head_k)
    for r in range(ranks):
        for i in range(2):
            columns = slice((2 * r + i) * HEAD_DIM, (2 * r + i + 1) * HEAD_DIM)
            attn_ref[:, columns] = gains[r, i : i + 1]
            ffn_ref[:, columns] = gains[r, 2 + i : 3 + i]

    def token_rows(p):
        return pl.ds(pl.multiple_of(p * pair_rows, pair_rows), pair_rows)

    def q_copy(m, p, to):
        return peer_copy(
            nat.at[pl.ds(2 * m, 2), token_rows(p)],
            q_ref.at[:, token_rows(p)],
            q_send.at[m, p],
            q_recv.at[p],
            to,
            plane,
        )

    def kv_copy(m, which, p, to):
        return peer_copy(
            nat.at[m, token_rows(p)],
            kv_ref.at[plane, which, token_rows(p)],
            kv_send.at[m, p],
            kv_recv.at[which, p],
            to,
            plane,
        )

    def q_local(p):
        return pltpu.make_async_copy(
            nat.at[pl.ds(0, 2), token_rows(p)], q_ref.at[:, token_rows(p)], local_sem.at[p]
        )

    def kv_local(m, which, p):
        return pltpu.make_async_copy(
            nat.at[m, token_rows(p)], kv_ref.at[plane, which, token_rows(p)], local_sem.at[p]
        )

    def flush(p):
        pair = pl.ds(2 * p, 2)
        return [
            pltpu.make_async_copy(xg.at[pair], xg_hbm.at[pair], flush_sem.at[0, p]),
            pltpu.make_async_copy(xa_ref.at[pair], xa_hbm.at[pair], flush_sem.at[1, p]),
            pltpu.make_async_copy(
                raw_ref.at[token_rows(p)], raw_hbm.at[token_rows(p)], flush_sem.at[2, p]
            ),
        ]

    def process(k):
        p = chip ^ (k // 2)
        inputs = xg[pl.ds(2 * p, 2)].reshape(pair_rows, width).astype(jnp.float32)
        normed = (inputs * inv_rms(inputs) * attn_ref[...]).astype(jnp.bfloat16)
        xa_ref[pl.ds(2 * p, 2)] = normed.reshape(2, rows, width)
        projected = mat_nt(normed, w_ref[...])
        raw_ref[token_rows(p)] = projected
        for copy in flush(p):
            copy.start()
        logits = mat_nt(normed, wg_ref[...])
        for head in range(gate_ref.shape[0]):
            gate_ref[head, token_rows(p)] = logits[:, head : head + 1]
        cosine, sine = cos_ref[token_rows(p)], sin_ref[token_rows(p)]
        for m in range(4):
            head = projected[:, m * HEAD_DIM : (m + 1) * HEAD_DIM]
            scaled = head * inv_rms(head) * head_ref[...]
            turned = scaled * cosine + pltpu.roll(scaled, half, 1) * sine
            nat[m, token_rows(p)] = jnp.where(rank >= 6, head, turned).astype(jnp.bfloat16)

        @pl.when(rank < 4)
        def _():
            for m in range(2):
                @pl.when(2 * rank + m != rank)
                def _():
                    q_copy(m, p, 2 * rank + m).start()

        @pl.when(rank == 0)
        def _():
            q_local(p).start()

        for which in range(2):
            first = 4 + 2 * which

            @pl.when((rank == first) | (rank == first + 1))
            def _():
                for m in range(4):
                    to = 4 * (rank - first) + m

                    @pl.when(to != rank)
                    def _():
                        kv_copy(m, which, p, to).start()

            @pl.when(rank == first + 1)
            def _():
                kv_local((first + 1) % 4, which, p).start()

    def line_piece(origin, which, p, side, j, to):
        piece = kv_ref.at[origin, which, token_rows(p)]
        return peer_copy(
            piece,
            piece,
            line_send.at[side, j, which, p],
            line_recv.at[side, j, which, p],
            rank,
            to,
        )

    def origin_of(side, j):
        return plane - j if side == 0 else plane + j

    def next_of(side):
        return plane + 1 if side == 0 else plane - 1

    def line_go(which, p, j):
        if j == 0:
            @pl.when(rank == 5 + 2 * which)
            def _():
                kv_local((5 + 2 * which) % 4, which, p).wait()

            @pl.when(rank != 5 + 2 * which)
            def _():
                kv_copy(0, which, p, 0).wait_recv()

        for side in range(2):
            if j:
                arrives = (plane >= j) if side == 0 else (plane + j <= planes - 1)

                @pl.when(arrives)
                def _():
                    line_piece(origin_of(side, j), which, p, side, j - 1, plane).wait_recv()

            if j < planes - 1:
                @pl.when(line_sends(planes, plane, j, side))
                def _():
                    line_piece(origin_of(side, j), which, p, side, j, next_of(side)).start()

    slots = (((0, 2), (1, 3)), ((0, 3), (1, 2)), ((0, 0), (1, 1)), ((0, 1), (1, 0)))

    def slot_go(slot, j):
        for which, p in slots[slot]:
            line_go(which, p, j)

    gather_wait(xg, *sems, (6,))
    process(0)
    slot_go(0, 0)
    gather_pass(xg, *sems, NEIGHBOURS_FIRST)
    gather_wait(xg, *sems, (7, 8))
    process(2)
    slot_go(0, 1)
    gather_wait(xg, *sems, (9, 10))
    process(4)
    gather_pass(xg, *sems, DIAGONAL)
    slot_go(1, 0)
    slot_go(0, 2)
    gather_wait(xg, *sems, (11, 12))
    process(6)
    sems2 = (ag_send.at[1], ag_recv.at[1])
    slot_go(2, 0)
    slot_go(1, 1)
    slot_go(3, 0)
    gather_start(dy_ref, *sems2, own=dyo_ref)
    slot_go(0, 3)
    slot_go(1, 2)
    slot_go(2, 1)
    slot_go(3, 1)
    slot_go(1, 3)
    slot_go(2, 2)
    gather_pass(dy_ref, *sems2, NEIGHBOURS_FIRST)
    slot_go(3, 2)
    slot_go(2, 3)
    gather_pass(dy_ref, *sems2, DIAGONAL)
    slot_go(3, 3)
    gather_wait(dy_ref, *sems2, FROM_SIBLING)

    for p in range(ranks // 2):
        @pl.when(rank == 0)
        def _():
            q_local(p).wait()

        @pl.when(rank != 0)
        def _():
            q_copy(0, p, 0).wait_recv()

    for p in range(ranks // 2):
        for copy in flush(p):
            copy.wait()
    for copy in small:
        copy.wait_send()
    gather_sent(xg, *sems)
    gather_sent(dy_ref, *sems2)
    own_block.wait()
    for p in range(ranks // 2):
        @pl.when(rank < 4)
        def _():
            for m in range(2):
                @pl.when(2 * rank + m != rank)
                def _():
                    q_copy(m, p, 0).wait_send()

        for which in range(2):
            first = 4 + 2 * which

            @pl.when((rank == first) | (rank == first + 1))
            def _():
                for m in range(4):
                    @pl.when(4 * (rank - first) + m != rank)
                    def _():
                        kv_copy(m, which, p, 0).wait_send()

            for j in range(planes - 1):
                for side in range(2):
                    @pl.when(line_sends(planes, plane, j, side))
                    def _():
                        line_piece(0, which, p, side, j, next_of(side)).wait_send()


def front(lengths, x, small, w_qkv, w_head_gate, grad, collective_id):
    rows, width = x.shape
    ranks, planes = lax.axis_size("fsdp"), lax.axis_size("sp")
    tokens = ranks * rows
    heads = w_head_gate.shape[0]
    vmem = pl.BlockSpec(memory_space=pltpu.VMEM)
    hbm = pl.BlockSpec(memory_space=pl.ANY)
    half, full = jnp.bfloat16, jnp.float32
    pairs = ranks // 2
    return pl.pallas_call(
        functools.partial(front_kernel, planes),
        out_shape=(
            jax.ShapeDtypeStruct((2, tokens, HEAD_DIM), half),
            jax.ShapeDtypeStruct((planes, 2, tokens, HEAD_DIM), half),
            jax.ShapeDtypeStruct((ranks, rows, width), half),
            jax.ShapeDtypeStruct((ranks, rows, width), half),
            jax.ShapeDtypeStruct((ranks, rows, width), half),
            jax.ShapeDtypeStruct((tokens, w_qkv.shape[0]), full),
            jax.ShapeDtypeStruct((heads, tokens, 1), full),
            jax.ShapeDtypeStruct((1, width), full),
            jax.ShapeDtypeStruct((1, width), full),
            jax.ShapeDtypeStruct((1, HEAD_DIM), full),
            jax.ShapeDtypeStruct((tokens, HEAD_DIM), full),
            jax.ShapeDtypeStruct((tokens, HEAD_DIM), full),
        ),
        in_specs=[pl.BlockSpec(memory_space=pltpu.SMEM), vmem, vmem, vmem, vmem, hbm],
        out_specs=(hbm,) * 6 + (vmem,) * 6,
        scratch_shapes=[
            pltpu.VMEM((ranks, rows, width), half),
            pltpu.VMEM((ranks, rows, width), half),
            pltpu.VMEM((tokens, w_qkv.shape[0]), full),
            pltpu.SemaphoreType.DMA((3, pairs)),
            pltpu.VMEM((4, tokens, HEAD_DIM), half),
            pltpu.VMEM((ranks,) + small.shape, small.dtype),
            pltpu.SemaphoreType.DMA((ranks - 1,)),
            pltpu.SemaphoreType.DMA((ranks - 1,)),
            pltpu.SemaphoreType.DMA((2, GATHER_COPIES)),
            pltpu.SemaphoreType.DMA((2, GATHER_COPIES)),
            pltpu.SemaphoreType.DMA,
            pltpu.SemaphoreType.DMA((pairs,)),
            pltpu.SemaphoreType.DMA((2, pairs)),
            pltpu.SemaphoreType.DMA((pairs,)),
            pltpu.SemaphoreType.DMA((4, pairs)),
            pltpu.SemaphoreType.DMA((2, pairs)),
            pltpu.SemaphoreType.DMA((2, planes - 1, 2, pairs)),
            pltpu.SemaphoreType.DMA((2, planes - 1, 2, pairs)),
        ],
        compiler_params=pltpu.CompilerParams(
            collective_id=collective_id, has_side_effects=True, vmem_limit_bytes=VMEM_LIMIT
        ),
        name="front",
    )(lengths, x, small, w_qkv, w_head_gate, grad)


def local_planes(
    hidden_in,
    grad_out,
    lengths,
    attn_gain,
    w_qkv,
    w_head_gate,
    q_gain,
    k_gain,
    w_out,
    ffn_gain,
    w_gate,
    w_up,
    w_down,
):
    ranks, planes = lax.axis_size("fsdp"), lax.axis_size("sp")
    rank, plane = lax.axis_index("fsdp"), lax.axis_index("sp")
    rows, model_width = hidden_in.shape
    tokens = ranks * rows
    own_heads = w_qkv.shape[0] // HEAD_DIM
    local_heads = HEADS // ranks

    thin = q_gain.shape[0]
    spread = jnp.zeros((2, HEAD_DIM), attn_gain.dtype)
    spread = lax.dynamic_update_slice(
        spread, jnp.stack([q_gain, k_gain]), (jnp.int32(0), rank * thin)
    )
    own_gains = jnp.concatenate(
        [
            attn_gain.reshape(-1, HEAD_DIM),
            ffn_gain.reshape(-1, HEAD_DIM),
            spread,
            jnp.zeros((2, HEAD_DIM), attn_gain.dtype),
        ],
        axis=0,
    ).astype(jnp.float32)
    (
        query,
        kv,
        plane_grad,
        gathered,
        normed_a,
        projected,
        gate_logit,
        attn_scale,
        ffn_scale,
        head_scale,
        cosine,
        sine,
    ) = front(lengths, hidden_in, own_gains, w_qkv, w_head_gate, grad_out, 0)
    attended, total, gated = attend(lengths, query, kv, gate_logit, rows)
    plane_b, line_blocks, down_part, middle, grad_middle, grad_ffn_gain_local, plane_mid, grad_gated, acts = middle_layer(
        gated.reshape(ranks, rows, -1),
        w_out,
        hidden_in,
        ffn_scale,
        plane_grad,
        w_gate,
        w_up,
        w_down,
        2,
    )
    grad_gated = grad_gated.reshape(tokens, -1)
    grad_query, grad_kv, gate_grad = attend_back(
        lengths, query, kv, gate_logit, attended, total, grad_gated, rows
    )
    back, out_part, first_grad = return_heads(
        grad_query, grad_kv, gated, plane_mid, line_blocks, 6
    )
    reduced = lax.psum_scatter(out_part, "sp", scatter_dimension=0, tiled=True)
    grad_a_part, qkv_part, gate_rows, attn_terms, head_terms, first_b = projection_back(
        back,
        projected,
        cosine,
        sine,
        normed_a,
        gathered,
        gate_grad,
        w_qkv,
        w_head_gate,
        head_scale,
        line_blocks,
        8,
    )
    reduced, grad_a_part = lax.optimization_barrier((reduced, grad_a_part))
    out_sum = lax.all_gather(reduced, "sp", axis=0, tiled=True)
    grad_in, gain_sums = scatter_gains(
        grad_a_part,
        attn_terms,
        grad_ffn_gain_local,
        head_terms,
        hidden_in,
        attn_scale,
        grad_middle,
        7,
    )
    out_sum, gain_sums = lax.optimization_barrier((out_sum, gain_sums))
    grad_w_out = out_sum.astype(jnp.float32)
    grad_w_gate, grad_w_up, grad_w_down, hidden_out, gain_total, grad_w_head_gate, qkv_total = feed_weights(
        plane_b,
        plane_grad,
        acts,
        line_blocks,
        first_b,
        first_grad,
        down_part,
        middle,
        gain_sums,
        gate_rows,
        qkv_part,
        w_gate,
        w_up,
        w_down,
        4,
    )
    grad_w_qkv = qkv_total.astype(jnp.float32)
    grad_attn_gain = gain_total[:2].reshape(-1)
    grad_ffn_gain = gain_total[2:4].reshape(-1)
    grad_q_gain = lax.dynamic_slice_in_dim(gain_total[4], rank * thin, thin)
    grad_k_gain = lax.dynamic_slice_in_dim(gain_total[5], rank * thin, thin)
    return (
        hidden_out,
        grad_in,
        grad_attn_gain,
        grad_w_qkv,
        grad_w_head_gate,
        grad_q_gain,
        grad_k_gain,
        grad_w_out,
        grad_ffn_gain,
        grad_w_gate,
        grad_w_up,
        grad_w_down,
    )


def solution(mesh):
    planar = mesh.shape["fsdp"] == 8 and mesh.shape["sp"] == 4
    return jax.shard_map(
        local_planes if planar else local,
        mesh=mesh,
        in_specs=(
            P(("fsdp", "sp"), None),
            P(("fsdp", "sp"), None),
            P(),
            P("fsdp"),
            P("fsdp", None),
            P("fsdp", None),
            P("fsdp"),
            P("fsdp"),
            P("fsdp", None),
            P("fsdp"),
            P("fsdp", None),
            P("fsdp", None),
            P("fsdp", None),
        ),
        out_specs=(
            P(("fsdp", "sp"), None),
            P(("fsdp", "sp"), None),
            P("fsdp"),
            P("fsdp", None),
            P("fsdp", None),
            P("fsdp"),
            P("fsdp"),
            P("fsdp", None),
            P("fsdp"),
            P("fsdp", None),
            P("fsdp", None),
            P("fsdp", None),
        ),
        check_vma=False,
    )
```
